32 devices in a mesh: wt: 4 (over y, core), ctx: 8 (over z, x).
Axes of the slice: x: 2, y: 2, z: 4, core: 2. Of those that a mesh axis runs over, the one named last changes fastest.
Arguments:
- tokens: bfloat16 [4, 2048, 768], P('wt', 'ctx'), may hold values from -6 to 6
- first_values: bfloat16 [4, 2048, 384], P('wt', 'ctx'), may hold values from -6 to 6
- cotangent: bfloat16 [4, 2048, 768], P('wt', 'ctx'), may hold values from -6 to 6
- deal: int32 [8], replicated, may hold values from 0 to 7, each once
- w_qkv: bfloat16 [768, 1920], P('wt'), may hold values from -0.21875 to 0.21875
- bias_qv: bfloat16 [1152], P('wt'), may hold values from -3 to 3
- w_out: bfloat16 [768, 768], P('wt'), may hold values from -6 to 6
- bias_out: bfloat16 [768], P('wt'), may hold values from -3 to 3
- gain_one: bfloat16 [768], P('wt'), may hold values from 0.25 to 1.75
- shift_one: bfloat16 [768], P('wt'), may hold values from -3 to 3
- gain_two: bfloat16 [768], P('wt'), may hold values from 0.25 to 1.75
- shift_two: bfloat16 [768], P('wt'), may hold values from -3 to 3
- w_up: bfloat16 [768, 3072], P('wt'), may hold values from -0.21875 to 0.21875
- bias_up: bfloat16 [3072], P('wt'), may hold values from -3 to 3
- w_down: bfloat16 [3072, 768], P('wt'), may hold values from -0.109375 to 0.109375
- bias_down: bfloat16 [768], P('wt'), may hold values from -3 to 3
Outputs:
- layer_out: bfloat16 [4, 2048, 768], P('wt', 'ctx')
- grad_tokens: float32 [4, 2048, 768], P('wt', 'ctx')
- grad_first: float32 [4, 2048, 384], P('wt', 'ctx')
- grad_qkv: float32 [768, 1920], P('wt')
- grad_bias_qv: float32 [1152], P('wt')
- grad_out: float32 [768, 768], P('wt')
- grad_bias_out: float32 [768], P('wt')
- grad_gain_one: float32 [768], P('wt')
- grad_shift_one: float32 [768], P('wt')
- grad_gain_two: float32 [768], P('wt')
- grad_shift_two: float32 [768], P('wt')
- grad_up: float32 [768, 3072], P('wt')
- grad_bias_up: float32 [3072], P('wt')
- grad_down: float32 [3072, 768], P('wt')
- grad_bias_down: float32 [768], P('wt')
The draws below stay inside these ranges and needn't reach their ends.
Inputs may be any that keep to these rules, and one draw needn't show every extreme that they name: deal holds each pair number once.
All inputs are finite; a program needn't handle non-finite values.
Results may differ from the reference program's by a relative error of at most 0.02.
Values may be sent and summed in bfloat16 or wider, within the bound.
A program may use at most 256 MiB of HBM per device.

```python
import jax
import jax.numpy as jnp
from jax import lax

D = 768
HEADS = 12
HEAD_DIM = 64
FF = 3072
BLK = 128
KEY_BLOCK = 1024
SEQ_LEN = 2048
PAIRS = 8
SEQS = 4


def steps_of(rng, extent, pieces, low, largest):
    def one(axis_at, shards_of):
        heights = jax.random.uniform(jax.random.fold_in(jax.random.fold_in(rng, 6), axis_at), (shards_of,), jnp.float32, low / len(pieces), largest / len(pieces))
        return jnp.repeat(jnp.exp(heights), extent[axis_at] // shards_of).reshape((-1,) + (1,) * (len(extent) - axis_at - 1))

    loudness = one(*pieces[0])
    for cut in pieces[1:]:
        loudness = loudness * one(*cut)
    return loudness


def gaussian(key, shape, scale, reach, shards=(), held_as=jnp.bfloat16):
    array = scale * jax.random.normal(key, shape, jnp.float32)
    if shards:
        array = array * steps_of(key, shape, shards, -0.22, 0.18)
    return jnp.clip(array, -reach, reach).astype(held_as)


def setup_inputs(seed: int = 0) -> dict:
    arg_keys = jax.random.split(jax.random.key(seed), 17)
    tokens = gaussian(arg_keys[0], (SEQS, SEQ_LEN, D), 1.0, 6.0, ((0, 4), (1, 8)))
    first_values = gaussian(arg_keys[1], (SEQS, SEQ_LEN, D // 2), 1.0, 6.0, ((0, 4), (1, 8)))
    cotangent = gaussian(arg_keys[2], (SEQS, SEQ_LEN, D), 1.0, 6.0, ((0, 4), (1, 8)))
    deal = jax.random.permutation(arg_keys[3], PAIRS).astype(jnp.int32)
    w_qkv = gaussian(arg_keys[4], (D, 5 * D // 2), D ** -0.5, 0.21875, ((0, 4),))
    bias_qv = gaussian(arg_keys[5], (3 * D // 2,), 0.5, 3.0, ((0, 4),))
    w_out = gaussian(arg_keys[6], (D, D), (max(1, SEQ_LEN // (5 * D)) ** 0.5), 6.0, ((0, 4),))
    bias_out = gaussian(arg_keys[7], (D,), 0.5, 3.0, ((0, 4),))
    gain_one = jnp.clip(1.0 + 0.15 * jax.random.normal(arg_keys[8], (D,), jnp.float32), 0.25, 1.75).astype(jnp.bfloat16)
    shift_one = gaussian(arg_keys[9], (D,), 0.5, 3.0, ((0, 4),))
    gain_two = jnp.clip(1.0 + 0.15 * jax.random.normal(arg_keys[10], (D,), jnp.float32), 0.25, 1.75).astype(jnp.bfloat16)
    shift_two = gaussian(arg_keys[11], (D,), 0.5, 3.0, ((0, 4),))
    w_up = gaussian(arg_keys[12], (D, FF), D ** -0.5, 0.21875, ((0, 4),))
    bias_up = gaussian(arg_keys[13], (FF,), 0.5, 3.0, ((0, 4),))
    w_down = gaussian(arg_keys[14], (FF, D), FF ** -0.5, 0.109375, ((0, 4),))
    bias_down = gaussian(arg_keys[15], (D,), 0.5, 3.0, ((0, 4),))
    return {"tokens": tokens, "first_values": first_values, "cotangent": cotangent, "deal": deal, "w_qkv": w_qkv, "bias_qv": bias_qv, "w_out": w_out, "bias_out": bias_out, "gain_one": gain_one, "shift_one": shift_one, "gain_two": gain_two, "shift_two": shift_two, "w_up": w_up, "bias_up": bias_up, "w_down": w_down, "bias_down": bias_down}


EPS = 1e-05
SLOPE = 0.7978845608028654
CUBIC = 0.044715
NEG = -1e+30

@jax.custom_vjp
def low(v):
    return lax.optimization_barrier(v.astype(jnp.bfloat16)).astype(jnp.float32)

@jax.custom_vjp
def low_back(v):
    return v

def low_keep(v):
    return (low(v), None)

def low_pass(kept, grad):
    return (grad,)

def back_keep(v):
    return (v, None)

def back_low(kept, grad):
    return (low(grad),)
low.defvjp(low_keep, low_pass)
low_back.defvjp(back_keep, back_low)

def layer_norm(value, gain, shift):
    mean = lax.optimization_barrier(jnp.mean(value, axis=-1, keepdims=True))
    centred = value - mean
    inverse = lax.rsqrt(lax.optimization_barrier(jnp.mean(centred * centred, axis=-1, keepdims=True)) + EPS)
    return centred * inverse * gain + shift

def gelu_tanh(value):
    return 0.5 * value * (1.0 + jnp.tanh(SLOPE * (value + CUBIC * value * value * value)))

def mat(left, right):
    return jnp.dot(left, right, precision=lax.Precision.HIGHEST, preferred_element_type=jnp.float32)

def dealt_blocks(deal):
    count = deal.shape[0] * 2
    pairs = jnp.repeat(deal, 2)
    parity = jnp.arange(count, dtype=jnp.int32) % 2
    return jnp.where(parity == 0, pairs, count - 1 - pairs).astype(jnp.int32)

def forward(inputs, first, params, block_of_row):
    qkv_w, qv_b, out_w, out_b, gain_a, shift_a, gain_b, shift_b, up_w, up_b, down_w, down_b = params
    length, width = inputs.shape
    scale = HEAD_DIM ** (-0.5)
    normed = low(layer_norm(inputs, gain_a, shift_a))
    projected = mat(normed, qkv_w)
    query = low_back(low(projected[:, :width] + qv_b[:width]))
    key = low_back(low(projected[:, width:2 * width]))
    fresh = low_back(low(projected[:, 2 * width:] + qv_b[width:]))
    values = jnp.concatenate([fresh, first], axis=1)
    key_heads = key.reshape(length, HEADS, HEAD_DIM)
    value_heads = values.reshape(length, HEADS, HEAD_DIM)
    count = length // KEY_BLOCK
    query_blocks = query.reshape(count, KEY_BLOCK, HEADS, HEAD_DIM)
    id_blocks = block_of_row.reshape(count, KEY_BLOCK)

    def attend(pair):
        query_part, ids = pair
        scores = jnp.einsum('qhd,khd->hqk', query_part, key_heads, precision=lax.Precision.HIGHEST)
        scores = low_back(scores * scale)
        allowed = block_of_row[None, :] <= ids[:, None]
        scores = jnp.where(allowed[None], scores, NEG)
        probs = jax.nn.softmax(scores, axis=-1)
        return jnp.einsum('hqk,khd->qhd', low(probs), value_heads, precision=lax.Precision.HIGHEST)
    attended = lax.map(jax.checkpoint(attend), (query_blocks, id_blocks)).reshape(length, width)
    attended = low_back(low(attended))
    branch = low_back(mat(attended, out_w) + out_b)
    mid = inputs + branch
    normed_two = low(layer_norm(mid, gain_b, shift_b))
    up_pre = low_back(mat(normed_two, up_w) + up_b)
    activated = low(gelu_tanh(up_pre))
    mlp = low_back(mat(activated, down_w) + down_b)
    return mid + mlp

def reference(tokens, first_values, cotangent, deal, w_qkv, bias_qv, w_out, bias_out, gain_one, shift_one, gain_two, shift_two, w_up, bias_up, w_down, bias_down):
    params = tuple((p.astype(jnp.float32) for p in (w_qkv, bias_qv, w_out, bias_out, gain_one, shift_one, gain_two, shift_two, w_up, bias_up, w_down, bias_down)))
    block_of_row = jnp.repeat(dealt_blocks(deal), BLK)

    def one(totals, seq):
        inputs, first, grad_in = seq
        inputs = inputs.astype(jnp.float32)
        first = first.astype(jnp.float32)
        result, pull = jax.vjp(lambda a, b, c: forward(a, b, c, block_of_row), inputs, first, params)
        grad_x, grad_f, grad_p = pull(grad_in.astype(jnp.float32))
        totals = jax.tree.map(jnp.add, totals, grad_p)
        return (totals, (result.astype(jnp.bfloat16), grad_x, grad_f))
    zeros = tuple((jnp.zeros_like(p) for p in params))
    totals, (layer, grad_x, grad_f) = lax.scan(one, zeros, (tokens, first_values, cotangent))
    return (layer, grad_x, grad_f, totals[0], totals[1], totals[2], totals[3], totals[4], totals[5], totals[6], totals[7], totals[8], totals[9], totals[10], totals[11])
```

```python
import functools

import jax
import jax.numpy as jnp
from jax import lax
from jax.experimental import pallas as pl
from jax.experimental.pallas import tpu as pltpu
from jax.sharding import PartitionSpec as P

HEADS = 12
HEAD_DIM = 64
BLK = 128
CHUNK = 512

EPS = 1e-05
SLOPE = 0.7978845608028654
CUBIC = 0.044715
NEG = -1e30

BF = jnp.bfloat16
F32 = jnp.float32
MESH = pl.DeviceIdType.MESH
ANY = pl.BlockSpec(memory_space=pl.ANY)
VM = pl.BlockSpec(memory_space=pltpu.VMEM)


def norm_rows(value, gain, shift):
    mean = jnp.mean(value, axis=-1, keepdims=True)
    centred = value - mean
    inverse = lax.rsqrt(jnp.mean(centred * centred, axis=-1, keepdims=True) + EPS)
    return centred * inverse * gain + shift


def gelu_tanh(value):
    return 0.5 * value * (1.0 + jnp.tanh(SLOPE * (value + CUBIC * value * value * value)))


def product(left, right):
    return jnp.dot(left, right, preferred_element_type=F32)


def product_left(left, right):
    return lax.dot_general(left, right, (((0,), (0,)), ((), ())), preferred_element_type=F32)


def product_right(left, right):
    return lax.dot_general(left, right, (((1,), (1,)), ((), ())), preferred_element_type=F32)


def dealt_blocks(deal):
    count = deal.shape[0] * 2
    pairs = jnp.repeat(deal, 2)
    parity = jnp.arange(count, dtype=jnp.int32) % 2
    return jnp.where(parity == 0, pairs, count - 1 - pairs)


def remote(src, dst, send, recv, device):
    return pltpu.make_async_remote_copy(
        src_ref=src,
        dst_ref=dst,
        send_sem=send,
        recv_sem=recv,
        device_id=device,
        device_id_type=MESH,
    )


def greet(peers):
    barrier = pltpu.get_barrier_semaphore()
    for peer in peers:
        pl.semaphore_signal(barrier, inc=1, device_id=peer, device_id_type=MESH)
    pl.semaphore_wait(barrier, len(peers))


def gather_kernel(
    nw, G, x, first, wqk, wf, small, X, Fv, WQK, WF, SM, rx, rf, rw, rv, rs, sa, sx, sfa, sfx, sw, loc
):
    w = lax.axis_index("wt")
    c = lax.axis_index("ctx")
    g = c // G
    m = c % G
    nc = nw * G
    core = w + 1 - 2 * (w % 2)
    other = (w + 2) % nw
    rel = lambda k: (w + k) % nw
    peers = [(rel(k), c) for k in range(1, nw)]
    peers += [(w, ((g + k) % nw) * G + m) for k in range(1, nw)]
    peers += [(w, g * G + (m + k) % G) for k in range(1, G)]
    greet(peers)
    is_a = w == g
    primary = (w + g) % 2 == 0
    high = w >= 2
    copies = []

    to_head = remote(x, X.at[c], sa.at[0], rx.at[c], (w, w * G + m))
    to_head_f = remote(first, Fv.at[c], sa.at[1], rf.at[c], (w, w * G + m))
    own_x = pltpu.make_async_copy(x, X.at[c], rx.at[c])
    own_f = pltpu.make_async_copy(first, Fv.at[c], rf.at[c])

    @pl.when(is_a)
    def _():
        own_x.start()
        own_f.start()

    @pl.when(jnp.logical_not(is_a))
    def _():
        to_head.start()
        to_head_f.start()

    own_w = pltpu.make_async_copy(wqk.at[w], WQK.at[w], loc.at[0])
    own_s = pltpu.make_async_copy(small, SM.at[w], loc.at[1])
    own_w.start()
    own_s.start()
    own_v = pltpu.make_async_copy(wf.at[w % 2], WF.at[w], loc.at[2])
    own_v.start()
    sends_w, sends_v, sends_s = [], [], []
    for k in range(1, nw):
        d = rel(k)
        s = remote(small, SM.at[w], sw.at[k, 0], rs.at[w], (d, c))
        s.start()
        q = remote(wqk.at[d], WQK.at[w], sw.at[k, 1], rw.at[w], (d, c))
        q.start()
        v = remote(wf.at[d % 2], WF.at[w], sw.at[k, 2], rv.at[w], (d, c))
        sends_w += [s, q]
        sends_v.append((d, v))

        @pl.when(d < 2)
        def _():
            v.start()

    def block_x(b):
        return pltpu.make_async_copy(X.at[b], X.at[b], rx.at[b])

    def block_f(b):
        return pltpu.make_async_copy(Fv.at[b], Fv.at[b], rf.at[b])

    fwd_core, fwd_other, fwd_member = [], [], []
    for k in range(nw):
        gp = (g + k) % nw
        b = gp * G + m
        to_core = remote(X.at[b], X.at[b], sx.at[0, b], rx.at[b], (core, c))
        to_other = remote(X.at[b], X.at[b], sx.at[1, b], rx.at[b], (other, c))
        to_core_f = remote(Fv.at[b], Fv.at[b], sfx.at[0, b], rf.at[b], (core, c))
        to_other_f = remote(Fv.at[b], Fv.at[b], sfx.at[1, b], rf.at[b], (other, c))
        members = [
            remote(X.at[b], X.at[b], sx.at[1 + e, b], rx.at[b], (w, g * G + (m + e) % G))
            for e in range(1, G)
        ]
        members_f = [
            remote(Fv.at[b], Fv.at[b], sfx.at[1 + e, b], rf.at[b], (w, g * G + (m + e) % G))
            for e in range(1, G)
        ]

        @pl.when(primary)
        def _():
            block_x(b).wait()

            @pl.when(is_a)
            def _():
                to_other.start()

            for r in members:
                r.start()
            to_core.start()

        @pl.when(jnp.logical_and(is_a, jnp.logical_not(high)))
        def _():
            block_f(b).wait()
            to_other_f.start()

        @pl.when(jnp.logical_and(primary, high))
        def _():
            block_f(b).wait()
            for r in members_f:
                r.start()
            to_core_f.start()

        fwd_core.append((to_core, to_core_f))
        fwd_other.append((to_other, to_other_f))
        fwd_member.append((members, members_f))
    for e in range(1, G):
        for k in range(nw):
            b = ((g + k) % nw) * G + (m + e) % G
            to_core = remote(X.at[b], X.at[b], sx.at[0, b], rx.at[b], (core, c))
            to_core_f = remote(Fv.at[b], Fv.at[b], sfx.at[0, b], rf.at[b], (core, c))

            @pl.when(primary)
            def _():
                block_x(b).wait()
                to_core.start()

            @pl.when(jnp.logical_and(primary, high))
            def _():
                block_f(b).wait()
                to_core_f.start()

            fwd_core.append((to_core, to_core_f))

    @pl.when(jnp.logical_not(primary))
    def _():
        for b in range(nc):
            block_x(b).wait()

        @pl.when(high)
        def _():
            for b in range(nc):
                block_f(b).wait()

    own_w.wait()
    own_s.wait()
    own_v.wait()
    for k in range(1, nw):
        src = (w + nw - k) % nw
        pltpu.make_async_copy(wqk.at[0], WQK.at[src], rw.at[src]).wait()
        pltpu.make_async_copy(small, SM.at[src], rs.at[src]).wait()

        @pl.when(w < 2)
        def _():
            pltpu.make_async_copy(wf.at[0], WF.at[src], rv.at[src]).wait()

    for s in sends_w:
        s.wait_send()
    for d, v in sends_v:

        @pl.when(d < 2)
        def _():
            v.wait_send()

    @pl.when(jnp.logical_not(is_a))
    def _():
        to_head.wait_send()
        to_head_f.wait_send()

    @pl.when(primary)
    def _():
        for a, _f in fwd_core:
            a.wait_send()
        for ms, _f in fwd_member:
            for a in ms:
                a.wait_send()

        @pl.when(high)
        def _():
            for _x, a in fwd_core:
                a.wait_send()
            for _x, ms in fwd_member:
                for a in ms:
                    a.wait_send()

    @pl.when(is_a)
    def _():
        for a, _f in fwd_other:
            a.wait_send()

        @pl.when(jnp.logical_not(high))
        def _():
            for _x, a in fwd_other:
                a.wait_send()


def gather(nw, G, x, first, wqk, wf, small):
    nc = nw * G
    rows, width = x.shape
    half = first.shape[1]
    d = width // nw
    dma = pltpu.SemaphoreType.DMA
    return pl.pallas_call(
        functools.partial(gather_kernel, nw, G),
        name="gather_tokens",
        out_shape=(
            jax.ShapeDtypeStruct((nc, rows, width), BF),
            jax.ShapeDtypeStruct((nc, rows, half), BF),
            jax.ShapeDtypeStruct((nw, d, 2 * d), BF),
            jax.ShapeDtypeStruct((nw, d, d), BF),
            jax.ShapeDtypeStruct((nw,) + small.shape, BF),
        ),
        in_specs=[ANY] * 5,
        out_specs=[ANY] * 5,
        scratch_shapes=[
            dma((nc,)),
            dma((nc,)),
            dma((nw,)),
            dma((nw,)),
            dma((nw,)),
            dma((2,)),
            dma((1 + G, nc)),
            dma((2,)),
            dma((1 + G, nc)),
            dma((nw, 3)),
            dma((3,)),
        ],
        compiler_params=pltpu.CompilerParams(collective_id=0, has_side_effects=True),
    )(x, first, wqk, wf, small)


def sum_kernel(T, p, out, b1, ab, b2, s1, r1, s2, r2, s3, r3):
    w = lax.axis_index("wt")
    c = lax.axis_index("ctx")
    core = w + 1 - 2 * (w % 2)
    other = (w + 2) % 4
    mine = w % 2
    theirs = 1 - mine
    half = p.shape[0] // 2
    n = half // T
    greet([(core, c), (other, c)])

    def rows(base, t):
        return pl.ds(pl.multiple_of(base * half + t * n, n), n)

    first = []
    for t in range(T):
        r = remote(p.at[rows(theirs, t)], b1.at[t], s1.at[t], r1.at[t], (core, c))
        r.start()
        first.append(r)
    second = []
    for t in range(T):
        first[t].wait_recv()
        ab[t] = (p[rows(mine, t), :].astype(F32) + b1[t].astype(F32)).astype(BF)
        r = remote(ab.at[t], b2.at[t], s2.at[t], r2.at[t], (other, c))
        r.start()
        second.append(r)
    third = []
    for t in range(T):
        second[t].wait_recv()
        out[rows(mine, t), :] = (ab[t].astype(F32) + b2[t].astype(F32)).astype(BF)
        r = remote(out.at[rows(mine, t)], out.at[rows(mine, t)], s3.at[t], r3.at[t], (core, c))
        r.start()
        third.append(r)
    for t in range(T):
        pltpu.make_async_copy(out.at[rows(theirs, t)], out.at[rows(theirs, t)], r3.at[t]).wait()
    for r in first + second + third:
        r.wait_send()


def sum_wt(p, cid):
    T = 4
    rows, width = p.shape
    n = rows // 2 // T
    dma = pltpu.SemaphoreType.DMA
    return pl.pallas_call(
        functools.partial(sum_kernel, T),
        name="sum_wt_%d" % cid,
        out_shape=jax.ShapeDtypeStruct((rows, width), BF),
        in_specs=[VM],
        out_specs=VM,
        scratch_shapes=[pltpu.VMEM((T, n, width), BF)] * 3 + [dma((T,))] * 6,
        compiler_params=pltpu.CompilerParams(
            collective_id=cid, has_side_effects=True, vmem_limit_bytes=32 << 20
        ),
    )(p)


def scatter_kernel(G, D, out, b1, ab, b2, st, b3, s1, r1, s2, r2, s3, r3):
    w = lax.axis_index("wt")
    c = lax.axis_index("ctx")
    g = c // G
    m = c % G
    core = w + 1 - 2 * (w % 2)
    other = (w + 2) % 4
    par = w % 2
    hi = w // 2
    greet([(core, c), (other, c)] + [(w, g * G + (m + e) % G) for e in range(1, G)])
    order = [e for e in range(1, G)] + [0]
    firsts = {}
    for j in (1, 0):
        for e in order:
            jj = (hi + j) % 2
            mm = (m + e) % G
            b = (2 * jj + 1 - par) * G + mm
            slot = jj * G + mm
            r = remote(D.at[b], b1.at[slot], s1.at[slot], r1.at[slot], (core, c))
            r.start()
            firsts[(j, e)] = r

    def arrived1(slot):
        pltpu.make_async_copy(b1.at[slot], b1.at[slot], r1.at[slot]).wait()

    seconds = []
    for e in order:
        jj = 1 - hi
        mm = (m + e) % G
        slot = jj * G + mm
        arrived1(slot)
        ab[mm] = (D[(2 * jj + par) * G + mm].astype(F32) + b1[slot].astype(F32)).astype(BF)
        r = remote(ab.at[mm], b2.at[mm], s2.at[mm], r2.at[mm], (other, c))
        r.start()
        seconds.append(r)
    thirds = []
    for e in order:
        mm = (m + e) % G
        slot = hi * G + mm
        arrived1(slot)
        pltpu.make_async_copy(b2.at[mm], b2.at[mm], r2.at[mm]).wait()
        total = D[w * G + mm].astype(F32) + b1[slot].astype(F32) + b2[mm].astype(F32)
        if e == 0:
            for f in range(1, G):
                q = (m + f) % G
                pltpu.make_async_copy(b3.at[q], b3.at[q], r3.at[q]).wait()
                total = total + b3[q].astype(F32)
            out[...] = total.astype(out.dtype)
        else:
            st[mm] = total.astype(BF)
            r = remote(st.at[mm], b3.at[m], s3.at[mm], r3.at[m], (w, g * G + mm))
            r.start()
            thirds.append(r)
    for r in list(firsts.values()) + seconds + thirds:
        r.wait_send()


def scatter_sum(G, D):
    nc, rows, C = D.shape
    dma = pltpu.SemaphoreType.DMA
    return pl.pallas_call(
        functools.partial(scatter_kernel, G),
        name="scatter_sum",
        out_shape=jax.ShapeDtypeStruct((rows, C), F32),
        in_specs=[VM],
        out_specs=VM,
        scratch_shapes=[
            pltpu.VMEM((2 * G, rows, C), BF),
            pltpu.VMEM((G, rows, C), BF),
            pltpu.VMEM((G, rows, C), BF),
            pltpu.VMEM((G, rows, C), BF),
            pltpu.VMEM((G, rows, C), BF),
            dma((2 * G,)),
            dma((2 * G,)),
            dma((G,)),
            dma((G,)),
            dma((G,)),
            dma((G,)),
        ],
        compiler_params=pltpu.CompilerParams(
            collective_id=3, has_side_effects=True, vmem_limit_bytes=60 << 20
        ),
    )(D)


def head_mask(shape, axis, h):
    lane = lax.broadcasted_iota(jnp.int32, shape, axis)
    return jnp.logical_and(lane >= h * HEAD_DIM, lane < (h + 1) * HEAD_DIM)


def sort_rows(ids, src, dst):
    def move(b, carry):
        to = pl.multiple_of(ids[b] * BLK, BLK)
        at = pl.multiple_of(b * BLK, BLK)
        dst[pl.ds(to, BLK), :] = src[pl.ds(at, BLK), :]
        return carry

    lax.fori_loop(0, src.shape[0] // BLK, move, 0)


def attend_kernel(H, qpos, qid, ids, q_ref, k_ref, v_ref, o_ref, lse_ref, ks, vs):
    i = pl.program_id(0)

    @pl.when(i == 0)
    def _():
        sort_rows(ids, k_ref, ks)
        sort_rows(ids, v_ref, vs)

    width = H * HEAD_DIM
    q = q_ref[...] * jnp.asarray(HEAD_DIM**-0.5, BF)
    masks = [head_mask((BLK, width), 1, h) for h in range(H)]
    qh = [jnp.where(masks[h], q, jnp.zeros_like(q)) for h in range(H)]
    limit = (qid[i] + 1) * BLK
    chunks = (limit + CHUNK - 1) // CHUNK

    def spread(values):
        out = values[H - 1]
        for h in range(H - 2, -1, -1):
            out = jnp.where(masks[h], values[h], out)
        return out

    def step(j, carry):
        tops, sums, acc = carry
        at = pl.multiple_of(j * CHUNK, CHUNK)
        kc = ks[pl.ds(at, CHUNK), :]
        vc = vs[pl.ds(at, CHUNK), :]
        allowed = lax.broadcasted_iota(jnp.int32, (BLK, CHUNK), 1) + at < limit
        new_tops, new_sums, shrink, parts = [], [], [], []
        for h in range(H):
            s = product_right(qh[h], kc)
            s = jnp.where(allowed, s, NEG)
            top = jnp.maximum(tops[h], jnp.max(s, axis=1, keepdims=True))
            a = jnp.exp(tops[h] - top)
            p = jnp.exp(s - top)
            new_sums.append(sums[h] * a + jnp.sum(p, axis=1, keepdims=True))
            new_tops.append(top)
            shrink.append(a)
            parts.append(product(p.astype(BF), vc))
        acc = acc * spread(shrink) + spread(parts)
        return new_tops, new_sums, acc

    start = (
        [jnp.full((BLK, 1), NEG, F32)] * H,
        [jnp.zeros((BLK, 1), F32)] * H,
        jnp.zeros((BLK, width), F32),
    )
    tops, sums, acc = lax.fori_loop(0, chunks, step, start)
    o_ref[...] = (acc / spread(sums)).astype(BF)
    for h in range(H):
        lse = tops[h] + jnp.log(sums[h])
        lse_ref[0, h : h + 1, :] = jnp.transpose(jnp.broadcast_to(lse, (BLK, BLK)))[0:1, :]


def attend(H, qpos, qid, ids, q, k, v):
    n = qpos.shape[0]
    width = H * HEAD_DIM
    N = k.shape[0]
    whole = pl.BlockSpec((N, width), lambda i, *_: (0, 0))
    return pl.pallas_call(
        functools.partial(attend_kernel, H),
        name="attend",
        out_shape=(
            jax.ShapeDtypeStruct((n * BLK, width), BF),
            jax.ShapeDtypeStruct((n, 8, BLK), F32),
        ),
        grid_spec=pltpu.PrefetchScalarGridSpec(
            num_scalar_prefetch=3,
            grid=(n,),
            in_specs=[pl.BlockSpec((BLK, width), lambda i, qp, qi, b: (qp[i], 0)), whole, whole],
            out_specs=[
                pl.BlockSpec((BLK, width), lambda i, *_: (i, 0)),
                pl.BlockSpec((1, 8, BLK), lambda i, *_: (i, 0, 0)),
            ],
            scratch_shapes=[pltpu.VMEM((N, width), BF)] * 2,
        ),
        compiler_params=pltpu.CompilerParams(vmem_limit_bytes=48 << 20),
    )(qpos, qid, ids, q, k, v)


def attend_back_kernel(
    H, qpos, qid, ids, q_ref, k_ref, v_ref, o_ref, do_ref, lse_ref, dqk_ref, dv_ref, ks, vs, kt, dk, dv
):
    i = pl.program_id(0)
    width = H * HEAD_DIM
    N = ks.shape[0]

    @pl.when(i == 0)
    def _():
        sort_rows(ids, k_ref, ks)
        sort_rows(ids, v_ref, vs)

        def flip(b, carry):
            at = pl.multiple_of(b * BLK, BLK)
            kt[:, pl.ds(at, BLK)] = jnp.transpose(ks[pl.ds(at, BLK), :])
            return carry

        lax.fori_loop(0, N // BLK, flip, 0)
        dk[...] = jnp.zeros_like(dk)
        dv[...] = jnp.zeros_like(dv)
        dqk_ref[...] = jnp.zeros_like(dqk_ref)

    scale = HEAD_DIM**-0.5
    q = q_ref[...] * jnp.asarray(scale, BF)
    do = do_ref[...]
    masks = [head_mask((BLK, width), 1, h) for h in range(H)]
    qh = [jnp.where(masks[h], q, jnp.zeros_like(q)) for h in range(H)]
    doh = [jnp.where(masks[h], do, jnp.zeros_like(do)) for h in range(H)]
    qcat = jnp.concatenate(qh, axis=0)
    docat = jnp.concatenate(doh, axis=0)
    pick = lax.broadcasted_iota(jnp.int32, (8, width), 1) // HEAD_DIM
    pick = (pick == lax.broadcasted_iota(jnp.int32, (8, width), 0)).astype(F32)
    delta = lax.dot_general(
        pick,
        do.astype(F32) * o_ref[...].astype(F32),
        (((1,), (1,)), ((), ())),
        precision=lax.Precision.HIGHEST,
        preferred_element_type=F32,
    )
    lse = lse_ref[0]
    limit = (qid[i] + 1) * BLK
    chunks = (limit + CHUNK - 1) // CHUNK

    def step(j, dqt):
        at = pl.multiple_of(j * CHUNK, CHUNK)
        kc = ks[pl.ds(at, CHUNK), :]
        vc = vs[pl.ds(at, CHUNK), :]
        allowed = lax.broadcasted_iota(jnp.int32, (CHUNK, BLK), 0) + at < limit
        ps, dss, dqs = [], [], []
        for h in range(H):
            s = product_right(kc, qh[h])
            s = jnp.where(allowed, s, NEG)
            p = jnp.exp(s - lse[h : h + 1, :])
            dp = product_right(vc, doh[h])
            ds = (p * (dp - delta[h : h + 1, :])).astype(BF)
            ps.append(p.astype(BF))
            dss.append(ds)
            dqs.append(product(kt[h * HEAD_DIM : (h + 1) * HEAD_DIM, pl.ds(at, CHUNK)], ds))
        dv[pl.ds(at, CHUNK), :] += product(jnp.concatenate(ps, axis=1), docat)
        dk[pl.ds(at, CHUNK), :] += product(jnp.concatenate(dss, axis=1), qcat)
        return dqt + jnp.concatenate(dqs, axis=0)

    dqt = lax.fori_loop(0, chunks, step, jnp.zeros((width, BLK), F32))
    here = pl.ds(pl.multiple_of(qpos[i] * BLK, BLK), BLK)
    dqk_ref[here, 0:width] = (jnp.transpose(dqt) * scale).astype(BF)

    @pl.when(i == pl.num_programs(0) - 1)
    def _():
        def move(b, carry):
            at = pl.ds(pl.multiple_of(ids[b] * BLK, BLK), BLK)
            to = pl.ds(pl.multiple_of(b * BLK, BLK), BLK)
            dqk_ref[to, width : 2 * width] = dk[at, :].astype(BF)
            dv_ref[to, :] = dv[at, :].astype(BF)
            return carry

        lax.fori_loop(0, N // BLK, move, 0)


def attend_back(H, qpos, qid, ids, q, k, v, o, do, lse):
    n = qpos.shape[0]
    width = H * HEAD_DIM
    N = k.shape[0]
    whole = pl.BlockSpec((N, width), lambda i, *_: (0, 0))
    row = pl.BlockSpec((BLK, width), lambda i, *_: (i, 0))
    return pl.pallas_call(
        functools.partial(attend_back_kernel, H),
        name="attend_back",
        out_shape=(
            jax.ShapeDtypeStruct((N, 2 * width), BF),
            jax.ShapeDtypeStruct((N, width), BF),
        ),
        grid_spec=pltpu.PrefetchScalarGridSpec(
            num_scalar_prefetch=3,
            grid=(n,),
            in_specs=[
                pl.BlockSpec((BLK, width), lambda i, qp, qi, b: (qp[i], 0)),
                whole,
                whole,
                row,
                row,
                pl.BlockSpec((1, 8, BLK), lambda i, *_: (i, 0, 0)),
            ],
            out_specs=[
                pl.BlockSpec((N, 2 * width), lambda i, *_: (0, 0)),
                pl.BlockSpec((N, width), lambda i, *_: (0, 0)),
            ],
            scratch_shapes=[
                pltpu.VMEM((N, width), BF),
                pltpu.VMEM((N, width), BF),
                pltpu.VMEM((width, N), BF),
                pltpu.VMEM((N, width), F32),
                pltpu.VMEM((N, width), F32),
            ],
        ),
        compiler_params=pltpu.CompilerParams(vmem_limit_bytes=60 << 20),
    )(qpos, qid, ids, q, k, v, o, do, lse)


def on_device(
    nw,
    nc,
    tokens,
    first_values,
    cotangent,
    deal,
    w_qkv,
    bias_qv,
    w_out,
    bias_out,
    gain_one,
    shift_one,
    gain_two,
    shift_two,
    w_up,
    bias_up,
    w_down,
    bias_down,
):
    G = nc // nw
    w = lax.axis_index("wt")
    c = lax.axis_index("ctx")
    m = c % G
    rows, width = tokens.shape[1:]
    d = width // nw
    H = HEADS // nw
    both = ("wt", "ctx")
    swap = [
        (a * nc + g * G + e, g * nc + a * G + e)
        for a in range(nw)
        for g in range(nw)
        for e in range(G)
    ]
    ring = [[(a, (a + k) % nw) for a in range(nw)] for k in range(nw)]

    def exchange(pieces):
        out = jnp.zeros_like(pieces)
        mine = lax.dynamic_index_in_dim(pieces, w, 0, keepdims=True)
        out = lax.dynamic_update_slice_in_dim(out, mine, w, 0)
        for k in range(1, nw):
            piece = lax.dynamic_index_in_dim(pieces, (w + k) % nw, 0, keepdims=True)
            got = lax.ppermute(piece, "wt", ring[k])
            out = lax.dynamic_update_slice_in_dim(out, got, (w + nw - k) % nw, 0)
        return out

    qk = w_qkv[:, : 2 * width].reshape(d, 2, nw, d).transpose(2, 0, 1, 3).reshape(nw, d, 2 * d)
    wf = w_qkv[:, 2 * width :].reshape(d, 2, d).transpose(1, 0, 2)
    small = jnp.concatenate(
        [bias_qv, bias_out, gain_one, shift_one, gain_two, shift_two, bias_down]
    )
    lanes = 16 * BLK
    small = jnp.concatenate([small, jnp.zeros((lanes - small.shape[0],), BF)]).reshape(16, BLK)
    X, Fv, WQK, WF, SM = gather(nw, G, tokens[0], first_values[0], qk, wf, small)
    X = X.reshape(nc * rows, width)
    Wqk = WQK.reshape(width, 2 * d)
    low = w < 2
    Wf = jnp.where(low, WF.reshape(width, d), jnp.zeros((width, d), BF))
    SM = SM.reshape(nw, lanes).astype(F32)
    nb = bias_qv.shape[0]
    qv_vector = SM[:, :nb].reshape(-1)
    vectors = [SM[:, nb + a * d : nb + (a + 1) * d].reshape(-1) for a in range(6)]
    out_vector, gain_a, shift_a, gain_b, shift_b, down_vector = vectors

    x32 = X.astype(F32)
    mean = jnp.mean(x32, axis=-1, keepdims=True)
    centred = x32 - mean
    inverse = lax.rsqrt(jnp.mean(centred * centred, axis=-1, keepdims=True) + EPS)
    n1 = (centred * inverse * gain_a + shift_a).astype(BF)
    pqk = product(n1, Wqk)
    q_bias = lax.dynamic_slice_in_dim(qv_vector, w * d, d)
    f_bias = lax.dynamic_slice_in_dim(qv_vector, width + (w % 2) * d, d)
    q = (pqk[:, :d] + q_bias).astype(BF)
    k = pqk[:, d:].astype(BF)
    f = (product(n1, Wf) + f_bias).astype(BF)
    Fv = Fv.reshape(nc * rows, 2 * d)
    first = jnp.where(w % 2 == 0, Fv[:, :d], Fv[:, d:])
    v = jnp.where(low, f, first)

    ids = dealt_blocks(deal)
    slots = jnp.arange(2 * nw, dtype=jnp.int32)
    qpos = ((slots // 2) * G + m) * 2 + slots % 2
    qid = ids[qpos]
    o, lse = attend(H, qpos, qid, ids, q, k, v)

    def own(a):
        return lax.dynamic_index_in_dim(
            a.reshape(nw, G, rows, a.shape[-1]), m, 1, keepdims=False
        ).reshape(nw * rows, a.shape[-1])

    part = product(o, w_out).astype(BF)
    branch = sum_wt(part, 1).astype(F32)
    mid = own(X).astype(F32) + branch + out_vector
    n2, pull_two = jax.vjp(norm_rows, mid, gain_b, shift_b)
    n2 = n2.astype(BF)

    Wup = exchange(w_up.reshape(d, nw, width).transpose(1, 0, 2)).reshape(width, width)
    cot = lax.all_gather(
        lax.ppermute(cotangent[0], both, swap), "wt", axis=0, tiled=True
    )
    up_pre = product(n2, Wup) + bias_up.astype(F32)
    act, pull_gelu = jax.vjp(gelu_tanh, up_pre)
    act = act.astype(BF)
    mlp = lax.psum_scatter(
        product(act, w_down).astype(BF), "wt", scatter_dimension=0, tiled=True
    )
    mid_own = lax.dynamic_slice_in_dim(mid, w * rows, rows)
    layer = (mid_own + mlp.astype(F32) + down_vector).astype(BF)
    layer = lax.ppermute(layer, both, swap)
    g_down = product_left(act, cot)
    d_up = pull_gelu(product_right(cot, w_down))[0].astype(BF)
    g_up = product_left(n2, d_up)
    d_n2 = sum_wt(product_right(d_up, Wup).astype(BF), 2).astype(F32)
    d_mid_norm, g_gain_two, g_shift_two = pull_two(d_n2)
    cot32 = cot.astype(F32)
    d_mid = cot32 + d_mid_norm
    d_b = d_mid.astype(BF)
    g_out = product_left(o, d_b)
    d_o = product_right(d_b, w_out).astype(BF)
    dqk, dv = attend_back(H, qpos, qid, ids, q, k, v, o, d_o, lse)
    zero = jnp.zeros_like(dv)
    df = jnp.where(low, dv, zero)
    dn1 = product_right(dqk, Wqk) + product_right(df, Wf)
    dn1_low = dn1.astype(BF)
    blank = jnp.zeros_like(dv)
    left = jnp.where(w == 2, dv, blank)
    right = jnp.where(w == 3, dv, blank)
    total = scatter_sum(
        G, jnp.concatenate([dn1_low, left, right], axis=1).reshape(nc, rows, width + 2 * d)
    )
    grad_first = lax.ppermute(total[:, width:].astype(BF), both, swap).astype(F32)
    block = (w * G + m) * rows
    x_own = lax.dynamic_slice_in_dim(X, block, rows).astype(F32)
    _, pull_one = jax.vjp(lambda a: norm_rows(a, gain_a, shift_a), x_own)
    d_x = lax.dynamic_slice_in_dim(d_mid, w * rows, rows) + pull_one(total[:, :width])[0]
    grad_tokens = lax.ppermute(d_x.astype(BF), both, swap).astype(F32)

    g_qk = product_left(n1, dqk)
    g_f = product_left(n1, df)
    normal = centred * inverse
    g_gain_one = jnp.sum(dn1_low.astype(F32) * normal, axis=0)
    g_shift_one = jnp.sum(dn1_low.astype(F32), axis=0)
    up_rows = exchange(g_up.astype(BF).reshape(nw, d, width)).transpose(1, 0, 2)
    s_up, s_down = lax.psum(
        (up_rows.reshape(d, nw * width), g_down.astype(BF)), "ctx"
    )

    def mine(vector):
        return lax.dynamic_slice_in_dim(vector, w * d, d)

    cols = jnp.concatenate(
        [
            g_qk.astype(BF),
            g_f.astype(BF),
            g_gain_one[:, None].astype(BF),
            g_shift_one[:, None].astype(BF),
            jnp.zeros((width, 62), BF),
        ],
        axis=1,
    ).reshape(nw, d, 640)
    sums = jnp.concatenate(
        [jnp.sum(dqk.astype(F32), axis=0), jnp.sum(df.astype(F32), axis=0), jnp.zeros((64,), F32)]
    ).astype(BF)
    foot = jnp.concatenate([sums[None], jnp.zeros((7, 640), BF)], axis=0)
    pack = jnp.concatenate([cols, jnp.broadcast_to(foot[None], (nw, 8, 640))], axis=1)
    pack = exchange(pack)
    vecs = jnp.concatenate(
        [
            jnp.sum(d_up.astype(F32), axis=0),
            mine(jnp.sum(cot32, axis=0)),
            mine(jnp.sum(d_b.astype(F32), axis=0)),
            mine(g_gain_two),
            mine(g_shift_two),
        ]
    ).astype(BF)
    pack = pack.at[0, d + 1 : d + 4, :512].set(vecs.reshape(3, 512))
    pack, s_out = lax.psum((pack, g_out.astype(BF)), "ctx")
    body = pack[:, :d]
    s_qkv = jnp.concatenate(
        [body[a, :, e * d : (e + 1) * d] for e in (0, 1) for a in range(nw)]
        + [body[a, :, 2 * d : 3 * d] for a in range(2)],
        axis=1,
    ).astype(F32)
    s_gain_one = jnp.sum(body[:, :, 576].astype(F32), axis=0)
    s_shift_one = jnp.sum(body[:, :, 577].astype(F32), axis=0)
    ends = pack[:, d]
    bias_all = jnp.concatenate([ends[:, :d].reshape(-1), ends[:2, 2 * d : 3 * d].reshape(-1)])
    s_bias_qv = lax.dynamic_slice_in_dim(bias_all, w * nb, nb).astype(F32)
    vecs = pack[0, d + 1 : d + 4, :512].reshape(-1).astype(F32)
    s_bias_up = vecs[:width]
    s_bias_down, s_bias_out, s_gain_two, s_shift_two = [
        vecs[width + a * d : width + (a + 1) * d] for a in range(4)
    ]
    return (
        layer[None],
        grad_tokens[None],
        grad_first[None],
        s_qkv,
        s_bias_qv,
        s_out.astype(F32),
        s_bias_out,
        s_gain_one,
        s_shift_one,
        s_gain_two,
        s_shift_two,
        s_up.astype(F32),
        s_bias_up,
        s_down.astype(F32),
        s_bias_down,
    )


def solution(mesh):
    rows3 = P("wt", "ctx", None)
    mat = P("wt", None)
    vec = P("wt")
    in_specs = (rows3, rows3, rows3, P(), mat, vec, mat) + (vec,) * 5 + (mat, vec, mat, vec)
    out_specs = (
        (rows3, rows3, rows3, mat, vec, mat) + (vec,) * 5 + (mat, vec, mat, vec)
    )
    return jax.shard_map(
        functools.partial(on_device, mesh.shape["wt"], mesh.shape["ctx"]),
        mesh=mesh,
        in_specs=in_specs,
        out_specs=out_specs,
        check_vma=False,
    )
```

```python
import functools

import jax
import jax.numpy as jnp
from jax import lax
from jax.experimental import pallas as pl
from jax.experimental.pallas import tpu as pltpu
from jax.sharding import PartitionSpec as P

HEADS = 12
HEAD_DIM = 64
BLK = 128
CHUNK = 512

EPS = 1e-05
SLOPE = 0.7978845608028654
CUBIC = 0.044715
NEG = -1e30

BF = jnp.bfloat16
F32 = jnp.float32
MESH = pl.DeviceIdType.MESH
ANY = pl.BlockSpec(memory_space=pl.ANY)
VM = pl.BlockSpec(memory_space=pltpu.VMEM)


def norm_rows(value, gain, shift):
    mean = jnp.mean(value, axis=-1, keepdims=True)
    centred = value - mean
    inverse = lax.rsqrt(jnp.mean(centred * centred, axis=-1, keepdims=True) + EPS)
    return centred * inverse * gain + shift


def gelu_tanh(value):
    return 0.5 * value * (1.0 + jnp.tanh(SLOPE * (value + CUBIC * value * value * value)))


def product(left, right):
    return jnp.dot(left, right, preferred_element_type=F32)


def product_left(left, right):
    return lax.dot_general(left, right, (((0,), (0,)), ((), ())), preferred_element_type=F32)


def product_right(left, right):
    return lax.dot_general(left, right, (((1,), (1,)), ((), ())), preferred_element_type=F32)


def dealt_blocks(deal):
    count = deal.shape[0] * 2
    pairs = jnp.repeat(deal, 2)
    parity = jnp.arange(count, dtype=jnp.int32) % 2
    return jnp.where(parity == 0, pairs, count - 1 - pairs)


def remote(src, dst, send, recv, device):
    return pltpu.make_async_remote_copy(
        src_ref=src,
        dst_ref=dst,
        send_sem=send,
        recv_sem=recv,
        device_id=device,
        device_id_type=MESH,
    )


def greet(peers):
    barrier = pltpu.get_barrier_semaphore()
    for peer in peers:
        pl.semaphore_signal(barrier, inc=1, device_id=peer, device_id_type=MESH)
    pl.semaphore_wait(barrier, len(peers))


def gather_kernel(
    nw, G, x, first, wqk, wf, small, X, Fv, WQK, WF, SM, rx, rf, rw, rv, rs, sa, sx, sfa, sfx, sw, loc
):
    w = lax.axis_index("wt")
    c = lax.axis_index("ctx")
    g = c // G
    m = c % G
    nc = nw * G
    core = w + 1 - 2 * (w % 2)
    other = (w + 2) % nw
    rel = lambda k: (w + k) % nw
    peers = [(rel(k), c) for k in range(1, nw)]
    peers += [(w, ((g + k) % nw) * G + m) for k in range(1, nw)]
    peers += [(w, g * G + (m + k) % G) for k in range(1, G)]
    greet(peers)
    is_a = w == g
    primary = (w + g) % 2 == 0
    high = w >= 2
    copies = []

    to_head = remote(x, X.at[c], sa.at[0], rx.at[c], (w, w * G + m))
    to_head_f = remote(first, Fv.at[c], sa.at[1], rf.at[c], (w, w * G + m))
    own_x = pltpu.make_async_copy(x, X.at[c], rx.at[c])
    own_f = pltpu.make_async_copy(first, Fv.at[c], rf.at[c])

    @pl.when(is_a)
    def _():
        own_x.start()
        own_f.start()

    @pl.when(jnp.logical_not(is_a))
    def _():
        to_head.start()
        to_head_f.start()

    own_w = pltpu.make_async_copy(wqk.at[w], WQK.at[w], loc.at[0])
    own_s = pltpu.make_async_copy(small, SM.at[w], loc.at[1])
    own_w.start()
    own_s.start()
    own_v = pltpu.make_async_copy(wf.at[w % 2], WF.at[w], loc.at[2])
    own_v.start()
    sends_w, sends_v, sends_s = [], [], []
    for k in range(1, nw):
        d = rel(k)
        s = remote(small, SM.at[w], sw.at[k, 0], rs.at[w], (d, c))
        s.start()
        q = remote(wqk.at[d], WQK.at[w], sw.at[k, 1], rw.at[w], (d, c))
        q.start()
        v = remote(wf.at[d % 2], WF.at[w], sw.at[k, 2], rv.at[w], (d, c))
        sends_w += [s, q]
        sends_v.append((d, v))

        @pl.when(d < 2)
        def _():
            v.start()

    def block_x(b):
        return pltpu.make_async_copy(X.at[b], X.at[b], rx.at[b])

    def block_f(b):
        return pltpu.make_async_copy(Fv.at[b], Fv.at[b], rf.at[b])

    fwd_core, fwd_other, fwd_member = [], [], []
    for k in range(nw):
        gp = (g + k) % nw
        b = gp * G + m
        to_core = remote(X.at[b], X.at[b], sx.at[0, b], rx.at[b], (core, c))
        to_other = remote(X.at[b], X.at[b], sx.at[1, b], rx.at[b], (other, c))
        to_core_f = remote(Fv.at[b], Fv.at[b], sfx.at[0, b], rf.at[b], (core, c))
        to_other_f = remote(Fv.at[b], Fv.at[b], sfx.at[1, b], rf.at[b], (other, c))
        members = [
            remote(X.at[b], X.at[b], sx.at[1 + e, b], rx.at[b], (w, g * G + (m + e) % G))
            for e in range(1, G)
        ]
        members_f = [
            remote(Fv.at[b], Fv.at[b], sfx.at[1 + e, b], rf.at[b], (w, g * G + (m + e) % G))
            for e in range(1, G)
        ]

        @pl.when(primary)
        def _():
            block_x(b).wait()

            @pl.when(is_a)
            def _():
                to_other.start()

            for r in members:
                r.start()
            to_core.start()

        @pl.when(jnp.logical_and(is_a, jnp.logical_not(high)))
        def _():
            block_f(b).wait()
            to_other_f.start()

        @pl.when(jnp.logical_and(primary, high))
        def _():
            block_f(b).wait()
            for r in members_f:
                r.start()
            to_core_f.start()

        fwd_core.append((to_core, to_core_f))
        fwd_other.append((to_other, to_other_f))
        fwd_member.append((members, members_f))
    for e in range(1, G):
        for k in range(nw):
            b = ((g + k) % nw) * G + (m + e) % G
            to_core = remote(X.at[b], X.at[b], sx.at[0, b], rx.at[b], (core, c))
            to_core_f = remote(Fv.at[b], Fv.at[b], sfx.at[0, b], rf.at[b], (core, c))

            @pl.when(primary)
            def _():
                block_x(b).wait()
                to_core.start()

            @pl.when(jnp.logical_and(primary, high))
            def _():
                block_f(b).wait()
                to_core_f.start()

            fwd_core.append((to_core, to_core_f))

    @pl.when(jnp.logical_not(primary))
    def _():
        for b in range(nc):
            block_x(b).wait()

        @pl.when(high)
        def _():
            for b in range(nc):
                block_f(b).wait()

    own_w.wait()
    own_s.wait()
    own_v.wait()
    for k in range(1, nw):
        src = (w + nw - k) % nw
        pltpu.make_async_copy(wqk.at[0], WQK.at[src], rw.at[src]).wait()
        pltpu.make_async_copy(small, SM.at[src], rs.at[src]).wait()

        @pl.when(w < 2)
        def _():
            pltpu.make_async_copy(wf.at[0], WF.at[src], rv.at[src]).wait()

    for s in sends_w:
        s.wait_send()
    for d, v in sends_v:

        @pl.when(d < 2)
        def _():
            v.wait_send()

    @pl.when(jnp.logical_not(is_a))
    def _():
        to_head.wait_send()
        to_head_f.wait_send()

    @pl.when(primary)
    def _():
        for a, _f in fwd_core:
            a.wait_send()
        for ms, _f in fwd_member:
            for a in ms:
                a.wait_send()

        @pl.when(high)
        def _():
            for _x, a in fwd_core:
                a.wait_send()
            for _x, ms in fwd_member:
                for a in ms:
                    a.wait_send()

    @pl.when(is_a)
    def _():
        for a, _f in fwd_other:
            a.wait_send()

        @pl.when(jnp.logical_not(high))
        def _():
            for _x, a in fwd_other:
                a.wait_send()


def gather(nw, G, x, first, wqk, wf, small):
    nc = nw * G
    rows, width = x.shape
    half = first.shape[1]
    d = width // nw
    dma = pltpu.SemaphoreType.DMA
    return pl.pallas_call(
        functools.partial(gather_kernel, nw, G),
        name="gather_tokens",
        out_shape=(
            jax.ShapeDtypeStruct((nc, rows, width), BF),
            jax.ShapeDtypeStruct((nc, rows, half), BF),
            jax.ShapeDtypeStruct((nw, d, 2 * d), BF),
            jax.ShapeDtypeStruct((nw, d, d), BF),
            jax.ShapeDtypeStruct((nw,) + small.shape, BF),
        ),
        in_specs=[ANY] * 5,
        out_specs=[ANY] * 5,
        scratch_shapes=[
            dma((nc,)),
            dma((nc,)),
            dma((nw,)),
            dma((nw,)),
            dma((nw,)),
            dma((2,)),
            dma((1 + G, nc)),
            dma((2,)),
            dma((1 + G, nc)),
            dma((nw, 3)),
            dma((3,)),
        ],
        compiler_params=pltpu.CompilerParams(collective_id=0, has_side_effects=True),
    )(x, first, wqk, wf, small)


def middle_kernel(
    T, G, p_hbm, X_hbm, cot_hbm, o_hbm, wup_hbm, wdn_hbm, wout_hbm, vec_hbm,
    mlp, mid_own, dmid_own, do_out, gup, gdn, gout, sums,
    p, x, cot, o, wup, wdn, wout, vec,
    b1, ab, b2, bs, mid, n2s, act, dus, q, b4, ab2, b5, dn, dbs,
    s1, r1, s2, r2, s3, r3, s4, r4, s5, r5, s6, r6, ld,
):
    w = lax.axis_index("wt")
    c = lax.axis_index("ctx")
    g = c // G
    m = c % G
    core = (w + 1 - 2 * (w % 2), c)
    other = ((w + 2) % 4, c)
    mine = w % 2
    theirs = 1 - mine
    rows = p.shape[0]
    half = rows // 2
    n = half // T
    R = rows // 4
    loads = [
        pltpu.make_async_copy(p_hbm, p, ld.at[0]),
        pltpu.make_async_copy(vec_hbm, vec, ld.at[1]),
    ]
    loads += [
        pltpu.make_async_copy(X_hbm.at[a * G + m], x.at[pl.ds(a * R, R)], ld.at[2 + a])
        for a in range(4)
    ]
    loads += [
        pltpu.make_async_copy(wup_hbm, wup, ld.at[6]),
        pltpu.make_async_copy(wdn_hbm, wdn, ld.at[7]),
        pltpu.make_async_copy(cot_hbm, cot, ld.at[8]),
        pltpu.make_async_copy(wout_hbm, wout, ld.at[9]),
        pltpu.make_async_copy(o_hbm, o, ld.at[10]),
    ]
    for copy in loads:
        copy.start()
    greet([core, other])

    def rs(base, t):
        return pl.ds(pl.multiple_of(base * half + t * n, n), n)

    loads[0].wait()
    first = []
    for t in range(T):
        r = remote(p.at[rs(theirs, t)], b1.at[t], s1.at[t], r1.at[t], core)
        r.start()
        first.append(r)
    second = []
    for t in range(T):
        first[t].wait_recv()
        ab[t] = (p[rs(mine, t), :].astype(F32) + b1[t].astype(F32)).astype(BF)
        r = remote(ab.at[t], b2.at[t], s2.at[t], r2.at[t], other)
        r.start()
        second.append(r)
    for copy in loads[1:]:
        copy.wait()
    out_b = vec[0:1, :]
    gain = vec[1:2, :]
    shift = vec[2:3, :]
    up_b = vec[3:4, :]
    sums[...] = jnp.zeros_like(sums)

    def two(ref, t):
        return jnp.concatenate([ref[rs(mine, t), :], ref[rs(theirs, t), :]], axis=0)

    def put(ref, t, value):
        ref[rs(mine, t), :] = value[:n]
        ref[rs(theirs, t), :] = value[n:]

    def add_sum(at, value):
        sums[at : at + 1, :] += jnp.sum(value, axis=0, keepdims=True)

    def chain(t):
        pltpu.make_async_copy(b4.at[t], b4.at[t], r4.at[t]).wait()
        ab2[t] = (q[rs(mine, t), :].astype(F32) + b4[t].astype(F32)).astype(BF)
        remote(ab2.at[t], b5.at[t], s5.at[t], r5.at[t], other).start()

    def forward(t, carry):
        pltpu.make_async_copy(b2.at[t], b2.at[t], r2.at[t]).wait()
        bs[rs(mine, t), :] = (ab[t].astype(F32) + b2[t].astype(F32)).astype(BF)
        remote(bs.at[rs(mine, t)], bs.at[rs(mine, t)], s3.at[t], r3.at[t], core).start()

        @pl.when(t > 0)
        def _():
            chain(t - 1)

        pltpu.make_async_copy(bs.at[rs(theirs, t)], bs.at[rs(theirs, t)], r3.at[t]).wait()
        value = two(x, t).astype(F32) + two(bs, t).astype(F32) + out_b
        put(mid, t, value)
        centred = value - jnp.mean(value, axis=-1, keepdims=True)
        inverse = lax.rsqrt(jnp.mean(centred * centred, axis=-1, keepdims=True) + EPS)
        n2 = (centred * inverse * gain + shift).astype(BF)
        put(n2s, t, n2)
        u = product(n2, wup[...]) + up_b
        th = jnp.tanh(SLOPE * (u + CUBIC * u * u * u))
        a = (0.5 * u * (1.0 + th)).astype(BF)
        slope = 0.5 * (1.0 + th) + 0.5 * u * (1.0 - th * th) * SLOPE * (1.0 + 3.0 * CUBIC * u * u)
        put(act, t, a)
        ct = two(cot, t)
        du = (product_right(ct, wdn[...]) * slope).astype(BF)
        put(dus, t, du)
        put(q, t, product_right(du, wup[...]).astype(BF))
        remote(q.at[rs(theirs, t)], b4.at[t], s4.at[t], r4.at[t], core).start()
        put(mlp, t, product(a, wdn[...]).astype(BF))
        add_sum(0, du.astype(F32))
        add_sum(1, ct.astype(F32))
        return carry

    lax.fori_loop(0, T, forward, 0)
    chain(T - 1)

    width = p.shape[1]
    tile = 256

    def grads(i, carry):
        at = pl.ds(pl.multiple_of(i * tile, tile), tile)
        gup[at, :] = product_left(n2s[:, at], dus[...]).astype(BF)
        gdn[at, :] = product_left(act[:, at], cot[...]).astype(BF)
        return carry

    lax.fori_loop(0, width // tile, grads, 0)

    def backward(t, carry):
        pltpu.make_async_copy(b5.at[t], b5.at[t], r5.at[t]).wait()
        dn[rs(mine, t), :] = (ab2[t].astype(F32) + b5[t].astype(F32)).astype(BF)
        remote(dn.at[rs(mine, t)], dn.at[rs(mine, t)], s6.at[t], r6.at[t], core).start()
        pltpu.make_async_copy(dn.at[rs(theirs, t)], dn.at[rs(theirs, t)], r6.at[t]).wait()
        value = two(mid, t)
        centred = value - jnp.mean(value, axis=-1, keepdims=True)
        inverse = lax.rsqrt(jnp.mean(centred * centred, axis=-1, keepdims=True) + EPS)
        normal = centred * inverse
        dn2 = two(dn, t).astype(F32)
        add_sum(3, dn2 * normal)
        add_sum(4, dn2)
        dx = dn2 * gain
        dx = dx - jnp.mean(dx, axis=-1, keepdims=True) - normal * jnp.mean(
            dx * normal, axis=-1, keepdims=True
        )
        dmid = two(cot, t).astype(F32) + inverse * dx
        db = dmid.astype(BF)
        put(dbs, t, db)
        add_sum(2, db.astype(F32))
        put(do_out, t, product_right(db, wout[...]).astype(BF))
        return carry

    lax.fori_loop(0, T, backward, 0)
    gout[...] = product_left(o[...], dbs[...]).astype(BF)
    own = pl.ds(pl.multiple_of(w * R, R), R)
    mid_own[...] = mid[own, :]
    dmid_own[...] = dbs[own, :]
    for t in range(T):
        first[t].wait_send()
        second[t].wait_send()
        remote(bs.at[rs(mine, t)], bs.at[rs(mine, t)], s3.at[t], r3.at[t], core).wait_send()
        remote(q.at[rs(theirs, t)], b4.at[t], s4.at[t], r4.at[t], core).wait_send()
        remote(ab2.at[t], b5.at[t], s5.at[t], r5.at[t], other).wait_send()
        remote(dn.at[rs(mine, t)], dn.at[rs(mine, t)], s6.at[t], r6.at[t], core).wait_send()


def middle(G, p, X, cot, o, wup, wdn, wout, vec):
    T = 4
    rows, width = p.shape
    n = rows // 2 // T
    R = rows // 4
    d = o.shape[1]
    dma = pltpu.SemaphoreType.DMA
    full = pltpu.VMEM((rows, width), BF)
    part = pltpu.VMEM((T, n, width), BF)
    square = pltpu.VMEM((width, width), BF)
    return pl.pallas_call(
        functools.partial(middle_kernel, T, G),
        name="middle",
        out_shape=(
            jax.ShapeDtypeStruct((rows, width), BF),
            jax.ShapeDtypeStruct((R, width), F32),
            jax.ShapeDtypeStruct((R, width), BF),
            jax.ShapeDtypeStruct((rows, d), BF),
            jax.ShapeDtypeStruct((width, width), BF),
            jax.ShapeDtypeStruct((width, width), BF),
            jax.ShapeDtypeStruct((d, width), BF),
            jax.ShapeDtypeStruct((8, width), F32),
        ),
        in_specs=[ANY] * 8,
        out_specs=[VM] * 8,
        scratch_shapes=[
            full, full, full, pltpu.VMEM((rows, d), BF), square, square,
            pltpu.VMEM((d, width), BF), pltpu.VMEM((8, width), F32),
            part, part, part, full, pltpu.VMEM((rows, width), F32), full, full, full, full,
            part, part, part, full, full,
        ]
        + [dma((T,))] * 12
        + [dma((11,))],
        compiler_params=pltpu.CompilerParams(
            collective_id=1, has_side_effects=True, vmem_limit_bytes=62 << 20
        ),
        cost_estimate=pl.CostEstimate(
            flops=14 * rows * width * width, bytes_accessed=40 << 20, transcendentals=rows * width
        ),
    )(p, X, cot, o, wup, wdn, wout, vec)


def scatter_kernel(G, D, out, b1, ab, b2, st, b3, s1, r1, s2, r2, s3, r3):
    w = lax.axis_index("wt")
    c = lax.axis_index("ctx")
    g = c // G
    m = c % G
    core = w + 1 - 2 * (w % 2)
    other = (w + 2) % 4
    par = w % 2
    hi = w // 2
    greet([(core, c), (other, c)] + [(w, g * G + (m + e) % G) for e in range(1, G)])
    order = [e for e in range(1, G)] + [0]
    firsts = {}
    for j in (1, 0):
        for e in order:
            jj = (hi + j) % 2
            mm = (m + e) % G
            b = (2 * jj + 1 - par) * G + mm
            slot = jj * G + mm
            r = remote(D.at[b], b1.at[slot], s1.at[slot], r1.at[slot], (core, c))
            r.start()
            firsts[(j, e)] = r

    def arrived1(slot):
        pltpu.make_async_copy(b1.at[slot], b1.at[slot], r1.at[slot]).wait()

    seconds = []
    for e in order:
        jj = 1 - hi
        mm = (m + e) % G
        slot = jj * G + mm
        arrived1(slot)
        ab[mm] = (D[(2 * jj + par) * G + mm].astype(F32) + b1[slot].astype(F32)).astype(BF)
        r = remote(ab.at[mm], b2.at[mm], s2.at[mm], r2.at[mm], (other, c))
        r.start()
        seconds.append(r)
    thirds = []
    for e in order:
        mm = (m + e) % G
        slot = hi * G + mm
        arrived1(slot)
        pltpu.make_async_copy(b2.at[mm], b2.at[mm], r2.at[mm]).wait()
        total = D[w * G + mm].astype(F32) + b1[slot].astype(F32) + b2[mm].astype(F32)
        if e == 0:
            for f in range(1, G):
                q = (m + f) % G
                pltpu.make_async_copy(b3.at[q], b3.at[q], r3.at[q]).wait()
                total = total + b3[q].astype(F32)
            out[...] = total.astype(out.dtype)
        else:
            st[mm] = total.astype(BF)
            r = remote(st.at[mm], b3.at[m], s3.at[mm], r3.at[m], (w, g * G + mm))
            r.start()
            thirds.append(r)
    for r in list(firsts.values()) + seconds + thirds:
        r.wait_send()


def scatter_sum(G, D):
    nc, rows, C = D.shape
    dma = pltpu.SemaphoreType.DMA
    return pl.pallas_call(
        functools.partial(scatter_kernel, G),
        name="scatter_sum",
        out_shape=jax.ShapeDtypeStruct((rows, C), F32),
        in_specs=[VM],
        out_specs=VM,
        scratch_shapes=[
            pltpu.VMEM((2 * G, rows, C), BF),
            pltpu.VMEM((G, rows, C), BF),
            pltpu.VMEM((G, rows, C), BF),
            pltpu.VMEM((G, rows, C), BF),
            pltpu.VMEM((G, rows, C), BF),
            dma((2 * G,)),
            dma((2 * G,)),
            dma((G,)),
            dma((G,)),
            dma((G,)),
            dma((G,)),
        ],
        compiler_params=pltpu.CompilerParams(
            collective_id=3, has_side_effects=True, vmem_limit_bytes=60 << 20
        ),
    )(D)


def head_mask(shape, axis, h):
    lane = lax.broadcasted_iota(jnp.int32, shape, axis)
    return jnp.logical_and(lane >= h * HEAD_DIM, lane < (h + 1) * HEAD_DIM)


def sort_rows(ids, src, dst):
    def move(b, carry):
        to = pl.multiple_of(ids[b] * BLK, BLK)
        at = pl.multiple_of(b * BLK, BLK)
        dst[pl.ds(to, BLK), :] = src[pl.ds(at, BLK), :]
        return carry

    lax.fori_loop(0, src.shape[0] // BLK, move, 0)


def attend_kernel(H, qpos, qid, ids, q_ref, k_ref, v_ref, o_ref, lse_ref, ks, vs):
    i = pl.program_id(0)

    @pl.when(i == 0)
    def _():
        sort_rows(ids, k_ref, ks)
        sort_rows(ids, v_ref, vs)

    width = H * HEAD_DIM
    q = q_ref[...] * jnp.asarray(HEAD_DIM**-0.5, BF)
    masks = [head_mask((BLK, width), 1, h) for h in range(H)]
    qh = [jnp.where(masks[h], q, jnp.zeros_like(q)) for h in range(H)]
    limit = (qid[i] + 1) * BLK
    chunks = (limit + CHUNK - 1) // CHUNK

    def spread(values):
        out = values[H - 1]
        for h in range(H - 2, -1, -1):
            out = jnp.where(masks[h], values[h], out)
        return out

    def step(j, carry):
        tops, sums, acc = carry
        at = pl.multiple_of(j * CHUNK, CHUNK)
        kc = ks[pl.ds(at, CHUNK), :]
        vc = vs[pl.ds(at, CHUNK), :]
        allowed = lax.broadcasted_iota(jnp.int32, (BLK, CHUNK), 1) + at < limit
        new_tops, new_sums, shrink, parts = [], [], [], []
        for h in range(H):
            s = product_right(qh[h], kc)
            s = jnp.where(allowed, s, NEG)
            top = jnp.maximum(tops[h], jnp.max(s, axis=1, keepdims=True))
            a = jnp.exp(tops[h] - top)
            p = jnp.exp(s - top)
            new_sums.append(sums[h] * a + jnp.sum(p, axis=1, keepdims=True))
            new_tops.append(top)
            shrink.append(a)
            parts.append(product(p.astype(BF), vc))
        acc = acc * spread(shrink) + spread(parts)
        return new_tops, new_sums, acc

    start = (
        [jnp.full((BLK, 1), NEG, F32)] * H,
        [jnp.zeros((BLK, 1), F32)] * H,
        jnp.zeros((BLK, width), F32),
    )
    tops, sums, acc = lax.fori_loop(0, chunks, step, start)
    o_ref[...] = (acc / spread(sums)).astype(BF)
    for h in range(H):
        lse = tops[h] + jnp.log(sums[h])
        lse_ref[0, h : h + 1, :] = jnp.transpose(jnp.broadcast_to(lse, (BLK, BLK)))[0:1, :]


def attend(H, qpos, qid, ids, q, k, v):
    n = qpos.shape[0]
    width = H * HEAD_DIM
    N = k.shape[0]
    whole = pl.BlockSpec((N, width), lambda i, *_: (0, 0))
    return pl.pallas_call(
        functools.partial(attend_kernel, H),
        name="attend",
        out_shape=(
            jax.ShapeDtypeStruct((n * BLK, width), BF),
            jax.ShapeDtypeStruct((n, 8, BLK), F32),
        ),
        grid_spec=pltpu.PrefetchScalarGridSpec(
            num_scalar_prefetch=3,
            grid=(n,),
            in_specs=[pl.BlockSpec((BLK, width), lambda i, qp, qi, b: (qp[i], 0)), whole, whole],
            out_specs=[
                pl.BlockSpec((BLK, width), lambda i, *_: (i, 0)),
                pl.BlockSpec((1, 8, BLK), lambda i, *_: (i, 0, 0)),
            ],
            scratch_shapes=[pltpu.VMEM((N, width), BF)] * 2,
        ),
        compiler_params=pltpu.CompilerParams(vmem_limit_bytes=48 << 20),
    )(qpos, qid, ids, q, k, v)


def attend_back_kernel(
    H, qpos, qid, ids, q_ref, k_ref, v_ref, o_ref, do_ref, lse_ref, dqk_ref, dv_ref, ks, vs, kt, dk, dv
):
    i = pl.program_id(0)
    width = H * HEAD_DIM
    N = ks.shape[0]

    @pl.when(i == 0)
    def _():
        sort_rows(ids, k_ref, ks)
        sort_rows(ids, v_ref, vs)

        def flip(b, carry):
            at = pl.multiple_of(b * BLK, BLK)
            kt[:, pl.ds(at, BLK)] = jnp.transpose(ks[pl.ds(at, BLK), :])
            return carry

        lax.fori_loop(0, N // BLK, flip, 0)
        dk[...] = jnp.zeros_like(dk)
        dv[...] = jnp.zeros_like(dv)
        dqk_ref[...] = jnp.zeros_like(dqk_ref)

    scale = HEAD_DIM**-0.5
    q = q_ref[...] * jnp.asarray(scale, BF)
    do = do_ref[...]
    masks = [head_mask((BLK, width), 1, h) for h in range(H)]
    qh = [jnp.where(masks[h], q, jnp.zeros_like(q)) for h in range(H)]
    doh = [jnp.where(masks[h], do, jnp.zeros_like(do)) for h in range(H)]
    qcat = jnp.concatenate(qh, axis=0)
    docat = jnp.concatenate(doh, axis=0)
    pick = lax.broadcasted_iota(jnp.int32, (8, width), 1) // HEAD_DIM
    pick = (pick == lax.broadcasted_iota(jnp.int32, (8, width), 0)).astype(F32)
    delta = lax.dot_general(
        pick,
        do.astype(F32) * o_ref[...].astype(F32),
        (((1,), (1,)), ((), ())),
        precision=lax.Precision.HIGHEST,
        preferred_element_type=F32,
    )
    lse = lse_ref[0]
    limit = (qid[i] + 1) * BLK
    chunks = (limit + CHUNK - 1) // CHUNK

    def step(j, dqt):
        at = pl.multiple_of(j * CHUNK, CHUNK)
        kc = ks[pl.ds(at, CHUNK), :]
        vc = vs[pl.ds(at, CHUNK), :]
        allowed = lax.broadcasted_iota(jnp.int32, (CHUNK, BLK), 0) + at < limit
        ps, dss, dqs = [], [], []
        for h in range(H):
            s = product_right(kc, qh[h])
            s = jnp.where(allowed, s, NEG)
            p = jnp.exp(s - lse[h : h + 1, :])
            dp = product_right(vc, doh[h])
            ds = (p * (dp - delta[h : h + 1, :])).astype(BF)
            ps.append(p.astype(BF))
            dss.append(ds)
            dqs.append(product(kt[h * HEAD_DIM : (h + 1) * HEAD_DIM, pl.ds(at, CHUNK)], ds))
        dv[pl.ds(at, CHUNK), :] += product(jnp.concatenate(ps, axis=1), docat)
        dk[pl.ds(at, CHUNK), :] += product(jnp.concatenate(dss, axis=1), qcat)
        return dqt + jnp.concatenate(dqs, axis=0)

    dqt = lax.fori_loop(0, chunks, step, jnp.zeros((width, BLK), F32))
    here = pl.ds(pl.multiple_of(qpos[i] * BLK, BLK), BLK)
    dqk_ref[here, 0:width] = (jnp.transpose(dqt) * scale).astype(BF)

    @pl.when(i == pl.num_programs(0) - 1)
    def _():
        def move(b, carry):
            at = pl.ds(pl.multiple_of(ids[b] * BLK, BLK), BLK)
            to = pl.ds(pl.multiple_of(b * BLK, BLK), BLK)
            dqk_ref[to, width : 2 * width] = dk[at, :].astype(BF)
            dv_ref[to, :] = dv[at, :].astype(BF)
            return carry

        lax.fori_loop(0, N // BLK, move, 0)


def attend_back(H, qpos, qid, ids, q, k, v, o, do, lse):
    n = qpos.shape[0]
    width = H * HEAD_DIM
    N = k.shape[0]
    whole = pl.BlockSpec((N, width), lambda i, *_: (0, 0))
    row = pl.BlockSpec((BLK, width), lambda i, *_: (i, 0))
    return pl.pallas_call(
        functools.partial(attend_back_kernel, H),
        name="attend_back",
        out_shape=(
            jax.ShapeDtypeStruct((N, 2 * width), BF),
            jax.ShapeDtypeStruct((N, width), BF),
        ),
        grid_spec=pltpu.PrefetchScalarGridSpec(
            num_scalar_prefetch=3,
            grid=(n,),
            in_specs=[
                pl.BlockSpec((BLK, width), lambda i, qp, qi, b: (qp[i], 0)),
                whole,
                whole,
                row,
                row,
                pl.BlockSpec((1, 8, BLK), lambda i, *_: (i, 0, 0)),
            ],
            out_specs=[
                pl.BlockSpec((N, 2 * width), lambda i, *_: (0, 0)),
                pl.BlockSpec((N, width), lambda i, *_: (0, 0)),
            ],
            scratch_shapes=[
                pltpu.VMEM((N, width), BF),
                pltpu.VMEM((N, width), BF),
                pltpu.VMEM((width, N), BF),
                pltpu.VMEM((N, width), F32),
                pltpu.VMEM((N, width), F32),
            ],
        ),
        compiler_params=pltpu.CompilerParams(vmem_limit_bytes=60 << 20),
    )(qpos, qid, ids, q, k, v, o, do, lse)


def on_device(
    nw,
    nc,
    tokens,
    first_values,
    cotangent,
    deal,
    w_qkv,
    bias_qv,
    w_out,
    bias_out,
    gain_one,
    shift_one,
    gain_two,
    shift_two,
    w_up,
    bias_up,
    w_down,
    bias_down,
):
    G = nc // nw
    w = lax.axis_index("wt")
    c = lax.axis_index("ctx")
    m = c % G
    rows, width = tokens.shape[1:]
    d = width // nw
    H = HEADS // nw
    both = ("wt", "ctx")
    swap = [
        (a * nc + g * G + e, g * nc + a * G + e)
        for a in range(nw)
        for g in range(nw)
        for e in range(G)
    ]
    ring = [[(a, (a + k) % nw) for a in range(nw)] for k in range(nw)]

    def exchange(pieces):
        out = jnp.zeros_like(pieces)
        mine = lax.dynamic_index_in_dim(pieces, w, 0, keepdims=True)
        out = lax.dynamic_update_slice_in_dim(out, mine, w, 0)
        for k in range(1, nw):
            piece = lax.dynamic_index_in_dim(pieces, (w + k) % nw, 0, keepdims=True)
            got = lax.ppermute(piece, "wt", ring[k])
            out = lax.dynamic_update_slice_in_dim(out, got, (w + nw - k) % nw, 0)
        return out

    qk = w_qkv[:, : 2 * width].reshape(d, 2, nw, d).transpose(2, 0, 1, 3).reshape(nw, d, 2 * d)
    wf = w_qkv[:, 2 * width :].reshape(d, 2, d).transpose(1, 0, 2)
    small = jnp.concatenate(
        [bias_qv, bias_out, gain_one, shift_one, gain_two, shift_two, bias_down]
    )
    lanes = 16 * BLK
    small = jnp.concatenate([small, jnp.zeros((lanes - small.shape[0],), BF)]).reshape(16, BLK)
    X, Fv, WQK, WF, SM = gather(nw, G, tokens[0], first_values[0], qk, wf, small)
    X = X.reshape(nc * rows, width)
    Wqk = WQK.reshape(width, 2 * d)
    low = w < 2
    Wf = jnp.where(low, WF.reshape(width, d), jnp.zeros((width, d), BF))
    SM = SM.reshape(nw, lanes).astype(F32)
    nb = bias_qv.shape[0]
    qv_vector = SM[:, :nb].reshape(-1)
    vectors = [SM[:, nb + a * d : nb + (a + 1) * d].reshape(-1) for a in range(6)]
    out_vector, gain_a, shift_a, gain_b, shift_b, down_vector = vectors

    x32 = X.astype(F32)
    mean = jnp.mean(x32, axis=-1, keepdims=True)
    centred = x32 - mean
    inverse = lax.rsqrt(jnp.mean(centred * centred, axis=-1, keepdims=True) + EPS)
    n1 = (centred * inverse * gain_a + shift_a).astype(BF)
    pqk = product(n1, Wqk)
    q_bias = lax.dynamic_slice_in_dim(qv_vector, w * d, d)
    f_bias = lax.dynamic_slice_in_dim(qv_vector, width + (w % 2) * d, d)
    q = (pqk[:, :d] + q_bias).astype(BF)
    k = pqk[:, d:].astype(BF)
    f = (product(n1, Wf) + f_bias).astype(BF)
    Fv = Fv.reshape(nc * rows, 2 * d)
    first = jnp.where(w % 2 == 0, Fv[:, :d], Fv[:, d:])
    v = jnp.where(low, f, first)

    ids = dealt_blocks(deal)
    slots = jnp.arange(2 * nw, dtype=jnp.int32)
    qpos = ((slots // 2) * G + m) * 2 + slots % 2
    qid = ids[qpos]
    o, lse = attend(H, qpos, qid, ids, q, k, v)

    part = product(o, w_out).astype(BF)
    pieces, spread = lax.optimization_barrier((w_up, cotangent[0], X))[:2]
    Wup = exchange(pieces.reshape(d, nw, width).transpose(1, 0, 2)).reshape(width, width)
    cot = lax.all_gather(lax.ppermute(spread, both, swap), "wt", axis=0, tiled=True)
    vec = jnp.stack([out_vector, gain_b, shift_b, bias_up.astype(F32)] + [out_vector] * 4)
    mlp, mid_own, d_mid, d_o, g_up, g_down, g_out, vsums = middle(
        G, part, X.reshape(nc, rows, width), cot, o, Wup, w_down, w_out, vec
    )
    mlp = lax.psum_scatter(mlp, "wt", scatter_dimension=0, tiled=True)
    layer = (mid_own + mlp.astype(F32) + down_vector).astype(BF)
    layer = lax.ppermute(layer, both, swap)
    up_rows = exchange(g_up.reshape(nw, d, width)).transpose(1, 0, 2)
    s_up, s_down = lax.psum((up_rows.reshape(d, nw * width), g_down), "ctx")
    dqk, dv = attend_back(H, qpos, qid, ids, q, k, v, o, d_o, lse)
    zero = jnp.zeros_like(dv)
    df = jnp.where(low, dv, zero)
    dn1 = product_right(dqk, Wqk) + product_right(df, Wf)
    dn1_low = dn1.astype(BF)
    blank = jnp.zeros_like(dv)
    left = jnp.where(w == 2, dv, blank)
    right = jnp.where(w == 3, dv, blank)
    total = scatter_sum(
        G, jnp.concatenate([dn1_low, left, right], axis=1).reshape(nc, rows, width + 2 * d)
    )
    grad_first = lax.ppermute(total[:, width:].astype(BF), both, swap).astype(F32)
    block = (w * G + m) * rows
    x_own = lax.dynamic_slice_in_dim(X, block, rows).astype(F32)
    _, pull_one = jax.vjp(lambda a: norm_rows(a, gain_a, shift_a), x_own)
    d_x = d_mid.astype(F32) + pull_one(total[:, :width])[0]
    grad_tokens = lax.ppermute(d_x.astype(BF), both, swap).astype(F32)

    g_qk = product_left(n1, dqk)
    g_f = product_left(n1, df)
    normal = centred * inverse
    g_gain_one = jnp.sum(dn1_low.astype(F32) * normal, axis=0)
    g_shift_one = jnp.sum(dn1_low.astype(F32), axis=0)
    def mine(vector):
        return lax.dynamic_slice_in_dim(vector, w * d, d)

    cols = jnp.concatenate(
        [
            g_qk.astype(BF),
            g_f.astype(BF),
            g_gain_one[:, None].astype(BF),
            g_shift_one[:, None].astype(BF),
            jnp.zeros((width, 62), BF),
        ],
        axis=1,
    ).reshape(nw, d, 640)
    sums = jnp.concatenate(
        [jnp.sum(dqk.astype(F32), axis=0), jnp.sum(df.astype(F32), axis=0), jnp.zeros((64,), F32)]
    ).astype(BF)
    foot = jnp.concatenate([sums[None], jnp.zeros((7, 640), BF)], axis=0)
    pack = jnp.concatenate([cols, jnp.broadcast_to(foot[None], (nw, 8, 640))], axis=1)
    pack = exchange(pack)
    vecs = jnp.concatenate(
        [
            vsums[0],
            mine(vsums[1]),
            mine(vsums[2]),
            mine(vsums[3]),
            mine(vsums[4]),
        ]
    ).astype(BF)
    pack = pack.at[0, d + 1 : d + 4, :512].set(vecs.reshape(3, 512))
    pack, s_up, s_down = lax.optimization_barrier((pack, s_up, s_down))
    pack, s_out = lax.psum((pack, g_out), "ctx")
    body = pack[:, :d]
    s_qkv = jnp.concatenate(
        [body[a, :, e * d : (e + 1) * d] for e in (0, 1) for a in range(nw)]
        + [body[a, :, 2 * d : 3 * d] for a in range(2)],
        axis=1,
    ).astype(F32)
    s_gain_one = jnp.sum(body[:, :, 576].astype(F32), axis=0)
    s_shift_one = jnp.sum(body[:, :, 577].astype(F32), axis=0)
    ends = pack[:, d]
    bias_all = jnp.concatenate([ends[:, :d].reshape(-1), ends[:2, 2 * d : 3 * d].reshape(-1)])
    s_bias_qv = lax.dynamic_slice_in_dim(bias_all, w * nb, nb).astype(F32)
    vecs = pack[0, d + 1 : d + 4, :512].reshape(-1).astype(F32)
    s_bias_up = vecs[:width]
    s_bias_down, s_bias_out, s_gain_two, s_shift_two = [
        vecs[width + a * d : width + (a + 1) * d] for a in range(4)
    ]
    return (
        layer[None],
        grad_tokens[None],
        grad_first[None],
        s_qkv,
        s_bias_qv,
        s_out.astype(F32),
        s_bias_out,
        s_gain_one,
        s_shift_one,
        s_gain_two,
        s_shift_two,
        s_up.astype(F32),
        s_bias_up,
        s_down.astype(F32),
        s_bias_down,
    )


def solution(mesh):
    rows3 = P("wt", "ctx", None)
    mat = P("wt", None)
    vec = P("wt")
    in_specs = (rows3, rows3, rows3, P(), mat, vec, mat) + (vec,) * 5 + (mat, vec, mat, vec)
    out_specs = (
        (rows3, rows3, rows3, mat, vec, mat) + (vec,) * 5 + (mat, vec, mat, vec)
    )
    return jax.shard_map(
        functools.partial(on_device, mesh.shape["wt"], mesh.shape["ctx"]),
        mesh=mesh,
        in_specs=in_specs,
        out_specs=out_specs,
        check_vma=False,
    )
```

```python
import functools

import jax
import jax.numpy as jnp
from jax import lax
from jax.experimental import pallas as pl
from jax.experimental.pallas import tpu as pltpu
from jax.sharding import PartitionSpec as P

HEADS = 12
HEAD_DIM = 64
BLK = 128
CHUNK = 1024

EPS = 1e-05
SLOPE = 0.7978845608028654
CUBIC = 0.044715
NEG = -1e30

BF = jnp.bfloat16
F32 = jnp.float32
MESH = pl.DeviceIdType.MESH
ANY = pl.BlockSpec(memory_space=pl.ANY)
VM = pl.BlockSpec(memory_space=pltpu.VMEM)


def norm_rows(value, gain, shift):
    mean = jnp.mean(value, axis=-1, keepdims=True)
    centred = value - mean
    inverse = lax.rsqrt(jnp.mean(centred * centred, axis=-1, keepdims=True) + EPS)
    return centred * inverse * gain + shift


def gelu_tanh(value):
    return 0.5 * value * (1.0 + jnp.tanh(SLOPE * (value + CUBIC * value * value * value)))


def product(left, right):
    return jnp.dot(left, right, preferred_element_type=F32)


def product_left(left, right):
    return lax.dot_general(left, right, (((0,), (0,)), ((), ())), preferred_element_type=F32)


def product_right(left, right):
    return lax.dot_general(left, right, (((1,), (1,)), ((), ())), preferred_element_type=F32)


def dealt_blocks(deal):
    count = deal.shape[0] * 2
    pairs = jnp.repeat(deal, 2)
    parity = jnp.arange(count, dtype=jnp.int32) % 2
    return jnp.where(parity == 0, pairs, count - 1 - pairs)


def remote(src, dst, send, recv, device):
    return pltpu.make_async_remote_copy(
        src_ref=src,
        dst_ref=dst,
        send_sem=send,
        recv_sem=recv,
        device_id=device,
        device_id_type=MESH,
    )


def greet(peers):
    barrier = pltpu.get_barrier_semaphore()
    for peer in peers:
        pl.semaphore_signal(barrier, inc=1, device_id=peer, device_id_type=MESH)
    pl.semaphore_wait(barrier, len(peers))


def gather_kernel(
    nw, G, x, first, wqk, wf, small, X, Fv, WQK, WF, SM, rx, rf, rw, rv, rs, sa, sx, sfa, sfx, sw, loc
):
    w = lax.axis_index("wt")
    c = lax.axis_index("ctx")
    g = c // G
    m = c % G
    nc = nw * G
    core = w + 1 - 2 * (w % 2)
    other = (w + 2) % nw
    rel = lambda k: (w + k) % nw
    peers = [(rel(k), c) for k in range(1, nw)]
    peers += [(w, ((g + k) % nw) * G + m) for k in range(1, nw)]
    peers += [(w, g * G + (m + k) % G) for k in range(1, G)]
    greet(peers)
    is_a = w == g
    primary = (w + g) % 2 == 0
    high = w >= 2
    copies = []

    to_head = remote(x, X.at[c], sa.at[0], rx.at[c], (w, w * G + m))
    to_head_f = remote(first, Fv.at[c], sa.at[1], rf.at[c], (w, w * G + m))
    own_x = pltpu.make_async_copy(x, X.at[c], rx.at[c])
    own_f = pltpu.make_async_copy(first, Fv.at[c], rf.at[c])

    @pl.when(is_a)
    def _():
        own_x.start()
        own_f.start()

    @pl.when(jnp.logical_not(is_a))
    def _():
        to_head.start()
        to_head_f.start()

    own_w = pltpu.make_async_copy(wqk.at[w], WQK.at[w], loc.at[0])
    own_s = pltpu.make_async_copy(small, SM.at[w], loc.at[1])
    own_w.start()
    own_s.start()
    own_v = pltpu.make_async_copy(wf.at[w % 2], WF.at[w], loc.at[2])
    own_v.start()
    sends_w, sends_v, sends_s = [], [], []
    for k in range(1, nw):
        d = rel(k)
        s = remote(small, SM.at[w], sw.at[k, 0], rs.at[w], (d, c))
        s.start()
        q = remote(wqk.at[d], WQK.at[w], sw.at[k, 1], rw.at[w], (d, c))
        q.start()
        v = remote(wf.at[d % 2], WF.at[w], sw.at[k, 2], rv.at[w], (d, c))
        sends_w += [s, q]
        sends_v.append((d, v))

        @pl.when(d < 2)
        def _():
            v.start()

    def block_x(b):
        return pltpu.make_async_copy(X.at[b], X.at[b], rx.at[b])

    def block_f(b):
        return pltpu.make_async_copy(Fv.at[b], Fv.at[b], rf.at[b])

    fwd_core, fwd_other, fwd_member = [], [], []
    for k in range(nw):
        gp = (g + k) % nw
        b = gp * G + m
        to_core = remote(X.at[b], X.at[b], sx.at[0, b], rx.at[b], (core, c))
        to_other = remote(X.at[b], X.at[b], sx.at[1, b], rx.at[b], (other, c))
        to_core_f = remote(Fv.at[b], Fv.at[b], sfx.at[0, b], rf.at[b], (core, c))
        to_other_f = remote(Fv.at[b], Fv.at[b], sfx.at[1, b], rf.at[b], (other, c))
        members = [
            remote(X.at[b], X.at[b], sx.at[1 + e, b], rx.at[b], (w, g * G + (m + e) % G))
            for e in range(1, G)
        ]
        members_f = [
            remote(Fv.at[b], Fv.at[b], sfx.at[1 + e, b], rf.at[b], (w, g * G + (m + e) % G))
            for e in range(1, G)
        ]

        @pl.when(primary)
        def _():
            block_x(b).wait()

            @pl.when(is_a)
            def _():
                to_other.start()

            for r in members:
                r.start()
            to_core.start()

        @pl.when(jnp.logical_and(is_a, jnp.logical_not(high)))
        def _():
            block_f(b).wait()
            to_other_f.start()

        @pl.when(jnp.logical_and(primary, high))
        def _():
            block_f(b).wait()
            for r in members_f:
                r.start()
            to_core_f.start()

        fwd_core.append((to_core, to_core_f))
        fwd_other.append((to_other, to_other_f))
        fwd_member.append((members, members_f))
    for e in range(1, G):
        for k in range(nw):
            b = ((g + k) % nw) * G + (m + e) % G
            to_core = remote(X.at[b], X.at[b], sx.at[0, b], rx.at[b], (core, c))
            to_core_f = remote(Fv.at[b], Fv.at[b], sfx.at[0, b], rf.at[b], (core, c))

            @pl.when(primary)
            def _():
                block_x(b).wait()
                to_core.start()

            @pl.when(jnp.logical_and(primary, high))
            def _():
                block_f(b).wait()
                to_core_f.start()

            fwd_core.append((to_core, to_core_f))

    @pl.when(jnp.logical_not(primary))
    def _():
        for b in range(nc):
            block_x(b).wait()

        @pl.when(high)
        def _():
            for b in range(nc):
                block_f(b).wait()

    own_w.wait()
    own_s.wait()
    own_v.wait()
    for k in range(1, nw):
        src = (w + nw - k) % nw
        pltpu.make_async_copy(wqk.at[0], WQK.at[src], rw.at[src]).wait()
        pltpu.make_async_copy(small, SM.at[src], rs.at[src]).wait()

        @pl.when(w < 2)
        def _():
            pltpu.make_async_copy(wf.at[0], WF.at[src], rv.at[src]).wait()

    for s in sends_w:
        s.wait_send()
    for d, v in sends_v:

        @pl.when(d < 2)
        def _():
            v.wait_send()

    @pl.when(jnp.logical_not(is_a))
    def _():
        to_head.wait_send()
        to_head_f.wait_send()

    @pl.when(primary)
    def _():
        for a, _f in fwd_core:
            a.wait_send()
        for ms, _f in fwd_member:
            for a in ms:
                a.wait_send()

        @pl.when(high)
        def _():
            for _x, a in fwd_core:
                a.wait_send()
            for _x, ms in fwd_member:
                for a in ms:
                    a.wait_send()

    @pl.when(is_a)
    def _():
        for a, _f in fwd_other:
            a.wait_send()

        @pl.when(jnp.logical_not(high))
        def _():
            for _x, a in fwd_other:
                a.wait_send()


def gather(nw, G, x, first, wqk, wf, small):
    nc = nw * G
    rows, width = x.shape
    half = first.shape[1]
    d = width // nw
    dma = pltpu.SemaphoreType.DMA
    return pl.pallas_call(
        functools.partial(gather_kernel, nw, G),
        name="gather_tokens",
        out_shape=(
            jax.ShapeDtypeStruct((nc, rows, width), BF),
            jax.ShapeDtypeStruct((nc, rows, half), BF),
            jax.ShapeDtypeStruct((nw, d, 2 * d), BF),
            jax.ShapeDtypeStruct((nw, d, d), BF),
            jax.ShapeDtypeStruct((nw,) + small.shape, BF),
        ),
        in_specs=[ANY] * 5,
        out_specs=[ANY] * 5,
        scratch_shapes=[
            dma((nc,)),
            dma((nc,)),
            dma((nw,)),
            dma((nw,)),
            dma((nw,)),
            dma((2,)),
            dma((1 + G, nc)),
            dma((2,)),
            dma((1 + G, nc)),
            dma((nw, 3)),
            dma((3,)),
        ],
        compiler_params=pltpu.CompilerParams(collective_id=0, has_side_effects=True),
    )(x, first, wqk, wf, small)


def middle_kernel(
    T, G, p_hbm, X_hbm, cot_hbm, o_hbm, wup_hbm, wdn_hbm, wout_hbm, vec_hbm,
    mlp, mid_own, dmid_own, do_out, upr, gdn, gout, sums,
    p, x, cot, o, wup, wdn, wout, vec,
    b1, ab, b2, bs, mid, n2s, act, dus, q, b4, ab2, b5, dn, dbs, gup,
    s1, r1, s2, r2, s3, r3, s4, r4, s5, r5, s6, r6, ld, sx, rx,
):
    w = lax.axis_index("wt")
    c = lax.axis_index("ctx")
    g = c // G
    m = c % G
    core = (w + 1 - 2 * (w % 2), c)
    other = ((w + 2) % 4, c)
    mine = w % 2
    theirs = 1 - mine
    rows = p.shape[0]
    half = rows // 2
    n = half // T
    R = rows // 4
    loads = [
        pltpu.make_async_copy(p_hbm, p, ld.at[0]),
        pltpu.make_async_copy(vec_hbm, vec, ld.at[1]),
    ]
    loads += [
        pltpu.make_async_copy(X_hbm.at[a * G + m], x.at[pl.ds(a * R, R)], ld.at[2 + a])
        for a in range(4)
    ]
    loads += [
        pltpu.make_async_copy(wup_hbm, wup, ld.at[6]),
        pltpu.make_async_copy(wdn_hbm, wdn, ld.at[7]),
        pltpu.make_async_copy(cot_hbm, cot, ld.at[8]),
        pltpu.make_async_copy(wout_hbm, wout, ld.at[9]),
        pltpu.make_async_copy(o_hbm, o, ld.at[10]),
    ]
    for copy in loads:
        copy.start()
    greet([core, other, ((w + 3 - 2 * (w % 2)) % 4, c)])

    def rs(base, t):
        return pl.ds(pl.multiple_of(base * half + t * n, n), n)

    loads[0].wait()
    first = []
    for t in range(T):
        r = remote(p.at[rs(theirs, t)], b1.at[t], s1.at[t], r1.at[t], core)
        r.start()
        first.append(r)
    second = []
    for t in range(T):
        first[t].wait_recv()
        ab[t] = (p[rs(mine, t), :].astype(F32) + b1[t].astype(F32)).astype(BF)
        r = remote(ab.at[t], b2.at[t], s2.at[t], r2.at[t], other)
        r.start()
        second.append(r)
    for copy in loads[1:]:
        copy.wait()
    out_b = vec[0:1, :]
    gain = vec[1:2, :]
    shift = vec[2:3, :]
    up_b = vec[3:4, :]
    sums[...] = jnp.zeros_like(sums)

    def two(ref, t):
        return jnp.concatenate([ref[rs(mine, t), :], ref[rs(theirs, t), :]], axis=0)

    def put(ref, t, value):
        ref[rs(mine, t), :] = value[:n]
        ref[rs(theirs, t), :] = value[n:]

    def add_sum(at, value):
        sums[at : at + 1, :] += jnp.sum(value, axis=0, keepdims=True)

    def chain(t):
        pltpu.make_async_copy(b4.at[t], b4.at[t], r4.at[t]).wait()
        ab2[t] = (q[rs(mine, t), :].astype(F32) + b4[t].astype(F32)).astype(BF)
        remote(ab2.at[t], b5.at[t], s5.at[t], r5.at[t], other).start()

    def forward(t, carry):
        pltpu.make_async_copy(b2.at[t], b2.at[t], r2.at[t]).wait()
        bs[rs(mine, t), :] = (ab[t].astype(F32) + b2[t].astype(F32)).astype(BF)
        remote(bs.at[rs(mine, t)], bs.at[rs(mine, t)], s3.at[t], r3.at[t], core).start()

        @pl.when(t > 0)
        def _():
            chain(t - 1)

        pltpu.make_async_copy(bs.at[rs(theirs, t)], bs.at[rs(theirs, t)], r3.at[t]).wait()
        value = two(x, t).astype(F32) + two(bs, t).astype(F32) + out_b
        put(mid, t, value)
        centred = value - jnp.mean(value, axis=-1, keepdims=True)
        inverse = lax.rsqrt(jnp.mean(centred * centred, axis=-1, keepdims=True) + EPS)
        n2 = (centred * inverse * gain + shift).astype(BF)
        put(n2s, t, n2)
        u = product(n2, wup[...]) + up_b
        th = jnp.tanh(SLOPE * (u + CUBIC * u * u * u))
        a = (0.5 * u * (1.0 + th)).astype(BF)
        slope = 0.5 * (1.0 + th) + 0.5 * u * (1.0 - th * th) * SLOPE * (1.0 + 3.0 * CUBIC * u * u)
        put(act, t, a)
        ct = two(cot, t)
        du = (product_right(ct, wdn[...]) * slope).astype(BF)
        put(dus, t, du)
        put(q, t, product_right(du, wup[...]).astype(BF))
        remote(q.at[rs(theirs, t)], b4.at[t], s4.at[t], r4.at[t], core).start()
        put(mlp, t, product(a, wdn[...]).astype(BF))
        add_sum(0, du.astype(F32))
        add_sum(1, ct.astype(F32))
        return carry

    lax.fori_loop(0, T, forward, 0)
    chain(T - 1)

    width = p.shape[1]
    tile = 256

    def grads(i, carry):
        at = pl.ds(pl.multiple_of(i * tile, tile), tile)
        gup[at, :] = product_left(n2s[:, at], dus[...]).astype(BF)
        gdn[at, :] = product_left(act[:, at], cot[...]).astype(BF)
        return carry

    lax.fori_loop(0, width // tile, grads, 0)
    d = width // 4
    block = lambda a: pl.ds(pl.multiple_of(a * d, 16), d)
    swaps = []
    for e in range(1, 4):
        to = (w + e) % 4
        r = remote(gup.at[block(to)], upr.at[block(w)], sx.at[e], rx.at[w], (to, c))
        r.start()
        swaps.append(r)
    upr[block(w), :] = gup[block(w), :]

    def backward(t, carry):
        pltpu.make_async_copy(b5.at[t], b5.at[t], r5.at[t]).wait()
        dn[rs(mine, t), :] = (ab2[t].astype(F32) + b5[t].astype(F32)).astype(BF)
        remote(dn.at[rs(mine, t)], dn.at[rs(mine, t)], s6.at[t], r6.at[t], core).start()
        pltpu.make_async_copy(dn.at[rs(theirs, t)], dn.at[rs(theirs, t)], r6.at[t]).wait()
        value = two(mid, t)
        centred = value - jnp.mean(value, axis=-1, keepdims=True)
        inverse = lax.rsqrt(jnp.mean(centred * centred, axis=-1, keepdims=True) + EPS)
        normal = centred * inverse
        dn2 = two(dn, t).astype(F32)
        add_sum(3, dn2 * normal)
        add_sum(4, dn2)
        dx = dn2 * gain
        dx = dx - jnp.mean(dx, axis=-1, keepdims=True) - normal * jnp.mean(
            dx * normal, axis=-1, keepdims=True
        )
        dmid = two(cot, t).astype(F32) + inverse * dx
        db = dmid.astype(BF)
        put(dbs, t, db)
        add_sum(2, db.astype(F32))
        put(do_out, t, product_right(db, wout[...]).astype(BF))
        return carry

    lax.fori_loop(0, T, backward, 0)
    gout[...] = product_left(o[...], dbs[...]).astype(BF)
    own = pl.ds(pl.multiple_of(w * R, R), R)
    mid_own[...] = mid[own, :]
    dmid_own[...] = dbs[own, :]
    for e in range(1, 4):
        src = (w + e) % 4
        pltpu.make_async_copy(upr.at[block(src)], upr.at[block(src)], rx.at[src]).wait()
    for r in swaps:
        r.wait_send()
    for t in range(T):
        first[t].wait_send()
        second[t].wait_send()
        remote(bs.at[rs(mine, t)], bs.at[rs(mine, t)], s3.at[t], r3.at[t], core).wait_send()
        remote(q.at[rs(theirs, t)], b4.at[t], s4.at[t], r4.at[t], core).wait_send()
        remote(ab2.at[t], b5.at[t], s5.at[t], r5.at[t], other).wait_send()
        remote(dn.at[rs(mine, t)], dn.at[rs(mine, t)], s6.at[t], r6.at[t], core).wait_send()


def middle(G, p, X, cot, o, wup, wdn, wout, vec):
    T = 4
    rows, width = p.shape
    n = rows // 2 // T
    R = rows // 4
    d = o.shape[1]
    dma = pltpu.SemaphoreType.DMA
    full = pltpu.VMEM((rows, width), BF)
    part = pltpu.VMEM((T, n, width), BF)
    square = pltpu.VMEM((width, width), BF)
    return pl.pallas_call(
        functools.partial(middle_kernel, T, G),
        name="middle",
        out_shape=(
            jax.ShapeDtypeStruct((rows, width), BF),
            jax.ShapeDtypeStruct((R, width), F32),
            jax.ShapeDtypeStruct((R, width), BF),
            jax.ShapeDtypeStruct((rows, d), BF),
            jax.ShapeDtypeStruct((width, width), BF),
            jax.ShapeDtypeStruct((width, width), BF),
            jax.ShapeDtypeStruct((d, width), BF),
            jax.ShapeDtypeStruct((8, width), F32),
        ),
        in_specs=[ANY] * 8,
        out_specs=[VM] * 8,
        scratch_shapes=[
            full, full, full, pltpu.VMEM((rows, d), BF), square, square,
            pltpu.VMEM((d, width), BF), pltpu.VMEM((8, width), F32),
            part, part, part, full, pltpu.VMEM((rows, width), F32), full, full, full, full,
            part, part, part, full, full, square,
        ]
        + [dma((T,))] * 12
        + [dma((11,)), dma((4,)), dma((4,))],
        compiler_params=pltpu.CompilerParams(
            collective_id=1, has_side_effects=True, vmem_limit_bytes=62 << 20
        ),
        cost_estimate=pl.CostEstimate(
            flops=14 * rows * width * width, bytes_accessed=40 << 20, transcendentals=rows * width
        ),
    )(p, X, cot, o, wup, wdn, wout, vec)


def scatter_kernel(G, D, out, b1, ab, b2, st, b3, s1, r1, s2, r2, s3, r3):
    w = lax.axis_index("wt")
    c = lax.axis_index("ctx")
    g = c // G
    m = c % G
    core = w + 1 - 2 * (w % 2)
    other = (w + 2) % 4
    par = w % 2
    hi = w // 2
    greet([(core, c), (other, c)] + [(w, g * G + (m + e) % G) for e in range(1, G)])
    order = [e for e in range(1, G)] + [0]
    firsts = {}
    for j in (1, 0):
        for e in order:
            jj = (hi + j) % 2
            mm = (m + e) % G
            b = (2 * jj + 1 - par) * G + mm
            slot = jj * G + mm
            r = remote(D.at[b], b1.at[slot], s1.at[slot], r1.at[slot], (core, c))
            r.start()
            firsts[(j, e)] = r

    def arrived1(slot):
        pltpu.make_async_copy(b1.at[slot], b1.at[slot], r1.at[slot]).wait()

    seconds = []
    for e in order:
        jj = 1 - hi
        mm = (m + e) % G
        slot = jj * G + mm
        arrived1(slot)
        ab[mm] = (D[(2 * jj + par) * G + mm].astype(F32) + b1[slot].astype(F32)).astype(BF)
        r = remote(ab.at[mm], b2.at[mm], s2.at[mm], r2.at[mm], (other, c))
        r.start()
        seconds.append(r)
    thirds = []
    for e in order:
        mm = (m + e) % G
        slot = hi * G + mm
        arrived1(slot)
        pltpu.make_async_copy(b2.at[mm], b2.at[mm], r2.at[mm]).wait()
        total = D[w * G + mm].astype(F32) + b1[slot].astype(F32) + b2[mm].astype(F32)
        if e == 0:
            for f in range(1, G):
                q = (m + f) % G
                pltpu.make_async_copy(b3.at[q], b3.at[q], r3.at[q]).wait()
                total = total + b3[q].astype(F32)
            out[...] = total.astype(out.dtype)
        else:
            st[mm] = total.astype(BF)
            r = remote(st.at[mm], b3.at[m], s3.at[mm], r3.at[m], (w, g * G + mm))
            r.start()
            thirds.append(r)
    for r in list(firsts.values()) + seconds + thirds:
        r.wait_send()


def scatter_sum(G, D):
    nc, rows, C = D.shape
    dma = pltpu.SemaphoreType.DMA
    return pl.pallas_call(
        functools.partial(scatter_kernel, G),
        name="scatter_sum",
        out_shape=jax.ShapeDtypeStruct((rows, C), F32),
        in_specs=[VM],
        out_specs=VM,
        scratch_shapes=[
            pltpu.VMEM((2 * G, rows, C), BF),
            pltpu.VMEM((G, rows, C), BF),
            pltpu.VMEM((G, rows, C), BF),
            pltpu.VMEM((G, rows, C), BF),
            pltpu.VMEM((G, rows, C), BF),
            dma((2 * G,)),
            dma((2 * G,)),
            dma((G,)),
            dma((G,)),
            dma((G,)),
            dma((G,)),
        ],
        compiler_params=pltpu.CompilerParams(
            collective_id=3, has_side_effects=True, vmem_limit_bytes=60 << 20
        ),
    )(D)


def head_mask(shape, h):
    lane = lax.broadcasted_iota(jnp.int32, shape, 1)
    return jnp.logical_and(lane >= h * HEAD_DIM, lane < (h + 1) * HEAD_DIM)


def split_heads(H, value):
    zero = jnp.zeros_like(value)
    return [jnp.where(head_mask(value.shape, h), value, zero) for h in range(H)]


def spread(H, shape, values):
    out = jnp.broadcast_to(values[H - 1], shape)
    for h in range(H - 2, -1, -1):
        out = jnp.where(head_mask(shape, h), values[h], out)
    return out


def attend_tile(H, q, k_ref, v_ref, bias_ref, at_bias):
    rows, width = q.shape
    N = k_ref.shape[0]
    step_keys = min(N, 1024)
    qh = split_heads(H, q * jnp.asarray(HEAD_DIM**-0.5, BF))
    top_half = lax.broadcasted_iota(jnp.int32, (rows, 1), 0) < BLK

    def step(j, carry):
        tops, sums, acc = carry
        at = pl.ds(pl.multiple_of(j * step_keys, step_keys), step_keys)
        kc = k_ref[at, :]
        vc = v_ref[at, :]
        low = bias_ref[at_bias, :, at]
        high = bias_ref[at_bias + 1, :, at]
        new_tops, new_sums, shrink, parts = [], [], [], []
        for h in range(H):
            s = product_right(qh[h], kc)
            s = jnp.concatenate([s[:BLK] + low, s[BLK:] + high], axis=0)
            top = jnp.maximum(tops[h], jnp.max(s, axis=1, keepdims=True))
            a = jnp.exp(tops[h] - top)
            p = jnp.exp(s - top)
            new_sums.append(sums[h] * a + jnp.sum(p, axis=1, keepdims=True))
            new_tops.append(top)
            shrink.append(a)
            parts.append(product(p.astype(BF), vc))
        acc = acc * spread(H, acc.shape, shrink) + spread(H, acc.shape, parts)
        return new_tops, new_sums, acc

    start = (
        [jnp.full((rows, 1), NEG, F32)] * H,
        [jnp.zeros((rows, 1), F32)] * H,
        jnp.zeros((rows, width), F32),
    )
    tops, sums, acc = lax.fori_loop(0, N // step_keys, step, start)
    out = (acc / spread(H, acc.shape, sums)).astype(BF)
    lse = []
    for h in range(H):
        column = tops[h] + jnp.log(sums[h])
        lse.append(jnp.transpose(jnp.broadcast_to(column, (rows, BLK)))[0:1, :])
    lse = jnp.concatenate(lse + [jnp.zeros((8 - H, rows), F32)], axis=0)
    return out, lse


def attend_kernel(H, qpos, q_ref, k_ref, v_ref, bias_ref, o_ref, lse_ref):
    o, lse = attend_tile(H, q_ref[...], k_ref, v_ref, bias_ref, 2 * pl.program_id(0))
    o_ref[...] = o
    lse_ref[0] = lse


def attend(H, qpos, bias, q, k, v):
    n = qpos.shape[0]
    width = H * HEAD_DIM
    N = k.shape[0]
    rows = 2 * BLK
    whole = pl.BlockSpec((N, width), lambda i, *_: (0, 0))
    return pl.pallas_call(
        functools.partial(attend_kernel, H),
        name="attend",
        out_shape=(
            jax.ShapeDtypeStruct((n * rows, width), BF),
            jax.ShapeDtypeStruct((n, 8, rows), F32),
        ),
        grid_spec=pltpu.PrefetchScalarGridSpec(
            num_scalar_prefetch=1,
            grid=(n,),
            in_specs=[
                pl.BlockSpec((rows, width), lambda i, qp: (qp[i], 0)),
                whole,
                whole,
                pl.BlockSpec((2 * n, 1, N), lambda i, *_: (0, 0, 0)),
            ],
            out_specs=[
                pl.BlockSpec((rows, width), lambda i, *_: (i, 0)),
                pl.BlockSpec((1, 8, rows), lambda i, *_: (i, 0, 0)),
            ],
        ),
        compiler_params=pltpu.CompilerParams(vmem_limit_bytes=48 << 20),
    )(qpos, q, k, v, bias)


def attend_back_tile(H, q, do, o, lse, k_ref, v_ref, kt, dk, dv, lift_ref, tile):
    rows, width = q.shape
    N = k_ref.shape[0]
    scale = HEAD_DIM**-0.5
    qh = split_heads(H, q * jnp.asarray(scale, BF))
    doh = split_heads(H, do)
    qcat = jnp.concatenate(qh, axis=0)
    docat = jnp.concatenate(doh, axis=0)
    pick = lax.broadcasted_iota(jnp.int32, (8, width), 1)
    base = lax.broadcasted_iota(jnp.int32, (8, width), 0) * HEAD_DIM
    pick = jnp.logical_and(pick >= base, pick < base + HEAD_DIM).astype(F32)
    delta = lax.dot_general(
        pick,
        do.astype(F32) * o.astype(F32),
        (((1,), (1,)), ((), ())),
        precision=lax.Precision.HIGHEST,
        preferred_element_type=F32,
    )

    def step(j, dqt):
        at = pl.ds(pl.multiple_of(j * CHUNK, CHUNK), CHUNK)
        kc = k_ref[at, :]
        vc = v_ref[at, :]
        ps, dss, dqs = [], [], []
        for h in range(H):
            s = product_right(kc, qh[h])
            dp = product_right(vc, doh[h])
            pieces, dpieces = [], []
            for b in range(CHUNK // BLK):
                lift = lift_ref[tile, pl.ds(j * (CHUNK // BLK) + b, 1), :]
                cut = slice(b * BLK, (b + 1) * BLK)
                p = jnp.exp(s[cut] - (lse[h : h + 1, :] + lift))
                pieces.append(p.astype(BF))
                dpieces.append((p * (dp[cut] - delta[h : h + 1, :])).astype(BF))
            p = jnp.concatenate(pieces, axis=0)
            ds = jnp.concatenate(dpieces, axis=0)
            ps.append(p)
            dss.append(ds)
            dqs.append(product(kt[h * HEAD_DIM : (h + 1) * HEAD_DIM, at], ds))
        dv[at, :] += product(jnp.concatenate(ps, axis=1), docat)
        dk[at, :] += product(jnp.concatenate(dss, axis=1), qcat)
        return dqt + jnp.concatenate(dqs, axis=0)

    dqt = lax.fori_loop(0, N // CHUNK, step, jnp.zeros((width, rows), F32))
    return dqt * scale


def flip_rows(src, dst):
    def flip(b, carry):
        at = pl.ds(pl.multiple_of(b * BLK, BLK), BLK)
        dst[:, at] = jnp.transpose(src[at, :])
        return carry

    lax.fori_loop(0, src.shape[0] // BLK, flip, 0)


def attend_back_kernel(
    H, qpos, q_ref, k_ref, v_ref, o_ref, do_ref, lse_ref, lift_ref, dqk_ref, dv_ref, kt, dk, dv
):
    i = pl.program_id(0)
    width = H * HEAD_DIM

    @pl.when(i == 0)
    def _():
        flip_rows(k_ref, kt)
        dk[...] = jnp.zeros_like(dk)
        dv[...] = jnp.zeros_like(dv)
        dqk_ref[...] = jnp.zeros_like(dqk_ref)

    dqt = attend_back_tile(
        H, q_ref[...], do_ref[...], o_ref[...], lse_ref[0], k_ref, v_ref, kt, dk, dv, lift_ref, i
    )
    rows = 2 * BLK
    here = pl.ds(pl.multiple_of(qpos[i] * rows, rows), rows)
    dqk_ref[here, 0:width] = jnp.transpose(dqt).astype(BF)

    @pl.when(i == pl.num_programs(0) - 1)
    def _():
        dqk_ref[:, width : 2 * width] = dk[...].astype(BF)
        dv_ref[...] = dv[...].astype(BF)


def attend_back(H, qpos, lift, q, k, v, o, do, lse):
    n = qpos.shape[0]
    width = H * HEAD_DIM
    N = k.shape[0]
    rows = 2 * BLK
    whole = pl.BlockSpec((N, width), lambda i, *_: (0, 0))
    row = pl.BlockSpec((rows, width), lambda i, *_: (i, 0))
    return pl.pallas_call(
        functools.partial(attend_back_kernel, H),
        name="attend_back",
        out_shape=(
            jax.ShapeDtypeStruct((N, 2 * width), BF),
            jax.ShapeDtypeStruct((N, width), BF),
        ),
        grid_spec=pltpu.PrefetchScalarGridSpec(
            num_scalar_prefetch=1,
            grid=(n,),
            in_specs=[
                pl.BlockSpec((rows, width), lambda i, qp: (qp[i], 0)),
                whole,
                whole,
                row,
                row,
                pl.BlockSpec((1, 8, rows), lambda i, *_: (i, 0, 0)),
                pl.BlockSpec((n, N // BLK, rows), lambda i, *_: (0, 0, 0)),
            ],
            out_specs=[
                pl.BlockSpec((N, 2 * width), lambda i, *_: (0, 0)),
                pl.BlockSpec((N, width), lambda i, *_: (0, 0)),
            ],
            scratch_shapes=[
                pltpu.VMEM((width, N), BF),
                pltpu.VMEM((N, width), F32),
                pltpu.VMEM((N, width), F32),
            ],
        ),
        compiler_params=pltpu.CompilerParams(vmem_limit_bytes=60 << 20),
    )(qpos, q, k, v, o, do, lse, lift)


class Ring:
    def __init__(self, nc, pos, right, left, seg, A, slots, out, ss, sr):
        self.nc, self.pos, self.right, self.left, self.seg = nc, pos, right, left, seg
        self.A, self.slots, self.out, self.ss, self.sr = A, slots, out, ss, sr

    def at(self, half, j):
        j = (j + 2 * self.nc) % self.nc
        return pl.ds(pl.multiple_of((half * self.nc + j) * self.seg, 16), self.seg)

    def reduce_copies(self, s):
        a, b = self.at(0, self.pos - s), self.at(1, self.pos + s)
        return (
            remote(self.A.at[a], self.slots.at[0, s], self.ss.at[0, s], self.sr.at[0, s], self.right),
            remote(self.A.at[b], self.slots.at[1, s], self.ss.at[1, s], self.sr.at[1, s], self.left),
        )

    def gather_copies(self, s):
        t = s - (self.nc - 1)
        a, b = self.at(0, self.pos + 1 - t), self.at(1, self.pos - 1 + t)
        return (
            remote(self.out.at[a], self.out.at[a], self.ss.at[0, s], self.sr.at[0, s], self.right),
            remote(self.out.at[b], self.out.at[b], self.ss.at[1, s], self.sr.at[1, s], self.left),
        )

    def copies(self, s, gathering):
        return self.gather_copies(s) if gathering else self.reduce_copies(s)

    def send(self, s, gathering=False):
        for r in self.copies(s, gathering):
            r.start()

    def add(self, s):
        for h, at in ((0, self.at(0, self.pos - s - 1)), (1, self.at(1, self.pos + s + 1))):
            pltpu.make_async_copy(self.slots.at[h, s], self.slots.at[h, s], self.sr.at[h, s]).wait()
            value = self.A[at, :].astype(F32) + self.slots[h, s].astype(F32)
            self.A[at, :] = value.astype(BF)

    def keep(self):
        for at in (self.at(0, self.pos + 1), self.at(1, self.pos - 1)):
            self.out[at, :] = self.A[at, :]

    def arrive(self, s):
        t = s - (self.nc - 1)
        for h, at in ((0, self.at(0, self.pos - t)), (1, self.at(1, self.pos + t))):
            pltpu.make_async_copy(self.out.at[at], self.out.at[at], self.sr.at[h, s]).wait()

    def step(self, s):
        last = self.nc - 2
        if s < last:
            self.add(s)
            self.send(s + 1)
        elif s == last:
            self.add(s)
            self.keep()
            self.send(s + 1, True)
        else:
            self.arrive(s)
            if s < 2 * last + 1:
                self.send(s + 1, True)

    def drain(self):
        for s in range(2 * (self.nc - 1)):
            for r in self.copies(s, s >= self.nc - 1):
                r.wait_send()


def tail_kernel(
    G, H, seg_a, seg_b,
    q_h, k_h, v_h, o_h, do_h, lse_h, lift_h, n1_h, X_h, wqk_h, wf_h, vec_h, dmid_h,
    up_h, down_h, gout_h, small_h,
    tokens_out, first_out, up_out, down_out, gout_out, small_out, qkv_out, ends_out,
    q, k, v, o, do, lse, lift, n1, X, wqk, wf, vec, dmid,
    kt, dk, dv, dqk, dvb, D, b1, ab, b2, st, b3, tot, tb, tr,
    A, slots_a, res_a, gq, B, slots_b, res_b, gs, f1, fs, fr,
    s1, r1, s2, r2, s3, r3, sT, rT, ssa, sra, ssb, srb, sx, rx, sf1, rf1, sf2, rf2, ld,
):
    w = lax.axis_index("wt")
    c = lax.axis_index("ctx")
    nw = 4
    nc = nw * G
    g = c // G
    m = c % G
    par = w % 2
    hi = w // 2
    core = (w + 1 - 2 * par, c)
    other = ((w + 2) % nw, c)
    R, width = dmid.shape
    d = width // nw
    N = n1.shape[0]
    odd = c % 2
    pos = (c // 2) * (1 - odd) + (nc - 1 - c // 2) * odd

    def ctx_at(p):
        p = (p + nc) % nc
        h = p // (nc // 2)
        return 2 * p * (1 - h) + (2 * (nc - 1 - p) + 1) * h

    right = (w, ctx_at(pos + 1))
    left = (w, ctx_at(pos - 1))
    loads = [
        (up_h, A.at[pl.ds(0, width)]),
        (down_h, A.at[pl.ds(width, width)]),
        (gout_h, A.at[pl.ds(2 * width, d)]),
        (small_h, A.at[pl.ds(2 * width + d, small_h.shape[0])]),
        (k_h, k), (v_h, v), (q_h, q), (o_h, o), (do_h, do), (lse_h, lse), (lift_h, lift),
        (n1_h, n1), (X_h, X), (wqk_h, wqk), (wf_h, wf), (vec_h, vec), (dmid_h, dmid),
    ]
    loads = [pltpu.make_async_copy(a, b, ld.at[i]) for i, (a, b) in enumerate(loads)]
    for copy in loads:
        copy.start()
    peers = [
        ((w + a) % nw, ((g + e) % nw) * G + m) for a in range(nw) for e in range(nw) if a or e
    ]
    peers += [(w, g * G + (m + e) % G) for e in range(1, G)]
    greet(peers + [right, left])
    ring_a = Ring(nc, pos, right, left, seg_a, A, slots_a, res_a, ssa, sra)
    ring_b = Ring(nc, pos, right, left, seg_b, B, slots_b, res_b, ssb, srb)
    for copy in loads[:4]:
        copy.wait()
    ring_a.send(0)
    for copy in loads[4:11]:
        copy.wait()

    flip_rows(k, kt)
    dk[...] = jnp.zeros_like(dk)
    dv[...] = jnp.zeros_like(dv)
    dqk[...] = jnp.zeros_like(dqk)
    wide = H * HEAD_DIM

    def tile(t, carry):
        here = pl.ds(pl.multiple_of((t * G + m) * R, R), R)
        mine = pl.ds(pl.multiple_of(t * R, R), R)
        dqt = attend_back_tile(
            H, q[here, :], do[mine, :], o[mine, :], lse[t], k, v, kt, dk, dv, lift, t
        )
        dqk[here, 0:wide] = jnp.transpose(dqt).astype(BF)
        ring_a.add(t)
        ring_a.send(t + 1)
        return carry

    lax.fori_loop(0, nw, tile, 0)
    dqk[:, wide : 2 * wide] = dk[...].astype(BF)
    dvb[...] = dv[...].astype(BF)
    at_a = nw
    for copy in loads[11:]:
        copy.wait()

    upper = w >= 2
    first_copies = []
    for e in range(1, G):
        mm = (m + e) % G
        for gp in range(nw):
            src = dvb.at[pl.ds(pl.multiple_of((gp * G + mm) * R, R), R)]
            first_copies.append(
                remote(src, f1.at[m, gp], sf1.at[e, gp], rf1.at[m, gp], (w, g * G + mm))
            )

    @pl.when(upper)
    def _():
        for r in first_copies:
            r.start()

    gs[...] = jnp.zeros_like(gs)

    def block(i, carry):
        phase = i // (2 * G)
        jj = (hi + 1 - (i // G) % 2 + 2) % 2
        mm = (m + 1 + i % G) % G
        parity = (1 - par) * (1 - phase) + par * phase
        b = (2 * jj + parity) * G + mm
        at = pl.ds(pl.multiple_of(b * R, R), R)
        dn = product_right(dqk[at, :], wqk[...]) + product_right(dvb[at, :], wf[...])
        low = dn.astype(BF)
        D[b] = low

        @pl.when(phase == 0)
        def _():
            slot = jj * G + mm
            remote(D.at[b], b1.at[slot], s1.at[slot], r1.at[slot], core).start()

        value = X[b].astype(F32)
        centred = value - jnp.mean(value, axis=-1, keepdims=True)
        normal = centred * lax.rsqrt(jnp.mean(centred * centred, axis=-1, keepdims=True) + EPS)
        low = low.astype(F32)
        gs[0:1, :] += jnp.sum(low * normal, axis=0, keepdims=True)
        gs[1:2, :] += jnp.sum(low, axis=0, keepdims=True)
        return carry

    lax.fori_loop(0, nc, block, 0)
    ring_a.step(at_a)
    at_a += 1

    tile_d = 256

    def grads(i, carry):
        at = pl.ds(pl.multiple_of(i * tile_d, tile_d), tile_d)
        gq[at, 0 : 2 * wide] = product_left(n1[:, at], dqk[...]).astype(BF)
        gq[at, 2 * wide : 3 * wide] = product_left(n1[:, at], dvb[...]).astype(BF)
        return carry

    lax.fori_loop(0, width // tile_d, grads, 0)
    ones = jnp.ones((N, BLK), BF)
    sum_qk = product_left(dqk[...], ones)
    sum_f = product_left(dvb[...], ones)
    gain_t = jnp.transpose(jnp.broadcast_to(gs[0:1, :], (BLK, width)))
    shift_t = jnp.transpose(jnp.broadcast_to(gs[1:2, :], (BLK, width)))
    lane = lax.broadcasted_iota(jnp.int32, (d, BLK), 1)
    edge = gq.shape[1] - BLK
    for a in range(nw):
        cut = slice(a * d, (a + 1) * d)
        ends = gq[cut, edge:].astype(F32)
        for j, column in enumerate(
            (gain_t[cut], shift_t[cut], sum_qk[:wide], sum_qk[wide:], sum_f)
        ):
            ends = jnp.where(lane == 64 + j, column, ends)
        gq[cut, edge:] = jnp.where(lane < 64 + 5, ends, 0.0).astype(BF)
    swaps = []
    mine = pl.ds(pl.multiple_of(w * d, 16), d)
    for e in range(1, nw):
        to = (w + e) % nw
        r = remote(
            gq.at[pl.ds(pl.multiple_of(to * d, 16), d)], B.at[mine], sx.at[e], rx.at[w], (to, c)
        )
        r.start()
        swaps.append(r)
    B[mine, :] = gq[mine, :]
    ring_a.step(at_a)
    at_a += 1
    for e in range(1, nw):
        src = (w + e) % nw
        at = pl.ds(pl.multiple_of(src * d, 16), d)
        pltpu.make_async_copy(B.at[at], B.at[at], rx.at[src]).wait()
    ring_b.send(0)

    order = list(range(1, G)) + [0]

    def chip_sum(jj, mm):
        slot = jj * G + mm
        pltpu.make_async_copy(b1.at[slot], b1.at[slot], r1.at[slot]).wait()
        return D[(2 * jj + par) * G + mm].astype(F32) + b1[slot].astype(F32)

    seconds = []
    for e in order:
        mm = (m + e) % G
        ab[mm] = chip_sum(1 - hi, mm).astype(BF)
        r = remote(ab.at[mm], b2.at[mm], s2.at[mm], r2.at[mm], other)
        r.start()
        seconds.append(r)
    thirds = []

    def sum_chips():
        for e in order:
            mm = (m + e) % G
            total = chip_sum(hi, mm)
            pltpu.make_async_copy(b2.at[mm], b2.at[mm], r2.at[mm]).wait()
            total = total + b2[mm].astype(F32)
            if e:
                st[mm] = total.astype(BF)
                r = remote(st.at[mm], b3.at[m], s3.at[mm], r3.at[m], (w, g * G + mm))
                r.start()
                thirds.append(r)
            else:
                tot[...] = total

    def sum_first():
        @pl.when(upper)
        def _():
            for gp in range(nw):
                total = dvb[pl.ds(pl.multiple_of((gp * G + m) * R, R), R), :].astype(F32)
                for e in range(1, G):
                    mm = (m + e) % G
                    pltpu.make_async_copy(f1.at[mm, gp], f1.at[mm, gp], rf1.at[mm, gp]).wait()
                    total = total + f1[mm, gp].astype(F32)
                fs[gp] = total.astype(BF)
                own = jnp.logical_and(w == g, g == gp)

                @pl.when(own)
                def _():
                    pltpu.make_async_copy(fs.at[gp], fr.at[par], rf2.at[par]).start()

                @pl.when(jnp.logical_not(own))
                def _():
                    remote(
                        fs.at[gp], fr.at[par], sf2.at[gp], rf2.at[par], (g, gp * G + m)
                    ).start()

    home = (g, w * G + m)
    back = remote(tb, tr, sT.at[0], rT.at[0], home)
    stay = pltpu.make_async_copy(tb, tr, rT.at[0])

    def norm_back():
        total = tot[...]
        for e in range(1, G):
            mm = (m + e) % G
            pltpu.make_async_copy(b3.at[mm], b3.at[mm], r3.at[mm]).wait()
            total = total + b3[mm].astype(F32)
        value = X[w * G + m].astype(F32)
        centred = value - jnp.mean(value, axis=-1, keepdims=True)
        inverse = lax.rsqrt(jnp.mean(centred * centred, axis=-1, keepdims=True) + EPS)
        normal = centred * inverse
        dx = total * vec[0:1, :]
        dx = dx - jnp.mean(dx, axis=-1, keepdims=True) - normal * jnp.mean(
            dx * normal, axis=-1, keepdims=True
        )
        tb[...] = (dmid[...].astype(F32) + inverse * dx).astype(BF)

        @pl.when(w == g)
        def _():
            stay.start()

        @pl.when(w != g)
        def _():
            back.start()

    steps = 2 * (nc - 1)
    at_b = 0
    turn = 0
    while at_a < steps or at_b < steps:
        if at_b < steps:
            ring_b.step(at_b)
            at_b += 1
        if at_a < steps:
            ring_a.step(at_a)
            at_a += 1
        if at_b < steps:
            ring_b.step(at_b)
            at_b += 1
        if turn == 0:
            sum_first()
        if turn == 2:
            sum_chips()
        if turn == 4:
            norm_back()
        turn += 1

    for a in range(nw):
        rows = slice(a * d, (a + 1) * d)
        up_out[:, a * width : (a + 1) * width] = res_a[rows, :].astype(F32)
        for part in range(2):
            qkv_out[:, part * width + a * d : part * width + (a + 1) * d] = res_b[
                rows, part * d : (part + 1) * d
            ].astype(F32)
        if a < 2:
            qkv_out[:, 2 * width + a * d : 2 * width + (a + 1) * d] = res_b[
                rows, 2 * d : 3 * d
            ].astype(F32)
    down_out[...] = res_a[width : 2 * width, :].astype(F32)
    gout_out[...] = res_a[2 * width : 2 * width + d, :].astype(F32)
    small_out[...] = res_a[2 * width + d : 2 * width + d + small_out.shape[0], :].astype(F32)
    ends_out[...] = res_b[0:width, edge:].astype(F32)
    pltpu.make_async_copy(tr, tr, rT.at[0]).wait()
    tokens_out[...] = tr[...].astype(F32)
    for u in range(2):
        pltpu.make_async_copy(fr.at[u], fr.at[u], rf2.at[u]).wait()
        first_out[:, u * d : (u + 1) * d] = fr[u].astype(F32)

    ring_a.drain()
    ring_b.drain()
    for r in swaps + seconds + thirds:
        r.wait_send()

    @pl.when(w != g)
    def _():
        back.wait_send()

    @pl.when(upper)
    def _():
        for r in first_copies:
            r.wait_send()
        for gp in range(nw):

            @pl.when(jnp.logical_not(jnp.logical_and(w == g, g == gp)))
            def _():
                remote(
                    fs.at[gp], fr.at[par], sf2.at[gp], rf2.at[par], (g, gp * G + m)
                ).wait_send()

    def drain(i, carry):
        jj = (hi + 1 - (i // G) % 2 + 2) % 2
        mm = (m + 1 + i % G) % G
        slot = jj * G + mm
        b = (2 * jj + 1 - par) * G + mm
        remote(D.at[b], b1.at[slot], s1.at[slot], r1.at[slot], core).wait_send()
        return carry

    lax.fori_loop(0, 2 * G, drain, 0)


def tail(G, H, q, k, v, o, do, lse, lift, n1, X, wqk, wf, vec, dmid, up, down, gout, small):
    nw = 4
    nc = nw * G
    R, width = dmid.shape
    d = width // nw
    N = n1.shape[0]
    wide = H * HEAD_DIM
    rows_a = 2 * width + d + small.shape[0]
    seg_a = -(-rows_a // (2 * nc * 16)) * 16
    seg_b = -(-width // (2 * nc * 16)) * 16
    cols = 5 * BLK
    dma = pltpu.SemaphoreType.DMA
    vm = pltpu.VMEM
    steps = 2 * (nc - 1)
    operands = (q, k, v, o, do, lse, lift, n1, X, wqk, wf, vec, dmid, up, down, gout, small)
    return pl.pallas_call(
        functools.partial(tail_kernel, G, H, seg_a, seg_b),
        name="tail",
        out_shape=(
            jax.ShapeDtypeStruct((R, width), F32),
            jax.ShapeDtypeStruct((R, 2 * d), F32),
            jax.ShapeDtypeStruct((d, nw * width), F32),
            jax.ShapeDtypeStruct((width, width), F32),
            jax.ShapeDtypeStruct((d, width), F32),
            jax.ShapeDtypeStruct(small.shape, F32),
            jax.ShapeDtypeStruct((d, 2 * width + 2 * d), F32),
            jax.ShapeDtypeStruct((width, BLK), F32),
        ),
        in_specs=[ANY] * len(operands),
        out_specs=[VM] * 8,
        scratch_shapes=[vm(a.shape, a.dtype) for a in operands[:13]]
        + [
            vm((wide, N), BF), vm((N, wide), F32), vm((N, wide), F32), vm((N, 2 * wide), BF),
            vm((N, wide), BF), vm((nc, R, width), BF), vm((2 * G, R, width), BF),
            vm((G, R, width), BF), vm((G, R, width), BF), vm((G, R, width), BF),
            vm((G, R, width), BF), vm((R, width), F32), vm((R, width), BF), vm((R, width), BF),
            vm((2 * nc * seg_a, width), BF), vm((2, nc - 1, seg_a, width), BF),
            vm((2 * nc * seg_a, width), BF),
            vm((width, cols), BF), vm((2 * nc * seg_b, cols), BF),
            vm((2, nc - 1, seg_b, cols), BF), vm((2 * nc * seg_b, cols), BF),
            vm((8, width), F32), vm((G, nw, R, d), BF), vm((nw, R, d), BF), vm((2, R, d), BF),
            dma((2 * G,)), dma((2 * G,)), dma((G,)), dma((G,)), dma((G,)), dma((G,)),
            dma((1,)), dma((1,)), dma((2, steps)), dma((2, steps)), dma((2, steps)),
            dma((2, steps)), dma((nw,)), dma((nw,)), dma((G, nw)), dma((G, nw)),
            dma((nw,)), dma((2,)), dma((len(operands),)),
        ],
        compiler_params=pltpu.CompilerParams(
            collective_id=2, has_side_effects=True, vmem_limit_bytes=63 << 20
        ),
        cost_estimate=pl.CostEstimate(
            flops=40 << 30, bytes_accessed=60 << 20, transcendentals=6 << 20
        ),
    )(*operands)


def on_device(
    nw,
    nc,
    tokens,
    first_values,
    cotangent,
    deal,
    w_qkv,
    bias_qv,
    w_out,
    bias_out,
    gain_one,
    shift_one,
    gain_two,
    shift_two,
    w_up,
    bias_up,
    w_down,
    bias_down,
):
    G = nc // nw
    w = lax.axis_index("wt")
    c = lax.axis_index("ctx")
    m = c % G
    rows, width = tokens.shape[1:]
    d = width // nw
    H = HEADS // nw
    both = ("wt", "ctx")
    swap = [
        (a * nc + g * G + e, g * nc + a * G + e)
        for a in range(nw)
        for g in range(nw)
        for e in range(G)
    ]
    ring = [[(a, (a + k) % nw) for a in range(nw)] for k in range(nw)]

    def exchange(pieces):
        out = jnp.zeros_like(pieces)
        mine = lax.dynamic_index_in_dim(pieces, w, 0, keepdims=True)
        out = lax.dynamic_update_slice_in_dim(out, mine, w, 0)
        for k in range(1, nw):
            piece = lax.dynamic_index_in_dim(pieces, (w + k) % nw, 0, keepdims=True)
            got = lax.ppermute(piece, "wt", ring[k])
            out = lax.dynamic_update_slice_in_dim(out, got, (w + nw - k) % nw, 0)
        return out

    qk = w_qkv[:, : 2 * width].reshape(d, 2, nw, d).transpose(2, 0, 1, 3).reshape(nw, d, 2 * d)
    wf = w_qkv[:, 2 * width :].reshape(d, 2, d).transpose(1, 0, 2)
    small = jnp.concatenate(
        [bias_qv, bias_out, gain_one, shift_one, gain_two, shift_two, bias_down]
    )
    lanes = 16 * BLK
    small = jnp.concatenate([small, jnp.zeros((lanes - small.shape[0],), BF)]).reshape(16, BLK)
    X, Fv, WQK, WF, SM = gather(nw, G, tokens[0], first_values[0], qk, wf, small)
    X = X.reshape(nc * rows, width)
    Wqk = WQK.reshape(width, 2 * d)
    low = w < 2
    Wf = jnp.where(low, WF.reshape(width, d), jnp.zeros((width, d), BF))
    SM = SM.reshape(nw, lanes).astype(F32)
    nb = bias_qv.shape[0]
    qv_vector = SM[:, :nb].reshape(-1)
    vectors = [SM[:, nb + a * d : nb + (a + 1) * d].reshape(-1) for a in range(6)]
    out_vector, gain_a, shift_a, gain_b, shift_b, down_vector = vectors

    x32 = X.astype(F32)
    mean = jnp.mean(x32, axis=-1, keepdims=True)
    centred = x32 - mean
    inverse = lax.rsqrt(jnp.mean(centred * centred, axis=-1, keepdims=True) + EPS)
    n1 = (centred * inverse * gain_a + shift_a).astype(BF)
    pqk = product(n1, Wqk)
    q_bias = lax.dynamic_slice_in_dim(qv_vector, w * d, d)
    f_bias = lax.dynamic_slice_in_dim(qv_vector, width + (w % 2) * d, d)
    q = (pqk[:, :d] + q_bias).astype(BF)
    k = pqk[:, d:].astype(BF)
    f = (product(n1, Wf) + f_bias).astype(BF)
    Fv = Fv.reshape(nc * rows, 2 * d)
    first = jnp.where(w % 2 == 0, Fv[:, :d], Fv[:, d:])
    v = jnp.where(low, f, first)

    ids = dealt_blocks(deal)
    qpos = jnp.arange(nw, dtype=jnp.int32) * G + m
    qid = jnp.take(ids.reshape(nc, 2), qpos, axis=0)
    hidden = (ids[None, None, :] > qid[:, :, None]).astype(F32) * -NEG
    bias = jnp.repeat(-hidden.reshape(2 * nw, 2 * nc), BLK, axis=1)[:, None, :]
    lift = jnp.repeat(hidden.transpose(0, 2, 1), BLK, axis=2)
    o, lse = attend(H, qpos, bias, q, k, v)

    part = product(o, w_out).astype(BF)
    pieces, spread = lax.optimization_barrier((w_up, cotangent[0], X))[:2]
    Wup = exchange(pieces.reshape(d, nw, width).transpose(1, 0, 2)).reshape(width, width)
    cot = lax.all_gather(lax.ppermute(spread, both, swap), "wt", axis=0, tiled=True)
    vec = jnp.stack([out_vector, gain_b, shift_b, bias_up.astype(F32)] + [out_vector] * 4)
    mlp, mid_own, d_mid, d_o, g_up, g_down, g_out, vsums = middle(
        G, part, X.reshape(nc, rows, width), cot, o, Wup, w_down, w_out, vec
    )
    mlp = lax.psum_scatter(mlp, "wt", scatter_dimension=0, tiled=True)
    layer = (mid_own + mlp.astype(F32) + down_vector).astype(BF)
    layer = lax.ppermute(layer, both, swap)

    def mine(vector):
        return lax.dynamic_slice_in_dim(vector, w * d, d)

    if nc <= 8:
        small = jnp.stack(
            [vsums[0], jnp.concatenate([mine(vsums[a]) for a in range(1, 5)])]
            + [jnp.zeros((width,), F32)] * 14
        ).astype(BF)
        rows_a = 2 * width + d + 16
        pad = -(-rows_a // (32 * nc)) * 32 * nc - rows_a
        small = jnp.concatenate([small, jnp.zeros((pad, width), BF)], axis=0)
        norm = jnp.broadcast_to(gain_a[None], (8, width))
        grad_tokens, grad_first, s_up, s_down, s_out, s_small, s_qkv, ends = tail(
            G, H, q, k, v, o, d_o, lse, lift, n1, X.reshape(nc, rows, width), Wqk, Wf, norm,
            d_mid, g_up, g_down, g_out, small,
        )
        ends = ends.reshape(nw, d, BLK)
        bias_all = jnp.concatenate([ends[:, :, 66].reshape(-1), ends[:2, :, 68].reshape(-1)])
        s_vec = s_small[1].reshape(nw, d)
        return (
            layer[None],
            grad_tokens[None],
            grad_first[None],
            s_qkv,
            lax.dynamic_slice_in_dim(bias_all, w * nb, nb),
            s_out,
            s_vec[1],
            jnp.sum(ends[:, :, 64], axis=0),
            jnp.sum(ends[:, :, 65], axis=0),
            s_vec[2],
            s_vec[3],
            s_up,
            s_small[0],
            s_down,
            s_vec[0],
        )
    up_rows = g_up.reshape(nw, d, width).transpose(1, 0, 2)
    s_up, s_down = lax.psum((up_rows.reshape(d, nw * width), g_down), "ctx")
    dqk, dv = attend_back(H, qpos, lift, q, k, v, o, d_o, lse)
    zero = jnp.zeros_like(dv)
    df = jnp.where(low, dv, zero)
    dn1 = product_right(dqk, Wqk) + product_right(df, Wf)
    dn1_low = dn1.astype(BF)
    blank = jnp.zeros_like(dv)
    left = jnp.where(w == 2, dv, blank)
    right = jnp.where(w == 3, dv, blank)
    total = scatter_sum(
        G, jnp.concatenate([dn1_low, left, right], axis=1).reshape(nc, rows, width + 2 * d)
    )
    grad_first = lax.ppermute(total[:, width:].astype(BF), both, swap).astype(F32)
    block = (w * G + m) * rows
    x_own = lax.dynamic_slice_in_dim(X, block, rows).astype(F32)
    _, pull_one = jax.vjp(lambda a: norm_rows(a, gain_a, shift_a), x_own)
    d_x = d_mid.astype(F32) + pull_one(total[:, :width])[0]
    grad_tokens = lax.ppermute(d_x.astype(BF), both, swap).astype(F32)

    g_qk = product_left(n1, dqk)
    g_f = product_left(n1, df)
    normal = centred * inverse
    g_gain_one = jnp.sum(dn1_low.astype(F32) * normal, axis=0)
    g_shift_one = jnp.sum(dn1_low.astype(F32), axis=0)
    cols = jnp.concatenate(
        [
            g_qk.astype(BF),
            g_f.astype(BF),
            g_gain_one[:, None].astype(BF),
            g_shift_one[:, None].astype(BF),
            jnp.zeros((width, 62), BF),
        ],
        axis=1,
    ).reshape(nw, d, 640)
    sums = jnp.concatenate(
        [jnp.sum(dqk.astype(F32), axis=0), jnp.sum(df.astype(F32), axis=0), jnp.zeros((64,), F32)]
    ).astype(BF)
    foot = jnp.concatenate([sums[None], jnp.zeros((7, 640), BF)], axis=0)
    pack = jnp.concatenate([cols, jnp.broadcast_to(foot[None], (nw, 8, 640))], axis=1)
    pack = exchange(pack)
    vecs = jnp.concatenate(
        [
            vsums[0],
            mine(vsums[1]),
            mine(vsums[2]),
            mine(vsums[3]),
            mine(vsums[4]),
        ]
    ).astype(BF)
    pack = pack.at[0, d + 1 : d + 4, :512].set(vecs.reshape(3, 512))
    pack, s_up, s_down = lax.optimization_barrier((pack, s_up, s_down))
    pack, s_out = lax.psum((pack, g_out), "ctx")
    body = pack[:, :d]
    s_qkv = jnp.concatenate(
        [body[a, :, e * d : (e + 1) * d] for e in (0, 1) for a in range(nw)]
        + [body[a, :, 2 * d : 3 * d] for a in range(2)],
        axis=1,
    ).astype(F32)
    s_gain_one = jnp.sum(body[:, :, 576].astype(F32), axis=0)
    s_shift_one = jnp.sum(body[:, :, 577].astype(F32), axis=0)
    ends = pack[:, d]
    bias_all = jnp.concatenate([ends[:, :d].reshape(-1), ends[:2, 2 * d : 3 * d].reshape(-1)])
    s_bias_qv = lax.dynamic_slice_in_dim(bias_all, w * nb, nb).astype(F32)
    vecs = pack[0, d + 1 : d + 4, :512].reshape(-1).astype(F32)
    s_bias_up = vecs[:width]
    s_bias_down, s_bias_out, s_gain_two, s_shift_two = [
        vecs[width + a * d : width + (a + 1) * d] for a in range(4)
    ]
    return (
        layer[None],
        grad_tokens[None],
        grad_first[None],
        s_qkv,
        s_bias_qv,
        s_out.astype(F32),
        s_bias_out,
        s_gain_one,
        s_shift_one,
        s_gain_two,
        s_shift_two,
        s_up.astype(F32),
        s_bias_up,
        s_down.astype(F32),
        s_bias_down,
    )


def solution(mesh):
    rows3 = P("wt", "ctx", None)
    mat = P("wt", None)
    vec = P("wt")
    in_specs = (rows3, rows3, rows3, P(), mat, vec, mat) + (vec,) * 5 + (mat, vec, mat, vec)
    out_specs = (
        (rows3, rows3, rows3, mat, vec, mat) + (vec,) * 5 + (mat, vec, mat, vec)
    )
    return jax.shard_map(
        functools.partial(on_device, mesh.shape["wt"], mesh.shape["ctx"]),
        mesh=mesh,
        in_specs=in_specs,
        out_specs=out_specs,
        check_vma=False,
    )
```

```python
import functools

import jax
import jax.numpy as jnp
from jax import lax
from jax.experimental import pallas as pl
from jax.experimental.pallas import tpu as pltpu
from jax.sharding import PartitionSpec as P

HEADS = 12
HEAD_DIM = 64
BLK = 128
CHUNK = 1024

EPS = 1e-05
SLOPE = 0.7978845608028654
CUBIC = 0.044715
NEG = -1e30

BF = jnp.bfloat16
F32 = jnp.float32
MESH = pl.DeviceIdType.MESH
ANY = pl.BlockSpec(memory_space=pl.ANY)
VM = pl.BlockSpec(memory_space=pltpu.VMEM)


def norm_rows(value, gain, shift):
    mean = jnp.mean(value, axis=-1, keepdims=True)
    centred = value - mean
    inverse = lax.rsqrt(jnp.mean(centred * centred, axis=-1, keepdims=True) + EPS)
    return centred * inverse * gain + shift


def gelu_tanh(value):
    return 0.5 * value * (1.0 + jnp.tanh(SLOPE * (value + CUBIC * value * value * value)))


def product(left, right):
    return jnp.dot(left, right, preferred_element_type=F32)


def product_left(left, right):
    return lax.dot_general(left, right, (((0,), (0,)), ((), ())), preferred_element_type=F32)


def product_right(left, right):
    return lax.dot_general(left, right, (((1,), (1,)), ((), ())), preferred_element_type=F32)


def dealt_blocks(deal):
    count = deal.shape[0] * 2
    pairs = jnp.repeat(deal, 2)
    parity = jnp.arange(count, dtype=jnp.int32) % 2
    return jnp.where(parity == 0, pairs, count - 1 - pairs)


def remote(src, dst, send, recv, device):
    return pltpu.make_async_remote_copy(
        src_ref=src,
        dst_ref=dst,
        send_sem=send,
        recv_sem=recv,
        device_id=device,
        device_id_type=MESH,
    )


def greet(peers):
    barrier = pltpu.get_barrier_semaphore()
    for peer in peers:
        pl.semaphore_signal(barrier, inc=1, device_id=peer, device_id_type=MESH)
    pl.semaphore_wait(barrier, len(peers))


def gather_kernel(
    nw, G, x, first, wqk, wf, small, X, Fv, WQK, WF, SM, rx, rf, rw, rv, rs, sa, sx, sfa, sfx, sw, loc
):
    w = lax.axis_index("wt")
    c = lax.axis_index("ctx")
    g = c // G
    m = c % G
    nc = nw * G
    core = w + 1 - 2 * (w % 2)
    other = (w + 2) % nw
    rel = lambda k: (w + k) % nw
    peers = [(rel(k), c) for k in range(1, nw)]
    peers += [(w, ((g + k) % nw) * G + m) for k in range(1, nw)]
    peers += [(w, g * G + (m + k) % G) for k in range(1, G)]
    greet(peers)
    seq = 2 * (g % 2) + g // 2
    goal = (2 * (w % 2) + w // 2) * G + m
    is_a = w == seq
    primary = (w + seq) % 2 == 0
    high = w >= 2
    copies = []

    to_head = remote(x, X.at[c], sa.at[0], rx.at[c], (w, goal))
    to_head_f = remote(first, Fv.at[c], sa.at[1], rf.at[c], (w, goal))
    own_x = pltpu.make_async_copy(x, X.at[c], rx.at[c])
    own_f = pltpu.make_async_copy(first, Fv.at[c], rf.at[c])

    @pl.when(is_a)
    def _():
        own_x.start()
        own_f.start()

    @pl.when(jnp.logical_not(is_a))
    def _():
        to_head.start()
        to_head_f.start()

    own_w = pltpu.make_async_copy(wqk.at[w], WQK.at[w], loc.at[0])
    own_s = pltpu.make_async_copy(small, SM.at[w], loc.at[1])
    own_w.start()
    own_s.start()
    own_v = pltpu.make_async_copy(wf.at[w % 2], WF.at[w], loc.at[2])
    own_v.start()
    sends_w, sends_v, sends_s = [], [], []
    for k in range(1, nw):
        d = rel(k)
        s = remote(small, SM.at[w], sw.at[k, 0], rs.at[w], (d, c))
        s.start()
        q = remote(wqk.at[d], WQK.at[w], sw.at[k, 1], rw.at[w], (d, c))
        q.start()
        v = remote(wf.at[d % 2], WF.at[w], sw.at[k, 2], rv.at[w], (d, c))
        sends_w += [s, q]
        sends_v.append((d, v))

        @pl.when(d < 2)
        def _():
            v.start()

    def block_x(b):
        return pltpu.make_async_copy(X.at[b], X.at[b], rx.at[b])

    def block_f(b):
        return pltpu.make_async_copy(Fv.at[b], Fv.at[b], rf.at[b])

    fwd_core, fwd_other, fwd_member = [], [], []
    for k in range(nw):
        gp = (g + k) % nw
        b = gp * G + m
        to_core = remote(X.at[b], X.at[b], sx.at[0, b], rx.at[b], (core, c))
        to_other = remote(X.at[b], X.at[b], sx.at[1, b], rx.at[b], (other, c))
        to_core_f = remote(Fv.at[b], Fv.at[b], sfx.at[0, b], rf.at[b], (core, c))
        to_other_f = remote(Fv.at[b], Fv.at[b], sfx.at[1, b], rf.at[b], (other, c))
        members = [
            remote(X.at[b], X.at[b], sx.at[1 + e, b], rx.at[b], (w, g * G + (m + e) % G))
            for e in range(1, G)
        ]
        members_f = [
            remote(Fv.at[b], Fv.at[b], sfx.at[1 + e, b], rf.at[b], (w, g * G + (m + e) % G))
            for e in range(1, G)
        ]

        @pl.when(primary)
        def _():
            block_x(b).wait()

            @pl.when(is_a)
            def _():
                to_other.start()

            for r in members:
                r.start()
            to_core.start()

        @pl.when(jnp.logical_and(is_a, jnp.logical_not(high)))
        def _():
            block_f(b).wait()
            to_other_f.start()

        @pl.when(jnp.logical_and(primary, high))
        def _():
            block_f(b).wait()
            for r in members_f:
                r.start()
            to_core_f.start()

        fwd_core.append((to_core, to_core_f))
        fwd_other.append((to_other, to_other_f))
        fwd_member.append((members, members_f))
    for e in range(1, G):
        for k in range(nw):
            b = ((g + k) % nw) * G + (m + e) % G
            to_core = remote(X.at[b], X.at[b], sx.at[0, b], rx.at[b], (core, c))
            to_core_f = remote(Fv.at[b], Fv.at[b], sfx.at[0, b], rf.at[b], (core, c))

            @pl.when(primary)
            def _():
                block_x(b).wait()
                to_core.start()

            @pl.when(jnp.logical_and(primary, high))
            def _():
                block_f(b).wait()
                to_core_f.start()

            fwd_core.append((to_core, to_core_f))

    @pl.when(jnp.logical_not(primary))
    def _():
        for b in range(nc):
            block_x(b).wait()

        @pl.when(high)
        def _():
            for b in range(nc):
                block_f(b).wait()

    own_w.wait()
    own_s.wait()
    own_v.wait()
    for k in range(1, nw):
        src = (w + nw - k) % nw
        pltpu.make_async_copy(wqk.at[0], WQK.at[src], rw.at[src]).wait()
        pltpu.make_async_copy(small, SM.at[src], rs.at[src]).wait()

        @pl.when(w < 2)
        def _():
            pltpu.make_async_copy(wf.at[0], WF.at[src], rv.at[src]).wait()

    for s in sends_w:
        s.wait_send()
    for d, v in sends_v:

        @pl.when(d < 2)
        def _():
            v.wait_send()

    @pl.when(jnp.logical_not(is_a))
    def _():
        to_head.wait_send()
        to_head_f.wait_send()

    @pl.when(primary)
    def _():
        for a, _f in fwd_core:
            a.wait_send()
        for ms, _f in fwd_member:
            for a in ms:
                a.wait_send()

        @pl.when(high)
        def _():
            for _x, a in fwd_core:
                a.wait_send()
            for _x, ms in fwd_member:
                for a in ms:
                    a.wait_send()

    @pl.when(is_a)
    def _():
        for a, _f in fwd_other:
            a.wait_send()

        @pl.when(jnp.logical_not(high))
        def _():
            for _x, a in fwd_other:
                a.wait_send()


def gather(nw, G, x, first, wqk, wf, small):
    nc = nw * G
    rows, width = x.shape
    half = first.shape[1]
    d = width // nw
    dma = pltpu.SemaphoreType.DMA
    return pl.pallas_call(
        functools.partial(gather_kernel, nw, G),
        name="gather_tokens",
        out_shape=(
            jax.ShapeDtypeStruct((nc, rows, width), BF),
            jax.ShapeDtypeStruct((nc, rows, half), BF),
            jax.ShapeDtypeStruct((nw, d, 2 * d), BF),
            jax.ShapeDtypeStruct((nw, d, d), BF),
            jax.ShapeDtypeStruct((nw,) + small.shape, BF),
        ),
        in_specs=[ANY] * 5,
        out_specs=[ANY] * 5,
        scratch_shapes=[
            dma((nc,)),
            dma((nc,)),
            dma((nw,)),
            dma((nw,)),
            dma((nw,)),
            dma((2,)),
            dma((1 + G, nc)),
            dma((2,)),
            dma((1 + G, nc)),
            dma((nw, 3)),
            dma((3,)),
        ],
        compiler_params=pltpu.CompilerParams(collective_id=0, has_side_effects=True),
    )(x, first, wqk, wf, small)


def middle_kernel(
    T, G, p_hbm, X_hbm, cot_hbm, o_hbm, wup_hbm, wdn_hbm, wout_hbm, vec_hbm,
    mlp, mid_own, dmid_own, do_out, upr, gdn, gout, sums,
    p, x, cot, o, wup, wdn, wout, vec,
    b1, ab, b2, bs, mid, n2s, act, dus, q, b4, ab2, b5, dn, dbs, gup,
    s1, r1, s2, r2, s3, r3, s4, r4, s5, r5, s6, r6, ld, sx, rx,
):
    w = lax.axis_index("wt")
    c = lax.axis_index("ctx")
    g = c // G
    m = c % G
    core = (w + 1 - 2 * (w % 2), c)
    other = ((w + 2) % 4, c)
    mine = w % 2
    theirs = 1 - mine
    rows = p.shape[0]
    half = rows // 2
    n = half // T
    R = rows // 4
    loads = [
        pltpu.make_async_copy(p_hbm, p, ld.at[0]),
        pltpu.make_async_copy(vec_hbm, vec, ld.at[1]),
    ]
    loads += [
        pltpu.make_async_copy(X_hbm.at[a * G + m], x.at[pl.ds(a * R, R)], ld.at[2 + a])
        for a in range(4)
    ]
    loads += [
        pltpu.make_async_copy(wup_hbm, wup, ld.at[6]),
        pltpu.make_async_copy(wdn_hbm, wdn, ld.at[7]),
        pltpu.make_async_copy(cot_hbm, cot, ld.at[8]),
        pltpu.make_async_copy(wout_hbm, wout, ld.at[9]),
        pltpu.make_async_copy(o_hbm, o, ld.at[10]),
    ]
    for copy in loads:
        copy.start()
    greet([core, other, ((w + 3 - 2 * (w % 2)) % 4, c)])

    def rs(base, t):
        return pl.ds(pl.multiple_of(base * half + t * n, n), n)

    loads[0].wait()
    first = []
    for t in range(T):
        r = remote(p.at[rs(theirs, t)], b1.at[t], s1.at[t], r1.at[t], core)
        r.start()
        first.append(r)
    second = []
    for t in range(T):
        first[t].wait_recv()
        ab[t] = (p[rs(mine, t), :].astype(F32) + b1[t].astype(F32)).astype(BF)
        r = remote(ab.at[t], b2.at[t], s2.at[t], r2.at[t], other)
        r.start()
        second.append(r)
    for copy in loads[1:]:
        copy.wait()
    out_b = vec[0:1, :]
    gain = vec[1:2, :]
    shift = vec[2:3, :]
    up_b = vec[3:4, :]
    sums[...] = jnp.zeros_like(sums)

    def two(ref, t):
        return jnp.concatenate([ref[rs(mine, t), :], ref[rs(theirs, t), :]], axis=0)

    def put(ref, t, value):
        ref[rs(mine, t), :] = value[:n]
        ref[rs(theirs, t), :] = value[n:]

    def add_sum(at, value):
        sums[at : at + 1, :] += jnp.sum(value, axis=0, keepdims=True)

    def chain(t):
        pltpu.make_async_copy(b4.at[t], b4.at[t], r4.at[t]).wait()
        ab2[t] = (q[rs(mine, t), :].astype(F32) + b4[t].astype(F32)).astype(BF)
        remote(ab2.at[t], b5.at[t], s5.at[t], r5.at[t], other).start()

    def forward(t, carry):
        pltpu.make_async_copy(b2.at[t], b2.at[t], r2.at[t]).wait()
        bs[rs(mine, t), :] = (ab[t].astype(F32) + b2[t].astype(F32)).astype(BF)
        remote(bs.at[rs(mine, t)], bs.at[rs(mine, t)], s3.at[t], r3.at[t], core).start()

        @pl.when(t > 0)
        def _():
            chain(t - 1)

        pltpu.make_async_copy(bs.at[rs(theirs, t)], bs.at[rs(theirs, t)], r3.at[t]).wait()
        value = two(x, t).astype(F32) + two(bs, t).astype(F32) + out_b
        put(mid, t, value)
        centred = value - jnp.mean(value, axis=-1, keepdims=True)
        inverse = lax.rsqrt(jnp.mean(centred * centred, axis=-1, keepdims=True) + EPS)
        n2 = (centred * inverse * gain + shift).astype(BF)
        put(n2s, t, n2)
        u = product(n2, wup[...]) + up_b
        th = jnp.tanh(SLOPE * (u + CUBIC * u * u * u))
        a = (0.5 * u * (1.0 + th)).astype(BF)
        slope = 0.5 * (1.0 + th) + 0.5 * u * (1.0 - th * th) * SLOPE * (1.0 + 3.0 * CUBIC * u * u)
        put(act, t, a)
        ct = two(cot, t)
        du = (product_right(ct, wdn[...]) * slope).astype(BF)
        put(dus, t, du)
        put(q, t, product_right(du, wup[...]).astype(BF))
        remote(q.at[rs(theirs, t)], b4.at[t], s4.at[t], r4.at[t], core).start()
        put(mlp, t, product(a, wdn[...]).astype(BF))
        add_sum(0, du.astype(F32))
        add_sum(1, ct.astype(F32))
        return carry

    lax.fori_loop(0, T, forward, 0)
    chain(T - 1)

    width = p.shape[1]
    tile = 256

    def grads(i, carry):
        at = pl.ds(pl.multiple_of(i * tile, tile), tile)
        gup[at, :] = product_left(n2s[:, at], dus[...]).astype(BF)
        gdn[at, :] = product_left(act[:, at], cot[...]).astype(BF)
        return carry

    lax.fori_loop(0, width // tile, grads, 0)
    d = width // 4
    block = lambda a: pl.ds(pl.multiple_of(a * d, 16), d)
    swaps = []
    for e in range(1, 4):
        to = (w + e) % 4
        r = remote(gup.at[block(to)], upr.at[block(w)], sx.at[e], rx.at[w], (to, c))
        r.start()
        swaps.append(r)
    upr[block(w), :] = gup[block(w), :]

    def backward(t, carry):
        pltpu.make_async_copy(b5.at[t], b5.at[t], r5.at[t]).wait()
        dn[rs(mine, t), :] = (ab2[t].astype(F32) + b5[t].astype(F32)).astype(BF)
        remote(dn.at[rs(mine, t)], dn.at[rs(mine, t)], s6.at[t], r6.at[t], core).start()
        pltpu.make_async_copy(dn.at[rs(theirs, t)], dn.at[rs(theirs, t)], r6.at[t]).wait()
        value = two(mid, t)
        centred = value - jnp.mean(value, axis=-1, keepdims=True)
        inverse = lax.rsqrt(jnp.mean(centred * centred, axis=-1, keepdims=True) + EPS)
        normal = centred * inverse
        dn2 = two(dn, t).astype(F32)
        add_sum(3, dn2 * normal)
        add_sum(4, dn2)
        dx = dn2 * gain
        dx = dx - jnp.mean(dx, axis=-1, keepdims=True) - normal * jnp.mean(
            dx * normal, axis=-1, keepdims=True
        )
        dmid = two(cot, t).astype(F32) + inverse * dx
        db = dmid.astype(BF)
        put(dbs, t, db)
        add_sum(2, db.astype(F32))
        put(do_out, t, product_right(db, wout[...]).astype(BF))
        return carry

    lax.fori_loop(0, T, backward, 0)
    gout[...] = product_left(o[...], dbs[...]).astype(BF)
    own = pl.ds(pl.multiple_of(w * R, R), R)
    mid_own[...] = mid[own, :]
    dmid_own[...] = dbs[own, :]
    for e in range(1, 4):
        src = (w + e) % 4
        pltpu.make_async_copy(upr.at[block(src)], upr.at[block(src)], rx.at[src]).wait()
    for r in swaps:
        r.wait_send()
    for t in range(T):
        first[t].wait_send()
        second[t].wait_send()
        remote(bs.at[rs(mine, t)], bs.at[rs(mine, t)], s3.at[t], r3.at[t], core).wait_send()
        remote(q.at[rs(theirs, t)], b4.at[t], s4.at[t], r4.at[t], core).wait_send()
        remote(ab2.at[t], b5.at[t], s5.at[t], r5.at[t], other).wait_send()
        remote(dn.at[rs(mine, t)], dn.at[rs(mine, t)], s6.at[t], r6.at[t], core).wait_send()


def middle(G, p, X, cot, o, wup, wdn, wout, vec):
    T = 4
    rows, width = p.shape
    n = rows // 2 // T
    R = rows // 4
    d = o.shape[1]
    dma = pltpu.SemaphoreType.DMA
    full = pltpu.VMEM((rows, width), BF)
    part = pltpu.VMEM((T, n, width), BF)
    square = pltpu.VMEM((width, width), BF)
    return pl.pallas_call(
        functools.partial(middle_kernel, T, G),
        name="middle",
        out_shape=(
            jax.ShapeDtypeStruct((rows, width), BF),
            jax.ShapeDtypeStruct((R, width), F32),
            jax.ShapeDtypeStruct((R, width), BF),
            jax.ShapeDtypeStruct((rows, d), BF),
            jax.ShapeDtypeStruct((width, width), BF),
            jax.ShapeDtypeStruct((width, width), BF),
            jax.ShapeDtypeStruct((d, width), BF),
            jax.ShapeDtypeStruct((8, width), F32),
        ),
        in_specs=[ANY] * 8,
        out_specs=[VM] * 8,
        scratch_shapes=[
            full, full, full, pltpu.VMEM((rows, d), BF), square, square,
            pltpu.VMEM((d, width), BF), pltpu.VMEM((8, width), F32),
            part, part, part, full, pltpu.VMEM((rows, width), F32), full, full, full, full,
            part, part, part, full, full, square,
        ]
        + [dma((T,))] * 12
        + [dma((11,)), dma((4,)), dma((4,))],
        compiler_params=pltpu.CompilerParams(
            collective_id=1, has_side_effects=True, vmem_limit_bytes=62 << 20
        ),
        cost_estimate=pl.CostEstimate(
            flops=14 * rows * width * width, bytes_accessed=40 << 20, transcendentals=rows * width
        ),
    )(p, X, cot, o, wup, wdn, wout, vec)


def scatter_kernel(G, D, out, b1, ab, b2, st, b3, s1, r1, s2, r2, s3, r3):
    w = lax.axis_index("wt")
    c = lax.axis_index("ctx")
    g = c // G
    m = c % G
    core = w + 1 - 2 * (w % 2)
    other = (w + 2) % 4
    par = w % 2
    hi = w // 2
    greet([(core, c), (other, c)] + [(w, g * G + (m + e) % G) for e in range(1, G)])
    order = [e for e in range(1, G)] + [0]
    firsts = {}
    for j in (1, 0):
        for e in order:
            jj = (hi + j) % 2
            mm = (m + e) % G
            b = (2 * jj + 1 - par) * G + mm
            slot = jj * G + mm
            r = remote(D.at[b], b1.at[slot], s1.at[slot], r1.at[slot], (core, c))
            r.start()
            firsts[(j, e)] = r

    def arrived1(slot):
        pltpu.make_async_copy(b1.at[slot], b1.at[slot], r1.at[slot]).wait()

    seconds = []
    for e in order:
        jj = 1 - hi
        mm = (m + e) % G
        slot = jj * G + mm
        arrived1(slot)
        ab[mm] = (D[(2 * jj + par) * G + mm].astype(F32) + b1[slot].astype(F32)).astype(BF)
        r = remote(ab.at[mm], b2.at[mm], s2.at[mm], r2.at[mm], (other, c))
        r.start()
        seconds.append(r)
    thirds = []
    for e in order:
        mm = (m + e) % G
        slot = hi * G + mm
        arrived1(slot)
        pltpu.make_async_copy(b2.at[mm], b2.at[mm], r2.at[mm]).wait()
        total = D[w * G + mm].astype(F32) + b1[slot].astype(F32) + b2[mm].astype(F32)
        if e == 0:
            for f in range(1, G):
                q = (m + f) % G
                pltpu.make_async_copy(b3.at[q], b3.at[q], r3.at[q]).wait()
                total = total + b3[q].astype(F32)
            out[...] = total.astype(out.dtype)
        else:
            st[mm] = total.astype(BF)
            r = remote(st.at[mm], b3.at[m], s3.at[mm], r3.at[m], (w, g * G + mm))
            r.start()
            thirds.append(r)
    for r in list(firsts.values()) + seconds + thirds:
        r.wait_send()


def scatter_sum(G, D):
    nc, rows, C = D.shape
    dma = pltpu.SemaphoreType.DMA
    return pl.pallas_call(
        functools.partial(scatter_kernel, G),
        name="scatter_sum",
        out_shape=jax.ShapeDtypeStruct((rows, C), F32),
        in_specs=[VM],
        out_specs=VM,
        scratch_shapes=[
            pltpu.VMEM((2 * G, rows, C), BF),
            pltpu.VMEM((G, rows, C), BF),
            pltpu.VMEM((G, rows, C), BF),
            pltpu.VMEM((G, rows, C), BF),
            pltpu.VMEM((G, rows, C), BF),
            dma((2 * G,)),
            dma((2 * G,)),
            dma((G,)),
            dma((G,)),
            dma((G,)),
            dma((G,)),
        ],
        compiler_params=pltpu.CompilerParams(
            collective_id=3, has_side_effects=True, vmem_limit_bytes=60 << 20
        ),
    )(D)


def head_mask(shape, h):
    lane = lax.broadcasted_iota(jnp.int32, shape, 1)
    return jnp.logical_and(lane >= h * HEAD_DIM, lane < (h + 1) * HEAD_DIM)


def split_heads(H, value):
    zero = jnp.zeros_like(value)
    return [jnp.where(head_mask(value.shape, h), value, zero) for h in range(H)]


def spread(H, shape, values):
    out = jnp.broadcast_to(values[H - 1], shape)
    for h in range(H - 2, -1, -1):
        out = jnp.where(head_mask(shape, h), values[h], out)
    return out


def attend_tile(H, q, k_ref, v_ref, bias_ref, at_bias):
    rows, width = q.shape
    N = k_ref.shape[0]
    step_keys = min(N, 1024)
    qh = split_heads(H, q * jnp.asarray(HEAD_DIM**-0.5, BF))
    top_half = lax.broadcasted_iota(jnp.int32, (rows, 1), 0) < BLK

    def step(j, carry):
        tops, sums, acc = carry
        at = pl.ds(pl.multiple_of(j * step_keys, step_keys), step_keys)
        kc = k_ref[at, :]
        vc = v_ref[at, :]
        low = bias_ref[at_bias, :, at]
        high = bias_ref[at_bias + 1, :, at]
        new_tops, new_sums, shrink, parts = [], [], [], []
        for h in range(H):
            s = product_right(qh[h], kc)
            s = jnp.concatenate([s[:BLK] + low, s[BLK:] + high], axis=0)
            top = jnp.maximum(tops[h], jnp.max(s, axis=1, keepdims=True))
            a = jnp.exp(tops[h] - top)
            p = jnp.exp(s - top)
            new_sums.append(sums[h] * a + jnp.sum(p, axis=1, keepdims=True))
            new_tops.append(top)
            shrink.append(a)
            parts.append(product(p.astype(BF), vc))
        acc = acc * spread(H, acc.shape, shrink) + spread(H, acc.shape, parts)
        return new_tops, new_sums, acc

    start = (
        [jnp.full((rows, 1), NEG, F32)] * H,
        [jnp.zeros((rows, 1), F32)] * H,
        jnp.zeros((rows, width), F32),
    )
    tops, sums, acc = lax.fori_loop(0, N // step_keys, step, start)
    out = (acc / spread(H, acc.shape, sums)).astype(BF)
    lse = []
    for h in range(H):
        column = tops[h] + jnp.log(sums[h])
        lse.append(jnp.transpose(jnp.broadcast_to(column, (rows, BLK)))[0:1, :])
    lse = jnp.concatenate(lse + [jnp.zeros((8 - H, rows), F32)], axis=0)
    return out, lse


def attend_kernel(H, qpos, q_ref, k_ref, v_ref, bias_ref, o_ref, lse_ref):
    o, lse = attend_tile(H, q_ref[...], k_ref, v_ref, bias_ref, 2 * pl.program_id(0))
    o_ref[...] = o
    lse_ref[0] = lse


def attend(H, qpos, bias, q, k, v):
    n = qpos.shape[0]
    width = H * HEAD_DIM
    N = k.shape[0]
    rows = 2 * BLK
    whole = pl.BlockSpec((N, width), lambda i, *_: (0, 0))
    return pl.pallas_call(
        functools.partial(attend_kernel, H),
        name="attend",
        out_shape=(
            jax.ShapeDtypeStruct((n * rows, width), BF),
            jax.ShapeDtypeStruct((n, 8, rows), F32),
        ),
        grid_spec=pltpu.PrefetchScalarGridSpec(
            num_scalar_prefetch=1,
            grid=(n,),
            in_specs=[
                pl.BlockSpec((rows, width), lambda i, qp: (qp[i], 0)),
                whole,
                whole,
                pl.BlockSpec((2 * n, 1, N), lambda i, *_: (0, 0, 0)),
            ],
            out_specs=[
                pl.BlockSpec((rows, width), lambda i, *_: (i, 0)),
                pl.BlockSpec((1, 8, rows), lambda i, *_: (i, 0, 0)),
            ],
        ),
        compiler_params=pltpu.CompilerParams(vmem_limit_bytes=48 << 20),
    )(qpos, q, k, v, bias)


def attend_back_tile(H, q, do, o, lse, k_ref, v_ref, kt, dk, dv, lift_ref, tile, poll=None):
    rows, width = q.shape
    N = k_ref.shape[0]
    scale = HEAD_DIM**-0.5
    qh = split_heads(H, q * jnp.asarray(scale, BF))
    doh = split_heads(H, do)
    qcat = jnp.concatenate(qh, axis=0)
    docat = jnp.concatenate(doh, axis=0)
    pick = lax.broadcasted_iota(jnp.int32, (8, width), 1)
    base = lax.broadcasted_iota(jnp.int32, (8, width), 0) * HEAD_DIM
    pick = jnp.logical_and(pick >= base, pick < base + HEAD_DIM).astype(F32)
    delta = lax.dot_general(
        pick,
        do.astype(F32) * o.astype(F32),
        (((1,), (1,)), ((), ())),
        precision=lax.Precision.HIGHEST,
        preferred_element_type=F32,
    )

    def step(j, dqt):
        at = pl.ds(pl.multiple_of(j * CHUNK, CHUNK), CHUNK)
        kc = k_ref[at, :]
        vc = v_ref[at, :]
        ps, dss, dqs = [], [], []
        for h in range(H):
            s = product_right(kc, qh[h])
            dp = product_right(vc, doh[h])
            pieces, dpieces = [], []
            for b in range(CHUNK // BLK):
                lift = lift_ref[tile, pl.ds(j * (CHUNK // BLK) + b, 1), :]
                cut = slice(b * BLK, (b + 1) * BLK)
                p = jnp.exp(s[cut] - (lse[h : h + 1, :] + lift))
                pieces.append(p.astype(BF))
                dpieces.append((p * (dp[cut] - delta[h : h + 1, :])).astype(BF))
            p = jnp.concatenate(pieces, axis=0)
            ds = jnp.concatenate(dpieces, axis=0)
            ps.append(p)
            dss.append(ds)
            dqs.append(product(kt[h * HEAD_DIM : (h + 1) * HEAD_DIM, at], ds))
        dv[at, :] += product(jnp.concatenate(ps, axis=1), docat)
        dk[at, :] += product(jnp.concatenate(dss, axis=1), qcat)
        if poll is not None:
            poll(tile * (N // CHUNK) + j)
        return dqt + jnp.concatenate(dqs, axis=0)

    dqt = lax.fori_loop(0, N // CHUNK, step, jnp.zeros((width, rows), F32))
    return dqt * scale


def flip_rows(src, dst):
    def flip(b, carry):
        at = pl.ds(pl.multiple_of(b * BLK, BLK), BLK)
        dst[:, at] = jnp.transpose(src[at, :])
        return carry

    lax.fori_loop(0, src.shape[0] // BLK, flip, 0)


def attend_back_kernel(
    H, qpos, q_ref, k_ref, v_ref, o_ref, do_ref, lse_ref, lift_ref, dqk_ref, dv_ref, kt, dk, dv
):
    i = pl.program_id(0)
    width = H * HEAD_DIM

    @pl.when(i == 0)
    def _():
        flip_rows(k_ref, kt)
        dk[...] = jnp.zeros_like(dk)
        dv[...] = jnp.zeros_like(dv)
        dqk_ref[...] = jnp.zeros_like(dqk_ref)

    dqt = attend_back_tile(
        H, q_ref[...], do_ref[...], o_ref[...], lse_ref[0], k_ref, v_ref, kt, dk, dv, lift_ref, i
    )
    rows = 2 * BLK
    here = pl.ds(pl.multiple_of(qpos[i] * rows, rows), rows)
    dqk_ref[here, 0:width] = jnp.transpose(dqt).astype(BF)

    @pl.when(i == pl.num_programs(0) - 1)
    def _():
        dqk_ref[:, width : 2 * width] = dk[...].astype(BF)
        dv_ref[...] = dv[...].astype(BF)


def attend_back(H, qpos, lift, q, k, v, o, do, lse):
    n = qpos.shape[0]
    width = H * HEAD_DIM
    N = k.shape[0]
    rows = 2 * BLK
    whole = pl.BlockSpec((N, width), lambda i, *_: (0, 0))
    row = pl.BlockSpec((rows, width), lambda i, *_: (i, 0))
    return pl.pallas_call(
        functools.partial(attend_back_kernel, H),
        name="attend_back",
        out_shape=(
            jax.ShapeDtypeStruct((N, 2 * width), BF),
            jax.ShapeDtypeStruct((N, width), BF),
        ),
        grid_spec=pltpu.PrefetchScalarGridSpec(
            num_scalar_prefetch=1,
            grid=(n,),
            in_specs=[
                pl.BlockSpec((rows, width), lambda i, qp: (qp[i], 0)),
                whole,
                whole,
                row,
                row,
                pl.BlockSpec((1, 8, rows), lambda i, *_: (i, 0, 0)),
                pl.BlockSpec((n, N // BLK, rows), lambda i, *_: (0, 0, 0)),
            ],
            out_specs=[
                pl.BlockSpec((N, 2 * width), lambda i, *_: (0, 0)),
                pl.BlockSpec((N, width), lambda i, *_: (0, 0)),
            ],
            scratch_shapes=[
                pltpu.VMEM((width, N), BF),
                pltpu.VMEM((N, width), F32),
                pltpu.VMEM((N, width), F32),
            ],
        ),
        compiler_params=pltpu.CompilerParams(vmem_limit_bytes=60 << 20),
    )(qpos, q, k, v, o, do, lse, lift)


def head_kernel(
    G, H,
    x_h, first_h, wqk_h, wf_h, small_h, bup_h, bias_h, cot_h, wup_h, wout_h,
    X_o, n1_o, k_o, v_o, wup_o, cot_o, q, o, lse, part, wqk, wf, vec,
    X, Fv, n1, k, v, small, vq, bias, wout, bup,
    rx, rf, rw, rv, rs, rc, ru, sh, sx, sf, sw, sc, su, loc, out,
):
    nw = 4
    w = lax.axis_index("wt")
    c = lax.axis_index("ctx")
    g = c // G
    m = c % G
    nc = nw * G
    R, width = x_h.shape
    d = width // nw
    par = w % 2
    core = (w + 1 - 2 * par, c)
    seq = 2 * (g % 2) + g // 2
    goal = (2 * par + w // 2) * G + m
    primary = (w + seq) % 2 == 0
    high = w >= 2
    low = w < 2
    peers = [
        ((w + a) % nw, ((g + e) % nw) * G + m) for a in range(nw) for e in range(nw) if a or e
    ]
    peers += [(w, g * G + (m + e) % G) for e in range(1, G)]
    loads = [
        pltpu.make_async_copy(a, b, loc.at[i])
        for i, (a, b) in enumerate(((bup_h, bup), (bias_h, bias), (wout_h, wout)))
    ]
    for copy in loads:
        copy.start()
    greet(peers)

    here = goal == c
    here_f = jnp.logical_and(here, high)
    to_one = remote(x_h, X.at[c], sh.at[0], rx.at[c], (w, goal))
    to_two = remote(x_h, X.at[c], sh.at[1], rx.at[c], ((w + 2) % nw, goal))
    to_first = remote(first_h, Fv.at[c], sh.at[2], rf.at[c], (par + 2, goal))
    own_cot = pl.ds(pl.multiple_of(g * R, R), R)
    cot_one = remote(cot_h, cot_o.at[own_cot], sh.at[3], rc.at[g], (w, goal))
    cot_two = remote(cot_h, cot_o.at[own_cot], sh.at[4], rc.at[g], ((w + 2) % nw, goal))

    @pl.when(here)
    def _():
        pltpu.make_async_copy(x_h, X.at[c], rx.at[c]).start()

    @pl.when(jnp.logical_not(here))
    def _():
        to_one.start()

    to_two.start()

    @pl.when(here_f)
    def _():
        pltpu.make_async_copy(first_h, Fv.at[c], rf.at[c]).start()

    @pl.when(jnp.logical_not(here_f))
    def _():
        to_first.start()

    def rows_of(a):
        return pl.ds(pl.multiple_of(a * d, 16), d)

    weights, fresh = [], []
    for e in range(1, nw):
        to = (w + e) % nw
        weights.append(remote(small_h, small.at[w], sw.at[e, 0], rs.at[w], (to, c)))
        weights.append(remote(wqk_h.at[to], wqk.at[rows_of(w)], sw.at[e, 1], rw.at[w], (to, c)))
        fresh.append(
            (to, remote(wf_h.at[to % 2], wf.at[rows_of(w)], sw.at[e, 2], rv.at[w], (to, c)))
        )
    for r in weights:
        r.start()
    for to, r in fresh:

        @pl.when(to < 2)
        def _():
            r.start()

    pltpu.make_async_copy(small_h, small.at[w], rs.at[w]).start()
    pltpu.make_async_copy(wqk_h.at[w], wqk.at[rows_of(w)], rw.at[w]).start()

    @pl.when(low)
    def _():
        pltpu.make_async_copy(wf_h.at[par], wf.at[rows_of(w)], rv.at[w]).start()

    @pl.when(high)
    def _():
        wf[...] = jnp.zeros_like(wf)

    def got(ref, sem):
        pltpu.make_async_copy(ref, ref, sem).wait()

    def core_x(b):
        return remote(X.at[b], X.at[b], sx.at[0, b], rx.at[b], core)

    def core_f(b):
        return remote(Fv.at[b], Fv.at[b], sf.at[0, b], rf.at[b], core)

    def member_x(b, e):
        return remote(X.at[b], X.at[b], sx.at[e, b], rx.at[b], (w, g * G + (m + e) % G))

    def member_f(b, e):
        return remote(Fv.at[b], Fv.at[b], sf.at[e, b], rf.at[b], (w, g * G + (m + e) % G))

    def take(b, onward):
        got(X.at[b], rx.at[b])

        @pl.when(primary)
        def _():
            for e in range(1, G if onward else 1):
                member_x(b, e).start()
            core_x(b).start()

        @pl.when(high)
        def _():
            got(Fv.at[b], rf.at[b])

            @pl.when(primary)
            def _():
                for e in range(1, G if onward else 1):
                    member_f(b, e).start()
                core_f(b).start()

    def project(b, a):
        at = pl.ds(pl.multiple_of(b * R, R), R)
        value = X[b].astype(F32)
        centred = value - jnp.mean(value, axis=-1, keepdims=True)
        inverse = lax.rsqrt(jnp.mean(centred * centred, axis=-1, keepdims=True) + EPS)
        n = (centred * inverse * vec[4:5, :] + vec[5:6, :]).astype(BF)
        n1[at, :] = n
        qk = product(n, wqk[...])
        k[at, :] = qk[:, d : 2 * d].astype(BF)
        if a is not None:
            q[pl.ds(pl.multiple_of(a * R, R), R), :] = (qk[:, :d] + vq[1:2, 0:d]).astype(BF)

        @pl.when(low)
        def _():
            v[at, :] = (product(n, wf[...]) + vq[2:3, 0:d]).astype(BF)

        @pl.when(high)
        def _():
            f = Fv[b]
            v[at, :] = jnp.where(par == 0, f[:, :d], f[:, d:])

    take(g * G + m, True)
    for copy in loads:
        copy.wait()
    for a in range(nw):
        got(small.at[a], rs.at[a])
        got(wqk.at[rows_of(a)], rw.at[a])

        @pl.when(low)
        def _():
            got(wf.at[rows_of(a)], rv.at[a])

    nb = 6 * d // 4
    for a in range(nw):
        piece = small[a].astype(F32)
        for row, src in ((0, 1), (1, 4), (2, 5), (4, 2), (5, 3), (6, 6)):
            vec[row : row + 1, a * d : (a + 1) * d] = piece[src : src + 1, :d]
        vq[0:1, a * nb : (a + 1) * nb] = piece[0:1, :nb]
    vec[3:4, :] = bup[0:1, :]
    vec[7:8, :] = jnp.zeros((1, width), F32)
    q_bias = vq[0:1, 0:d]
    for a in range(1, nw):
        q_bias = jnp.where(w == a, vq[0:1, a * d : (a + 1) * d], q_bias)
    f_bias = jnp.where(
        par == 0, vq[0:1, width : width + d], vq[0:1, width + d : width + 2 * d]
    )
    vq[1:2, 0:d] = q_bias
    vq[2:3, 0:d] = f_bias
    project(g * G + m, g)

    def own(i, carry):
        a = (g + i) % nw
        take(a * G + m, True)
        project(a * G + m, a)
        return carry

    lax.fori_loop(1, nw, own, 0)

    @pl.when(here)
    def _():
        pltpu.make_async_copy(cot_h, cot_o.at[own_cot], rc.at[g]).start()

    @pl.when(jnp.logical_not(here))
    def _():
        cot_one.start()

    cot_two.start()
    ups = []
    for e in range(1, nw):
        to = (w + e) % nw
        src = wup_h.at[:, pl.ds(pl.multiple_of(to * width, BLK), width)]
        ups.append(remote(src, wup_o.at[rows_of(w)], su.at[e], ru.at[w], (to, c)))
    for r in ups:
        r.start()
    src = wup_h.at[:, pl.ds(pl.multiple_of(w * width, BLK), width)]
    pltpu.make_async_copy(src, wup_o.at[rows_of(w)], ru.at[w]).start()

    def others(i, carry):
        b = ((g + i % nw) % nw) * G + (m + 1 + i // nw) % G
        take(b, False)
        project(b, None)
        return carry

    lax.fori_loop(0, nw * (G - 1), others, 0)
    outs = [(X, X_o), (n1, n1_o), (k, k_o), (v, v_o)]
    outs = [pltpu.make_async_copy(a, b, out.at[i]) for i, (a, b) in enumerate(outs)]
    for copy in outs:
        copy.start()

    def cot_rows(a):
        return cot_o.at[pl.ds(pl.multiple_of(a * R, R), R)]

    def core_c(a):
        return remote(cot_rows(a), cot_rows(a), sc.at[a], rc.at[a], core)

    def attend_one(t, carry):
        at = pl.ds(pl.multiple_of(t * R, R), R)
        ot, lt = attend_tile(H, q[at, :], k, v, bias, 2 * t)
        o[at, :] = ot
        lse[t] = lt
        part[at, :] = product(ot, wout[...]).astype(BF)
        return carry

    lax.fori_loop(0, nw, attend_one, 0)

    @pl.when(primary)
    def _():
        for a in range(nw):
            got(cot_rows(a), rc.at[a])
            core_c(a).start()

    for copy in outs:
        copy.wait()
    for a in range(nw):
        got(wup_o.at[rows_of(a)], ru.at[a])

    @pl.when(jnp.logical_not(primary))
    def _():
        for a in range(nw):
            got(cot_rows(a), rc.at[a])

    for r in weights + ups + [to_two, cot_two]:
        r.wait_send()
    for to, r in fresh:

        @pl.when(to < 2)
        def _():
            r.wait_send()

    @pl.when(jnp.logical_not(here))
    def _():
        to_one.wait_send()
        cot_one.wait_send()

    @pl.when(jnp.logical_not(here_f))
    def _():
        to_first.wait_send()

    @pl.when(primary)
    def _():
        for a in range(nw):
            core_c(a).wait_send()

        def sent(b, carry):
            core_x(b).wait_send()

            @pl.when(b % G == m)
            def _():
                for e in range(1, G):
                    member_x(b, e).wait_send()

            @pl.when(high)
            def _():
                core_f(b).wait_send()

                @pl.when(b % G == m)
                def _():
                    for e in range(1, G):
                        member_f(b, e).wait_send()

            return carry

        lax.fori_loop(0, nc, sent, 0)


def head(G, H, x, first, wqk, wf, small, bup, bias, cot, wup, wout):
    nw = 4
    nc = nw * G
    R, width = x.shape
    d = width // nw
    N = nc * R
    dma = pltpu.SemaphoreType.DMA
    vm = pltpu.VMEM
    shape = jax.ShapeDtypeStruct
    operands = (x, first, wqk, wf, small, bup, bias, cot, wup, wout)
    return pl.pallas_call(
        functools.partial(head_kernel, G, H),
        name="head",
        out_shape=(
            shape((nc, R, width), BF),
            shape((N, width), BF),
            shape((N, d), BF),
            shape((N, d), BF),
            shape((width, width), BF),
            shape((nw * R, width), BF),
            shape((nw * R, d), BF),
            shape((nw * R, d), BF),
            shape((nw, 8, R), F32),
            shape((nw * R, width), BF),
            shape((width, 2 * d), BF),
            shape((width, d), BF),
            shape((8, width), F32),
        ),
        in_specs=[ANY] * len(operands),
        out_specs=[ANY] * 6 + [VM] * 7,
        scratch_shapes=[
            vm((nc, R, width), BF), vm((nc, R, 2 * d), BF), vm((N, width), BF), vm((N, d), BF),
            vm((N, d), BF), vm((nw,) + small.shape, BF), vm((8, 6 * d), F32),
            vm(bias.shape, F32), vm(wout.shape, BF), vm(bup.shape, F32),
            dma((nc,)), dma((nc,)), dma((nw,)), dma((nw,)), dma((nw,)), dma((nw,)), dma((nw,)),
            dma((5,)), dma((G, nc)), dma((G, nc)), dma((nw, 3)), dma((nw,)), dma((nw,)),
            dma((3,)), dma((4,)),
        ],
        compiler_params=pltpu.CompilerParams(
            collective_id=0, has_side_effects=True, vmem_limit_bytes=56 << 20
        ),
        cost_estimate=pl.CostEstimate(
            flops=14 << 30, bytes_accessed=40 << 20, transcendentals=6 << 20
        ),
    )(*operands)


class Ring:
    def __init__(self, nc, pos, right, left, seg, chains, A, slots, out, ss, sr):
        self.nc, self.pos, self.right, self.left, self.seg = nc, pos, right, left, seg
        self.chains, self.A, self.slots, self.out, self.ss, self.sr = chains, A, slots, out, ss, sr
        self.steps = 2 * (nc - 1)
        self.turns = self.steps * chains
        self.cut = A.shape[1] // chains

    def at(self, half, j):
        j = (j + 2 * self.nc) % self.nc
        return pl.ds(pl.multiple_of((half * self.nc + j) * self.seg, 16), self.seg)

    def cols(self, i):
        if self.chains == 1:
            return pl.ds(0, self.cut)
        return pl.ds(pl.multiple_of(i * self.cut, BLK), self.cut)

    def reduce_copies(self, i, s):
        k = self.cols(i)
        return [
            remote(
                self.A.at[self.at(h, j), k],
                self.slots.at[h, s, :, k],
                self.ss.at[h, i, s],
                self.sr.at[h, i, s],
                to,
            )
            for h, j, to in ((0, self.pos - s, self.right), (1, self.pos + s, self.left))
        ]

    def gather_copies(self, i, s):
        k = self.cols(i)
        t = s - (self.nc - 1)
        return [
            remote(
                self.out.at[self.at(h, j), k],
                self.out.at[self.at(h, j), k],
                self.ss.at[h, i, s],
                self.sr.at[h, i, s],
                to,
            )
            for h, j, to in ((0, self.pos + 1 - t, self.right), (1, self.pos - 1 + t, self.left))
        ]

    def send(self, i, s, gathering=False):
        for r in (self.gather_copies if gathering else self.reduce_copies)(i, s):
            r.start()

    def begin(self):
        for i in range(self.chains):
            self.send(i, 0)

    def add(self, i, s):
        k = self.cols(i)
        for h, j in ((0, self.pos - s - 1), (1, self.pos + s + 1)):
            at = self.at(h, j)
            slot = self.slots.at[h, s, :, k]
            pltpu.make_async_copy(slot, slot, self.sr.at[h, i, s]).wait()
            value = self.A[at, k].astype(F32) + self.slots[h, s, :, k].astype(F32)
            self.A[at, k] = value.astype(BF)

    def keep(self, i):
        k = self.cols(i)
        for h, j in ((0, self.pos + 1), (1, self.pos - 1)):
            self.out[self.at(h, j), k] = self.A[self.at(h, j), k]

    def arrive(self, i, s):
        t = s - (self.nc - 1)
        for h, j in ((0, self.pos - t), (1, self.pos + t)):
            at = self.out.at[self.at(h, j), self.cols(i)]
            pltpu.make_async_copy(at, at, self.sr.at[h, i, s]).wait()

    def turn(self, t):
        last = self.nc - 2
        i, s = t % self.chains, t // self.chains
        if isinstance(t, int):
            when = lambda cond: (lambda body: body() if cond else None)
            both = lambda a, b: a and b
        else:
            when, both = pl.when, jnp.logical_and

        @when(s < last)
        def _():
            self.add(i, s)
            self.send(i, s + 1)

        @when(s == last)
        def _():
            self.add(i, last)
            self.keep(i)
            self.send(i, last + 1, True)

        @when(both(s > last, s < self.steps))
        def _():
            self.arrive(i, s)

        @when(both(s > last, s < self.steps - 1))
        def _():
            self.send(i, s + 1, True)

    def drain(self):
        for gathering in (False, True):

            def one(t, carry):
                i, s = t % self.chains, t // self.chains
                for r in (self.gather_copies if gathering else self.reduce_copies)(i, s):
                    r.wait_send()
                return carry

            half = self.turns // 2
            lax.fori_loop(half * gathering, half * (1 + gathering), one, 0)


def tail_kernel(
    G, H, seg_a, seg_b,
    q_h, k_h, v_h, o_h, do_h, lse_h, lift_h, n1_h, X_h, wqk_h, wf_h, vec_h, dmid_h,
    up_h, down_h, gout_h, small_h, mlp_h, mid_h,
    layer_out, tokens_out, first_out, up_out, down_out, gout_out, small_out, qkv_out, ends_out,
    q, k, v, o, do, lse, lift, n1, X, wqk, wf, vec, dmid,
    kt, dk, dv, dqk, dvb, D, b1, ab, b2, st, b3, tot, tb, tr,
    A, slots_a, res_a, gq, B, slots_b, res_b, gs, f1, fs, fr,
    mlp, mid, lb, ly, lr, sl, rl, sL, rL, s1, r1, s2, r2, s3, r3, sT, rT, ssa, sra, ssb, srb, sx, rx, sf1, rf1, sf2, rf2, ld,
):
    w = lax.axis_index("wt")
    c = lax.axis_index("ctx")
    nw = 4
    nc = nw * G
    g = c // G
    m = c % G
    par = w % 2
    hi = w // 2
    core = (w + 1 - 2 * par, c)
    other = ((w + 2) % nw, c)
    R, width = dmid.shape
    d = width // nw
    N = n1.shape[0]
    odd = c % 2
    pos = (c // 2) * (1 - odd) + (nc - 1 - c // 2) * odd

    def ctx_at(p):
        p = (p + nc) % nc
        h = p // (nc // 2)
        return 2 * p * (1 - h) + (2 * (nc - 1 - p) + 1) * h

    right = (w, ctx_at(pos + 1))
    left = (w, ctx_at(pos - 1))
    loads = [
        (up_h, A.at[pl.ds(0, width)]),
        (down_h, A.at[pl.ds(width, width)]),
        (gout_h, A.at[pl.ds(2 * width, d)]),
        (small_h, A.at[pl.ds(2 * width + d, small_h.shape[0])]),
        (k_h, k), (v_h, v), (q_h, q), (o_h, o), (do_h, do), (lse_h, lse), (lift_h, lift),
        (n1_h, n1), (X_h, X), (wqk_h, wqk), (wf_h, wf), (vec_h, vec), (dmid_h, dmid), (mid_h, mid), (mlp_h, mlp),
    ]
    loads = [pltpu.make_async_copy(a, b, ld.at[i]) for i, (a, b) in enumerate(loads)]
    for copy in loads:
        copy.start()
    peers = [
        ((w + a) % nw, ((g + e) % nw) * G + m) for a in range(nw) for e in range(nw) if a or e
    ]
    peers += [(w, g * G + (m + e) % G) for e in range(1, G)]
    greet(peers + [right, left])
    ring_a = Ring(nc, pos, right, left, seg_a, 3, A, slots_a, res_a, ssa, sra)
    ring_b = Ring(nc, pos, right, left, seg_b, 1, B, slots_b, res_b, ssb, srb)
    for copy in loads[:4]:
        copy.wait()
    ring_a.begin()
    for copy in loads[4:11] + loads[17:]:
        copy.wait()
    seq = 2 * (g % 2) + g // 2
    home = (seq, w * G + m)
    home_self = jnp.logical_and(w == g, w == seq)
    shares = []
    for e in range(1, nw):
        to = (w + e) % nw
        src = mlp.at[pl.ds(pl.multiple_of(to * R, R), R)]
        r = remote(src, lb.at[w], sl.at[e], rl.at[w], (to, c))
        r.start()
        shares.append(r)

    flip_rows(k, kt)
    dk[...] = jnp.zeros_like(dk)
    dv[...] = jnp.zeros_like(dv)
    dqk[...] = jnp.zeros_like(dqk)
    wide = H * HEAD_DIM

    def tile(t, carry):
        here = pl.ds(pl.multiple_of((t * G + m) * R, R), R)
        mine = pl.ds(pl.multiple_of(t * R, R), R)
        dqt = attend_back_tile(
            H, q[mine, :], do[mine, :], o[mine, :], lse[t], k, v, kt, dk, dv, lift, t, ring_a.turn
        )
        dqk[here, 0:wide] = jnp.transpose(dqt).astype(BF)
        return carry

    lax.fori_loop(0, nw, tile, 0)
    dqk[:, wide : 2 * wide] = dk[...].astype(BF)
    dvb[...] = dv[...].astype(BF)
    at_a = nw * (N // CHUNK)
    for copy in loads[11:17]:
        copy.wait()

    layer = mid[...] + vec[6:7, :] + mlp[pl.ds(pl.multiple_of(w * R, R), R), :].astype(F32)
    for e in range(1, nw):
        src = (w + e) % nw
        pltpu.make_async_copy(lb.at[src], lb.at[src], rl.at[src]).wait()
        layer = layer + lb[src].astype(F32)
    ly[...] = layer.astype(BF)
    layer_back = remote(ly, lr, sL.at[0], rL.at[0], home)
    layer_stay = pltpu.make_async_copy(ly, lr, rL.at[0])

    @pl.when(home_self)
    def _():
        layer_stay.start()

    @pl.when(jnp.logical_not(home_self))
    def _():
        layer_back.start()

    upper = w >= 2
    first_copies = []
    for e in range(1, G):
        mm = (m + e) % G
        for gp in range(nw):
            src = dvb.at[pl.ds(pl.multiple_of((gp * G + mm) * R, R), R)]
            first_copies.append(
                remote(src, f1.at[m, gp], sf1.at[e, gp], rf1.at[m, gp], (w, g * G + mm))
            )

    @pl.when(upper)
    def _():
        for r in first_copies:
            r.start()

    gs[...] = jnp.zeros_like(gs)

    def block(i, carry):
        phase = i // (2 * G)
        jj = (hi + 1 - (i // G) % 2 + 2) % 2
        mm = (m + 1 + i % G) % G
        parity = (1 - par) * (1 - phase) + par * phase
        b = (2 * jj + parity) * G + mm
        at = pl.ds(pl.multiple_of(b * R, R), R)
        dn = product_right(dqk[at, :], wqk[...]) + product_right(dvb[at, :], wf[...])
        low = dn.astype(BF)
        D[b] = low

        @pl.when(phase == 0)
        def _():
            slot = jj * G + mm
            remote(D.at[b], b1.at[slot], s1.at[slot], r1.at[slot], core).start()

        value = X[b].astype(F32)
        centred = value - jnp.mean(value, axis=-1, keepdims=True)
        normal = centred * lax.rsqrt(jnp.mean(centred * centred, axis=-1, keepdims=True) + EPS)
        low = low.astype(F32)
        gs[0:1, :] += jnp.sum(low * normal, axis=0, keepdims=True)
        gs[1:2, :] += jnp.sum(low, axis=0, keepdims=True)

        ring_a.turn(at_a + i)
        return carry

    lax.fori_loop(0, nc, block, 0)
    at_a += nc

    tile_d = 128

    def grads(i, carry):
        at = pl.ds(pl.multiple_of(i * tile_d, tile_d), tile_d)
        gq[at, 0 : 2 * wide] = product_left(n1[:, at], dqk[...]).astype(BF)
        gq[at, 2 * wide : 3 * wide] = product_left(n1[:, at], dvb[...]).astype(BF)
        ring_a.turn(at_a + i)
        return carry

    lax.fori_loop(0, width // tile_d, grads, 0)
    at_a += width // tile_d
    ones = jnp.ones((N, BLK), BF)
    sum_qk = product_left(dqk[...], ones)
    sum_f = product_left(dvb[...], ones)
    gain_t = jnp.transpose(jnp.broadcast_to(gs[0:1, :], (BLK, width)))
    shift_t = jnp.transpose(jnp.broadcast_to(gs[1:2, :], (BLK, width)))
    lane = lax.broadcasted_iota(jnp.int32, (d, BLK), 1)
    edge = gq.shape[1] - BLK
    for a in range(nw):
        cut = slice(a * d, (a + 1) * d)
        ends = gq[cut, edge:].astype(F32)
        for j, column in enumerate(
            (gain_t[cut], shift_t[cut], sum_qk[:wide], sum_qk[wide:], sum_f)
        ):
            ends = jnp.where(lane == 64 + j, column, ends)
        gq[cut, edge:] = jnp.where(lane < 64 + 5, ends, 0.0).astype(BF)
    swaps = []
    mine = pl.ds(pl.multiple_of(w * d, 16), d)
    for e in range(1, nw):
        to = (w + e) % nw
        r = remote(
            gq.at[pl.ds(pl.multiple_of(to * d, 16), d)], B.at[mine], sx.at[e], rx.at[w], (to, c)
        )
        r.start()
        swaps.append(r)
    B[mine, :] = gq[mine, :]
    for _ in range(6):
        ring_a.turn(at_a)
        at_a += 1
    for e in range(1, nw):
        src = (w + e) % nw
        at = pl.ds(pl.multiple_of(src * d, 16), d)
        pltpu.make_async_copy(B.at[at], B.at[at], rx.at[src]).wait()
    ring_b.begin()

    order = list(range(1, G)) + [0]

    def chip_sum(jj, mm):
        slot = jj * G + mm
        pltpu.make_async_copy(b1.at[slot], b1.at[slot], r1.at[slot]).wait()
        return D[(2 * jj + par) * G + mm].astype(F32) + b1[slot].astype(F32)

    seconds = []
    for e in order:
        mm = (m + e) % G
        ab[mm] = chip_sum(1 - hi, mm).astype(BF)
        r = remote(ab.at[mm], b2.at[mm], s2.at[mm], r2.at[mm], other)
        r.start()
        seconds.append(r)
    thirds = []

    def sum_chips():
        for e in order:
            mm = (m + e) % G
            total = chip_sum(hi, mm)
            pltpu.make_async_copy(b2.at[mm], b2.at[mm], r2.at[mm]).wait()
            total = total + b2[mm].astype(F32)
            if e:
                st[mm] = total.astype(BF)
                r = remote(st.at[mm], b3.at[m], s3.at[mm], r3.at[m], (w, g * G + mm))
                r.start()
                thirds.append(r)
            else:
                tot[...] = total

    def sum_first():
        @pl.when(upper)
        def _():
            for gp in range(nw):
                total = dvb[pl.ds(pl.multiple_of((gp * G + m) * R, R), R), :].astype(F32)
                for e in range(1, G):
                    mm = (m + e) % G
                    pltpu.make_async_copy(f1.at[mm, gp], f1.at[mm, gp], rf1.at[mm, gp]).wait()
                    total = total + f1[mm, gp].astype(F32)
                fs[gp] = total.astype(BF)
                own = jnp.logical_and(w == seq, g == gp)

                @pl.when(own)
                def _():
                    pltpu.make_async_copy(fs.at[gp], fr.at[par], rf2.at[par]).start()

                @pl.when(jnp.logical_not(own))
                def _():
                    remote(
                        fs.at[gp], fr.at[par], sf2.at[gp], rf2.at[par], (seq, gp * G + m)
                    ).start()

    back = remote(tb, tr, sT.at[0], rT.at[0], home)
    stay = pltpu.make_async_copy(tb, tr, rT.at[0])

    def norm_back():
        total = tot[...]
        for e in range(1, G):
            mm = (m + e) % G
            pltpu.make_async_copy(b3.at[mm], b3.at[mm], r3.at[mm]).wait()
            total = total + b3[mm].astype(F32)
        value = X[w * G + m].astype(F32)
        centred = value - jnp.mean(value, axis=-1, keepdims=True)
        inverse = lax.rsqrt(jnp.mean(centred * centred, axis=-1, keepdims=True) + EPS)
        normal = centred * inverse
        dx = total * vec[4:5, :]
        dx = dx - jnp.mean(dx, axis=-1, keepdims=True) - normal * jnp.mean(
            dx * normal, axis=-1, keepdims=True
        )
        tb[...] = (dmid[...].astype(F32) + inverse * dx).astype(BF)

        @pl.when(home_self)
        def _():
            stay.start()

        @pl.when(jnp.logical_not(home_self))
        def _():
            back.start()

    for at_b in range(ring_b.turns):
        if at_a < ring_a.turns:
            ring_a.turn(at_a)
            at_a += 1
        ring_b.turn(at_b)
        if at_b == 0:
            sum_first()
        if at_b == 5:
            sum_chips()
        if at_b == 9:
            norm_back()
    while at_a < ring_a.turns:
        ring_a.turn(at_a)
        at_a += 1

    for a in range(nw):
        rows = slice(a * d, (a + 1) * d)
        up_out[:, a * width : (a + 1) * width] = res_a[rows, :].astype(F32)
        for part in range(2):
            qkv_out[:, part * width + a * d : part * width + (a + 1) * d] = res_b[
                rows, part * d : (part + 1) * d
            ].astype(F32)
        if a < 2:
            qkv_out[:, 2 * width + a * d : 2 * width + (a + 1) * d] = res_b[
                rows, 2 * d : 3 * d
            ].astype(F32)
    down_out[...] = res_a[width : 2 * width, :].astype(F32)
    gout_out[...] = res_a[2 * width : 2 * width + d, :].astype(F32)
    small_out[...] = res_a[2 * width + d : 2 * width + d + small_out.shape[0], :].astype(F32)
    ends_out[...] = res_b[0:width, edge:].astype(F32)
    pltpu.make_async_copy(tr, tr, rT.at[0]).wait()
    tokens_out[...] = tr[...].astype(F32)
    for u in range(2):
        pltpu.make_async_copy(fr.at[u], fr.at[u], rf2.at[u]).wait()
        first_out[:, u * d : (u + 1) * d] = fr[u].astype(F32)

    pltpu.make_async_copy(lr, lr, rL.at[0]).wait()
    layer_out[...] = lr[...]
    ring_a.drain()
    ring_b.drain()
    for r in swaps + seconds + thirds + shares:
        r.wait_send()

    @pl.when(jnp.logical_not(home_self))
    def _():
        back.wait_send()
        layer_back.wait_send()

    @pl.when(upper)
    def _():
        for r in first_copies:
            r.wait_send()
        for gp in range(nw):

            @pl.when(jnp.logical_not(jnp.logical_and(w == seq, g == gp)))
            def _():
                remote(
                    fs.at[gp], fr.at[par], sf2.at[gp], rf2.at[par], (seq, gp * G + m)
                ).wait_send()

    def drain(i, carry):
        jj = (hi + 1 - (i // G) % 2 + 2) % 2
        mm = (m + 1 + i % G) % G
        slot = jj * G + mm
        b = (2 * jj + 1 - par) * G + mm
        remote(D.at[b], b1.at[slot], s1.at[slot], r1.at[slot], core).wait_send()
        return carry

    lax.fori_loop(0, 2 * G, drain, 0)


def tail(
    G, H, q, k, v, o, do, lse, lift, n1, X, wqk, wf, vec, dmid, up, down, gout, small, mlp, mid
):
    nw = 4
    nc = nw * G
    R, width = dmid.shape
    d = width // nw
    N = n1.shape[0]
    wide = H * HEAD_DIM
    rows_a = 2 * width + d + small.shape[0]
    seg_a = -(-rows_a // (2 * nc * 16)) * 16
    seg_b = -(-width // (2 * nc * 16)) * 16
    cols = 5 * BLK
    dma = pltpu.SemaphoreType.DMA
    vm = pltpu.VMEM
    steps = 2 * (nc - 1)
    operands = (
        q, k, v, o, do, lse, lift, n1, X, wqk, wf, vec, dmid, up, down, gout, small, mlp, mid
    )
    return pl.pallas_call(
        functools.partial(tail_kernel, G, H, seg_a, seg_b),
        name="tail",
        out_shape=(
            jax.ShapeDtypeStruct((R, width), BF),
            jax.ShapeDtypeStruct((R, width), F32),
            jax.ShapeDtypeStruct((R, 2 * d), F32),
            jax.ShapeDtypeStruct((d, nw * width), F32),
            jax.ShapeDtypeStruct((width, width), F32),
            jax.ShapeDtypeStruct((d, width), F32),
            jax.ShapeDtypeStruct(small.shape, F32),
            jax.ShapeDtypeStruct((d, 2 * width + 2 * d), F32),
            jax.ShapeDtypeStruct((width, BLK), F32),
        ),
        in_specs=[ANY] * len(operands),
        out_specs=[VM] * 9,
        scratch_shapes=[vm(a.shape, a.dtype) for a in operands[:13]]
        + [
            vm((wide, N), BF), vm((N, wide), F32), vm((N, wide), F32), vm((N, 2 * wide), BF),
            vm((N, wide), BF), vm((nc, R, width), BF), vm((2 * G, R, width), BF),
            vm((G, R, width), BF), vm((G, R, width), BF), vm((G, R, width), BF),
            vm((G, R, width), BF), vm((R, width), F32), vm((R, width), BF), vm((R, width), BF),
            vm((2 * nc * seg_a, width), BF), vm((2, nc - 1, seg_a, width), BF),
            vm((2 * nc * seg_a, width), BF),
            vm((width, cols), BF), vm((2 * nc * seg_b, cols), BF),
            vm((2, nc - 1, seg_b, cols), BF), vm((2 * nc * seg_b, cols), BF),
            vm((8, width), F32), vm((G, nw, R, d), BF), vm((nw, R, d), BF), vm((2, R, d), BF),
            vm((nw * R, width), BF), vm((R, width), F32), vm((nw, R, width), BF),
            vm((R, width), BF), vm((R, width), BF), dma((nw,)), dma((nw,)), dma((1,)), dma((1,)),
            dma((2 * G,)), dma((2 * G,)), dma((G,)), dma((G,)), dma((G,)), dma((G,)),
            dma((1,)), dma((1,)), dma((2, 3, steps)), dma((2, 3, steps)),
            dma((2, 1, steps)), dma((2, 1, steps)), dma((nw,)), dma((nw,)), dma((G, nw)), dma((G, nw)),
            dma((nw,)), dma((2,)), dma((len(operands),)),
        ],
        compiler_params=pltpu.CompilerParams(
            collective_id=2, has_side_effects=True, vmem_limit_bytes=63 << 20
        ),
        cost_estimate=pl.CostEstimate(
            flops=40 << 30, bytes_accessed=60 << 20, transcendentals=6 << 20
        ),
    )(*operands)


def on_device(
    nw,
    nc,
    tokens,
    first_values,
    cotangent,
    deal,
    w_qkv,
    bias_qv,
    w_out,
    bias_out,
    gain_one,
    shift_one,
    gain_two,
    shift_two,
    w_up,
    bias_up,
    w_down,
    bias_down,
):
    G = nc // nw
    w = lax.axis_index("wt")
    c = lax.axis_index("ctx")
    m = c % G
    rows, width = tokens.shape[1:]
    d = width // nw
    H = HEADS // nw
    both = ("wt", "ctx")
    seq = lambda g: 2 * (g % 2) + g // 2
    swap = [
        (a * nc + g * G + e, seq(g) * nc + a * G + e)
        for a in range(nw)
        for g in range(nw)
        for e in range(G)
    ]
    ring = [[(a, (a + k) % nw) for a in range(nw)] for k in range(nw)]

    def exchange(pieces):
        out = jnp.zeros_like(pieces)
        mine = lax.dynamic_index_in_dim(pieces, w, 0, keepdims=True)
        out = lax.dynamic_update_slice_in_dim(out, mine, w, 0)
        for k in range(1, nw):
            piece = lax.dynamic_index_in_dim(pieces, (w + k) % nw, 0, keepdims=True)
            got = lax.ppermute(piece, "wt", ring[k])
            out = lax.dynamic_update_slice_in_dim(out, got, (w + nw - k) % nw, 0)
        return out

    qk = w_qkv[:, : 2 * width].reshape(d, 2, nw, d).transpose(2, 0, 1, 3).reshape(nw, d, 2 * d)
    wf = w_qkv[:, 2 * width :].reshape(d, 2, d).transpose(1, 0, 2)
    nb = bias_qv.shape[0]
    ids = dealt_blocks(deal)
    qpos = jnp.arange(nw, dtype=jnp.int32) * G + m
    qid = jnp.take(ids.reshape(nc, 2), qpos, axis=0)
    hidden = (ids[None, None, :] > qid[:, :, None]).astype(F32) * -NEG
    bias = jnp.repeat(-hidden.reshape(2 * nw, 2 * nc), BLK, axis=1)[:, None, :]
    lift = jnp.repeat(hidden.transpose(0, 2, 1), BLK, axis=2)

    def mine(vector):
        return lax.dynamic_slice_in_dim(vector, w * d, d)

    if nc <= 8:
        wide = lambda a: jnp.concatenate([a, jnp.zeros((2 * d - a.shape[0],), BF)])
        small = jnp.stack(
            [
                wide(a)
                for a in (bias_qv, bias_out, gain_one, shift_one, gain_two, shift_two, bias_down)
            ]
            + [jnp.zeros((2 * d,), BF)]
        )
        bup = jnp.broadcast_to(bias_up.astype(F32)[None], (8, width))
        X, n1, k, v, Wup, cot, q, o, lse, part, Wqk, Wf, vec = head(
            G, H, tokens[0], first_values[0], qk, wf, small, bup, bias, cotangent[0], w_up, w_out
        )
        mlp, mid_own, d_mid, d_o, g_up, g_down, g_out, vsums = middle(
            G, part, X, cot, o, Wup, w_down, w_out, vec
        )
        small = jnp.stack(
            [vsums[0], jnp.concatenate([mine(vsums[a]) for a in range(1, 5)])]
            + [jnp.zeros((width,), F32)] * 14
        ).astype(BF)
        rows_a = 2 * width + d + 16
        pad = -(-rows_a // (32 * nc)) * 32 * nc - rows_a
        small = jnp.concatenate([small, jnp.zeros((pad, width), BF)], axis=0)
        layer, grad_tokens, grad_first, s_up, s_down, s_out, s_small, s_qkv, ends = tail(
            G, H, q, k, v, o, d_o, lse, lift, n1, X, Wqk, Wf, vec,
            d_mid, g_up, g_down, g_out, small, mlp, mid_own,
        )
        ends = ends.reshape(nw, d, BLK)
        bias_all = jnp.concatenate([ends[:, :, 66].reshape(-1), ends[:2, :, 68].reshape(-1)])
        s_vec = s_small[1].reshape(nw, d)
        return (
            layer[None],
            grad_tokens[None],
            grad_first[None],
            s_qkv,
            lax.dynamic_slice_in_dim(bias_all, w * nb, nb),
            s_out,
            s_vec[1],
            jnp.sum(ends[:, :, 64], axis=0),
            jnp.sum(ends[:, :, 65], axis=0),
            s_vec[2],
            s_vec[3],
            s_up,
            s_small[0],
            s_down,
            s_vec[0],
        )
    small = jnp.concatenate(
        [bias_qv, bias_out, gain_one, shift_one, gain_two, shift_two, bias_down]
    )
    lanes = 16 * BLK
    small = jnp.concatenate([small, jnp.zeros((lanes - small.shape[0],), BF)]).reshape(16, BLK)
    X, Fv, WQK, WF, SM = gather(nw, G, tokens[0], first_values[0], qk, wf, small)
    X = X.reshape(nc * rows, width)
    Wqk = WQK.reshape(width, 2 * d)
    low = w < 2
    Wf = jnp.where(low, WF.reshape(width, d), jnp.zeros((width, d), BF))
    SM = SM.reshape(nw, lanes).astype(F32)
    qv_vector = SM[:, :nb].reshape(-1)
    vectors = [SM[:, nb + a * d : nb + (a + 1) * d].reshape(-1) for a in range(6)]
    out_vector, gain_a, shift_a, gain_b, shift_b, down_vector = vectors

    x32 = X.astype(F32)
    mean = jnp.mean(x32, axis=-1, keepdims=True)
    centred = x32 - mean
    inverse = lax.rsqrt(jnp.mean(centred * centred, axis=-1, keepdims=True) + EPS)
    n1 = (centred * inverse * gain_a + shift_a).astype(BF)
    pqk = product(n1, Wqk)
    q_bias = lax.dynamic_slice_in_dim(qv_vector, w * d, d)
    f_bias = lax.dynamic_slice_in_dim(qv_vector, width + (w % 2) * d, d)
    q = (pqk[:, :d] + q_bias).astype(BF)
    k = pqk[:, d:].astype(BF)
    f = (product(n1, Wf) + f_bias).astype(BF)
    Fv = Fv.reshape(nc * rows, 2 * d)
    first = jnp.where(w % 2 == 0, Fv[:, :d], Fv[:, d:])
    v = jnp.where(low, f, first)

    o, lse = attend(H, qpos, bias, q, k, v)

    part = product(o, w_out).astype(BF)
    pieces, spread = lax.optimization_barrier((w_up, cotangent[0], X))[:2]
    Wup = exchange(pieces.reshape(d, nw, width).transpose(1, 0, 2)).reshape(width, width)
    unswap = [(b, a) for a, b in swap]
    cot = lax.all_gather(lax.ppermute(spread, both, unswap), "wt", axis=0, tiled=True)
    vec = jnp.stack([out_vector, gain_b, shift_b, bias_up.astype(F32)] + [out_vector] * 4)
    mlp, mid_own, d_mid, d_o, g_up, g_down, g_out, vsums = middle(
        G, part, X.reshape(nc, rows, width), cot, o, Wup, w_down, w_out, vec
    )

    mlp = lax.psum_scatter(mlp, "wt", scatter_dimension=0, tiled=True)
    layer = (mid_own + mlp.astype(F32) + down_vector).astype(BF)
    layer = lax.ppermute(layer, both, swap)
    up_rows = g_up.reshape(nw, d, width).transpose(1, 0, 2)
    s_up, s_down = lax.psum((up_rows.reshape(d, nw * width), g_down), "ctx")
    dqk, dv = attend_back(H, qpos, lift, q, k, v, o, d_o, lse)
    zero = jnp.zeros_like(dv)
    df = jnp.where(low, dv, zero)
    dn1 = product_right(dqk, Wqk) + product_right(df, Wf)
    dn1_low = dn1.astype(BF)
    blank = jnp.zeros_like(dv)
    left = jnp.where(w == 2, dv, blank)
    right = jnp.where(w == 3, dv, blank)
    total = scatter_sum(
        G, jnp.concatenate([dn1_low, left, right], axis=1).reshape(nc, rows, width + 2 * d)
    )
    grad_first = lax.ppermute(total[:, width:].astype(BF), both, swap).astype(F32)
    block = (w * G + m) * rows
    x_own = lax.dynamic_slice_in_dim(X, block, rows).astype(F32)
    _, pull_one = jax.vjp(lambda a: norm_rows(a, gain_a, shift_a), x_own)
    d_x = d_mid.astype(F32) + pull_one(total[:, :width])[0]
    grad_tokens = lax.ppermute(d_x.astype(BF), both, swap).astype(F32)

    g_qk = product_left(n1, dqk)
    g_f = product_left(n1, df)
    normal = centred * inverse
    g_gain_one = jnp.sum(dn1_low.astype(F32) * normal, axis=0)
    g_shift_one = jnp.sum(dn1_low.astype(F32), axis=0)
    cols = jnp.concatenate(
        [
            g_qk.astype(BF),
            g_f.astype(BF),
            g_gain_one[:, None].astype(BF),
            g_shift_one[:, None].astype(BF),
            jnp.zeros((width, 62), BF),
        ],
        axis=1,
    ).reshape(nw, d, 640)
    sums = jnp.concatenate(
        [jnp.sum(dqk.astype(F32), axis=0), jnp.sum(df.astype(F32), axis=0), jnp.zeros((64,), F32)]
    ).astype(BF)
    foot = jnp.concatenate([sums[None], jnp.zeros((7, 640), BF)], axis=0)
    pack = jnp.concatenate([cols, jnp.broadcast_to(foot[None], (nw, 8, 640))], axis=1)
    pack = exchange(pack)
    vecs = jnp.concatenate(
        [
            vsums[0],
            mine(vsums[1]),
            mine(vsums[2]),
            mine(vsums[3]),
            mine(vsums[4]),
        ]
    ).astype(BF)
    pack = pack.at[0, d + 1 : d + 4, :512].set(vecs.reshape(3, 512))
    pack, s_up, s_down = lax.optimization_barrier((pack, s_up, s_down))
    pack, s_out = lax.psum((pack, g_out), "ctx")
    body = pack[:, :d]
    s_qkv = jnp.concatenate(
        [body[a, :, e * d : (e + 1) * d] for e in (0, 1) for a in range(nw)]
        + [body[a, :, 2 * d : 3 * d] for a in range(2)],
        axis=1,
    ).astype(F32)
    s_gain_one = jnp.sum(body[:, :, 576].astype(F32), axis=0)
    s_shift_one = jnp.sum(body[:, :, 577].astype(F32), axis=0)
    ends = pack[:, d]
    bias_all = jnp.concatenate([ends[:, :d].reshape(-1), ends[:2, 2 * d : 3 * d].reshape(-1)])
    s_bias_qv = lax.dynamic_slice_in_dim(bias_all, w * nb, nb).astype(F32)
    vecs = pack[0, d + 1 : d + 4, :512].reshape(-1).astype(F32)
    s_bias_up = vecs[:width]
    s_bias_down, s_bias_out, s_gain_two, s_shift_two = [
        vecs[width + a * d : width + (a + 1) * d] for a in range(4)
    ]
    return (
        layer[None],
        grad_tokens[None],
        grad_first[None],
        s_qkv,
        s_bias_qv,
        s_out.astype(F32),
        s_bias_out,
        s_gain_one,
        s_shift_one,
        s_gain_two,
        s_shift_two,
        s_up.astype(F32),
        s_bias_up,
        s_down.astype(F32),
        s_bias_down,
    )


def solution(mesh):
    rows3 = P("wt", "ctx", None)
    mat = P("wt", None)
    vec = P("wt")
    in_specs = (rows3, rows3, rows3, P(), mat, vec, mat) + (vec,) * 5 + (mat, vec, mat, vec)
    out_specs = (
        (rows3, rows3, rows3, mat, vec, mat) + (vec,) * 5 + (mat, vec, mat, vec)
    )
    return jax.shard_map(
        functools.partial(on_device, mesh.shape["wt"], mesh.shape["ctx"]),
        mesh=mesh,
        in_specs=in_specs,
        out_specs=out_specs,
        check_vma=False,
    )
```

```python
import functools

import jax
import jax.numpy as jnp
from jax import lax
from jax.experimental import pallas as pl
from jax.experimental.pallas import tpu as pltpu
from jax.sharding import PartitionSpec as P

HEADS = 12
HEAD_DIM = 64
BLK = 128
CHUNK = 1024

EPS = 1e-05
SLOPE = 0.7978845608028654
CUBIC = 0.044715
NEG = -1e30

BF = jnp.bfloat16
F32 = jnp.float32
MESH = pl.DeviceIdType.MESH
ANY = pl.BlockSpec(memory_space=pl.ANY)
VM = pl.BlockSpec(memory_space=pltpu.VMEM)


def norm_rows(value, gain, shift):
    mean = jnp.mean(value, axis=-1, keepdims=True)
    centred = value - mean
    inverse = lax.rsqrt(jnp.mean(centred * centred, axis=-1, keepdims=True) + EPS)
    return centred * inverse * gain + shift


def gelu_tanh(value):
    return 0.5 * value * (1.0 + jnp.tanh(SLOPE * (value + CUBIC * value * value * value)))


def product(left, right):
    return jnp.dot(left, right, preferred_element_type=F32)


def product_left(left, right):
    return lax.dot_general(left, right, (((0,), (0,)), ((), ())), preferred_element_type=F32)


def product_right(left, right):
    return lax.dot_general(left, right, (((1,), (1,)), ((), ())), preferred_element_type=F32)


def dealt_blocks(deal):
    count = deal.shape[0] * 2
    pairs = jnp.repeat(deal, 2)
    parity = jnp.arange(count, dtype=jnp.int32) % 2
    return jnp.where(parity == 0, pairs, count - 1 - pairs)


def remote(src, dst, send, recv, device):
    return pltpu.make_async_remote_copy(
        src_ref=src,
        dst_ref=dst,
        send_sem=send,
        recv_sem=recv,
        device_id=device,
        device_id_type=MESH,
    )


def greet(peers):
    barrier = pltpu.get_barrier_semaphore()
    for peer in peers:
        pl.semaphore_signal(barrier, inc=1, device_id=peer, device_id_type=MESH)
    pl.semaphore_wait(barrier, len(peers))


def gather_kernel(
    nw, G, x, first, wqk, wf, small, X, Fv, WQK, WF, SM, rx, rf, rw, rv, rs, sa, sx, sfa, sfx, sw, loc
):
    w = lax.axis_index("wt")
    c = lax.axis_index("ctx")
    g = c // G
    m = c % G
    nc = nw * G
    core = w + 1 - 2 * (w % 2)
    other = (w + 2) % nw
    rel = lambda k: (w + k) % nw
    peers = [(rel(k), c) for k in range(1, nw)]
    peers += [(w, ((g + k) % nw) * G + m) for k in range(1, nw)]
    peers += [(w, g * G + (m + k) % G) for k in range(1, G)]
    greet(peers)
    seq = 2 * (g % 2) + g // 2
    goal = (2 * (w % 2) + w // 2) * G + m
    is_a = w == seq
    primary = (w + seq) % 2 == 0
    high = w >= 2
    copies = []

    to_head = remote(x, X.at[c], sa.at[0], rx.at[c], (w, goal))
    to_head_f = remote(first, Fv.at[c], sa.at[1], rf.at[c], (w, goal))
    own_x = pltpu.make_async_copy(x, X.at[c], rx.at[c])
    own_f = pltpu.make_async_copy(first, Fv.at[c], rf.at[c])

    @pl.when(is_a)
    def _():
        own_x.start()
        own_f.start()

    @pl.when(jnp.logical_not(is_a))
    def _():
        to_head.start()
        to_head_f.start()

    own_w = pltpu.make_async_copy(wqk.at[w], WQK.at[w], loc.at[0])
    own_s = pltpu.make_async_copy(small, SM.at[w], loc.at[1])
    own_w.start()
    own_s.start()
    own_v = pltpu.make_async_copy(wf.at[w % 2], WF.at[w], loc.at[2])
    own_v.start()
    sends_w, sends_v, sends_s = [], [], []
    for k in range(1, nw):
        d = rel(k)
        s = remote(small, SM.at[w], sw.at[k, 0], rs.at[w], (d, c))
        s.start()
        q = remote(wqk.at[d], WQK.at[w], sw.at[k, 1], rw.at[w], (d, c))
        q.start()
        v = remote(wf.at[d % 2], WF.at[w], sw.at[k, 2], rv.at[w], (d, c))
        sends_w += [s, q]
        sends_v.append((d, v))

        @pl.when(d < 2)
        def _():
            v.start()

    def block_x(b):
        return pltpu.make_async_copy(X.at[b], X.at[b], rx.at[b])

    def block_f(b):
        return pltpu.make_async_copy(Fv.at[b], Fv.at[b], rf.at[b])

    fwd_core, fwd_other, fwd_member = [], [], []
    for k in range(nw):
        gp = (g + k) % nw
        b = gp * G + m
        to_core = remote(X.at[b], X.at[b], sx.at[0, b], rx.at[b], (core, c))
        to_other = remote(X.at[b], X.at[b], sx.at[1, b], rx.at[b], (other, c))
        to_core_f = remote(Fv.at[b], Fv.at[b], sfx.at[0, b], rf.at[b], (core, c))
        to_other_f = remote(Fv.at[b], Fv.at[b], sfx.at[1, b], rf.at[b], (other, c))
        members = [
            remote(X.at[b], X.at[b], sx.at[1 + e, b], rx.at[b], (w, g * G + (m + e) % G))
            for e in range(1, G)
        ]
        members_f = [
            remote(Fv.at[b], Fv.at[b], sfx.at[1 + e, b], rf.at[b], (w, g * G + (m + e) % G))
            for e in range(1, G)
        ]

        @pl.when(primary)
        def _():
            block_x(b).wait()

            @pl.when(is_a)
            def _():
                to_other.start()

            for r in members:
                r.start()
            to_core.start()

        @pl.when(jnp.logical_and(is_a, jnp.logical_not(high)))
        def _():
            block_f(b).wait()
            to_other_f.start()

        @pl.when(jnp.logical_and(primary, high))
        def _():
            block_f(b).wait()
            for r in members_f:
                r.start()
            to_core_f.start()

        fwd_core.append((to_core, to_core_f))
        fwd_other.append((to_other, to_other_f))
        fwd_member.append((members, members_f))
    for e in range(1, G):
        for k in range(nw):
            b = ((g + k) % nw) * G + (m + e) % G
            to_core = remote(X.at[b], X.at[b], sx.at[0, b], rx.at[b], (core, c))
            to_core_f = remote(Fv.at[b], Fv.at[b], sfx.at[0, b], rf.at[b], (core, c))

            @pl.when(primary)
            def _():
                block_x(b).wait()
                to_core.start()

            @pl.when(jnp.logical_and(primary, high))
            def _():
                block_f(b).wait()
                to_core_f.start()

            fwd_core.append((to_core, to_core_f))

    @pl.when(jnp.logical_not(primary))
    def _():
        for b in range(nc):
            block_x(b).wait()

        @pl.when(high)
        def _():
            for b in range(nc):
                block_f(b).wait()

    own_w.wait()
    own_s.wait()
    own_v.wait()
    for k in range(1, nw):
        src = (w + nw - k) % nw
        pltpu.make_async_copy(wqk.at[0], WQK.at[src], rw.at[src]).wait()
        pltpu.make_async_copy(small, SM.at[src], rs.at[src]).wait()

        @pl.when(w < 2)
        def _():
            pltpu.make_async_copy(wf.at[0], WF.at[src], rv.at[src]).wait()

    for s in sends_w:
        s.wait_send()
    for d, v in sends_v:

        @pl.when(d < 2)
        def _():
            v.wait_send()

    @pl.when(jnp.logical_not(is_a))
    def _():
        to_head.wait_send()
        to_head_f.wait_send()

    @pl.when(primary)
    def _():
        for a, _f in fwd_core:
            a.wait_send()
        for ms, _f in fwd_member:
            for a in ms:
                a.wait_send()

        @pl.when(high)
        def _():
            for _x, a in fwd_core:
                a.wait_send()
            for _x, ms in fwd_member:
                for a in ms:
                    a.wait_send()

    @pl.when(is_a)
    def _():
        for a, _f in fwd_other:
            a.wait_send()

        @pl.when(jnp.logical_not(high))
        def _():
            for _x, a in fwd_other:
                a.wait_send()


def gather(nw, G, x, first, wqk, wf, small):
    nc = nw * G
    rows, width = x.shape
    half = first.shape[1]
    d = width // nw
    dma = pltpu.SemaphoreType.DMA
    return pl.pallas_call(
        functools.partial(gather_kernel, nw, G),
        name="gather_tokens",
        out_shape=(
            jax.ShapeDtypeStruct((nc, rows, width), BF),
            jax.ShapeDtypeStruct((nc, rows, half), BF),
            jax.ShapeDtypeStruct((nw, d, 2 * d), BF),
            jax.ShapeDtypeStruct((nw, d, d), BF),
            jax.ShapeDtypeStruct((nw,) + small.shape, BF),
        ),
        in_specs=[ANY] * 5,
        out_specs=[ANY] * 5,
        scratch_shapes=[
            dma((nc,)),
            dma((nc,)),
            dma((nw,)),
            dma((nw,)),
            dma((nw,)),
            dma((2,)),
            dma((1 + G, nc)),
            dma((2,)),
            dma((1 + G, nc)),
            dma((nw, 3)),
            dma((3,)),
        ],
        compiler_params=pltpu.CompilerParams(collective_id=0, has_side_effects=True),
    )(x, first, wqk, wf, small)


def middle_kernel(
    T, G, crossed, p_hbm, X_hbm, cot_hbm, o_hbm, wup_hbm, wdn_hbm, wout_hbm, vec_hbm,
    mlp, mid_own, dmid_own, do_out, gup, gdn, gout, sums,
    p, x, cot, o, wup, wdn, wout, vec,
    b1, ab, b2, bs, mid, n2s, act, dus, q, b4, ab2, b5, dn, dbs,
    s1, r1, s2, r2, s3, r3, s4, r4, s5, r5, s6, r6, ld,
):
    w = lax.axis_index("wt")
    c = lax.axis_index("ctx")
    g = c // G
    m = c % G
    core = (w + 1 - 2 * (w % 2), c)
    other = ((w + 2) % 4, c)
    mine = w % 2
    theirs = 1 - mine
    rows = p.shape[0]
    half = rows // 2
    n = half // T
    R = rows // 4
    loads = [
        pltpu.make_async_copy(p_hbm, p, ld.at[0]),
        pltpu.make_async_copy(vec_hbm, vec, ld.at[1]),
    ]
    loads += [
        pltpu.make_async_copy(X_hbm.at[a * G + m], x.at[pl.ds(a * R, R)], ld.at[2 + a])
        for a in range(4)
    ]
    loads += [
        pltpu.make_async_copy(wup_hbm, wup, ld.at[6]),
        pltpu.make_async_copy(wdn_hbm, wdn, ld.at[7]),
        pltpu.make_async_copy(cot_hbm, cot, ld.at[8]),
        pltpu.make_async_copy(wout_hbm, wout, ld.at[9]),
        pltpu.make_async_copy(o_hbm, o, ld.at[10]),
    ]
    for copy in loads:
        copy.start()
    greet([core, other])

    def rs(base, t):
        return pl.ds(pl.multiple_of(base * half + t * n, n), n)

    loads[0].wait()
    first = []
    for t in range(T):
        r = remote(p.at[rs(theirs, t)], b1.at[t], s1.at[t], r1.at[t], core)
        r.start()
        first.append(r)
    second = []
    for t in range(T):
        first[t].wait_recv()
        ab[t] = (p[rs(mine, t), :].astype(F32) + b1[t].astype(F32)).astype(BF)
        r = remote(ab.at[t], b2.at[t], s2.at[t], r2.at[t], other)
        r.start()
        second.append(r)
    for copy in loads[1:]:
        copy.wait()
    out_b = vec[0:1, :]
    gain = vec[1:2, :]
    shift = vec[2:3, :]
    up_b = vec[3:4, :]
    sums[...] = jnp.zeros_like(sums)

    def two(ref, t):
        return jnp.concatenate([ref[rs(mine, t), :], ref[rs(theirs, t), :]], axis=0)

    def put(ref, t, value):
        ref[rs(mine, t), :] = value[:n]
        ref[rs(theirs, t), :] = value[n:]

    def add_sum(at, value):
        sums[at : at + 1, :] += jnp.sum(value, axis=0, keepdims=True)

    def chain(t):
        pltpu.make_async_copy(b4.at[t], b4.at[t], r4.at[t]).wait()
        ab2[t] = (q[rs(mine, t), :].astype(F32) + b4[t].astype(F32)).astype(BF)
        remote(ab2.at[t], b5.at[t], s5.at[t], r5.at[t], other).start()

    def forward(t, carry):
        pltpu.make_async_copy(b2.at[t], b2.at[t], r2.at[t]).wait()
        bs[rs(mine, t), :] = (ab[t].astype(F32) + b2[t].astype(F32)).astype(BF)
        remote(bs.at[rs(mine, t)], bs.at[rs(mine, t)], s3.at[t], r3.at[t], core).start()

        @pl.when(t > 0)
        def _():
            chain(t - 1)

        pltpu.make_async_copy(bs.at[rs(theirs, t)], bs.at[rs(theirs, t)], r3.at[t]).wait()
        value = two(x, t).astype(F32) + two(bs, t).astype(F32) + out_b
        put(mid, t, value)
        centred = value - jnp.mean(value, axis=-1, keepdims=True)
        inverse = lax.rsqrt(jnp.mean(centred * centred, axis=-1, keepdims=True) + EPS)
        n2 = (centred * inverse * gain + shift).astype(BF)
        put(n2s, t, n2)
        u = product(n2, wup[...]) + up_b
        th = jnp.tanh(SLOPE * (u + CUBIC * u * u * u))
        a = (0.5 * u * (1.0 + th)).astype(BF)
        slope = 0.5 * (1.0 + th) + 0.5 * u * (1.0 - th * th) * SLOPE * (1.0 + 3.0 * CUBIC * u * u)
        put(act, t, a)
        ct = two(cot, t)
        du = (product_right(ct, wdn[...]) * slope).astype(BF)
        put(dus, t, du)
        put(q, t, product_right(du, wup[...]).astype(BF))
        remote(q.at[rs(theirs, t)], b4.at[t], s4.at[t], r4.at[t], core).start()
        put(mlp, t, product(a, wdn[...]).astype(BF))
        add_sum(0, du.astype(F32))
        add_sum(1, ct.astype(F32))
        return carry

    lax.fori_loop(0, T, forward, 0)
    chain(T - 1)

    width = p.shape[1]
    tile = 256

    def grads(i, carry):
        at = pl.ds(pl.multiple_of(i * tile, tile), tile)
        gup[at, :] = product_left(n2s[:, at], dus[...]).astype(BF)
        gdn[at, :] = product_left(act[:, at], cot[...]).astype(BF)
        return carry

    lax.fori_loop(0, width // tile, grads, 0)
    def backward(t, carry):
        pltpu.make_async_copy(b5.at[t], b5.at[t], r5.at[t]).wait()
        dn[rs(mine, t), :] = (ab2[t].astype(F32) + b5[t].astype(F32)).astype(BF)
        remote(dn.at[rs(mine, t)], dn.at[rs(mine, t)], s6.at[t], r6.at[t], core).start()
        pltpu.make_async_copy(dn.at[rs(theirs, t)], dn.at[rs(theirs, t)], r6.at[t]).wait()
        value = two(mid, t)
        centred = value - jnp.mean(value, axis=-1, keepdims=True)
        inverse = lax.rsqrt(jnp.mean(centred * centred, axis=-1, keepdims=True) + EPS)
        normal = centred * inverse
        dn2 = two(dn, t).astype(F32)
        add_sum(3, dn2 * normal)
        add_sum(4, dn2)
        dx = dn2 * gain
        dx = dx - jnp.mean(dx, axis=-1, keepdims=True) - normal * jnp.mean(
            dx * normal, axis=-1, keepdims=True
        )
        dmid = two(cot, t).astype(F32) + inverse * dx
        db = dmid.astype(BF)
        put(dbs, t, db)
        add_sum(2, db.astype(F32))
        put(do_out, t, product_right(db, wout[...]).astype(BF))
        return carry

    lax.fori_loop(0, T, backward, 0)
    gout[...] = product_left(o[...], dbs[...]).astype(BF)
    block_at = 2 * (w % 2) + w // 2 if crossed else w
    own = pl.ds(pl.multiple_of(block_at * R, R), R)
    mid_own[...] = mid[own, :]
    dmid_own[...] = dbs[own, :]
    for t in range(T):
        first[t].wait_send()
        second[t].wait_send()
        remote(bs.at[rs(mine, t)], bs.at[rs(mine, t)], s3.at[t], r3.at[t], core).wait_send()
        remote(q.at[rs(theirs, t)], b4.at[t], s4.at[t], r4.at[t], core).wait_send()
        remote(ab2.at[t], b5.at[t], s5.at[t], r5.at[t], other).wait_send()
        remote(dn.at[rs(mine, t)], dn.at[rs(mine, t)], s6.at[t], r6.at[t], core).wait_send()


def middle(G, crossed, p, X, cot, o, wup, wdn, wout, vec):
    T = 4
    rows, width = p.shape
    n = rows // 2 // T
    R = rows // 4
    d = o.shape[1]
    dma = pltpu.SemaphoreType.DMA
    full = pltpu.VMEM((rows, width), BF)
    part = pltpu.VMEM((T, n, width), BF)
    square = pltpu.VMEM((width, width), BF)
    return pl.pallas_call(
        functools.partial(middle_kernel, T, G, crossed),
        name="middle",
        out_shape=(
            jax.ShapeDtypeStruct((rows, width), BF),
            jax.ShapeDtypeStruct((R, width), F32),
            jax.ShapeDtypeStruct((R, width), BF),
            jax.ShapeDtypeStruct((rows, d), BF),
            jax.ShapeDtypeStruct((width, width), BF),
            jax.ShapeDtypeStruct((width, width), BF),
            jax.ShapeDtypeStruct((d, width), BF),
            jax.ShapeDtypeStruct((8, width), F32),
        ),
        in_specs=[ANY] * 8,
        out_specs=[VM] * 8,
        scratch_shapes=[
            full, full, full, pltpu.VMEM((rows, d), BF), square, square,
            pltpu.VMEM((d, width), BF), pltpu.VMEM((8, width), F32),
            part, part, part, full, pltpu.VMEM((rows, width), F32), full, full, full, full,
            part, part, part, full, full,
        ]
        + [dma((T,))] * 12
        + [dma((11,))],
        compiler_params=pltpu.CompilerParams(
            collective_id=1, has_side_effects=True, vmem_limit_bytes=62 << 20
        ),
        cost_estimate=pl.CostEstimate(
            flops=14 * rows * width * width, bytes_accessed=40 << 20, transcendentals=rows * width
        ),
    )(p, X, cot, o, wup, wdn, wout, vec)


def scatter_kernel(G, D, out, b1, ab, b2, st, b3, s1, r1, s2, r2, s3, r3):
    w = lax.axis_index("wt")
    c = lax.axis_index("ctx")
    g = c // G
    m = c % G
    core = w + 1 - 2 * (w % 2)
    other = (w + 2) % 4
    par = w % 2
    hi = w // 2
    greet([(core, c), (other, c)] + [(w, g * G + (m + e) % G) for e in range(1, G)])
    order = [e for e in range(1, G)] + [0]
    firsts = {}
    for j in (1, 0):
        for e in order:
            jj = (hi + j) % 2
            mm = (m + e) % G
            b = (2 * jj + 1 - par) * G + mm
            slot = jj * G + mm
            r = remote(D.at[b], b1.at[slot], s1.at[slot], r1.at[slot], (core, c))
            r.start()
            firsts[(j, e)] = r

    def arrived1(slot):
        pltpu.make_async_copy(b1.at[slot], b1.at[slot], r1.at[slot]).wait()

    seconds = []
    for e in order:
        jj = 1 - hi
        mm = (m + e) % G
        slot = jj * G + mm
        arrived1(slot)
        ab[mm] = (D[(2 * jj + par) * G + mm].astype(F32) + b1[slot].astype(F32)).astype(BF)
        r = remote(ab.at[mm], b2.at[mm], s2.at[mm], r2.at[mm], (other, c))
        r.start()
        seconds.append(r)
    thirds = []
    for e in order:
        mm = (m + e) % G
        slot = hi * G + mm
        arrived1(slot)
        pltpu.make_async_copy(b2.at[mm], b2.at[mm], r2.at[mm]).wait()
        total = D[w * G + mm].astype(F32) + b1[slot].astype(F32) + b2[mm].astype(F32)
        if e == 0:
            for f in range(1, G):
                q = (m + f) % G
                pltpu.make_async_copy(b3.at[q], b3.at[q], r3.at[q]).wait()
                total = total + b3[q].astype(F32)
            out[...] = total.astype(out.dtype)
        else:
            st[mm] = total.astype(BF)
            r = remote(st.at[mm], b3.at[m], s3.at[mm], r3.at[m], (w, g * G + mm))
            r.start()
            thirds.append(r)
    for r in list(firsts.values()) + seconds + thirds:
        r.wait_send()


def scatter_sum(G, D):
    nc, rows, C = D.shape
    dma = pltpu.SemaphoreType.DMA
    return pl.pallas_call(
        functools.partial(scatter_kernel, G),
        name="scatter_sum",
        out_shape=jax.ShapeDtypeStruct((rows, C), F32),
        in_specs=[VM],
        out_specs=VM,
        scratch_shapes=[
            pltpu.VMEM((2 * G, rows, C), BF),
            pltpu.VMEM((G, rows, C), BF),
            pltpu.VMEM((G, rows, C), BF),
            pltpu.VMEM((G, rows, C), BF),
            pltpu.VMEM((G, rows, C), BF),
            dma((2 * G,)),
            dma((2 * G,)),
            dma((G,)),
            dma((G,)),
            dma((G,)),
            dma((G,)),
        ],
        compiler_params=pltpu.CompilerParams(
            collective_id=3, has_side_effects=True, vmem_limit_bytes=60 << 20
        ),
    )(D)


def head_mask(shape, h):
    lane = lax.broadcasted_iota(jnp.int32, shape, 1)
    return jnp.logical_and(lane >= h * HEAD_DIM, lane < (h + 1) * HEAD_DIM)


def split_heads(H, value):
    zero = jnp.zeros_like(value)
    return [jnp.where(head_mask(value.shape, h), value, zero) for h in range(H)]


def spread(H, shape, values):
    out = jnp.broadcast_to(values[H - 1], shape)
    for h in range(H - 2, -1, -1):
        out = jnp.where(head_mask(shape, h), values[h], out)
    return out


def attend_tile(H, q, k_ref, v_ref, bias_ref, at_bias):
    rows, width = q.shape
    N = k_ref.shape[0]
    step_keys = min(N, 1024)
    qh = split_heads(H, q * jnp.asarray(HEAD_DIM**-0.5, BF))
    top_half = lax.broadcasted_iota(jnp.int32, (rows, 1), 0) < BLK

    def step(j, carry):
        tops, sums, acc = carry
        at = pl.ds(pl.multiple_of(j * step_keys, step_keys), step_keys)
        kc = k_ref[at, :]
        vc = v_ref[at, :]
        low = bias_ref[at_bias, :, at]
        high = bias_ref[at_bias + 1, :, at]
        new_tops, new_sums, shrink, parts = [], [], [], []
        for h in range(H):
            s = product_right(qh[h], kc)
            s = jnp.concatenate([s[:BLK] + low, s[BLK:] + high], axis=0)
            top = jnp.maximum(tops[h], jnp.max(s, axis=1, keepdims=True))
            a = jnp.exp(tops[h] - top)
            p = jnp.exp(s - top)
            new_sums.append(sums[h] * a + jnp.sum(p, axis=1, keepdims=True))
            new_tops.append(top)
            shrink.append(a)
            parts.append(product(p.astype(BF), vc))
        acc = acc * spread(H, acc.shape, shrink) + spread(H, acc.shape, parts)
        return new_tops, new_sums, acc

    start = (
        [jnp.full((rows, 1), NEG, F32)] * H,
        [jnp.zeros((rows, 1), F32)] * H,
        jnp.zeros((rows, width), F32),
    )
    tops, sums, acc = lax.fori_loop(0, N // step_keys, step, start)
    out = (acc / spread(H, acc.shape, sums)).astype(BF)
    lse = []
    for h in range(H):
        column = tops[h] + jnp.log(sums[h])
        lse.append(jnp.transpose(jnp.broadcast_to(column, (rows, BLK)))[0:1, :])
    lse = jnp.concatenate(lse + [jnp.zeros((8 - H, rows), F32)], axis=0)
    return out, lse


def attend_kernel(H, qpos, q_ref, k_ref, v_ref, bias_ref, o_ref, lse_ref):
    o, lse = attend_tile(H, q_ref[...], k_ref, v_ref, bias_ref, 2 * pl.program_id(0))
    o_ref[...] = o
    lse_ref[0] = lse


def attend(H, qpos, bias, q, k, v):
    n = qpos.shape[0]
    width = H * HEAD_DIM
    N = k.shape[0]
    rows = 2 * BLK
    whole = pl.BlockSpec((N, width), lambda i, *_: (0, 0))
    return pl.pallas_call(
        functools.partial(attend_kernel, H),
        name="attend",
        out_shape=(
            jax.ShapeDtypeStruct((n * rows, width), BF),
            jax.ShapeDtypeStruct((n, 8, rows), F32),
        ),
        grid_spec=pltpu.PrefetchScalarGridSpec(
            num_scalar_prefetch=1,
            grid=(n,),
            in_specs=[
                pl.BlockSpec((rows, width), lambda i, qp: (qp[i], 0)),
                whole,
                whole,
                pl.BlockSpec((2 * n, 1, N), lambda i, *_: (0, 0, 0)),
            ],
            out_specs=[
                pl.BlockSpec((rows, width), lambda i, *_: (i, 0)),
                pl.BlockSpec((1, 8, rows), lambda i, *_: (i, 0, 0)),
            ],
        ),
        compiler_params=pltpu.CompilerParams(vmem_limit_bytes=48 << 20),
    )(qpos, q, k, v, bias)


def attend_back_tile(H, q, do, o, lse, k_ref, v_ref, kt, dk, dv, lift_ref, tile, poll=None):
    rows, width = q.shape
    N = k_ref.shape[0]
    scale = HEAD_DIM**-0.5
    qh = split_heads(H, q * jnp.asarray(scale, BF))
    doh = split_heads(H, do)
    qcat = jnp.concatenate(qh, axis=0)
    docat = jnp.concatenate(doh, axis=0)
    pick = lax.broadcasted_iota(jnp.int32, (8, width), 1)
    base = lax.broadcasted_iota(jnp.int32, (8, width), 0) * HEAD_DIM
    pick = jnp.logical_and(pick >= base, pick < base + HEAD_DIM).astype(F32)
    delta = lax.dot_general(
        pick,
        do.astype(F32) * o.astype(F32),
        (((1,), (1,)), ((), ())),
        precision=lax.Precision.HIGHEST,
        preferred_element_type=F32,
    )

    def step(j, dqt):
        at = pl.ds(pl.multiple_of(j * CHUNK, CHUNK), CHUNK)
        kc = k_ref[at, :]
        vc = v_ref[at, :]
        ps, dss, dqs = [], [], []
        for h in range(H):
            s = product_right(kc, qh[h])
            dp = product_right(vc, doh[h])
            pieces, dpieces = [], []
            for b in range(CHUNK // BLK):
                lift = lift_ref[tile, pl.ds(j * (CHUNK // BLK) + b, 1), :]
                cut = slice(b * BLK, (b + 1) * BLK)
                p = jnp.exp(s[cut] - (lse[h : h + 1, :] + lift))
                pieces.append(p.astype(BF))
                dpieces.append((p * (dp[cut] - delta[h : h + 1, :])).astype(BF))
            p = jnp.concatenate(pieces, axis=0)
            ds = jnp.concatenate(dpieces, axis=0)
            ps.append(p)
            dss.append(ds)
            dqs.append(product(kt[h * HEAD_DIM : (h + 1) * HEAD_DIM, at], ds))
        dv[at, :] += product(jnp.concatenate(ps, axis=1), docat)
        dk[at, :] += product(jnp.concatenate(dss, axis=1), qcat)
        if poll is not None:
            poll(tile * (N // CHUNK) + j)
        return dqt + jnp.concatenate(dqs, axis=0)

    dqt = lax.fori_loop(0, N // CHUNK, step, jnp.zeros((width, rows), F32))
    return dqt * scale


def flip_rows(src, dst):
    def flip(b, carry):
        at = pl.ds(pl.multiple_of(b * BLK, BLK), BLK)
        dst[:, at] = jnp.transpose(src[at, :])
        return carry

    lax.fori_loop(0, src.shape[0] // BLK, flip, 0)


def attend_back_kernel(
    H, qpos, q_ref, k_ref, v_ref, o_ref, do_ref, lse_ref, lift_ref, dqk_ref, dv_ref, kt, dk, dv
):
    i = pl.program_id(0)
    width = H * HEAD_DIM

    @pl.when(i == 0)
    def _():
        flip_rows(k_ref, kt)
        dk[...] = jnp.zeros_like(dk)
        dv[...] = jnp.zeros_like(dv)
        dqk_ref[...] = jnp.zeros_like(dqk_ref)

    dqt = attend_back_tile(
        H, q_ref[...], do_ref[...], o_ref[...], lse_ref[0], k_ref, v_ref, kt, dk, dv, lift_ref, i
    )
    rows = 2 * BLK
    here = pl.ds(pl.multiple_of(qpos[i] * rows, rows), rows)
    dqk_ref[here, 0:width] = jnp.transpose(dqt).astype(BF)

    @pl.when(i == pl.num_programs(0) - 1)
    def _():
        dqk_ref[:, width : 2 * width] = dk[...].astype(BF)
        dv_ref[...] = dv[...].astype(BF)


def attend_back(H, qpos, lift, q, k, v, o, do, lse):
    n = qpos.shape[0]
    width = H * HEAD_DIM
    N = k.shape[0]
    rows = 2 * BLK
    whole = pl.BlockSpec((N, width), lambda i, *_: (0, 0))
    row = pl.BlockSpec((rows, width), lambda i, *_: (i, 0))
    return pl.pallas_call(
        functools.partial(attend_back_kernel, H),
        name="attend_back",
        out_shape=(
            jax.ShapeDtypeStruct((N, 2 * width), BF),
            jax.ShapeDtypeStruct((N, width), BF),
        ),
        grid_spec=pltpu.PrefetchScalarGridSpec(
            num_scalar_prefetch=1,
            grid=(n,),
            in_specs=[
                pl.BlockSpec((rows, width), lambda i, qp: (qp[i], 0)),
                whole,
                whole,
                row,
                row,
                pl.BlockSpec((1, 8, rows), lambda i, *_: (i, 0, 0)),
                pl.BlockSpec((n, N // BLK, rows), lambda i, *_: (0, 0, 0)),
            ],
            out_specs=[
                pl.BlockSpec((N, 2 * width), lambda i, *_: (0, 0)),
                pl.BlockSpec((N, width), lambda i, *_: (0, 0)),
            ],
            scratch_shapes=[
                pltpu.VMEM((width, N), BF),
                pltpu.VMEM((N, width), F32),
                pltpu.VMEM((N, width), F32),
            ],
        ),
        compiler_params=pltpu.CompilerParams(vmem_limit_bytes=60 << 20),
    )(qpos, q, k, v, o, do, lse, lift)


def head_kernel(
    G, H,
    x_h, first_h, wqk_h, wf_h, small_h, bup_h, bias_h, cot_h, wup_h, wout_h,
    X_o, xh_o, k_o, v_o, wup_o, cot_o, q, o, lse, part, wqk, wf, vec,
    X, Fv, xh, k, v, small, vq, bias, wout, bup, Y,
    rx, rf, rw, rv, rs, rc, ru, sh, sx, sf, sw, sc, su, loc, out, ry, sy,
):
    nw = 4
    w = lax.axis_index("wt")
    c = lax.axis_index("ctx")
    g = c // G
    m = c % G
    nc = nw * G
    R, width = x_h.shape
    d = width // nw
    par = w % 2
    core = (w + 1 - 2 * par, c)
    seq = 2 * (g % 2) + g // 2
    og = 2 * par + w // 2
    goal = og * G + m
    two = (w + 2) % nw
    goal_two = (2 * par + two // 2) * G + m
    is_a = w == seq
    primary = (w + seq) % 2 == 0
    high = w >= 2
    low = w < 2
    peers = [
        ((w + a) % nw, ((g + e) % nw) * G + m) for a in range(nw) for e in range(nw) if a or e
    ]
    peers += [(w, g * G + (m + e) % G) for e in range(1, G)]
    loads = [
        pltpu.make_async_copy(a, b, loc.at[i])
        for i, (a, b) in enumerate(((bup_h, bup), (bias_h, bias), (wout_h, wout)))
    ]
    for copy in loads:
        copy.start()
    greet(peers)

    here = goal == c
    here_two = goal_two == c
    to_y = remote(x_h, Y, sh.at[0], ry.at[0], (two, c))
    to_one = remote(x_h, X.at[c], sh.at[1], rx.at[c], (w, goal))
    to_two = remote(Y, X.at[c], sh.at[4], rx.at[c], (w, goal_two))
    to_first = remote(first_h, Fv.at[c], sh.at[2], rf.at[c], (w, goal))
    home_cot = jnp.logical_and(here, is_a)
    own_cot = pl.ds(pl.multiple_of(g * R, R), R)
    to_cot = remote(cot_h, cot_o.at[own_cot], sh.at[3], rc.at[g], (seq, goal))
    to_y.start()

    @pl.when(here)
    def _():
        pltpu.make_async_copy(x_h, X.at[c], rx.at[c]).start()
        pltpu.make_async_copy(first_h, Fv.at[c], rf.at[c]).start()

    @pl.when(jnp.logical_not(here))
    def _():
        to_one.start()
        to_first.start()

    def rows_of(a):
        return pl.ds(pl.multiple_of(a * d, 16), d)

    weights, fresh = [], []
    for e in range(1, nw):
        to = (w + e) % nw
        weights.append(remote(small_h, small.at[w], sw.at[e, 0], rs.at[w], (to, c)))
        weights.append(remote(wqk_h.at[to], wqk.at[rows_of(w)], sw.at[e, 1], rw.at[w], (to, c)))
        fresh.append(
            (to, remote(wf_h.at[to % 2], wf.at[rows_of(w)], sw.at[e, 2], rv.at[w], (to, c)))
        )
    for r in weights:
        r.start()
    for to, r in fresh:

        @pl.when(to < 2)
        def _():
            r.start()

    pltpu.make_async_copy(small_h, small.at[w], rs.at[w]).start()
    pltpu.make_async_copy(wqk_h.at[w], wqk.at[rows_of(w)], rw.at[w]).start()

    @pl.when(low)
    def _():
        pltpu.make_async_copy(wf_h.at[par], wf.at[rows_of(w)], rv.at[w]).start()

    @pl.when(high)
    def _():
        wf[...] = jnp.zeros_like(wf)

    def got(ref, sem):
        pltpu.make_async_copy(ref, ref, sem).wait()

    got(Y, ry.at[0])

    @pl.when(here_two)
    def _():
        pltpu.make_async_copy(Y, X.at[c], rx.at[c]).start()

    @pl.when(jnp.logical_not(here_two))
    def _():
        to_two.start()

    def core_x(b):
        return remote(X.at[b], X.at[b], sx.at[0, b], rx.at[b], core)

    def core_f(b):
        return remote(Fv.at[b], Fv.at[b], sf.at[0, b], rf.at[b], core)

    def member_x(b, e):
        return remote(X.at[b], X.at[b], sx.at[e, b], rx.at[b], (w, g * G + (m + e) % G))

    def member_f(b, e):
        return remote(Fv.at[b], Fv.at[b], sf.at[e, b], rf.at[b], (w, g * G + (m + e) % G))

    def cross_f(b):
        return remote(Fv.at[b], Fv.at[b], sy.at[b], rf.at[b], (two, c))

    crossing = jnp.logical_and(is_a, low)

    def take(b, onward):
        got(X.at[b], rx.at[b])

        if onward:

            @pl.when(crossing)
            def _():
                got(Fv.at[b], rf.at[b])
                cross_f(b).start()

        @pl.when(primary)
        def _():
            for e in range(1, G if onward else 1):
                member_x(b, e).start()
            core_x(b).start()

        @pl.when(high)
        def _():
            got(Fv.at[b], rf.at[b])

            @pl.when(primary)
            def _():
                for e in range(1, G if onward else 1):
                    member_f(b, e).start()
                core_f(b).start()

    def project(b, a):
        at = pl.ds(pl.multiple_of(b * R, R), R)
        value = X[b].astype(F32)
        centred = value - jnp.mean(value, axis=-1, keepdims=True)
        inverse = lax.rsqrt(jnp.mean(centred * centred, axis=-1, keepdims=True) + EPS)
        normal = centred * inverse
        xh[at, :] = normal.astype(BF)
        n = (normal * vec[4:5, :] + vec[5:6, :]).astype(BF)
        qk = product(n, wqk[...])
        k[at, :] = qk[:, d : 2 * d].astype(BF)
        if a is not None:
            q[pl.ds(pl.multiple_of(a * R, R), R), :] = (qk[:, :d] + vq[1:2, 0:d]).astype(BF)

        @pl.when(low)
        def _():
            v[at, :] = (product(n, wf[...]) + vq[2:3, 0:d]).astype(BF)

        @pl.when(high)
        def _():
            f = Fv[b]
            v[at, :] = jnp.where(par == 0, f[:, :d], f[:, d:])

    take(g * G + m, True)
    for copy in loads:
        copy.wait()
    for a in range(nw):
        got(small.at[a], rs.at[a])
        got(wqk.at[rows_of(a)], rw.at[a])

        @pl.when(low)
        def _():
            got(wf.at[rows_of(a)], rv.at[a])

    nb = 6 * d // 4
    for a in range(nw):
        piece = small[a].astype(F32)
        for row, src in ((0, 1), (1, 4), (2, 5), (4, 2), (5, 3), (6, 6)):
            vec[row : row + 1, a * d : (a + 1) * d] = piece[src : src + 1, :d]
        vq[0:1, a * nb : (a + 1) * nb] = piece[0:1, :nb]
    vec[3:4, :] = bup[0:1, :]
    vec[7:8, :] = jnp.zeros((1, width), F32)
    q_bias = vq[0:1, 0:d]
    for a in range(1, nw):
        q_bias = jnp.where(w == a, vq[0:1, a * d : (a + 1) * d], q_bias)
    f_bias = jnp.where(
        par == 0, vq[0:1, width : width + d], vq[0:1, width + d : width + 2 * d]
    )
    vq[1:2, 0:d] = q_bias
    vq[2:3, 0:d] = f_bias
    project(g * G + m, g)

    def own(i, carry):
        a = (g + i) % nw
        take(a * G + m, True)
        project(a * G + m, a)
        return carry

    lax.fori_loop(1, nw, own, 0)

    @pl.when(home_cot)
    def _():
        pltpu.make_async_copy(cot_h, cot_o.at[own_cot], rc.at[g]).start()

    @pl.when(jnp.logical_not(home_cot))
    def _():
        to_cot.start()

    ups = []
    for e in range(1, nw):
        to = (w + e) % nw
        src = wup_h.at[:, pl.ds(pl.multiple_of(to * width, BLK), width)]
        ups.append(remote(src, wup_o.at[rows_of(w)], su.at[e], ru.at[w], (to, c)))
    for r in ups:
        r.start()
    src = wup_h.at[:, pl.ds(pl.multiple_of(w * width, BLK), width)]
    pltpu.make_async_copy(src, wup_o.at[rows_of(w)], ru.at[w]).start()

    def others(i, carry):
        b = ((g + i % nw) % nw) * G + (m + 1 + i // nw) % G
        take(b, False)
        project(b, None)
        return carry

    lax.fori_loop(0, nw * (G - 1), others, 0)
    outs = [(X, X_o), (xh, xh_o), (k, k_o), (v, v_o)]
    outs = [pltpu.make_async_copy(a, b, out.at[i]) for i, (a, b) in enumerate(outs)]
    for copy in outs:
        copy.start()

    def cot_rows(a):
        return cot_o.at[pl.ds(pl.multiple_of(a * R, R), R)]

    og_two = 2 * par + two // 2
    spread_cot = [
        remote(cot_rows(og), cot_rows(og), sc.at[0], rc.at[og], (two, c)),
        remote(cot_rows(og), cot_rows(og), sc.at[1], rc.at[og], core),
        remote(cot_rows(og_two), cot_rows(og_two), sc.at[2], rc.at[og_two], core),
    ]
    got(cot_rows(og), rc.at[og])
    spread_cot[0].start()
    spread_cot[1].start()

    def attend_one(t, carry):
        at = pl.ds(pl.multiple_of(t * R, R), R)
        ot, lt = attend_tile(H, q[at, :], k, v, bias, 2 * t)
        o[at, :] = ot
        lse[t] = lt
        part[at, :] = product(ot, wout[...]).astype(BF)
        return carry

    lax.fori_loop(0, nw, attend_one, 0)

    got(cot_rows(og_two), rc.at[og_two])
    spread_cot[2].start()
    for copy in outs:
        copy.wait()
    for a in range(nw):
        got(wup_o.at[rows_of(a)], ru.at[a])

    for hi in range(2):
        a = 2 * (1 - par) + hi
        got(cot_rows(a), rc.at[a])

    for r in weights + ups + spread_cot + [to_y]:
        r.wait_send()
    for to, r in fresh:

        @pl.when(to < 2)
        def _():
            r.wait_send()

    @pl.when(jnp.logical_not(here))
    def _():
        to_one.wait_send()
        to_first.wait_send()

    @pl.when(jnp.logical_not(here_two))
    def _():
        to_two.wait_send()

    @pl.when(jnp.logical_not(home_cot))
    def _():
        to_cot.wait_send()

    @pl.when(crossing)
    def _():
        for a in range(nw):
            cross_f(a * G + m).wait_send()

    @pl.when(primary)
    def _():

        def sent(b, carry):
            core_x(b).wait_send()

            @pl.when(b % G == m)
            def _():
                for e in range(1, G):
                    member_x(b, e).wait_send()

            @pl.when(high)
            def _():
                core_f(b).wait_send()

                @pl.when(b % G == m)
                def _():
                    for e in range(1, G):
                        member_f(b, e).wait_send()

            return carry

        lax.fori_loop(0, nc, sent, 0)


def head(G, H, x, first, wqk, wf, small, bup, bias, cot, wup, wout):
    nw = 4
    nc = nw * G
    R, width = x.shape
    d = width // nw
    N = nc * R
    dma = pltpu.SemaphoreType.DMA
    vm = pltpu.VMEM
    shape = jax.ShapeDtypeStruct
    operands = (x, first, wqk, wf, small, bup, bias, cot, wup, wout)
    return pl.pallas_call(
        functools.partial(head_kernel, G, H),
        name="head",
        out_shape=(
            shape((nc, R, width), BF),
            shape((N, width), BF),
            shape((N, d), BF),
            shape((N, d), BF),
            shape((width, width), BF),
            shape((nw * R, width), BF),
            shape((nw * R, d), BF),
            shape((nw * R, d), BF),
            shape((nw, 8, R), F32),
            shape((nw * R, width), BF),
            shape((width, 2 * d), BF),
            shape((width, d), BF),
            shape((8, width), F32),
        ),
        in_specs=[ANY] * len(operands),
        out_specs=[ANY] * 6 + [VM] * 7,
        scratch_shapes=[
            vm((nc, R, width), BF), vm((nc, R, 2 * d), BF), vm((N, width), BF), vm((N, d), BF),
            vm((N, d), BF), vm((nw,) + small.shape, BF), vm((8, 6 * d), F32),
            vm(bias.shape, F32), vm(wout.shape, BF), vm(bup.shape, F32), vm((R, width), BF),
            dma((nc,)), dma((nc,)), dma((nw,)), dma((nw,)), dma((nw,)), dma((nw,)), dma((nw,)),
            dma((5,)), dma((G, nc)), dma((G, nc)), dma((nw, 3)), dma((nw,)), dma((nw,)),
            dma((3,)), dma((4,)), dma((1,)), dma((nc,)),
        ],
        compiler_params=pltpu.CompilerParams(
            collective_id=0, has_side_effects=True, vmem_limit_bytes=56 << 20
        ),
        cost_estimate=pl.CostEstimate(
            flops=14 << 30, bytes_accessed=40 << 20, transcendentals=6 << 20
        ),
    )(*operands)


class Ring:
    def __init__(self, nc, pos, right, left, seg, chains, A, slots, out, ss, sr):
        self.nc, self.pos, self.right, self.left, self.seg = nc, pos, right, left, seg
        self.chains, self.A, self.slots, self.out, self.ss, self.sr = chains, A, slots, out, ss, sr
        self.steps = 2 * (nc - 1)
        self.cut = A.shape[1] // chains

    def at(self, half, j):
        j = (j + 2 * self.nc) % self.nc
        return pl.ds(pl.multiple_of((half * self.nc + j) * self.seg, 16), self.seg)

    def cols(self, i):
        if self.chains == 1:
            return pl.ds(0, self.cut)
        return pl.ds(pl.multiple_of(i * self.cut, BLK), self.cut)

    def reduce_copies(self, i, s):
        k = self.cols(i)
        return [
            remote(
                self.A.at[self.at(h, j), k],
                self.slots.at[h, s, :, k],
                self.ss.at[h, i, s],
                self.sr.at[h, i, s],
                to,
            )
            for h, j, to in ((0, self.pos - s, self.right), (1, self.pos + s, self.left))
        ]

    def gather_copies(self, i, s):
        k = self.cols(i)
        t = s - (self.nc - 1)
        return [
            remote(
                self.out.at[self.at(h, j), k],
                self.out.at[self.at(h, j), k],
                self.ss.at[h, i, s],
                self.sr.at[h, i, s],
                to,
            )
            for h, j, to in ((0, self.pos + 1 - t, self.right), (1, self.pos - 1 + t, self.left))
        ]

    def send(self, i, s, gathering=False):
        for r in (self.gather_copies if gathering else self.reduce_copies)(i, s):
            r.start()

    def begin(self):
        for i in range(self.chains):
            self.send(i, 0)

    def add(self, i, s):
        k = self.cols(i)
        for h, j in ((0, self.pos - s - 1), (1, self.pos + s + 1)):
            at = self.at(h, j)
            slot = self.slots.at[h, s, :, k]
            pltpu.make_async_copy(slot, slot, self.sr.at[h, i, s]).wait()
            value = self.A[at, k].astype(F32) + self.slots[h, s, :, k].astype(F32)
            self.A[at, k] = value.astype(BF)

    def keep(self, i):
        k = self.cols(i)
        for h, j in ((0, self.pos + 1), (1, self.pos - 1)):
            self.out[self.at(h, j), k] = self.A[self.at(h, j), k]

    def arrive(self, i, s):
        t = s - (self.nc - 1)
        for h, j in ((0, self.pos - t), (1, self.pos + t)):
            at = self.out.at[self.at(h, j), self.cols(i)]
            pltpu.make_async_copy(at, at, self.sr.at[h, i, s]).wait()

    def step(self, s):
        for i in range(self.chains):
            self.turn(i, s)

    def turn(self, i, s):
        last = self.nc - 2
        if isinstance(s, int):
            when = lambda cond: (lambda body: body() if cond else None)
            both = lambda a, b: a and b
        else:
            when, both = pl.when, jnp.logical_and

        @when(s < last)
        def _():
            self.add(i, s)
            self.send(i, s + 1)

        @when(s == last)
        def _():
            self.add(i, last)
            self.keep(i)
            self.send(i, last + 1, True)

        @when(both(s > last, s < self.steps))
        def _():
            self.arrive(i, s)

        @when(both(s > last, s < self.steps - 1))
        def _():
            self.send(i, s + 1, True)

    def drain(self):
        for gathering in (False, True):

            def one(t, carry):
                i, s = t % self.chains, t // self.chains
                for r in (self.gather_copies if gathering else self.reduce_copies)(i, s):
                    r.wait_send()
                return carry

            half = self.steps * self.chains // 2
            lax.fori_loop(half * gathering, half * (1 + gathering), one, 0)


class SplitRing(Ring):
    def __init__(self, nc, pos, right, left, seg, chains, A, slots, out, ss, sr, own, sems):
        super().__init__(nc, pos, right, left, seg, chains, A, slots, out, ss, sr)
        self.turns = nc - 1
        self.w, self.c = own
        self.s_ex, self.r_ex, self.s_hop, self.r_hop = sems
        self.group = nc // 2
        self.reach = (nc // 2, nc // 2 - 1)

    def turn(self, i, s):
        last = self.nc - 2
        if isinstance(s, int):
            when = lambda cond: (lambda body: body() if cond else None)
        else:
            when = pl.when

        @when(s <= last)
        def _():
            self.add(i, s)

        @when(s < last)
        def _():
            self.send(i, s + 1)

    def parts(self):
        for h, j in ((0, self.pos + 1), (1, self.pos - 1)):
            j = (j + self.nc) % self.nc
            to = 2 * h + j // self.group
            src = self.A.at[self.at(h, j)]
            dst = self.out.at[j % self.group, self.w]
            yield h, to, src, dst

    def exchange(self):
        for h, to, src, dst in self.parts():
            local = pltpu.make_async_copy(src, dst, self.r_ex.at[self.w])
            far = remote(src, dst, self.s_ex.at[h], self.r_ex.at[self.w], (to, self.c))

            @pl.when(to == self.w)
            def _():
                local.start()

            @pl.when(to != self.w)
            def _():
                far.start()

    def held(self, position):
        j = (position + 1 - 2 * (self.w // 2) + 2 * self.nc) % self.nc
        return j // self.group == self.w % 2, j % self.group

    def hop_copy(self, way, h, j):
        ref = self.out.at[j]
        to = (self.right, self.left)[way]
        return remote(ref, ref, self.s_hop.at[way, h], self.r_hop.at[way, h], to)

    def spread(self):
        have, j = self.held(self.pos)

        @pl.when(have)
        def _():
            for a in range(4):
                ref = self.out.at[j, a]
                pltpu.make_async_copy(ref, ref, self.r_ex.at[a]).wait()
            for way in range(2):
                self.hop_copy(way, 1, j).start()

    def hop(self, h):
        for way in range(2):
            if h > self.reach[way]:
                continue
            have, j = self.held(self.pos - h if way == 0 else self.pos + h)

            @pl.when(have)
            def _():
                ref = self.out.at[j]
                pltpu.make_async_copy(ref, ref, self.r_hop.at[way, h]).wait()
                if h < self.reach[way]:
                    self.hop_copy(way, h + 1, j).start()

    def drain(self):
        def one(t, carry):
            i, s = t % self.chains, t // self.chains
            for r in self.reduce_copies(i, s):
                r.wait_send()
            return carry

        lax.fori_loop(0, self.turns * self.chains, one, 0)
        for h, to, src, dst in self.parts():

            @pl.when(to != self.w)
            def _():
                remote(src, dst, self.s_ex.at[h], self.r_ex.at[self.w], (to, self.c)).wait_send()

        for way in range(2):
            for h in range(self.reach[way]):
                have, j = self.held(self.pos - h if way == 0 else self.pos + h)

                @pl.when(have)
                def _():
                    self.hop_copy(way, h + 1, j).wait_send()


def tail_kernel(
    G, H, seg_a, seg_u, seg_b,
    q_h, k_h, v_h, o_h, do_h, lse_h, lift_h, xh_h, X_h, wqk_h, wf_h, vec_h, dmid_h,
    up_h, down_h, gout_h, small_h, mlp_h, mid_h,
    layer_out, tokens_out, first_out, up_out, down_out, gout_out, small_out, qkv_out, ends_out,
    q, k, v, o, do, lse, lift, xh, X, wqk, wf, vec, dmid,
    kt, dk, dv, dqk, dvb, D, b1, ab, b2, st, b3, tot, tb, tr,
    A, slots_a, res_a, U, slots_u, res_u, gq, slots_b, res_b, gain_t, shift_t, sums_t, f1, fs, fr,
    mlp, mid, lb, ly, lr, sl, rl, sL, rL, s1, r1, s2, r2, s3, r3, sT, rT, ssa, sra, ssu, sru, seu, reu, shu, rhu, ssb, srb, seb, reb, shb, rhb, sf1, rf1, sf2, rf2, ld,
):
    w = lax.axis_index("wt")
    c = lax.axis_index("ctx")
    nw = 4
    nc = nw * G
    g = c // G
    m = c % G
    par = w % 2
    hi = w // 2
    core = (w + 1 - 2 * par, c)
    other = ((w + 2) % nw, c)
    R, width = dmid.shape
    d = width // nw
    N = xh.shape[0]
    odd = c % 2
    pos = (c // 2) * (1 - odd) + (nc - 1 - c // 2) * odd

    def ctx_at(p):
        p = (p + nc) % nc
        h = p // (nc // 2)
        return 2 * p * (1 - h) + (2 * (nc - 1 - p) + 1) * h

    right = (w, ctx_at(pos + 1))
    left = (w, ctx_at(pos - 1))
    loads = [
        (up_h, U),
        (down_h, A.at[pl.ds(0, width)]),
        (gout_h, A.at[pl.ds(width, d)]),
        (small_h, A.at[pl.ds(width + d, small_h.shape[0])]),
        (k_h, k), (v_h, v), (q_h, q), (o_h, o), (do_h, do), (lse_h, lse), (lift_h, lift),
        (xh_h, xh), (X_h, X), (wqk_h, wqk), (wf_h, wf), (vec_h, vec), (dmid_h, dmid), (mid_h, mid), (mlp_h, mlp),
    ]
    loads = [pltpu.make_async_copy(a, b, ld.at[i]) for i, (a, b) in enumerate(loads)]
    for copy in loads:
        copy.start()
    peers = [
        ((w + a) % nw, ((g + e) % nw) * G + m) for a in range(nw) for e in range(nw) if a or e
    ]
    peers += [(w, g * G + (m + e) % G) for e in range(1, G)]
    greet(peers + [right, left])
    ring_a = Ring(nc, pos, right, left, seg_a, 2, A, slots_a, res_a, ssa, sra)
    ring_u = SplitRing(
        nc, pos, right, left, seg_u, 2, U, slots_u, res_u, ssu, sru, (w, c), (seu, reu, shu, rhu)
    )
    ring_b = SplitRing(
        nc, pos, right, left, seg_b, 1, gq, slots_b, res_b, ssb, srb, (w, c), (seb, reb, shb, rhb)
    )
    for copy in loads[:4]:
        copy.wait()
    ring_u.begin()
    ring_a.begin()
    for copy in loads[4:11] + loads[17:]:
        copy.wait()
    seq = 2 * (g % 2) + g // 2
    og = 2 * par + hi
    home = (seq, og * G + m)
    home_self = jnp.logical_and(og == g, w == seq)
    shares = []
    for e in range(1, nw):
        to = (w + e) % nw
        src = mlp.at[pl.ds(pl.multiple_of((2 * (to % 2) + to // 2) * R, R), R)]
        r = remote(src, lb.at[w], sl.at[e], rl.at[w], (to, c))
        r.start()
        shares.append(r)

    flip_rows(k, kt)
    dk[...] = jnp.zeros_like(dk)
    dv[...] = jnp.zeros_like(dv)
    dqk[...] = jnp.zeros_like(dqk)
    wide = H * HEAD_DIM

    def poll(n):
        for r in range(4):

            @pl.when(n % 4 == r)
            def _():
                (ring_a if r % 2 else ring_u).turn(r // 2, n // 4)

    def tile(t, carry):
        here = pl.ds(pl.multiple_of((t * G + m) * R, R), R)
        mine = pl.ds(pl.multiple_of(t * R, R), R)
        dqt = attend_back_tile(
            H, q[mine, :], do[mine, :], o[mine, :], lse[t], k, v, kt, dk, dv, lift, t, poll
        )
        dqk[here, 0:wide] = jnp.transpose(dqt).astype(BF)
        return carry

    lax.fori_loop(0, nw, tile, 0)
    dqk[:, wide : 2 * wide] = dk[...].astype(BF)
    dvb[...] = dv[...].astype(BF)
    polls = nw * (N // CHUNK)
    for copy in loads[11:17]:
        copy.wait()

    layer = mid[...] + vec[6:7, :] + mlp[pl.ds(pl.multiple_of(og * R, R), R), :].astype(F32)
    for e in range(1, nw):
        src = (w + e) % nw
        pltpu.make_async_copy(lb.at[src], lb.at[src], rl.at[src]).wait()
        layer = layer + lb[src].astype(F32)
    ly[...] = layer.astype(BF)
    layer_back = remote(ly, lr, sL.at[0], rL.at[0], home)
    layer_stay = pltpu.make_async_copy(ly, lr, rL.at[0])

    @pl.when(home_self)
    def _():
        layer_stay.start()

    @pl.when(jnp.logical_not(home_self))
    def _():
        layer_back.start()

    upper = w >= 2
    first_copies = []
    for e in range(1, G):
        mm = (m + e) % G
        for gp in range(nw):
            src = dvb.at[pl.ds(pl.multiple_of((gp * G + mm) * R, R), R)]
            first_copies.append(
                remote(src, f1.at[m, gp], sf1.at[e, gp], rf1.at[m, gp], (w, g * G + mm))
            )

    @pl.when(upper)
    def _():
        for r in first_copies:
            r.start()

    tile_d = 128
    ones = jnp.ones((N, BLK), BF)
    row_qk = product_left(ones, dqk[...])[0:1, :]
    row_f = product_left(ones, dvb[...])[0:1, :]
    sum_qk = product_left(dqk[...], ones)
    sum_f = product_left(dvb[...], ones)
    gain_t[...] = jnp.transpose(jnp.broadcast_to(vec[4:5, :], (BLK, width)))
    shift_t[...] = jnp.transpose(jnp.broadcast_to(vec[5:6, :], (BLK, width)))
    lane = lax.broadcasted_iota(jnp.int32, (d, BLK), 1)
    edge = gq.shape[1] - BLK
    for a in range(nw):
        sums_t[a * d : (a + 1) * d, :] = jnp.where(
            lane == 66, sum_qk[:wide], jnp.where(lane == 67, sum_qk[wide:], sum_f)
        )
    lane = lax.broadcasted_iota(jnp.int32, (tile_d, BLK), 1)

    def grads(i, carry):
        at = pl.ds(pl.multiple_of(i * tile_d, tile_d), tile_d)
        x_qk = product_left(xh[:, at], dqk[...])
        x_f = product_left(xh[:, at], dvb[...])
        w_qk = wqk[at, :].astype(F32)
        w_f = wf[at, :].astype(F32)
        add = lambda a, b: jnp.sum(a, axis=1, keepdims=True) + jnp.sum(b, axis=1, keepdims=True)
        for_gain = add(w_qk * x_qk, w_f * x_f)
        for_shift = add(w_qk * row_qk, w_f * row_f)
        gain = gain_t[at, 0:1]
        shift = shift_t[at, 0:1]
        gq[at, 0 : 2 * wide] = (gain * x_qk + shift * row_qk).astype(BF)
        gq[at, 2 * wide : 3 * wide] = (gain * x_f + shift * row_f).astype(BF)
        ends = gq[at, edge:].astype(F32)
        ends = jnp.where(lane == 64, for_gain, jnp.where(lane == 65, for_shift, ends))
        ends = jnp.where(lane > 65, sums_t[at, :], ends)
        gq[at, edge:] = jnp.where(lane < 69, ends, 0.0).astype(BF)
        poll(polls + i)
        return carry

    lax.fori_loop(0, width // tile_d, grads, 0)
    polls += width // tile_d
    ring_b.begin()

    def block(i, carry):
        phase = i // (2 * G)
        jj = (hi + 1 - (i // G) % 2 + 2) % 2
        mm = (m + 1 + i % G) % G
        parity = (1 - par) * (1 - phase) + par * phase
        b = (2 * parity + jj) * G + mm
        at = pl.ds(pl.multiple_of(b * R, R), R)
        dn = product_right(dqk[at, :], wqk[...]) + product_right(dvb[at, :], wf[...])
        D[b] = dn.astype(BF)

        @pl.when(phase == 0)
        def _():
            slot = jj * G + mm
            remote(D.at[b], b1.at[slot], s1.at[slot], r1.at[slot], core).start()

        poll(polls + i)

        @pl.when(i % 4 == 3)
        def _():
            ring_b.step(i // 4)

        return carry

    lax.fori_loop(0, nc, block, 0)
    polls += nc
    done_b = nc // 4

    order = list(range(1, G)) + [0]

    def chip_sum(jj, mm):
        slot = jj * G + mm
        pltpu.make_async_copy(b1.at[slot], b1.at[slot], r1.at[slot]).wait()
        return D[(2 * par + jj) * G + mm].astype(F32) + b1[slot].astype(F32)

    seconds = []
    for e in order:
        mm = (m + e) % G
        ab[mm] = chip_sum(1 - hi, mm).astype(BF)
        r = remote(ab.at[mm], b2.at[mm], s2.at[mm], r2.at[mm], other)
        r.start()
        seconds.append(r)
    thirds = []

    def sum_chips():
        for e in order:
            mm = (m + e) % G
            total = chip_sum(hi, mm)
            pltpu.make_async_copy(b2.at[mm], b2.at[mm], r2.at[mm]).wait()
            total = total + b2[mm].astype(F32)
            if e:
                st[mm] = total.astype(BF)
                r = remote(st.at[mm], b3.at[m], s3.at[mm], r3.at[m], (w, g * G + mm))
                r.start()
                thirds.append(r)
            else:
                tot[...] = total

    def sum_first():
        @pl.when(upper)
        def _():
            for gp in range(nw):
                total = dvb[pl.ds(pl.multiple_of((gp * G + m) * R, R), R), :].astype(F32)
                for e in range(1, G):
                    mm = (m + e) % G
                    pltpu.make_async_copy(f1.at[mm, gp], f1.at[mm, gp], rf1.at[mm, gp]).wait()
                    total = total + f1[mm, gp].astype(F32)
                fs[gp] = total.astype(BF)
                own = jnp.logical_and(w == seq, g == gp)

                @pl.when(own)
                def _():
                    pltpu.make_async_copy(fs.at[gp], fr.at[par], rf2.at[par]).start()

                @pl.when(jnp.logical_not(own))
                def _():
                    remote(
                        fs.at[gp], fr.at[par], sf2.at[gp], rf2.at[par], (seq, gp * G + m)
                    ).start()

    back = remote(tb, tr, sT.at[0], rT.at[0], home)
    stay = pltpu.make_async_copy(tb, tr, rT.at[0])

    def norm_back():
        total = tot[...]
        for e in range(1, G):
            mm = (m + e) % G
            pltpu.make_async_copy(b3.at[mm], b3.at[mm], r3.at[mm]).wait()
            total = total + b3[mm].astype(F32)
        value = X[og * G + m].astype(F32)
        centred = value - jnp.mean(value, axis=-1, keepdims=True)
        inverse = lax.rsqrt(jnp.mean(centred * centred, axis=-1, keepdims=True) + EPS)
        normal = centred * inverse
        dx = total * vec[4:5, :]
        dx = dx - jnp.mean(dx, axis=-1, keepdims=True) - normal * jnp.mean(
            dx * normal, axis=-1, keepdims=True
        )
        tb[...] = (dmid[...].astype(F32) + inverse * dx).astype(BF)

        @pl.when(home_self)
        def _():
            stay.start()

        @pl.when(jnp.logical_not(home_self))
        def _():
            back.start()

    turns = []
    for n in range(polls, 4 * ring_a.steps):
        r, s = n % 4, n // 4
        if r % 2:
            turns.append(functools.partial(ring_a.turn, r // 2, s))
        elif s < ring_u.turns:
            turns.append(functools.partial(ring_u.turn, r // 2, s))
            if r == 2 and s == ring_u.turns - 1:
                turns.append(ring_u.exchange)
        elif r == 0 and s - ring_u.turns <= ring_u.reach[0]:
            h = s - ring_u.turns
            turns.append(functools.partial(ring_u.hop, h) if h else ring_u.spread)

    def others():
        for _ in range(2):
            if turns:
                turns.pop(0)()

    for at_b in range(done_b, ring_b.turns):
        ring_b.step(at_b)
        others()
        if at_b == done_b:
            sum_first()
        if at_b == done_b + 4:
            sum_chips()
    ring_b.exchange()
    others()
    ring_b.spread()
    others()
    norm_back()
    for h in range(1, ring_b.reach[0] + 1):
        ring_b.hop(h)
        others()
    while turns:
        others()

    down_out[...] = res_a[0:width, :].astype(F32)
    gout_out[...] = res_a[width : width + d, :].astype(F32)
    small_out[...] = res_a[width + d : width + d + small_out.shape[0], :].astype(F32)
    for j in range(ring_u.group):
        rows = slice(j * seg_u, (j + 1) * seg_u)
        for a in range(nw):
            up_out[rows, a * width : (a + 1) * width] = res_u[j, a].astype(F32)
    for j in range(ring_b.group):
        rows = slice(j * seg_b, (j + 1) * seg_b)
        for a in range(nw):
            for part in range(2):
                at = part * width + a * d
                qkv_out[rows, at : at + d] = res_b[j, a, :, part * d : (part + 1) * d].astype(F32)
            if a < 2:
                at = 2 * width + a * d
                qkv_out[rows, at : at + d] = res_b[j, a, :, 2 * d : 3 * d].astype(F32)
            at = a * d + j * seg_b
            ends_out[at : at + seg_b, :] = res_b[j, a, :, edge:].astype(F32)
    pltpu.make_async_copy(tr, tr, rT.at[0]).wait()
    tokens_out[...] = tr[...].astype(F32)
    for u in range(2):
        pltpu.make_async_copy(fr.at[u], fr.at[u], rf2.at[u]).wait()
        first_out[:, u * d : (u + 1) * d] = fr[u].astype(F32)

    pltpu.make_async_copy(lr, lr, rL.at[0]).wait()
    layer_out[...] = lr[...]
    ring_a.drain()
    ring_u.drain()
    ring_b.drain()
    for r in seconds + thirds + shares:
        r.wait_send()

    @pl.when(jnp.logical_not(home_self))
    def _():
        back.wait_send()
        layer_back.wait_send()

    @pl.when(upper)
    def _():
        for r in first_copies:
            r.wait_send()
        for gp in range(nw):

            @pl.when(jnp.logical_not(jnp.logical_and(w == seq, g == gp)))
            def _():
                remote(
                    fs.at[gp], fr.at[par], sf2.at[gp], rf2.at[par], (seq, gp * G + m)
                ).wait_send()

    def drain(i, carry):
        jj = (hi + 1 - (i // G) % 2 + 2) % 2
        mm = (m + 1 + i % G) % G
        slot = jj * G + mm
        b = (2 * (1 - par) + jj) * G + mm
        remote(D.at[b], b1.at[slot], s1.at[slot], r1.at[slot], core).wait_send()
        return carry

    lax.fori_loop(0, 2 * G, drain, 0)


def tail(
    G, H, q, k, v, o, do, lse, lift, xh, X, wqk, wf, vec, dmid, up, down, gout, small, mlp, mid
):
    nw = 4
    nc = nw * G
    R, width = dmid.shape
    d = width // nw
    N = xh.shape[0]
    wide = H * HEAD_DIM
    seg_a = (width + d + small.shape[0]) // (2 * nc)
    seg_u = seg_b = width // (2 * nc)
    cols = 5 * BLK
    dma = pltpu.SemaphoreType.DMA
    vm = pltpu.VMEM
    steps = 2 * (nc - 1)
    operands = (
        q, k, v, o, do, lse, lift, xh, X, wqk, wf, vec, dmid, up, down, gout, small, mlp, mid
    )
    return pl.pallas_call(
        functools.partial(tail_kernel, G, H, seg_a, seg_u, seg_b),
        name="tail",
        out_shape=(
            jax.ShapeDtypeStruct((R, width), BF),
            jax.ShapeDtypeStruct((R, width), F32),
            jax.ShapeDtypeStruct((R, 2 * d), F32),
            jax.ShapeDtypeStruct((d, nw * width), F32),
            jax.ShapeDtypeStruct((width, width), F32),
            jax.ShapeDtypeStruct((d, width), F32),
            jax.ShapeDtypeStruct(small.shape, F32),
            jax.ShapeDtypeStruct((d, 2 * width + 2 * d), F32),
            jax.ShapeDtypeStruct((width, BLK), F32),
        ),
        in_specs=[ANY] * len(operands),
        out_specs=[VM] * 9,
        scratch_shapes=[vm(a.shape, a.dtype) for a in operands[:13]]
        + [
            vm((wide, N), BF), vm((N, wide), F32), vm((N, wide), F32), vm((N, 2 * wide), BF),
            vm((N, wide), BF), vm((nc, R, width), BF), vm((2 * G, R, width), BF),
            vm((G, R, width), BF), vm((G, R, width), BF), vm((G, R, width), BF),
            vm((G, R, width), BF), vm((R, width), F32), vm((R, width), BF), vm((R, width), BF),
            vm((2 * nc * seg_a, width), BF), vm((2, nc - 1, seg_a, width), BF),
            vm((2 * nc * seg_a, width), BF),
            vm((width, width), BF), vm((2, nc - 1, seg_u, width), BF),
            vm((nc // 2, nw, seg_u, width), BF),
            vm((width, cols), BF), vm((2, nc - 1, seg_b, cols), BF),
            vm((nc // 2, nw, seg_b, cols), BF),
            vm((width, BLK), F32), vm((width, BLK), F32), vm((width, BLK), F32),
            vm((G, nw, R, d), BF), vm((nw, R, d), BF), vm((2, R, d), BF),
            vm((nw * R, width), BF), vm((R, width), F32), vm((nw, R, width), BF),
            vm((R, width), BF), vm((R, width), BF), dma((nw,)), dma((nw,)), dma((1,)), dma((1,)),
            dma((2 * G,)), dma((2 * G,)), dma((G,)), dma((G,)), dma((G,)), dma((G,)),
            dma((1,)), dma((1,)), dma((2, 2, steps)), dma((2, 2, steps)),
        ]
        + [
            dma(a)
            for chains in (2, 1)
            for a in (
                (2, chains, nc - 1), (2, chains, nc - 1), (2,), (nw,), (2, nc // 2 + 1),
                (2, nc // 2 + 1),
            )
        ]
        + [
            dma((G, nw)), dma((G, nw)),
            dma((nw,)), dma((2,)), dma((len(operands),)),
        ],
        compiler_params=pltpu.CompilerParams(
            collective_id=2, has_side_effects=True, vmem_limit_bytes=63 << 20
        ),
        cost_estimate=pl.CostEstimate(
            flops=40 << 30, bytes_accessed=60 << 20, transcendentals=6 << 20
        ),
    )(*operands)


def on_device(
    nw,
    nc,
    tokens,
    first_values,
    cotangent,
    deal,
    w_qkv,
    bias_qv,
    w_out,
    bias_out,
    gain_one,
    shift_one,
    gain_two,
    shift_two,
    w_up,
    bias_up,
    w_down,
    bias_down,
):
    G = nc // nw
    w = lax.axis_index("wt")
    c = lax.axis_index("ctx")
    m = c % G
    rows, width = tokens.shape[1:]
    d = width // nw
    H = HEADS // nw
    both = ("wt", "ctx")
    seq = lambda g: 2 * (g % 2) + g // 2
    swap = [
        (a * nc + g * G + e, seq(g) * nc + a * G + e)
        for a in range(nw)
        for g in range(nw)
        for e in range(G)
    ]
    ring = [[(a, (a + k) % nw) for a in range(nw)] for k in range(nw)]

    def exchange(pieces):
        out = jnp.zeros_like(pieces)
        mine = lax.dynamic_index_in_dim(pieces, w, 0, keepdims=True)
        out = lax.dynamic_update_slice_in_dim(out, mine, w, 0)
        for k in range(1, nw):
            piece = lax.dynamic_index_in_dim(pieces, (w + k) % nw, 0, keepdims=True)
            got = lax.ppermute(piece, "wt", ring[k])
            out = lax.dynamic_update_slice_in_dim(out, got, (w + nw - k) % nw, 0)
        return out

    qk = w_qkv[:, : 2 * width].reshape(d, 2, nw, d).transpose(2, 0, 1, 3).reshape(nw, d, 2 * d)
    wf = w_qkv[:, 2 * width :].reshape(d, 2, d).transpose(1, 0, 2)
    nb = bias_qv.shape[0]
    ids = dealt_blocks(deal)
    qpos = jnp.arange(nw, dtype=jnp.int32) * G + m
    qid = jnp.take(ids.reshape(nc, 2), qpos, axis=0)
    hidden = (ids[None, None, :] > qid[:, :, None]).astype(F32) * -NEG
    bias = jnp.repeat(-hidden.reshape(2 * nw, 2 * nc), BLK, axis=1)[:, None, :]
    lift = jnp.repeat(hidden.transpose(0, 2, 1), BLK, axis=2)

    def mine(vector):
        return lax.dynamic_slice_in_dim(vector, w * d, d)

    if nc <= 8:
        wide = lambda a: jnp.concatenate([a, jnp.zeros((2 * d - a.shape[0],), BF)])
        small = jnp.stack(
            [
                wide(a)
                for a in (bias_qv, bias_out, gain_one, shift_one, gain_two, shift_two, bias_down)
            ]
            + [jnp.zeros((2 * d,), BF)]
        )
        bup = jnp.broadcast_to(bias_up.astype(F32)[None], (8, width))
        X, xhat, k, v, Wup, cot, q, o, lse, part, Wqk, Wf, vec = head(
            G, H, tokens[0], first_values[0], qk, wf, small, bup, bias, cotangent[0], w_up, w_out
        )
        mlp, mid_own, d_mid, d_o, g_up, g_down, g_out, vsums = middle(
            G, True, part, X, cot, o, Wup, w_down, w_out, vec
        )
        small = jnp.stack(
            [vsums[0], jnp.concatenate([mine(vsums[a]) for a in range(1, 5)])]
            + [jnp.zeros((width,), F32)] * 14
        ).astype(BF)
        rows_a = width + d + 16
        pad = -(-rows_a // (32 * nc)) * 32 * nc - rows_a
        small = jnp.concatenate([small, jnp.zeros((pad, width), BF)], axis=0)
        layer, grad_tokens, grad_first, s_up, s_down, s_out, s_small, s_qkv, ends = tail(
            G, H, q, k, v, o, d_o, lse, lift, xhat, X, Wqk, Wf, vec,
            d_mid, g_up, g_down, g_out, small, mlp, mid_own,
        )
        ends = ends.reshape(nw, d, BLK)
        bias_all = jnp.concatenate([ends[:, :, 66].reshape(-1), ends[:2, :, 68].reshape(-1)])
        s_vec = s_small[1].reshape(nw, d)
        return (
            layer[None],
            grad_tokens[None],
            grad_first[None],
            s_qkv,
            lax.dynamic_slice_in_dim(bias_all, w * nb, nb),
            s_out,
            s_vec[1],
            jnp.sum(ends[:, :, 64], axis=0),
            jnp.sum(ends[:, :, 65], axis=0),
            s_vec[2],
            s_vec[3],
            s_up,
            s_small[0],
            s_down,
            s_vec[0],
        )
    small = jnp.concatenate(
        [bias_qv, bias_out, gain_one, shift_one, gain_two, shift_two, bias_down]
    )
    lanes = 16 * BLK
    small = jnp.concatenate([small, jnp.zeros((lanes - small.shape[0],), BF)]).reshape(16, BLK)
    X, Fv, WQK, WF, SM = gather(nw, G, tokens[0], first_values[0], qk, wf, small)
    X = X.reshape(nc * rows, width)
    Wqk = WQK.reshape(width, 2 * d)
    low = w < 2
    Wf = jnp.where(low, WF.reshape(width, d), jnp.zeros((width, d), BF))
    SM = SM.reshape(nw, lanes).astype(F32)
    qv_vector = SM[:, :nb].reshape(-1)
    vectors = [SM[:, nb + a * d : nb + (a + 1) * d].reshape(-1) for a in range(6)]
    out_vector, gain_a, shift_a, gain_b, shift_b, down_vector = vectors

    x32 = X.astype(F32)
    mean = jnp.mean(x32, axis=-1, keepdims=True)
    centred = x32 - mean
    inverse = lax.rsqrt(jnp.mean(centred * centred, axis=-1, keepdims=True) + EPS)
    n1 = (centred * inverse * gain_a + shift_a).astype(BF)
    pqk = product(n1, Wqk)
    q_bias = lax.dynamic_slice_in_dim(qv_vector, w * d, d)
    f_bias = lax.dynamic_slice_in_dim(qv_vector, width + (w % 2) * d, d)
    q = (pqk[:, :d] + q_bias).astype(BF)
    k = pqk[:, d:].astype(BF)
    f = (product(n1, Wf) + f_bias).astype(BF)
    Fv = Fv.reshape(nc * rows, 2 * d)
    first = jnp.where(w % 2 == 0, Fv[:, :d], Fv[:, d:])
    v = jnp.where(low, f, first)

    o, lse = attend(H, qpos, bias, q, k, v)

    part = product(o, w_out).astype(BF)
    pieces, spread = lax.optimization_barrier((w_up, cotangent[0], X))[:2]
    Wup = exchange(pieces.reshape(d, nw, width).transpose(1, 0, 2)).reshape(width, width)
    unswap = [(b, a) for a, b in swap]
    cot = lax.all_gather(lax.ppermute(spread, both, unswap), "wt", axis=0, tiled=True)
    vec = jnp.stack([out_vector, gain_b, shift_b, bias_up.astype(F32)] + [out_vector] * 4)
    mlp, mid_own, d_mid, d_o, g_up, g_down, g_out, vsums = middle(
        G, False, part, X.reshape(nc, rows, width), cot, o, Wup, w_down, w_out, vec
    )

    mlp = lax.psum_scatter(mlp, "wt", scatter_dimension=0, tiled=True)
    layer = (mid_own + mlp.astype(F32) + down_vector).astype(BF)
    layer = lax.ppermute(layer, both, swap)
    up_rows = exchange(g_up.reshape(nw, d, width)).transpose(1, 0, 2)
    s_up, s_down = lax.psum((up_rows.reshape(d, nw * width), g_down), "ctx")
    dqk, dv = attend_back(H, qpos, lift, q, k, v, o, d_o, lse)
    zero = jnp.zeros_like(dv)
    df = jnp.where(low, dv, zero)
    dn1 = product_right(dqk, Wqk) + product_right(df, Wf)
    dn1_low = dn1.astype(BF)
    blank = jnp.zeros_like(dv)
    left = jnp.where(w == 2, dv, blank)
    right = jnp.where(w == 3, dv, blank)
    total = scatter_sum(
        G, jnp.concatenate([dn1_low, left, right], axis=1).reshape(nc, rows, width + 2 * d)
    )
    grad_first = lax.ppermute(total[:, width:].astype(BF), both, swap).astype(F32)
    block = (w * G + m) * rows
    x_own = lax.dynamic_slice_in_dim(X, block, rows).astype(F32)
    _, pull_one = jax.vjp(lambda a: norm_rows(a, gain_a, shift_a), x_own)
    d_x = d_mid.astype(F32) + pull_one(total[:, :width])[0]
    grad_tokens = lax.ppermute(d_x.astype(BF), both, swap).astype(F32)

    g_qk = product_left(n1, dqk)
    g_f = product_left(n1, df)
    normal = centred * inverse
    g_gain_one = jnp.sum(dn1_low.astype(F32) * normal, axis=0)
    g_shift_one = jnp.sum(dn1_low.astype(F32), axis=0)
    cols = jnp.concatenate(
        [
            g_qk.astype(BF),
            g_f.astype(BF),
            g_gain_one[:, None].astype(BF),
            g_shift_one[:, None].astype(BF),
            jnp.zeros((width, 62), BF),
        ],
        axis=1,
    ).reshape(nw, d, 640)
    sums = jnp.concatenate(
        [jnp.sum(dqk.astype(F32), axis=0), jnp.sum(df.astype(F32), axis=0), jnp.zeros((64,), F32)]
    ).astype(BF)
    foot = jnp.concatenate([sums[None], jnp.zeros((7, 640), BF)], axis=0)
    pack = jnp.concatenate([cols, jnp.broadcast_to(foot[None], (nw, 8, 640))], axis=1)
    pack = exchange(pack)
    vecs = jnp.concatenate(
        [
            vsums[0],
            mine(vsums[1]),
            mine(vsums[2]),
            mine(vsums[3]),
            mine(vsums[4]),
        ]
    ).astype(BF)
    pack = pack.at[0, d + 1 : d + 4, :512].set(vecs.reshape(3, 512))
    pack, s_up, s_down = lax.optimization_barrier((pack, s_up, s_down))
    pack, s_out = lax.psum((pack, g_out), "ctx")
    body = pack[:, :d]
    s_qkv = jnp.concatenate(
        [body[a, :, e * d : (e + 1) * d] for e in (0, 1) for a in range(nw)]
        + [body[a, :, 2 * d : 3 * d] for a in range(2)],
        axis=1,
    ).astype(F32)
    s_gain_one = jnp.sum(body[:, :, 576].astype(F32), axis=0)
    s_shift_one = jnp.sum(body[:, :, 577].astype(F32), axis=0)
    ends = pack[:, d]
    bias_all = jnp.concatenate([ends[:, :d].reshape(-1), ends[:2, 2 * d : 3 * d].reshape(-1)])
    s_bias_qv = lax.dynamic_slice_in_dim(bias_all, w * nb, nb).astype(F32)
    vecs = pack[0, d + 1 : d + 4, :512].reshape(-1).astype(F32)
    s_bias_up = vecs[:width]
    s_bias_down, s_bias_out, s_gain_two, s_shift_two = [
        vecs[width + a * d : width + (a + 1) * d] for a in range(4)
    ]
    return (
        layer[None],
        grad_tokens[None],
        grad_first[None],
        s_qkv,
        s_bias_qv,
        s_out.astype(F32),
        s_bias_out,
        s_gain_one,
        s_shift_one,
        s_gain_two,
        s_shift_two,
        s_up.astype(F32),
        s_bias_up,
        s_down.astype(F32),
        s_bias_down,
    )


def solution(mesh):
    rows3 = P("wt", "ctx", None)
    mat = P("wt", None)
    vec = P("wt")
    in_specs = (rows3, rows3, rows3, P(), mat, vec, mat) + (vec,) * 5 + (mat, vec, mat, vec)
    out_specs = (
        (rows3, rows3, rows3, mat, vec, mat) + (vec,) * 5 + (mat, vec, mat, vec)
    )
    return jax.shard_map(
        functools.partial(on_device, mesh.shape["wt"], mesh.shape["ctx"]),
        mesh=mesh,
        in_specs=in_specs,
        out_specs=out_specs,
        check_vma=False,
    )
```

```python
import functools

import jax
import jax.numpy as jnp
from jax import lax
from jax.experimental import pallas as pl
from jax.experimental.pallas import tpu as pltpu
from jax.sharding import PartitionSpec as P

HEADS = 12
HEAD_DIM = 64
BLK = 128
CHUNK = 1024

EPS = 1e-05
SLOPE = 0.7978845608028654
CUBIC = 0.044715
NEG = -1e30

BF = jnp.bfloat16
F32 = jnp.float32
MESH = pl.DeviceIdType.MESH
ANY = pl.BlockSpec(memory_space=pl.ANY)
VM = pl.BlockSpec(memory_space=pltpu.VMEM)


def norm_rows(value, gain, shift):
    mean = jnp.mean(value, axis=-1, keepdims=True)
    centred = value - mean
    inverse = lax.rsqrt(jnp.mean(centred * centred, axis=-1, keepdims=True) + EPS)
    return centred * inverse * gain + shift


def gelu_tanh(value):
    return 0.5 * value * (1.0 + jnp.tanh(SLOPE * (value + CUBIC * value * value * value)))


def product(left, right):
    return jnp.dot(left, right, preferred_element_type=F32)


def product_left(left, right):
    return lax.dot_general(left, right, (((0,), (0,)), ((), ())), preferred_element_type=F32)


def product_right(left, right):
    return lax.dot_general(left, right, (((1,), (1,)), ((), ())), preferred_element_type=F32)


def dealt_blocks(deal):
    count = deal.shape[0] * 2
    pairs = jnp.repeat(deal, 2)
    parity = jnp.arange(count, dtype=jnp.int32) % 2
    return jnp.where(parity == 0, pairs, count - 1 - pairs)


def remote(src, dst, send, recv, device):
    return pltpu.make_async_remote_copy(
        src_ref=src,
        dst_ref=dst,
        send_sem=send,
        recv_sem=recv,
        device_id=device,
        device_id_type=MESH,
    )


def greet(peers):
    barrier = pltpu.get_barrier_semaphore()
    for peer in peers:
        pl.semaphore_signal(barrier, inc=1, device_id=peer, device_id_type=MESH)
    pl.semaphore_wait(barrier, len(peers))


def gather_kernel(
    nw, G, x, first, wqk, wf, small, X, Fv, WQK, WF, SM, rx, rf, rw, rv, rs, sa, sx, sfa, sfx, sw, loc
):
    w = lax.axis_index("wt")
    c = lax.axis_index("ctx")
    g = c // G
    m = c % G
    nc = nw * G
    core = w + 1 - 2 * (w % 2)
    other = (w + 2) % nw
    rel = lambda k: (w + k) % nw
    peers = [(rel(k), c) for k in range(1, nw)]
    peers += [(w, ((g + k) % nw) * G + m) for k in range(1, nw)]
    peers += [(w, g * G + (m + k) % G) for k in range(1, G)]
    greet(peers)
    seq = 2 * (g % 2) + g // 2
    goal = (2 * (w % 2) + w // 2) * G + m
    is_a = w == seq
    primary = (w + seq) % 2 == 0
    high = w >= 2
    copies = []

    to_head = remote(x, X.at[c], sa.at[0], rx.at[c], (w, goal))
    to_head_f = remote(first, Fv.at[c], sa.at[1], rf.at[c], (w, goal))
    own_x = pltpu.make_async_copy(x, X.at[c], rx.at[c])
    own_f = pltpu.make_async_copy(first, Fv.at[c], rf.at[c])

    @pl.when(is_a)
    def _():
        own_x.start()
        own_f.start()

    @pl.when(jnp.logical_not(is_a))
    def _():
        to_head.start()
        to_head_f.start()

    own_w = pltpu.make_async_copy(wqk.at[w], WQK.at[w], loc.at[0])
    own_s = pltpu.make_async_copy(small, SM.at[w], loc.at[1])
    own_w.start()
    own_s.start()
    own_v = pltpu.make_async_copy(wf.at[w % 2], WF.at[w], loc.at[2])
    own_v.start()
    sends_w, sends_v, sends_s = [], [], []
    for k in range(1, nw):
        d = rel(k)
        s = remote(small, SM.at[w], sw.at[k, 0], rs.at[w], (d, c))
        s.start()
        q = remote(wqk.at[d], WQK.at[w], sw.at[k, 1], rw.at[w], (d, c))
        q.start()
        v = remote(wf.at[d % 2], WF.at[w], sw.at[k, 2], rv.at[w], (d, c))
        sends_w += [s, q]
        sends_v.append((d, v))

        @pl.when(d < 2)
        def _():
            v.start()

    def block_x(b):
        return pltpu.make_async_copy(X.at[b], X.at[b], rx.at[b])

    def block_f(b):
        return pltpu.make_async_copy(Fv.at[b], Fv.at[b], rf.at[b])

    fwd_core, fwd_other, fwd_member = [], [], []
    for k in range(nw):
        gp = (g + k) % nw
        b = gp * G + m
        to_core = remote(X.at[b], X.at[b], sx.at[0, b], rx.at[b], (core, c))
        to_other = remote(X.at[b], X.at[b], sx.at[1, b], rx.at[b], (other, c))
        to_core_f = remote(Fv.at[b], Fv.at[b], sfx.at[0, b], rf.at[b], (core, c))
        to_other_f = remote(Fv.at[b], Fv.at[b], sfx.at[1, b], rf.at[b], (other, c))
        members = [
            remote(X.at[b], X.at[b], sx.at[1 + e, b], rx.at[b], (w, g * G + (m + e) % G))
            for e in range(1, G)
        ]
        members_f = [
            remote(Fv.at[b], Fv.at[b], sfx.at[1 + e, b], rf.at[b], (w, g * G + (m + e) % G))
            for e in range(1, G)
        ]

        @pl.when(primary)
        def _():
            block_x(b).wait()

            @pl.when(is_a)
            def _():
                to_other.start()

            for r in members:
                r.start()
            to_core.start()

        @pl.when(jnp.logical_and(is_a, jnp.logical_not(high)))
        def _():
            block_f(b).wait()
            to_other_f.start()

        @pl.when(jnp.logical_and(primary, high))
        def _():
            block_f(b).wait()
            for r in members_f:
                r.start()
            to_core_f.start()

        fwd_core.append((to_core, to_core_f))
        fwd_other.append((to_other, to_other_f))
        fwd_member.append((members, members_f))
    for e in range(1, G):
        for k in range(nw):
            b = ((g + k) % nw) * G + (m + e) % G
            to_core = remote(X.at[b], X.at[b], sx.at[0, b], rx.at[b], (core, c))
            to_core_f = remote(Fv.at[b], Fv.at[b], sfx.at[0, b], rf.at[b], (core, c))

            @pl.when(primary)
            def _():
                block_x(b).wait()
                to_core.start()

            @pl.when(jnp.logical_and(primary, high))
            def _():
                block_f(b).wait()
                to_core_f.start()

            fwd_core.append((to_core, to_core_f))

    @pl.when(jnp.logical_not(primary))
    def _():
        for b in range(nc):
            block_x(b).wait()

        @pl.when(high)
        def _():
            for b in range(nc):
                block_f(b).wait()

    own_w.wait()
    own_s.wait()
    own_v.wait()
    for k in range(1, nw):
        src = (w + nw - k) % nw
        pltpu.make_async_copy(wqk.at[0], WQK.at[src], rw.at[src]).wait()
        pltpu.make_async_copy(small, SM.at[src], rs.at[src]).wait()

        @pl.when(w < 2)
        def _():
            pltpu.make_async_copy(wf.at[0], WF.at[src], rv.at[src]).wait()

    for s in sends_w:
        s.wait_send()
    for d, v in sends_v:

        @pl.when(d < 2)
        def _():
            v.wait_send()

    @pl.when(jnp.logical_not(is_a))
    def _():
        to_head.wait_send()
        to_head_f.wait_send()

    @pl.when(primary)
    def _():
        for a, _f in fwd_core:
            a.wait_send()
        for ms, _f in fwd_member:
            for a in ms:
                a.wait_send()

        @pl.when(high)
        def _():
            for _x, a in fwd_core:
                a.wait_send()
            for _x, ms in fwd_member:
                for a in ms:
                    a.wait_send()

    @pl.when(is_a)
    def _():
        for a, _f in fwd_other:
            a.wait_send()

        @pl.when(jnp.logical_not(high))
        def _():
            for _x, a in fwd_other:
                a.wait_send()


def gather(nw, G, x, first, wqk, wf, small):
    nc = nw * G
    rows, width = x.shape
    half = first.shape[1]
    d = width // nw
    dma = pltpu.SemaphoreType.DMA
    return pl.pallas_call(
        functools.partial(gather_kernel, nw, G),
        name="gather_tokens",
        out_shape=(
            jax.ShapeDtypeStruct((nc, rows, width), BF),
            jax.ShapeDtypeStruct((nc, rows, half), BF),
            jax.ShapeDtypeStruct((nw, d, 2 * d), BF),
            jax.ShapeDtypeStruct((nw, d, d), BF),
            jax.ShapeDtypeStruct((nw,) + small.shape, BF),
        ),
        in_specs=[ANY] * 5,
        out_specs=[ANY] * 5,
        scratch_shapes=[
            dma((nc,)),
            dma((nc,)),
            dma((nw,)),
            dma((nw,)),
            dma((nw,)),
            dma((2,)),
            dma((1 + G, nc)),
            dma((2,)),
            dma((1 + G, nc)),
            dma((nw, 3)),
            dma((3,)),
        ],
        compiler_params=pltpu.CompilerParams(collective_id=0, has_side_effects=True),
    )(x, first, wqk, wf, small)


def middle_kernel(
    T, G, crossed, p_hbm, X_hbm, cot_hbm, o_hbm, wup_hbm, wdn_hbm, wout_hbm, vec_hbm,
    mlp, mid_own, dmid_own, do_out, gup, gdn, gout, sums,
    p, x, cot, o, wup, wdn, wout, vec,
    b1, ab, b2, bs, mid, n2s, act, dus, q, b4, ab2, b5, dn, dbs,
    s1, r1, s2, r2, s3, r3, s4, r4, s5, r5, s6, r6, ld,
):
    w = lax.axis_index("wt")
    c = lax.axis_index("ctx")
    g = c // G
    m = c % G
    core = (w + 1 - 2 * (w % 2), c)
    other = ((w + 2) % 4, c)
    mine = w % 2
    theirs = 1 - mine
    rows = p.shape[0]
    half = rows // 2
    n = half // T
    R = rows // 4
    loads = [
        pltpu.make_async_copy(p_hbm, p, ld.at[0]),
        pltpu.make_async_copy(vec_hbm, vec, ld.at[1]),
    ]
    loads += [
        pltpu.make_async_copy(X_hbm.at[a * G + m], x.at[pl.ds(a * R, R)], ld.at[2 + a])
        for a in range(4)
    ]
    loads += [
        pltpu.make_async_copy(wup_hbm, wup, ld.at[6]),
        pltpu.make_async_copy(wdn_hbm, wdn, ld.at[7]),
        pltpu.make_async_copy(cot_hbm, cot, ld.at[8]),
        pltpu.make_async_copy(wout_hbm, wout, ld.at[9]),
        pltpu.make_async_copy(o_hbm, o, ld.at[10]),
    ]
    for copy in loads:
        copy.start()
    greet([core, other])

    def rs(base, t):
        return pl.ds(pl.multiple_of(base * half + t * n, n), n)

    loads[0].wait()
    first = []
    for t in range(T):
        r = remote(p.at[rs(theirs, t)], b1.at[t], s1.at[t], r1.at[t], core)
        r.start()
        first.append(r)
    second = []
    for t in range(T):
        first[t].wait_recv()
        ab[t] = (p[rs(mine, t), :].astype(F32) + b1[t].astype(F32)).astype(BF)
        r = remote(ab.at[t], b2.at[t], s2.at[t], r2.at[t], other)
        r.start()
        second.append(r)
    for copy in loads[1:]:
        copy.wait()
    out_b = vec[0:1, :]
    gain = vec[1:2, :]
    shift = vec[2:3, :]
    up_b = vec[3:4, :]
    sums[...] = jnp.zeros_like(sums)

    def two(ref, t):
        return jnp.concatenate([ref[rs(mine, t), :], ref[rs(theirs, t), :]], axis=0)

    def put(ref, t, value):
        ref[rs(mine, t), :] = value[:n]
        ref[rs(theirs, t), :] = value[n:]

    def add_sum(at, value):
        sums[at : at + 1, :] += jnp.sum(value, axis=0, keepdims=True)

    def chain(t):
        pltpu.make_async_copy(b4.at[t], b4.at[t], r4.at[t]).wait()
        ab2[t] = (q[rs(mine, t), :].astype(F32) + b4[t].astype(F32)).astype(BF)
        remote(ab2.at[t], b5.at[t], s5.at[t], r5.at[t], other).start()

    def forward(t, carry):
        pltpu.make_async_copy(b2.at[t], b2.at[t], r2.at[t]).wait()
        bs[rs(mine, t), :] = (ab[t].astype(F32) + b2[t].astype(F32)).astype(BF)
        remote(bs.at[rs(mine, t)], bs.at[rs(mine, t)], s3.at[t], r3.at[t], core).start()

        @pl.when(t > 0)
        def _():
            chain(t - 1)

        pltpu.make_async_copy(bs.at[rs(theirs, t)], bs.at[rs(theirs, t)], r3.at[t]).wait()
        value = two(x, t).astype(F32) + two(bs, t).astype(F32) + out_b
        put(mid, t, value)
        centred = value - jnp.mean(value, axis=-1, keepdims=True)
        inverse = lax.rsqrt(jnp.mean(centred * centred, axis=-1, keepdims=True) + EPS)
        n2 = (centred * inverse * gain + shift).astype(BF)
        put(n2s, t, n2)
        u = product(n2, wup[...]) + up_b
        th = jnp.tanh(SLOPE * (u + CUBIC * u * u * u))
        a = (0.5 * u * (1.0 + th)).astype(BF)
        slope = 0.5 * (1.0 + th) + 0.5 * u * (1.0 - th * th) * SLOPE * (1.0 + 3.0 * CUBIC * u * u)
        put(act, t, a)
        ct = two(cot, t)
        du = (product_right(ct, wdn[...]) * slope).astype(BF)
        put(dus, t, du)
        put(q, t, product_right(du, wup[...]).astype(BF))
        remote(q.at[rs(theirs, t)], b4.at[t], s4.at[t], r4.at[t], core).start()
        put(mlp, t, product(a, wdn[...]).astype(BF))
        add_sum(0, du.astype(F32))
        add_sum(1, ct.astype(F32))
        return carry

    lax.fori_loop(0, T, forward, 0)
    chain(T - 1)

    width = p.shape[1]
    tile = 256

    def grads(i, carry):
        at = pl.ds(pl.multiple_of(i * tile, tile), tile)
        gup[at, :] = product_left(n2s[:, at], dus[...]).astype(BF)
        gdn[at, :] = product_left(act[:, at], cot[...]).astype(BF)
        return carry

    lax.fori_loop(0, width // tile, grads, 0)
    def backward(t, carry):
        pltpu.make_async_copy(b5.at[t], b5.at[t], r5.at[t]).wait()
        dn[rs(mine, t), :] = (ab2[t].astype(F32) + b5[t].astype(F32)).astype(BF)
        remote(dn.at[rs(mine, t)], dn.at[rs(mine, t)], s6.at[t], r6.at[t], core).start()
        pltpu.make_async_copy(dn.at[rs(theirs, t)], dn.at[rs(theirs, t)], r6.at[t]).wait()
        value = two(mid, t)
        centred = value - jnp.mean(value, axis=-1, keepdims=True)
        inverse = lax.rsqrt(jnp.mean(centred * centred, axis=-1, keepdims=True) + EPS)
        normal = centred * inverse
        dn2 = two(dn, t).astype(F32)
        add_sum(3, dn2 * normal)
        add_sum(4, dn2)
        dx = dn2 * gain
        dx = dx - jnp.mean(dx, axis=-1, keepdims=True) - normal * jnp.mean(
            dx * normal, axis=-1, keepdims=True
        )
        dmid = two(cot, t).astype(F32) + inverse * dx
        db = dmid.astype(BF)
        put(dbs, t, db)
        add_sum(2, db.astype(F32))
        put(do_out, t, product_right(db, wout[...]).astype(BF))
        return carry

    lax.fori_loop(0, T, backward, 0)
    gout[...] = product_left(o[...], dbs[...]).astype(BF)
    block_at = 2 * (w % 2) + w // 2 if crossed else w
    own = pl.ds(pl.multiple_of(block_at * R, R), R)
    mid_own[...] = mid[own, :]
    dmid_own[...] = dbs[own, :]
    for t in range(T):
        first[t].wait_send()
        second[t].wait_send()
        remote(bs.at[rs(mine, t)], bs.at[rs(mine, t)], s3.at[t], r3.at[t], core).wait_send()
        remote(q.at[rs(theirs, t)], b4.at[t], s4.at[t], r4.at[t], core).wait_send()
        remote(ab2.at[t], b5.at[t], s5.at[t], r5.at[t], other).wait_send()
        remote(dn.at[rs(mine, t)], dn.at[rs(mine, t)], s6.at[t], r6.at[t], core).wait_send()


def middle(G, crossed, p, X, cot, o, wup, wdn, wout, vec):
    T = 4
    rows, width = p.shape
    n = rows // 2 // T
    R = rows // 4
    d = o.shape[1]
    dma = pltpu.SemaphoreType.DMA
    full = pltpu.VMEM((rows, width), BF)
    part = pltpu.VMEM((T, n, width), BF)
    square = pltpu.VMEM((width, width), BF)
    return pl.pallas_call(
        functools.partial(middle_kernel, T, G, crossed),
        name="middle",
        out_shape=(
            jax.ShapeDtypeStruct((rows, width), BF),
            jax.ShapeDtypeStruct((R, width), F32),
            jax.ShapeDtypeStruct((R, width), BF),
            jax.ShapeDtypeStruct((rows, d), BF),
            jax.ShapeDtypeStruct((width, width), BF),
            jax.ShapeDtypeStruct((width, width), BF),
            jax.ShapeDtypeStruct((d, width), BF),
            jax.ShapeDtypeStruct((8, width), F32),
        ),
        in_specs=[ANY] * 8,
        out_specs=[VM] * 8,
        scratch_shapes=[
            full, full, full, pltpu.VMEM((rows, d), BF), square, square,
            pltpu.VMEM((d, width), BF), pltpu.VMEM((8, width), F32),
            part, part, part, full, pltpu.VMEM((rows, width), F32), full, full, full, full,
            part, part, part, full, full,
        ]
        + [dma((T,))] * 12
        + [dma((11,))],
        compiler_params=pltpu.CompilerParams(
            collective_id=1, has_side_effects=True, vmem_limit_bytes=62 << 20
        ),
        cost_estimate=pl.CostEstimate(
            flops=14 * rows * width * width, bytes_accessed=40 << 20, transcendentals=rows * width
        ),
    )(p, X, cot, o, wup, wdn, wout, vec)


def scatter_kernel(G, D, out, b1, ab, b2, st, b3, s1, r1, s2, r2, s3, r3):
    w = lax.axis_index("wt")
    c = lax.axis_index("ctx")
    g = c // G
    m = c % G
    core = w + 1 - 2 * (w % 2)
    other = (w + 2) % 4
    par = w % 2
    hi = w // 2
    greet([(core, c), (other, c)] + [(w, g * G + (m + e) % G) for e in range(1, G)])
    order = [e for e in range(1, G)] + [0]
    firsts = {}
    for j in (1, 0):
        for e in order:
            jj = (hi + j) % 2
            mm = (m + e) % G
            b = (2 * jj + 1 - par) * G + mm
            slot = jj * G + mm
            r = remote(D.at[b], b1.at[slot], s1.at[slot], r1.at[slot], (core, c))
            r.start()
            firsts[(j, e)] = r

    def arrived1(slot):
        pltpu.make_async_copy(b1.at[slot], b1.at[slot], r1.at[slot]).wait()

    seconds = []
    for e in order:
        jj = 1 - hi
        mm = (m + e) % G
        slot = jj * G + mm
        arrived1(slot)
        ab[mm] = (D[(2 * jj + par) * G + mm].astype(F32) + b1[slot].astype(F32)).astype(BF)
        r = remote(ab.at[mm], b2.at[mm], s2.at[mm], r2.at[mm], (other, c))
        r.start()
        seconds.append(r)
    thirds = []
    for e in order:
        mm = (m + e) % G
        slot = hi * G + mm
        arrived1(slot)
        pltpu.make_async_copy(b2.at[mm], b2.at[mm], r2.at[mm]).wait()
        total = D[w * G + mm].astype(F32) + b1[slot].astype(F32) + b2[mm].astype(F32)
        if e == 0:
            for f in range(1, G):
                q = (m + f) % G
                pltpu.make_async_copy(b3.at[q], b3.at[q], r3.at[q]).wait()
                total = total + b3[q].astype(F32)
            out[...] = total.astype(out.dtype)
        else:
            st[mm] = total.astype(BF)
            r = remote(st.at[mm], b3.at[m], s3.at[mm], r3.at[m], (w, g * G + mm))
            r.start()
            thirds.append(r)
    for r in list(firsts.values()) + seconds + thirds:
        r.wait_send()


def scatter_sum(G, D):
    nc, rows, C = D.shape
    dma = pltpu.SemaphoreType.DMA
    return pl.pallas_call(
        functools.partial(scatter_kernel, G),
        name="scatter_sum",
        out_shape=jax.ShapeDtypeStruct((rows, C), F32),
        in_specs=[VM],
        out_specs=VM,
        scratch_shapes=[
            pltpu.VMEM((2 * G, rows, C), BF),
            pltpu.VMEM((G, rows, C), BF),
            pltpu.VMEM((G, rows, C), BF),
            pltpu.VMEM((G, rows, C), BF),
            pltpu.VMEM((G, rows, C), BF),
            dma((2 * G,)),
            dma((2 * G,)),
            dma((G,)),
            dma((G,)),
            dma((G,)),
            dma((G,)),
        ],
        compiler_params=pltpu.CompilerParams(
            collective_id=3, has_side_effects=True, vmem_limit_bytes=60 << 20
        ),
    )(D)


def head_mask(shape, h):
    lane = lax.broadcasted_iota(jnp.int32, shape, 1)
    return jnp.logical_and(lane >= h * HEAD_DIM, lane < (h + 1) * HEAD_DIM)


def split_heads(H, value):
    zero = jnp.zeros_like(value)
    return [jnp.where(head_mask(value.shape, h), value, zero) for h in range(H)]


def spread(H, shape, values):
    out = jnp.broadcast_to(values[H - 1], shape)
    for h in range(H - 2, -1, -1):
        out = jnp.where(head_mask(shape, h), values[h], out)
    return out


def attend_tile(H, q, k_ref, v_ref, bias_ref, at_bias, chunks=None):
    rows, width = q.shape
    N = k_ref.shape[0]
    step_keys = min(N, 1024)
    qh = split_heads(H, q * jnp.asarray(HEAD_DIM**-0.5, BF))
    top_half = lax.broadcasted_iota(jnp.int32, (rows, 1), 0) < BLK

    def step(j, carry):
        tops, sums, acc = carry
        at = pl.ds(pl.multiple_of(j * step_keys, step_keys), step_keys)
        kc = k_ref[at, :]
        vc = v_ref[at, :]
        low = bias_ref[at_bias, :, at]
        high = bias_ref[at_bias + 1, :, at]
        new_tops, new_sums, shrink, parts = [], [], [], []
        for h in range(H):
            s = product_right(qh[h], kc)
            s = jnp.concatenate([s[:BLK] + low, s[BLK:] + high], axis=0)
            top = jnp.maximum(tops[h], jnp.max(s, axis=1, keepdims=True))
            a = jnp.exp(tops[h] - top)
            p = jnp.exp(s - top)
            new_sums.append(sums[h] * a + jnp.sum(p, axis=1, keepdims=True))
            new_tops.append(top)
            shrink.append(a)
            parts.append(product(p.astype(BF), vc))
        acc = acc * spread(H, acc.shape, shrink) + spread(H, acc.shape, parts)
        return new_tops, new_sums, acc

    start = (
        [jnp.full((rows, 1), NEG, F32)] * H,
        [jnp.zeros((rows, 1), F32)] * H,
        jnp.zeros((rows, width), F32),
    )
    chunks = N // step_keys if chunks is None else chunks
    tops, sums, acc = lax.fori_loop(0, chunks, step, start)
    out = (acc / spread(H, acc.shape, sums)).astype(BF)
    lse = []
    for h in range(H):
        column = tops[h] + jnp.log(sums[h])
        lse.append(jnp.transpose(jnp.broadcast_to(column, (rows, BLK)))[0:1, :])
    lse = jnp.concatenate(lse + [jnp.zeros((8 - H, rows), F32)], axis=0)
    return out, lse


def attend_kernel(H, qpos, q_ref, k_ref, v_ref, bias_ref, o_ref, lse_ref):
    o, lse = attend_tile(H, q_ref[...], k_ref, v_ref, bias_ref, 2 * pl.program_id(0))
    o_ref[...] = o
    lse_ref[0] = lse


def attend(H, qpos, bias, q, k, v):
    n = qpos.shape[0]
    width = H * HEAD_DIM
    N = k.shape[0]
    rows = 2 * BLK
    whole = pl.BlockSpec((N, width), lambda i, *_: (0, 0))
    return pl.pallas_call(
        functools.partial(attend_kernel, H),
        name="attend",
        out_shape=(
            jax.ShapeDtypeStruct((n * rows, width), BF),
            jax.ShapeDtypeStruct((n, 8, rows), F32),
        ),
        grid_spec=pltpu.PrefetchScalarGridSpec(
            num_scalar_prefetch=1,
            grid=(n,),
            in_specs=[
                pl.BlockSpec((rows, width), lambda i, qp: (qp[i], 0)),
                whole,
                whole,
                pl.BlockSpec((2 * n, 1, N), lambda i, *_: (0, 0, 0)),
            ],
            out_specs=[
                pl.BlockSpec((rows, width), lambda i, *_: (i, 0)),
                pl.BlockSpec((1, 8, rows), lambda i, *_: (i, 0, 0)),
            ],
        ),
        compiler_params=pltpu.CompilerParams(vmem_limit_bytes=48 << 20),
    )(qpos, q, k, v, bias)


def attend_back_tile(
    H, q, do, o, lse, k_ref, v_ref, kt, dk, dv, lift_ref, tile, chunks=None, poll=None
):
    rows, width = q.shape
    N = k_ref.shape[0]
    scale = HEAD_DIM**-0.5
    qh = split_heads(H, q * jnp.asarray(scale, BF))
    doh = split_heads(H, do)
    qcat = jnp.concatenate(qh, axis=0)
    docat = jnp.concatenate(doh, axis=0)
    pick = lax.broadcasted_iota(jnp.int32, (8, width), 1)
    base = lax.broadcasted_iota(jnp.int32, (8, width), 0) * HEAD_DIM
    pick = jnp.logical_and(pick >= base, pick < base + HEAD_DIM).astype(F32)
    delta = lax.dot_general(
        pick,
        do.astype(F32) * o.astype(F32),
        (((1,), (1,)), ((), ())),
        precision=lax.Precision.HIGHEST,
        preferred_element_type=F32,
    )

    def step(j, dqt):
        at = pl.ds(pl.multiple_of(j * CHUNK, CHUNK), CHUNK)
        kc = k_ref[at, :]
        vc = v_ref[at, :]
        ps, dss, dqs = [], [], []
        for h in range(H):
            s = product_right(kc, qh[h])
            dp = product_right(vc, doh[h])
            pieces, dpieces = [], []
            for b in range(CHUNK // BLK):
                lift = lift_ref[tile, pl.ds(j * (CHUNK // BLK) + b, 1), :]
                cut = slice(b * BLK, (b + 1) * BLK)
                p = jnp.exp(s[cut] - (lse[h : h + 1, :] + lift))
                pieces.append(p.astype(BF))
                dpieces.append((p * (dp[cut] - delta[h : h + 1, :])).astype(BF))
            p = jnp.concatenate(pieces, axis=0)
            ds = jnp.concatenate(dpieces, axis=0)
            ps.append(p)
            dss.append(ds)
            dqs.append(product(kt[h * HEAD_DIM : (h + 1) * HEAD_DIM, at], ds))
        dv[at, :] += product(jnp.concatenate(ps, axis=1), docat)
        dk[at, :] += product(jnp.concatenate(dss, axis=1), qcat)
        if poll is not None:
            poll(j)
        return dqt + jnp.concatenate(dqs, axis=0)

    chunks = N // CHUNK if chunks is None else chunks
    dqt = lax.fori_loop(0, chunks, step, jnp.zeros((width, rows), F32))
    return dqt * scale


def flip_rows(src, dst):
    def flip(b, carry):
        at = pl.ds(pl.multiple_of(b * BLK, BLK), BLK)
        dst[:, at] = jnp.transpose(src[at, :])
        return carry

    lax.fori_loop(0, src.shape[0] // BLK, flip, 0)


def attend_back_kernel(
    H, qpos, q_ref, k_ref, v_ref, o_ref, do_ref, lse_ref, lift_ref, dqk_ref, dv_ref, kt, dk, dv
):
    i = pl.program_id(0)
    width = H * HEAD_DIM

    @pl.when(i == 0)
    def _():
        flip_rows(k_ref, kt)
        dk[...] = jnp.zeros_like(dk)
        dv[...] = jnp.zeros_like(dv)
        dqk_ref[...] = jnp.zeros_like(dqk_ref)

    dqt = attend_back_tile(
        H, q_ref[...], do_ref[...], o_ref[...], lse_ref[0], k_ref, v_ref, kt, dk, dv, lift_ref, i
    )
    rows = 2 * BLK
    here = pl.ds(pl.multiple_of(qpos[i] * rows, rows), rows)
    dqk_ref[here, 0:width] = jnp.transpose(dqt).astype(BF)

    @pl.when(i == pl.num_programs(0) - 1)
    def _():
        dqk_ref[:, width : 2 * width] = dk[...].astype(BF)
        dv_ref[...] = dv[...].astype(BF)


def attend_back(H, qpos, lift, q, k, v, o, do, lse):
    n = qpos.shape[0]
    width = H * HEAD_DIM
    N = k.shape[0]
    rows = 2 * BLK
    whole = pl.BlockSpec((N, width), lambda i, *_: (0, 0))
    row = pl.BlockSpec((rows, width), lambda i, *_: (i, 0))
    return pl.pallas_call(
        functools.partial(attend_back_kernel, H),
        name="attend_back",
        out_shape=(
            jax.ShapeDtypeStruct((N, 2 * width), BF),
            jax.ShapeDtypeStruct((N, width), BF),
        ),
        grid_spec=pltpu.PrefetchScalarGridSpec(
            num_scalar_prefetch=1,
            grid=(n,),
            in_specs=[
                pl.BlockSpec((rows, width), lambda i, qp: (qp[i], 0)),
                whole,
                whole,
                row,
                row,
                pl.BlockSpec((1, 8, rows), lambda i, *_: (i, 0, 0)),
                pl.BlockSpec((n, N // BLK, rows), lambda i, *_: (0, 0, 0)),
            ],
            out_specs=[
                pl.BlockSpec((N, 2 * width), lambda i, *_: (0, 0)),
                pl.BlockSpec((N, width), lambda i, *_: (0, 0)),
            ],
            scratch_shapes=[
                pltpu.VMEM((width, N), BF),
                pltpu.VMEM((N, width), F32),
                pltpu.VMEM((N, width), F32),
            ],
        ),
        compiler_params=pltpu.CompilerParams(vmem_limit_bytes=60 << 20),
    )(qpos, q, k, v, o, do, lse, lift)


def head_kernel(
    G, H,
    deal, x_h, first_h, wqkv_h, small_h, cot_h, wup_h, wout_h,
    X_o, xh_o, k_o, v_o, wup_o, cot_o, q, o, lse, part, wqk, wf, vec,
    X, Fv, xh, k, v, small, vq, bias, wout, wl, wqk_h, wf_h, Y,
    rx, rf, rw, rv, rs, rc, ru, sh, sx, sf, sw, sc, su, loc, out, ry, sy,
):
    nw = 4
    w = lax.axis_index("wt")
    c = lax.axis_index("ctx")
    g = c // G
    m = c % G
    nc = nw * G
    R, width = x_h.shape
    d = width // nw
    par = w % 2
    core = (w + 1 - 2 * par, c)
    seq = 2 * (g % 2) + g // 2
    og = 2 * par + w // 2
    goal = og * G + m
    two = (w + 2) % nw
    goal_two = (2 * par + two // 2) * G + m
    is_a = w == seq
    primary = (w + seq) % 2 == 0
    high = w >= 2
    low = w < 2
    peers = [
        ((w + a) % nw, ((g + e) % nw) * G + m) for a in range(nw) for e in range(nw) if a or e
    ]
    peers += [(w, g * G + (m + e) % G) for e in range(1, G)]
    loads = [
        pltpu.make_async_copy(a, b, loc.at[i])
        for i, (a, b) in enumerate(((wqkv_h, wl), (wout_h, wout)))
    ]
    for copy in loads:
        copy.start()
    greet(peers)

    here = goal == c
    here_two = goal_two == c
    to_y = remote(x_h, Y, sh.at[0], ry.at[0], (two, c))
    to_one = remote(x_h, X.at[c], sh.at[1], rx.at[c], (w, goal))
    to_two = remote(Y, X.at[c], sh.at[4], rx.at[c], (w, goal_two))
    to_first = remote(first_h, Fv.at[c], sh.at[2], rf.at[c], (w, goal))
    home_cot = jnp.logical_and(here, is_a)
    own_cot = pl.ds(pl.multiple_of(g * R, R), R)
    to_cot = remote(cot_h, cot_o.at[own_cot], sh.at[3], rc.at[g], (seq, goal))
    to_y.start()

    @pl.when(here)
    def _():
        pltpu.make_async_copy(x_h, X.at[c], rx.at[c]).start()
        pltpu.make_async_copy(first_h, Fv.at[c], rf.at[c]).start()

    @pl.when(jnp.logical_not(here))
    def _():
        to_one.start()
        to_first.start()

    loads[0].wait()
    for a in range(nw):
        for half in range(2):
            at = half * width + a * d
            wqk_h[a, :, half * d : (half + 1) * d] = wl[:, at : at + d]
    for a in range(2):
        at = 2 * width + a * d
        wf_h[a] = wl[:, at : at + d]

    def rows_of(a):
        return pl.ds(pl.multiple_of(a * d, 16), d)

    weights, fresh = [], []
    for e in range(1, nw):
        to = (w + e) % nw
        weights.append(remote(small_h, small.at[w], sw.at[e, 0], rs.at[w], (to, c)))
        weights.append(remote(wqk_h.at[to], wqk.at[rows_of(w)], sw.at[e, 1], rw.at[w], (to, c)))
        fresh.append(
            (to, remote(wf_h.at[to % 2], wf.at[rows_of(w)], sw.at[e, 2], rv.at[w], (to, c)))
        )
    for r in weights:
        r.start()
    for to, r in fresh:

        @pl.when(to < 2)
        def _():
            r.start()

    pltpu.make_async_copy(small_h, small.at[w], rs.at[w]).start()
    pltpu.make_async_copy(wqk_h.at[w], wqk.at[rows_of(w)], rw.at[w]).start()

    @pl.when(low)
    def _():
        pltpu.make_async_copy(wf_h.at[par], wf.at[rows_of(w)], rv.at[w]).start()

    @pl.when(high)
    def _():
        wf[...] = jnp.zeros_like(wf)

    def got(ref, sem):
        pltpu.make_async_copy(ref, ref, sem).wait()

    got(Y, ry.at[0])

    @pl.when(here_two)
    def _():
        pltpu.make_async_copy(Y, X.at[c], rx.at[c]).start()

    @pl.when(jnp.logical_not(here_two))
    def _():
        to_two.start()

    def core_x(b):
        return remote(X.at[b], X.at[b], sx.at[0, b], rx.at[b], core)

    def core_f(b):
        return remote(Fv.at[b], Fv.at[b], sf.at[0, b], rf.at[b], core)

    def member_x(b, e):
        return remote(X.at[b], X.at[b], sx.at[e, b], rx.at[b], (w, g * G + (m + e) % G))

    def member_f(b, e):
        return remote(Fv.at[b], Fv.at[b], sf.at[e, b], rf.at[b], (w, g * G + (m + e) % G))

    def cross_f(b):
        return remote(Fv.at[b], Fv.at[b], sy.at[b], rf.at[b], (two, c))

    crossing = jnp.logical_and(is_a, low)

    def take(b, onward):
        got(X.at[b], rx.at[b])

        if onward:

            @pl.when(crossing)
            def _():
                got(Fv.at[b], rf.at[b])
                cross_f(b).start()

        @pl.when(primary)
        def _():
            for e in range(1, G if onward else 1):
                member_x(b, e).start()
            core_x(b).start()

        @pl.when(high)
        def _():
            got(Fv.at[b], rf.at[b])

            @pl.when(primary)
            def _():
                for e in range(1, G if onward else 1):
                    member_f(b, e).start()
                core_f(b).start()

    half_rows = nc * R // 2

    def halves(ref, b, gap, value):
        ref[pl.ds(pl.multiple_of(b * BLK, BLK), BLK), :] = value[:BLK]
        ref[pl.ds(pl.multiple_of(b * BLK + gap, BLK), BLK), :] = value[BLK:]

    def project(b, a):
        at = pl.ds(pl.multiple_of(b * R, R), R)
        value = X[b].astype(F32)
        centred = value - jnp.mean(value, axis=-1, keepdims=True)
        inverse = lax.rsqrt(jnp.mean(centred * centred, axis=-1, keepdims=True) + EPS)
        normal = centred * inverse
        xh[at, :] = normal.astype(BF)
        n = (normal * vec[4:5, :] + vec[5:6, :]).astype(BF)
        qk = product(n, wqk[...])
        halves(k, b, half_rows, qk[:, d : 2 * d].astype(BF))
        if a is not None:
            halves(q, a, 2 * R, (qk[:, :d] + vq[1:2, 0:d]).astype(BF))

        @pl.when(low)
        def _():
            halves(v, b, half_rows, (product(n, wf[...]) + vq[2:3, 0:d]).astype(BF))

        @pl.when(high)
        def _():
            f = Fv[b]
            halves(v, b, half_rows, jnp.where(par == 0, f[:, :d], f[:, d:]))

    for t in range(nw):
        for e in range(2):
            own_pair = deal[(2 * (t % 2) + e) * G + m]
            for b in range(nc):
                seen = deal[b] <= own_pair if t < 2 else deal[b] >= own_pair
                at = b * BLK + (half_rows if t >= 2 else 0)
                bias[2 * t + e, :, at : at + BLK] = jnp.full(
                    (1, BLK), jnp.where(seen, 0.0, NEG), F32
                )
            if t >= 2:
                bias[2 * t + e, :, 0:half_rows] = jnp.zeros((1, half_rows), F32)
    take(g * G + m, True)
    loads[1].wait()
    for a in range(nw):
        got(small.at[a], rs.at[a])
        got(wqk.at[rows_of(a)], rw.at[a])

        @pl.when(low)
        def _():
            got(wf.at[rows_of(a)], rv.at[a])

    nb = 6 * d // 4
    for a in range(nw):
        piece = small[a].astype(F32)
        for row, src in ((0, 1), (1, 4), (2, 5), (4, 2), (5, 3), (6, 6)):
            vec[row : row + 1, a * d : (a + 1) * d] = piece[src : src + 1, :d]
        vq[0:1, a * nb : (a + 1) * nb] = piece[0:1, :nb]
    piece = small[w].astype(F32)
    vec[3:4, : 2 * d] = piece[8:9, :]
    vec[3:4, 2 * d :] = piece[9:10, :]
    vec[7:8, :] = jnp.zeros((1, width), F32)
    q_bias = vq[0:1, 0:d]
    for a in range(1, nw):
        q_bias = jnp.where(w == a, vq[0:1, a * d : (a + 1) * d], q_bias)
    f_bias = jnp.where(
        par == 0, vq[0:1, width : width + d], vq[0:1, width + d : width + 2 * d]
    )
    vq[1:2, 0:d] = q_bias
    vq[2:3, 0:d] = f_bias
    project(g * G + m, g)

    def own(i, carry):
        a = (g + i) % nw
        take(a * G + m, True)
        project(a * G + m, a)
        return carry

    lax.fori_loop(1, nw, own, 0)

    @pl.when(home_cot)
    def _():
        pltpu.make_async_copy(cot_h, cot_o.at[own_cot], rc.at[g]).start()

    @pl.when(jnp.logical_not(home_cot))
    def _():
        to_cot.start()

    ups = []
    for e in range(1, nw):
        to = (w + e) % nw
        src = wup_h.at[:, pl.ds(pl.multiple_of(to * width, BLK), width)]
        ups.append(remote(src, wup_o.at[rows_of(w)], su.at[e], ru.at[w], (to, c)))
    for r in ups:
        r.start()
    src = wup_h.at[:, pl.ds(pl.multiple_of(w * width, BLK), width)]
    pltpu.make_async_copy(src, wup_o.at[rows_of(w)], ru.at[w]).start()

    def others(i, carry):
        b = ((g + i % nw) % nw) * G + (m + 1 + i // nw) % G
        take(b, False)
        project(b, None)
        return carry

    lax.fori_loop(0, nw * (G - 1), others, 0)
    outs = [(X, X_o), (xh, xh_o), (k, k_o), (v, v_o)]
    outs = [pltpu.make_async_copy(a, b, out.at[i]) for i, (a, b) in enumerate(outs)]
    for copy in outs:
        copy.start()

    def cot_rows(a):
        return cot_o.at[pl.ds(pl.multiple_of(a * R, R), R)]

    og_two = 2 * par + two // 2
    spread_cot = [
        remote(cot_rows(og), cot_rows(og), sc.at[0], rc.at[og], (two, c)),
        remote(cot_rows(og), cot_rows(og), sc.at[1], rc.at[og], core),
        remote(cot_rows(og_two), cot_rows(og_two), sc.at[2], rc.at[og_two], core),
    ]
    got(cot_rows(og), rc.at[og])
    spread_cot[0].start()
    spread_cot[1].start()

    def attend_one(t, carry):
        at = pl.ds(pl.multiple_of(t * R, R), R)
        ot, lt = attend_tile(H, q[at, :], k, v, bias, 2 * t, 1 + t // 2)
        lse[t] = lt
        pt = product(ot, wout[...]).astype(BF)
        for e in range(2):
            to = (2 * (t % 2) + e) * R + (t // 2) * BLK
            to = pl.ds(pl.multiple_of(to, BLK), BLK)
            o[to, :] = ot[e * BLK : (e + 1) * BLK]
            part[to, :] = pt[e * BLK : (e + 1) * BLK]
        return carry

    lax.fori_loop(0, nw, attend_one, 0)

    got(cot_rows(og_two), rc.at[og_two])
    spread_cot[2].start()
    for copy in outs:
        copy.wait()
    for a in range(nw):
        got(wup_o.at[rows_of(a)], ru.at[a])

    for hi in range(2):
        a = 2 * (1 - par) + hi
        got(cot_rows(a), rc.at[a])

    for r in weights + ups + spread_cot + [to_y]:
        r.wait_send()
    for to, r in fresh:

        @pl.when(to < 2)
        def _():
            r.wait_send()

    @pl.when(jnp.logical_not(here))
    def _():
        to_one.wait_send()
        to_first.wait_send()

    @pl.when(jnp.logical_not(here_two))
    def _():
        to_two.wait_send()

    @pl.when(jnp.logical_not(home_cot))
    def _():
        to_cot.wait_send()

    @pl.when(crossing)
    def _():
        for a in range(nw):
            cross_f(a * G + m).wait_send()

    @pl.when(primary)
    def _():

        def sent(b, carry):
            core_x(b).wait_send()

            @pl.when(b % G == m)
            def _():
                for e in range(1, G):
                    member_x(b, e).wait_send()

            @pl.when(high)
            def _():
                core_f(b).wait_send()

                @pl.when(b % G == m)
                def _():
                    for e in range(1, G):
                        member_f(b, e).wait_send()

            return carry

        lax.fori_loop(0, nc, sent, 0)


def head(G, H, deal, x, first, wqkv, small, cot, wup, wout):
    nw = 4
    nc = nw * G
    R, width = x.shape
    d = width // nw
    N = nc * R
    dma = pltpu.SemaphoreType.DMA
    vm = pltpu.VMEM
    shape = jax.ShapeDtypeStruct
    operands = (deal, x, first, wqkv, small, cot, wup, wout)
    return pl.pallas_call(
        functools.partial(head_kernel, G, H),
        name="head",
        out_shape=(
            shape((nc, R, width), BF),
            shape((N, width), BF),
            shape((N, d), BF),
            shape((N, d), BF),
            shape((width, width), BF),
            shape((nw * R, width), BF),
            shape((nw * R, d), BF),
            shape((nw * R, d), BF),
            shape((nw, 8, R), F32),
            shape((nw * R, width), BF),
            shape((width, 2 * d), BF),
            shape((width, d), BF),
            shape((8, width), F32),
        ),
        in_specs=[pl.BlockSpec(memory_space=pltpu.SMEM)] + [ANY] * (len(operands) - 1),
        out_specs=[ANY] * 6 + [VM] * 7,
        scratch_shapes=[
            vm((nc, R, width), BF), vm((nc, R, 2 * d), BF), vm((N, width), BF), vm((N, d), BF),
            vm((N, d), BF), vm((nw,) + small.shape, BF), vm((8, 6 * d), F32),
            vm((2 * nw, 1, N), F32), vm(wout.shape, BF), vm(wqkv.shape, BF),
            vm((nw, d, 2 * d), BF), vm((2, d, d), BF), vm((R, width), BF),
            dma((nc,)), dma((nc,)), dma((nw,)), dma((nw,)), dma((nw,)), dma((nw,)), dma((nw,)),
            dma((5,)), dma((G, nc)), dma((G, nc)), dma((nw, 3)), dma((nw,)), dma((nw,)),
            dma((2,)), dma((4,)), dma((1,)), dma((nc,)),
        ],
        compiler_params=pltpu.CompilerParams(
            collective_id=0, has_side_effects=True, vmem_limit_bytes=56 << 20
        ),
        cost_estimate=pl.CostEstimate(
            flops=14 << 30, bytes_accessed=40 << 20, transcendentals=6 << 20
        ),
    )(*operands)


class Ring:
    def __init__(self, nc, pos, right, left, seg, chains, A, slots, out, ss, sr):
        self.nc, self.pos, self.right, self.left, self.seg = nc, pos, right, left, seg
        self.chains, self.A, self.slots, self.out, self.ss, self.sr = chains, A, slots, out, ss, sr
        self.steps = 2 * (nc - 1)
        self.cut = A.shape[1] // chains

    def at(self, half, j):
        j = (j + 2 * self.nc) % self.nc
        return pl.ds(pl.multiple_of((half * self.nc + j) * self.seg, 16), self.seg)

    def cols(self, i):
        if self.chains == 1:
            return pl.ds(0, self.cut)
        return pl.ds(pl.multiple_of(i * self.cut, BLK), self.cut)

    def reduce_copies(self, i, s):
        k = self.cols(i)
        return [
            remote(
                self.A.at[self.at(h, j), k],
                self.slots.at[h, s, :, k],
                self.ss.at[h, i, s],
                self.sr.at[h, i, s],
                to,
            )
            for h, j, to in ((0, self.pos - s, self.right), (1, self.pos + s, self.left))
        ]

    def gather_copies(self, i, s):
        k = self.cols(i)
        t = s - (self.nc - 1)
        return [
            remote(
                self.out.at[self.at(h, j), k],
                self.out.at[self.at(h, j), k],
                self.ss.at[h, i, s],
                self.sr.at[h, i, s],
                to,
            )
            for h, j, to in ((0, self.pos + 1 - t, self.right), (1, self.pos - 1 + t, self.left))
        ]

    def send(self, i, s, gathering=False):
        for r in (self.gather_copies if gathering else self.reduce_copies)(i, s):
            r.start()

    def begin(self):
        for i in range(self.chains):
            self.send(i, 0)

    def add(self, i, s):
        k = self.cols(i)
        for h, j in ((0, self.pos - s - 1), (1, self.pos + s + 1)):
            at = self.at(h, j)
            slot = self.slots.at[h, s, :, k]
            pltpu.make_async_copy(slot, slot, self.sr.at[h, i, s]).wait()
            value = self.A[at, k].astype(F32) + self.slots[h, s, :, k].astype(F32)
            self.A[at, k] = value.astype(BF)

    def keep(self, i):
        k = self.cols(i)
        for h, j in ((0, self.pos + 1), (1, self.pos - 1)):
            self.out[self.at(h, j), k] = self.A[self.at(h, j), k]

    def arrive(self, i, s):
        t = s - (self.nc - 1)
        for h, j in ((0, self.pos - t), (1, self.pos + t)):
            at = self.out.at[self.at(h, j), self.cols(i)]
            pltpu.make_async_copy(at, at, self.sr.at[h, i, s]).wait()

    def step(self, s):
        for i in range(self.chains):
            self.turn(i, s)

    def turn(self, i, s):
        last = self.nc - 2
        if isinstance(s, int):
            when = lambda cond: (lambda body: body() if cond else None)
            both = lambda a, b: a and b
        else:
            when, both = pl.when, jnp.logical_and

        @when(s < last)
        def _():
            self.add(i, s)
            self.send(i, s + 1)

        @when(s == last)
        def _():
            self.add(i, last)
            self.keep(i)
            self.send(i, last + 1, True)

        @when(both(s > last, s < self.steps))
        def _():
            self.arrive(i, s)

        @when(both(s > last, s < self.steps - 1))
        def _():
            self.send(i, s + 1, True)

    def drain(self):
        for gathering in (False, True):

            def one(t, carry):
                i, s = t % self.chains, t // self.chains
                for r in (self.gather_copies if gathering else self.reduce_copies)(i, s):
                    r.wait_send()
                return carry

            half = self.steps * self.chains // 2
            lax.fori_loop(half * gathering, half * (1 + gathering), one, 0)


class SplitRing(Ring):
    def __init__(self, nc, pos, right, left, seg, chains, A, slots, out, ss, sr, own, sems):
        super().__init__(nc, pos, right, left, seg, chains, A, slots, out, ss, sr)
        self.turns = nc - 1
        self.w, self.c = own
        self.s_ex, self.r_ex, self.s_hop, self.r_hop = sems
        self.group = nc // 2
        self.reach = (nc // 2, nc // 2 - 1)

    def turn(self, i, s):
        last = self.nc - 2
        if isinstance(s, int):
            when = lambda cond: (lambda body: body() if cond else None)
        else:
            when = pl.when

        @when(s <= last)
        def _():
            self.add(i, s)

        @when(s < last)
        def _():
            self.send(i, s + 1)

    def parts(self):
        for h, j in ((0, self.pos + 1), (1, self.pos - 1)):
            j = (j + self.nc) % self.nc
            to = 2 * h + j // self.group
            src = self.A.at[self.at(h, j)]
            dst = self.out.at[j % self.group, self.w]
            yield h, to, src, dst

    def exchange(self):
        for h, to, src, dst in self.parts():
            local = pltpu.make_async_copy(src, dst, self.r_ex.at[self.w])
            far = remote(src, dst, self.s_ex.at[h], self.r_ex.at[self.w], (to, self.c))

            @pl.when(to == self.w)
            def _():
                local.start()

            @pl.when(to != self.w)
            def _():
                far.start()

    def held(self, position):
        j = (position + 1 - 2 * (self.w // 2) + 2 * self.nc) % self.nc
        return j // self.group == self.w % 2, j % self.group

    def hop_copy(self, way, h, j):
        ref = self.out.at[j]
        to = (self.right, self.left)[way]
        return remote(ref, ref, self.s_hop.at[way, h], self.r_hop.at[way, h], to)

    def spread(self):
        have, j = self.held(self.pos)

        @pl.when(have)
        def _():
            for a in range(4):
                ref = self.out.at[j, a]
                pltpu.make_async_copy(ref, ref, self.r_ex.at[a]).wait()
            for way in range(2):
                self.hop_copy(way, 1, j).start()

    def hop(self, h):
        for way in range(2):
            if h > self.reach[way]:
                continue
            have, j = self.held(self.pos - h if way == 0 else self.pos + h)

            @pl.when(have)
            def _():
                ref = self.out.at[j]
                pltpu.make_async_copy(ref, ref, self.r_hop.at[way, h]).wait()
                if h < self.reach[way]:
                    self.hop_copy(way, h + 1, j).start()

    def drain(self):
        def one(t, carry):
            i, s = t % self.chains, t // self.chains
            for r in self.reduce_copies(i, s):
                r.wait_send()
            return carry

        lax.fori_loop(0, self.turns * self.chains, one, 0)
        for h, to, src, dst in self.parts():

            @pl.when(to != self.w)
            def _():
                remote(src, dst, self.s_ex.at[h], self.r_ex.at[self.w], (to, self.c)).wait_send()

        for way in range(2):
            for h in range(self.reach[way]):
                have, j = self.held(self.pos - h if way == 0 else self.pos + h)

                @pl.when(have)
                def _():
                    self.hop_copy(way, h + 1, j).wait_send()


def tail_kernel(
    G, H, seg_a, seg_u, seg_b,
    deal, q_h, k_h, v_h, o_h, do_h, lse_h, xh_h, X_h, wqk_h, wf_h, vec_h, dmid_h,
    up_h, down_h, gout_h, small_h, mlp_h, mid_h,
    layer_out, tokens_out, first_out, up_out, down_out, gout_out, small_out, qkv_out, ends_out,
    q, k, v, o, do, lse, lift, xh, X, wqk, wf, vec, dmid,
    kt, dk, dv, dqk, dvb, D, b1, ab, b2, st, b3, tot, tb, tr,
    A, slots_a, res_a, U, slots_u, res_u, gq, slots_b, res_b, gain_t, shift_t, sums_t, f1, fs, fr,
    mlp, mid, lb, ly, lr, sl, rl, sL, rL, s1, r1, s2, r2, s3, r3, sT, rT, ssa, sra, ssu, sru, seu, reu, shu, rhu, ssb, srb, seb, reb, shb, rhb, sf1, rf1, sf2, rf2, ld,
):
    w = lax.axis_index("wt")
    c = lax.axis_index("ctx")
    nw = 4
    nc = nw * G
    g = c // G
    m = c % G
    par = w % 2
    hi = w // 2
    core = (w + 1 - 2 * par, c)
    other = ((w + 2) % nw, c)
    R, width = dmid.shape
    d = width // nw
    N = xh.shape[0]
    odd = c % 2
    pos = (c // 2) * (1 - odd) + (nc - 1 - c // 2) * odd

    def ctx_at(p):
        p = (p + nc) % nc
        h = p // (nc // 2)
        return 2 * p * (1 - h) + (2 * (nc - 1 - p) + 1) * h

    right = (w, ctx_at(pos + 1))
    left = (w, ctx_at(pos - 1))
    loads = [
        (up_h, U),
        (down_h, A.at[pl.ds(0, width)]),
        (gout_h, A.at[pl.ds(width, d)]),
        (small_h, A.at[pl.ds(width + d, small_h.shape[0])]),
        (k_h, k), (v_h, v), (q_h, q), (o_h, o), (do_h, do), (lse_h, lse),
        (xh_h, xh), (X_h, X), (wqk_h, wqk), (wf_h, wf), (vec_h, vec), (dmid_h, dmid), (mid_h, mid), (mlp_h, mlp),
    ]
    loads = [pltpu.make_async_copy(a, b, ld.at[i]) for i, (a, b) in enumerate(loads)]
    for copy in loads:
        copy.start()
    peers = [
        ((w + a) % nw, ((g + e) % nw) * G + m) for a in range(nw) for e in range(nw) if a or e
    ]
    peers += [(w, g * G + (m + e) % G) for e in range(1, G)]
    greet(peers + [right, left])
    ring_a = Ring(nc, pos, right, left, seg_a, 2, A, slots_a, res_a, ssa, sra)
    ring_u = SplitRing(
        nc, pos, right, left, seg_u, 2, U, slots_u, res_u, ssu, sru, (w, c), (seu, reu, shu, rhu)
    )
    ring_b = SplitRing(
        nc, pos, right, left, seg_b, 1, gq, slots_b, res_b, ssb, srb, (w, c), (seb, reb, shb, rhb)
    )
    for copy in loads[:4]:
        copy.wait()
    ring_u.begin()
    ring_a.begin()
    for copy in loads[4:10] + loads[16:]:
        copy.wait()
    seq = 2 * (g % 2) + g // 2
    og = 2 * par + hi
    home = (seq, og * G + m)
    home_self = jnp.logical_and(og == g, w == seq)
    shares = []
    for e in range(1, nw):
        to = (w + e) % nw
        src = mlp.at[pl.ds(pl.multiple_of((2 * (to % 2) + to // 2) * R, R), R)]
        r = remote(src, lb.at[w], sl.at[e], rl.at[w], (to, c))
        r.start()
        shares.append(r)

    flip_rows(k, kt)
    dk[...] = jnp.zeros_like(dk)
    dv[...] = jnp.zeros_like(dv)
    dqk[...] = jnp.zeros_like(dqk)
    wide = H * HEAD_DIM

    def poll(n):
        for r in range(4):

            @pl.when(n % 4 == r)
            def _():
                (ring_a if r % 2 else ring_u).turn(r // 2, n // 4)

    pairs = lax.broadcasted_iota(jnp.int32, (1, 2 * BLK), 1) < BLK
    for t in range(nw):
        mine = [deal[(2 * (t % 2) + e) * G + m] for e in range(2)]
        for b in range(nc):
            unseen = [
                jnp.where(deal[b] <= a if t < 2 else deal[b] >= a, 0.0, -NEG) for a in mine
            ]
            at = b if t < 2 else nc + b
            lift[t, at : at + 1, :] = jnp.where(pairs, unseen[0], unseen[1])
        if t >= 2:
            lift[t, 0:nc, :] = jnp.zeros((nc, 2 * BLK), F32)

    def tile(t, carry):
        rows = []
        for e in range(2):
            at = (2 * (t % 2) + e) * R + (t // 2) * BLK
            rows.append(pl.ds(pl.multiple_of(at, BLK), BLK))
        pick = lambda ref: jnp.concatenate([ref[rows[0], :], ref[rows[1], :]], axis=0)
        mine = pl.ds(pl.multiple_of(t * R, R), R)

        def polls_at(j):
            n = 2 * (t + t // 3 + j)
            poll(n)
            poll(n + 1)

        dqt = attend_back_tile(
            H, q[mine, :], pick(do), pick(o), lse[t], k, v, kt, dk, dv, lift, t, 1 + t // 2,
            polls_at,
        )
        dq = jnp.transpose(dqt).astype(BF)
        for e in range(2):
            at = ((2 * (t % 2) + e) * G + m) * R + (t // 2) * BLK
            at = pl.ds(pl.multiple_of(at, BLK), BLK)
            dqk[at, 0:wide] = dq[e * BLK : (e + 1) * BLK]
        return carry

    lax.fori_loop(0, nw, tile, 0)

    def deal_back(b, carry):
        for e in range(2):
            src = pl.ds(pl.multiple_of(b * BLK + e * (N // 2), BLK), BLK)
            to = pl.ds(pl.multiple_of(b * R + e * BLK, BLK), BLK)
            dqk[to, wide : 2 * wide] = dk[src, :].astype(BF)
            dvb[to, :] = dv[src, :].astype(BF)
        return carry

    lax.fori_loop(0, nc, deal_back, 0)
    polls = 12
    for copy in loads[10:16]:
        copy.wait()

    layer = mid[...] + vec[6:7, :] + mlp[pl.ds(pl.multiple_of(og * R, R), R), :].astype(F32)
    for e in range(1, nw):
        src = (w + e) % nw
        pltpu.make_async_copy(lb.at[src], lb.at[src], rl.at[src]).wait()
        layer = layer + lb[src].astype(F32)
    ly[...] = layer.astype(BF)
    layer_back = remote(ly, lr, sL.at[0], rL.at[0], home)
    layer_stay = pltpu.make_async_copy(ly, lr, rL.at[0])

    @pl.when(home_self)
    def _():
        layer_stay.start()

    @pl.when(jnp.logical_not(home_self))
    def _():
        layer_back.start()

    upper = w >= 2
    first_copies = []
    for e in range(1, G):
        mm = (m + e) % G
        for gp in range(nw):
            src = dvb.at[pl.ds(pl.multiple_of((gp * G + mm) * R, R), R)]
            first_copies.append(
                remote(src, f1.at[m, gp], sf1.at[e, gp], rf1.at[m, gp], (w, g * G + mm))
            )

    @pl.when(upper)
    def _():
        for r in first_copies:
            r.start()

    tile_d = 128
    ones = jnp.ones((N, BLK), BF)
    row_qk = product_left(ones, dqk[...])[0:1, :]
    row_f = product_left(ones, dvb[...])[0:1, :]
    sum_qk = product_left(dqk[...], ones)
    sum_f = product_left(dvb[...], ones)
    gain_t[...] = jnp.transpose(jnp.broadcast_to(vec[4:5, :], (BLK, width)))
    shift_t[...] = jnp.transpose(jnp.broadcast_to(vec[5:6, :], (BLK, width)))
    lane = lax.broadcasted_iota(jnp.int32, (d, BLK), 1)
    edge = gq.shape[1] - BLK
    for a in range(nw):
        sums_t[a * d : (a + 1) * d, :] = jnp.where(
            lane == 66, sum_qk[:wide], jnp.where(lane == 67, sum_qk[wide:], sum_f)
        )
    lane = lax.broadcasted_iota(jnp.int32, (tile_d, BLK), 1)

    def grads(i, carry):
        at = pl.ds(pl.multiple_of(i * tile_d, tile_d), tile_d)
        x_qk = product_left(xh[:, at], dqk[...])
        x_f = product_left(xh[:, at], dvb[...])
        w_qk = wqk[at, :].astype(F32)
        w_f = wf[at, :].astype(F32)
        add = lambda a, b: jnp.sum(a, axis=1, keepdims=True) + jnp.sum(b, axis=1, keepdims=True)
        for_gain = add(w_qk * x_qk, w_f * x_f)
        for_shift = add(w_qk * row_qk, w_f * row_f)
        gain = gain_t[at, 0:1]
        shift = shift_t[at, 0:1]
        gq[at, 0 : 2 * wide] = (gain * x_qk + shift * row_qk).astype(BF)
        gq[at, 2 * wide : 3 * wide] = (gain * x_f + shift * row_f).astype(BF)
        ends = gq[at, edge:].astype(F32)
        ends = jnp.where(lane == 64, for_gain, jnp.where(lane == 65, for_shift, ends))
        ends = jnp.where(lane > 65, sums_t[at, :], ends)
        gq[at, edge:] = jnp.where(lane < 69, ends, 0.0).astype(BF)
        poll(polls + i)
        return carry

    lax.fori_loop(0, width // tile_d, grads, 0)
    polls += width // tile_d
    ring_b.begin()

    def block(i, carry):
        phase = i // (2 * G)
        jj = (hi + 1 - (i // G) % 2 + 2) % 2
        mm = (m + 1 + i % G) % G
        parity = (1 - par) * (1 - phase) + par * phase
        b = (2 * parity + jj) * G + mm
        at = pl.ds(pl.multiple_of(b * R, R), R)
        dn = product_right(dqk[at, :], wqk[...]) + product_right(dvb[at, :], wf[...])
        D[b] = dn.astype(BF)

        @pl.when(phase == 0)
        def _():
            slot = jj * G + mm
            remote(D.at[b], b1.at[slot], s1.at[slot], r1.at[slot], core).start()

        poll(polls + i)

        @pl.when(i % 4 == 3)
        def _():
            ring_b.step(i // 4)

        return carry

    lax.fori_loop(0, nc, block, 0)
    polls += nc
    done_b = nc // 4

    order = list(range(1, G)) + [0]

    def chip_sum(jj, mm):
        slot = jj * G + mm
        pltpu.make_async_copy(b1.at[slot], b1.at[slot], r1.at[slot]).wait()
        return D[(2 * par + jj) * G + mm].astype(F32) + b1[slot].astype(F32)

    seconds = []
    for e in order:
        mm = (m + e) % G
        ab[mm] = chip_sum(1 - hi, mm).astype(BF)
        r = remote(ab.at[mm], b2.at[mm], s2.at[mm], r2.at[mm], other)
        r.start()
        seconds.append(r)
    thirds = []

    def sum_chips():
        for e in order:
            mm = (m + e) % G
            total = chip_sum(hi, mm)
            pltpu.make_async_copy(b2.at[mm], b2.at[mm], r2.at[mm]).wait()
            total = total + b2[mm].astype(F32)
            if e:
                st[mm] = total.astype(BF)
                r = remote(st.at[mm], b3.at[m], s3.at[mm], r3.at[m], (w, g * G + mm))
                r.start()
                thirds.append(r)
            else:
                tot[...] = total

    def sum_first():
        @pl.when(upper)
        def _():
            for gp in range(nw):
                total = dvb[pl.ds(pl.multiple_of((gp * G + m) * R, R), R), :].astype(F32)
                for e in range(1, G):
                    mm = (m + e) % G
                    pltpu.make_async_copy(f1.at[mm, gp], f1.at[mm, gp], rf1.at[mm, gp]).wait()
                    total = total + f1[mm, gp].astype(F32)
                fs[gp] = total.astype(BF)
                own = jnp.logical_and(w == seq, g == gp)

                @pl.when(own)
                def _():
                    pltpu.make_async_copy(fs.at[gp], fr.at[par], rf2.at[par]).start()

                @pl.when(jnp.logical_not(own))
                def _():
                    remote(
                        fs.at[gp], fr.at[par], sf2.at[gp], rf2.at[par], (seq, gp * G + m)
                    ).start()

    back = remote(tb, tr, sT.at[0], rT.at[0], home)
    stay = pltpu.make_async_copy(tb, tr, rT.at[0])

    def norm_back():
        total = tot[...]
        for e in range(1, G):
            mm = (m + e) % G
            pltpu.make_async_copy(b3.at[mm], b3.at[mm], r3.at[mm]).wait()
            total = total + b3[mm].astype(F32)
        value = X[og * G + m].astype(F32)
        centred = value - jnp.mean(value, axis=-1, keepdims=True)
        inverse = lax.rsqrt(jnp.mean(centred * centred, axis=-1, keepdims=True) + EPS)
        normal = centred * inverse
        dx = total * vec[4:5, :]
        dx = dx - jnp.mean(dx, axis=-1, keepdims=True) - normal * jnp.mean(
            dx * normal, axis=-1, keepdims=True
        )
        tb[...] = (dmid[...].astype(F32) + inverse * dx).astype(BF)

        @pl.when(home_self)
        def _():
            stay.start()

        @pl.when(jnp.logical_not(home_self))
        def _():
            back.start()

    turns = []
    extras = [ring_u.exchange, ring_u.spread]
    extras += [functools.partial(ring_u.hop, h) for h in range(1, ring_u.reach[0] + 1)]
    for n in range(polls, 4 * ring_a.steps):
        r, s = n % 4, n // 4
        if r % 2:
            turns.append(functools.partial(ring_a.turn, r // 2, s))
        elif s < ring_u.turns:
            turns.append(functools.partial(ring_u.turn, r // 2, s))
        elif r == 0 or n == polls:
            turns.append(extras.pop(0) if extras else lambda: None)
    turns += extras

    def others():
        for _ in range(2):
            if turns:
                turns.pop(0)()

    for at_b in range(done_b, ring_b.turns):
        ring_b.step(at_b)
        others()
        if at_b == done_b:
            sum_first()
    ring_b.exchange()
    others()
    sum_chips()
    ring_b.spread()
    others()
    for h in range(1, ring_b.reach[0] + 1):
        ring_b.hop(h)
        others()
        if h == 3:
            norm_back()
    while turns:
        others()

    down_out[...] = res_a[0:width, :].astype(F32)
    gout_out[...] = res_a[width : width + d, :].astype(F32)
    small_out[...] = res_a[width + d : width + d + small_out.shape[0], :].astype(F32)
    for j in range(ring_u.group):
        rows = slice(j * seg_u, (j + 1) * seg_u)
        for a in range(nw):
            up_out[rows, a * width : (a + 1) * width] = res_u[j, a].astype(F32)
    for j in range(ring_b.group):
        rows = slice(j * seg_b, (j + 1) * seg_b)
        for a in range(nw):
            for part in range(2):
                at = part * width + a * d
                qkv_out[rows, at : at + d] = res_b[j, a, :, part * d : (part + 1) * d].astype(F32)
            if a < 2:
                at = 2 * width + a * d
                qkv_out[rows, at : at + d] = res_b[j, a, :, 2 * d : 3 * d].astype(F32)
            at = a * d + j * seg_b
            ends_out[at : at + seg_b, :] = res_b[j, a, :, edge:].astype(F32)
    pltpu.make_async_copy(tr, tr, rT.at[0]).wait()
    tokens_out[...] = tr[...].astype(F32)
    for u in range(2):
        pltpu.make_async_copy(fr.at[u], fr.at[u], rf2.at[u]).wait()
        first_out[:, u * d : (u + 1) * d] = fr[u].astype(F32)

    pltpu.make_async_copy(lr, lr, rL.at[0]).wait()
    layer_out[...] = lr[...]
    ring_a.drain()
    ring_u.drain()
    ring_b.drain()
    for r in seconds + thirds + shares:
        r.wait_send()

    @pl.when(jnp.logical_not(home_self))
    def _():
        back.wait_send()
        layer_back.wait_send()

    @pl.when(upper)
    def _():
        for r in first_copies:
            r.wait_send()
        for gp in range(nw):

            @pl.when(jnp.logical_not(jnp.logical_and(w == seq, g == gp)))
            def _():
                remote(
                    fs.at[gp], fr.at[par], sf2.at[gp], rf2.at[par], (seq, gp * G + m)
                ).wait_send()

    def drain(i, carry):
        jj = (hi + 1 - (i // G) % 2 + 2) % 2
        mm = (m + 1 + i % G) % G
        slot = jj * G + mm
        b = (2 * (1 - par) + jj) * G + mm
        remote(D.at[b], b1.at[slot], s1.at[slot], r1.at[slot], core).wait_send()
        return carry

    lax.fori_loop(0, 2 * G, drain, 0)


def tail(
    G, H, deal, q, k, v, o, do, lse, xh, X, wqk, wf, vec, dmid, up, down, gout, small, mlp, mid
):
    nw = 4
    nc = nw * G
    R, width = dmid.shape
    d = width // nw
    N = xh.shape[0]
    wide = H * HEAD_DIM
    seg_a = (width + d + small.shape[0]) // (2 * nc)
    seg_u = seg_b = width // (2 * nc)
    cols = 5 * BLK
    dma = pltpu.SemaphoreType.DMA
    vm = pltpu.VMEM
    steps = 2 * (nc - 1)
    operands = (
        deal, q, k, v, o, do, lse, xh, X, wqk, wf, vec, dmid, up, down, gout, small, mlp, mid
    )
    return pl.pallas_call(
        functools.partial(tail_kernel, G, H, seg_a, seg_u, seg_b),
        name="tail",
        out_shape=(
            jax.ShapeDtypeStruct((R, width), BF),
            jax.ShapeDtypeStruct((R, width), F32),
            jax.ShapeDtypeStruct((R, 2 * d), F32),
            jax.ShapeDtypeStruct((d, nw * width), F32),
            jax.ShapeDtypeStruct((width, width), F32),
            jax.ShapeDtypeStruct((d, width), F32),
            jax.ShapeDtypeStruct(small.shape, F32),
            jax.ShapeDtypeStruct((d, 2 * width + 2 * d), F32),
            jax.ShapeDtypeStruct((width, BLK), F32),
        ),
        in_specs=[pl.BlockSpec(memory_space=pltpu.SMEM)] + [ANY] * (len(operands) - 1),
        out_specs=[VM] * 9,
        scratch_shapes=[vm(a.shape, a.dtype) for a in operands[1:7]]
        + [vm((nw, 2 * nc, R), F32)]
        + [vm(a.shape, a.dtype) for a in operands[7:13]]
        + [
            vm((wide, N), BF), vm((N, wide), F32), vm((N, wide), F32), vm((N, 2 * wide), BF),
            vm((N, wide), BF), vm((nc, R, width), BF), vm((2 * G, R, width), BF),
            vm((G, R, width), BF), vm((G, R, width), BF), vm((G, R, width), BF),
            vm((G, R, width), BF), vm((R, width), F32), vm((R, width), BF), vm((R, width), BF),
            vm((2 * nc * seg_a, width), BF), vm((2, nc - 1, seg_a, width), BF),
            vm((2 * nc * seg_a, width), BF),
            vm((width, width), BF), vm((2, nc - 1, seg_u, width), BF),
            vm((nc // 2, nw, seg_u, width), BF),
            vm((width, cols), BF), vm((2, nc - 1, seg_b, cols), BF),
            vm((nc // 2, nw, seg_b, cols), BF),
            vm((width, BLK), F32), vm((width, BLK), F32), vm((width, BLK), F32),
            vm((G, nw, R, d), BF), vm((nw, R, d), BF), vm((2, R, d), BF),
            vm((nw * R, width), BF), vm((R, width), F32), vm((nw, R, width), BF),
            vm((R, width), BF), vm((R, width), BF), dma((nw,)), dma((nw,)), dma((1,)), dma((1,)),
            dma((2 * G,)), dma((2 * G,)), dma((G,)), dma((G,)), dma((G,)), dma((G,)),
            dma((1,)), dma((1,)), dma((2, 2, steps)), dma((2, 2, steps)),
        ]
        + [
            dma(a)
            for chains in (2, 1)
            for a in (
                (2, chains, nc - 1), (2, chains, nc - 1), (2,), (nw,), (2, nc // 2 + 1),
                (2, nc // 2 + 1),
            )
        ]
        + [
            dma((G, nw)), dma((G, nw)),
            dma((nw,)), dma((2,)), dma((len(operands),)),
        ],
        compiler_params=pltpu.CompilerParams(
            collective_id=2, has_side_effects=True, vmem_limit_bytes=63 << 20
        ),
        cost_estimate=pl.CostEstimate(
            flops=40 << 30, bytes_accessed=60 << 20, transcendentals=6 << 20
        ),
    )(*operands)


def on_device(
    nw,
    nc,
    tokens,
    first_values,
    cotangent,
    deal,
    w_qkv,
    bias_qv,
    w_out,
    bias_out,
    gain_one,
    shift_one,
    gain_two,
    shift_two,
    w_up,
    bias_up,
    w_down,
    bias_down,
):
    G = nc // nw
    w = lax.axis_index("wt")
    c = lax.axis_index("ctx")
    m = c % G
    rows, width = tokens.shape[1:]
    d = width // nw
    H = HEADS // nw
    both = ("wt", "ctx")
    seq = lambda g: 2 * (g % 2) + g // 2
    swap = [
        (a * nc + g * G + e, seq(g) * nc + a * G + e)
        for a in range(nw)
        for g in range(nw)
        for e in range(G)
    ]
    ring = [[(a, (a + k) % nw) for a in range(nw)] for k in range(nw)]

    def exchange(pieces):
        out = jnp.zeros_like(pieces)
        mine = lax.dynamic_index_in_dim(pieces, w, 0, keepdims=True)
        out = lax.dynamic_update_slice_in_dim(out, mine, w, 0)
        for k in range(1, nw):
            piece = lax.dynamic_index_in_dim(pieces, (w + k) % nw, 0, keepdims=True)
            got = lax.ppermute(piece, "wt", ring[k])
            out = lax.dynamic_update_slice_in_dim(out, got, (w + nw - k) % nw, 0)
        return out

    qk = w_qkv[:, : 2 * width].reshape(d, 2, nw, d).transpose(2, 0, 1, 3).reshape(nw, d, 2 * d)
    wf = w_qkv[:, 2 * width :].reshape(d, 2, d).transpose(1, 0, 2)
    nb = bias_qv.shape[0]
    ids = dealt_blocks(deal)
    qpos = jnp.arange(nw, dtype=jnp.int32) * G + m
    qid = jnp.take(ids.reshape(nc, 2), qpos, axis=0)
    hidden = (ids[None, None, :] > qid[:, :, None]).astype(F32) * -NEG
    bias = jnp.repeat(-hidden.reshape(2 * nw, 2 * nc), BLK, axis=1)[:, None, :]
    lift = jnp.repeat(hidden.transpose(0, 2, 1), BLK, axis=2)

    def mine(vector):
        return lax.dynamic_slice_in_dim(vector, w * d, d)

    if nc <= 8:
        rows_of = (bias_qv, bias_out, gain_one, shift_one, gain_two, shift_two, bias_down)
        pieces = []
        for a in rows_of:
            pieces += [a, jnp.zeros((2 * d - a.shape[0],), BF)]
        pieces += [jnp.zeros((2 * d,), BF), bias_up, jnp.zeros((12 * d,), BF)]
        small = jnp.concatenate(pieces).reshape(16, 2 * d)
        X, xhat, k, v, Wup, cot, q, o, lse, part, Wqk, Wf, vec = head(
            G, H, deal, tokens[0], first_values[0], w_qkv, small, cotangent[0], w_up, w_out
        )
        mlp, mid_own, d_mid, d_o, g_up, g_down, g_out, vsums = middle(
            G, True, part, X, cot, o, Wup, w_down, w_out, vec
        )
        small = jnp.stack(
            [vsums[0], jnp.concatenate([mine(vsums[a]) for a in range(1, 5)])]
            + [jnp.zeros((width,), F32)] * 14
        ).astype(BF)
        rows_a = width + d + 16
        pad = -(-rows_a // (32 * nc)) * 32 * nc - rows_a
        small = jnp.concatenate([small, jnp.zeros((pad, width), BF)], axis=0)
        layer, grad_tokens, grad_first, s_up, s_down, s_out, s_small, s_qkv, ends = tail(
            G, H, deal, q, k, v, o, d_o, lse, xhat, X, Wqk, Wf, vec,
            d_mid, g_up, g_down, g_out, small, mlp, mid_own,
        )
        ends = ends.reshape(nw, d, BLK)
        bias_all = jnp.concatenate([ends[:, :, 66].reshape(-1), ends[:2, :, 68].reshape(-1)])
        s_vec = s_small[1].reshape(nw, d)
        return (
            layer[None],
            grad_tokens[None],
            grad_first[None],
            s_qkv,
            lax.dynamic_slice_in_dim(bias_all, w * nb, nb),
            s_out,
            s_vec[1],
            jnp.sum(ends[:, :, 64], axis=0),
            jnp.sum(ends[:, :, 65], axis=0),
            s_vec[2],
            s_vec[3],
            s_up,
            s_small[0],
            s_down,
            s_vec[0],
        )
    small = jnp.concatenate(
        [bias_qv, bias_out, gain_one, shift_one, gain_two, shift_two, bias_down]
    )
    lanes = 16 * BLK
    small = jnp.concatenate([small, jnp.zeros((lanes - small.shape[0],), BF)]).reshape(16, BLK)
    X, Fv, WQK, WF, SM = gather(nw, G, tokens[0], first_values[0], qk, wf, small)
    X = X.reshape(nc * rows, width)
    Wqk = WQK.reshape(width, 2 * d)
    low = w < 2
    Wf = jnp.where(low, WF.reshape(width, d), jnp.zeros((width, d), BF))
    SM = SM.reshape(nw, lanes).astype(F32)
    qv_vector = SM[:, :nb].reshape(-1)
    vectors = [SM[:, nb + a * d : nb + (a + 1) * d].reshape(-1) for a in range(6)]
    out_vector, gain_a, shift_a, gain_b, shift_b, down_vector = vectors

    x32 = X.astype(F32)
    mean = jnp.mean(x32, axis=-1, keepdims=True)
    centred = x32 - mean
    inverse = lax.rsqrt(jnp.mean(centred * centred, axis=-1, keepdims=True) + EPS)
    n1 = (centred * inverse * gain_a + shift_a).astype(BF)
    pqk = product(n1, Wqk)
    q_bias = lax.dynamic_slice_in_dim(qv_vector, w * d, d)
    f_bias = lax.dynamic_slice_in_dim(qv_vector, width + (w % 2) * d, d)
    q = (pqk[:, :d] + q_bias).astype(BF)
    k = pqk[:, d:].astype(BF)
    f = (product(n1, Wf) + f_bias).astype(BF)
    Fv = Fv.reshape(nc * rows, 2 * d)
    first = jnp.where(w % 2 == 0, Fv[:, :d], Fv[:, d:])
    v = jnp.where(low, f, first)

    o, lse = attend(H, qpos, bias, q, k, v)

    part = product(o, w_out).astype(BF)
    pieces, spread = lax.optimization_barrier((w_up, cotangent[0], X))[:2]
    Wup = exchange(pieces.reshape(d, nw, width).transpose(1, 0, 2)).reshape(width, width)
    unswap = [(b, a) for a, b in swap]
    cot = lax.all_gather(lax.ppermute(spread, both, unswap), "wt", axis=0, tiled=True)
    vec = jnp.stack([out_vector, gain_b, shift_b, bias_up.astype(F32)] + [out_vector] * 4)
    mlp, mid_own, d_mid, d_o, g_up, g_down, g_out, vsums = middle(
        G, False, part, X.reshape(nc, rows, width), cot, o, Wup, w_down, w_out, vec
    )

    mlp = lax.psum_scatter(mlp, "wt", scatter_dimension=0, tiled=True)
    layer = (mid_own + mlp.astype(F32) + down_vector).astype(BF)
    layer = lax.ppermute(layer, both, swap)
    up_rows = exchange(g_up.reshape(nw, d, width)).transpose(1, 0, 2)
    s_up, s_down = lax.psum((up_rows.reshape(d, nw * width), g_down), "ctx")
    dqk, dv = attend_back(H, qpos, lift, q, k, v, o, d_o, lse)
    zero = jnp.zeros_like(dv)
    df = jnp.where(low, dv, zero)
    dn1 = product_right(dqk, Wqk) + product_right(df, Wf)
    dn1_low = dn1.astype(BF)
    blank = jnp.zeros_like(dv)
    left = jnp.where(w == 2, dv, blank)
    right = jnp.where(w == 3, dv, blank)
    total = scatter_sum(
        G, jnp.concatenate([dn1_low, left, right], axis=1).reshape(nc, rows, width + 2 * d)
    )
    grad_first = lax.ppermute(total[:, width:].astype(BF), both, swap).astype(F32)
    block = (w * G + m) * rows
    x_own = lax.dynamic_slice_in_dim(X, block, rows).astype(F32)
    _, pull_one = jax.vjp(lambda a: norm_rows(a, gain_a, shift_a), x_own)
    d_x = d_mid.astype(F32) + pull_one(total[:, :width])[0]
    grad_tokens = lax.ppermute(d_x.astype(BF), both, swap).astype(F32)

    g_qk = product_left(n1, dqk)
    g_f = product_left(n1, df)
    normal = centred * inverse
    g_gain_one = jnp.sum(dn1_low.astype(F32) * normal, axis=0)
    g_shift_one = jnp.sum(dn1_low.astype(F32), axis=0)
    cols = jnp.concatenate(
        [
            g_qk.astype(BF),
            g_f.astype(BF),
            g_gain_one[:, None].astype(BF),
            g_shift_one[:, None].astype(BF),
            jnp.zeros((width, 62), BF),
        ],
        axis=1,
    ).reshape(nw, d, 640)
    sums = jnp.concatenate(
        [jnp.sum(dqk.astype(F32), axis=0), jnp.sum(df.astype(F32), axis=0), jnp.zeros((64,), F32)]
    ).astype(BF)
    foot = jnp.concatenate([sums[None], jnp.zeros((7, 640), BF)], axis=0)
    pack = jnp.concatenate([cols, jnp.broadcast_to(foot[None], (nw, 8, 640))], axis=1)
    pack = exchange(pack)
    vecs = jnp.concatenate(
        [
            vsums[0],
            mine(vsums[1]),
            mine(vsums[2]),
            mine(vsums[3]),
            mine(vsums[4]),
        ]
    ).astype(BF)
    pack = pack.at[0, d + 1 : d + 4, :512].set(vecs.reshape(3, 512))
    pack, s_up, s_down = lax.optimization_barrier((pack, s_up, s_down))
    pack, s_out = lax.psum((pack, g_out), "ctx")
    body = pack[:, :d]
    s_qkv = jnp.concatenate(
        [body[a, :, e * d : (e + 1) * d] for e in (0, 1) for a in range(nw)]
        + [body[a, :, 2 * d : 3 * d] for a in range(2)],
        axis=1,
    ).astype(F32)
    s_gain_one = jnp.sum(body[:, :, 576].astype(F32), axis=0)
    s_shift_one = jnp.sum(body[:, :, 577].astype(F32), axis=0)
    ends = pack[:, d]
    bias_all = jnp.concatenate([ends[:, :d].reshape(-1), ends[:2, 2 * d : 3 * d].reshape(-1)])
    s_bias_qv = lax.dynamic_slice_in_dim(bias_all, w * nb, nb).astype(F32)
    vecs = pack[0, d + 1 : d + 4, :512].reshape(-1).astype(F32)
    s_bias_up = vecs[:width]
    s_bias_down, s_bias_out, s_gain_two, s_shift_two = [
        vecs[width + a * d : width + (a + 1) * d] for a in range(4)
    ]
    return (
        layer[None],
        grad_tokens[None],
        grad_first[None],
        s_qkv,
        s_bias_qv,
        s_out.astype(F32),
        s_bias_out,
        s_gain_one,
        s_shift_one,
        s_gain_two,
        s_shift_two,
        s_up.astype(F32),
        s_bias_up,
        s_down.astype(F32),
        s_bias_down,
    )


def solution(mesh):
    rows3 = P("wt", "ctx", None)
    mat = P("wt", None)
    vec = P("wt")
    in_specs = (rows3, rows3, rows3, P(), mat, vec, mat) + (vec,) * 5 + (mat, vec, mat, vec)
    out_specs = (
        (rows3, rows3, rows3, mat, vec, mat) + (vec,) * 5 + (mat, vec, mat, vec)
    )
    return jax.shard_map(
        functools.partial(on_device, mesh.shape["wt"], mesh.shape["ctx"]),
        mesh=mesh,
        in_specs=in_specs,
        out_specs=out_specs,
        check_vma=False,
    )
```

```python
import functools

import jax
import jax.numpy as jnp
from jax import lax
from jax.experimental import pallas as pl
from jax.experimental.pallas import tpu as pltpu
from jax.sharding import PartitionSpec as P

HEADS = 12
HEAD_DIM = 64
BLK = 128
CHUNK = 1024

EPS = 1e-05
SLOPE = 0.7978845608028654
CUBIC = 0.044715
NEG = -1e30

BF = jnp.bfloat16
F32 = jnp.float32
MESH = pl.DeviceIdType.MESH
ANY = pl.BlockSpec(memory_space=pl.ANY)
VM = pl.BlockSpec(memory_space=pltpu.VMEM)


def norm_rows(value, gain, shift):
    mean = jnp.mean(value, axis=-1, keepdims=True)
    centred = value - mean
    inverse = lax.rsqrt(jnp.mean(centred * centred, axis=-1, keepdims=True) + EPS)
    return centred * inverse * gain + shift


def gelu_tanh(value):
    return 0.5 * value * (1.0 + jnp.tanh(SLOPE * (value + CUBIC * value * value * value)))


def product(left, right):
    return jnp.dot(left, right, preferred_element_type=F32)


def product_left(left, right):
    return lax.dot_general(left, right, (((0,), (0,)), ((), ())), preferred_element_type=F32)


def product_right(left, right):
    return lax.dot_general(left, right, (((1,), (1,)), ((), ())), preferred_element_type=F32)


def dealt_blocks(deal):
    count = deal.shape[0] * 2
    pairs = jnp.repeat(deal, 2)
    parity = jnp.arange(count, dtype=jnp.int32) % 2
    return jnp.where(parity == 0, pairs, count - 1 - pairs)


def remote(src, dst, send, recv, device):
    return pltpu.make_async_remote_copy(
        src_ref=src,
        dst_ref=dst,
        send_sem=send,
        recv_sem=recv,
        device_id=device,
        device_id_type=MESH,
    )


def greet(peers):
    barrier = pltpu.get_barrier_semaphore()
    for peer in peers:
        pl.semaphore_signal(barrier, inc=1, device_id=peer, device_id_type=MESH)
    pl.semaphore_wait(barrier, len(peers))


def gather_kernel(
    nw, G, x, first, wqk, wf, small, X, Fv, WQK, WF, SM, rx, rf, rw, rv, rs, sa, sx, sfa, sfx, sw, loc
):
    w = lax.axis_index("wt")
    c = lax.axis_index("ctx")
    g = c // G
    m = c % G
    nc = nw * G
    core = w + 1 - 2 * (w % 2)
    other = (w + 2) % nw
    rel = lambda k: (w + k) % nw
    peers = [(rel(k), c) for k in range(1, nw)]
    peers += [(w, ((g + k) % nw) * G + m) for k in range(1, nw)]
    peers += [(w, g * G + (m + k) % G) for k in range(1, G)]
    greet(peers)
    seq = 2 * (g % 2) + g // 2
    goal = (2 * (w % 2) + w // 2) * G + m
    is_a = w == seq
    primary = (w + seq) % 2 == 0
    high = w >= 2
    copies = []

    to_head = remote(x, X.at[c], sa.at[0], rx.at[c], (w, goal))
    to_head_f = remote(first, Fv.at[c], sa.at[1], rf.at[c], (w, goal))
    own_x = pltpu.make_async_copy(x, X.at[c], rx.at[c])
    own_f = pltpu.make_async_copy(first, Fv.at[c], rf.at[c])

    @pl.when(is_a)
    def _():
        own_x.start()
        own_f.start()

    @pl.when(jnp.logical_not(is_a))
    def _():
        to_head.start()
        to_head_f.start()

    own_w = pltpu.make_async_copy(wqk.at[w], WQK.at[w], loc.at[0])
    own_s = pltpu.make_async_copy(small, SM.at[w], loc.at[1])
    own_w.start()
    own_s.start()
    own_v = pltpu.make_async_copy(wf.at[w % 2], WF.at[w], loc.at[2])
    own_v.start()
    sends_w, sends_v, sends_s = [], [], []
    for k in range(1, nw):
        d = rel(k)
        s = remote(small, SM.at[w], sw.at[k, 0], rs.at[w], (d, c))
        s.start()
        q = remote(wqk.at[d], WQK.at[w], sw.at[k, 1], rw.at[w], (d, c))
        q.start()
        v = remote(wf.at[d % 2], WF.at[w], sw.at[k, 2], rv.at[w], (d, c))
        sends_w += [s, q]
        sends_v.append((d, v))

        @pl.when(d < 2)
        def _():
            v.start()

    def block_x(b):
        return pltpu.make_async_copy(X.at[b], X.at[b], rx.at[b])

    def block_f(b):
        return pltpu.make_async_copy(Fv.at[b], Fv.at[b], rf.at[b])

    fwd_core, fwd_other, fwd_member = [], [], []
    for k in range(nw):
        gp = (g + k) % nw
        b = gp * G + m
        to_core = remote(X.at[b], X.at[b], sx.at[0, b], rx.at[b], (core, c))
        to_other = remote(X.at[b], X.at[b], sx.at[1, b], rx.at[b], (other, c))
        to_core_f = remote(Fv.at[b], Fv.at[b], sfx.at[0, b], rf.at[b], (core, c))
        to_other_f = remote(Fv.at[b], Fv.at[b], sfx.at[1, b], rf.at[b], (other, c))
        members = [
            remote(X.at[b], X.at[b], sx.at[1 + e, b], rx.at[b], (w, g * G + (m + e) % G))
            for e in range(1, G)
        ]
        members_f = [
            remote(Fv.at[b], Fv.at[b], sfx.at[1 + e, b], rf.at[b], (w, g * G + (m + e) % G))
            for e in range(1, G)
        ]

        @pl.when(primary)
        def _():
            block_x(b).wait()

            @pl.when(is_a)
            def _():
                to_other.start()

            for r in members:
                r.start()
            to_core.start()

        @pl.when(jnp.logical_and(is_a, jnp.logical_not(high)))
        def _():
            block_f(b).wait()
            to_other_f.start()

        @pl.when(jnp.logical_and(primary, high))
        def _():
            block_f(b).wait()
            for r in members_f:
                r.start()
            to_core_f.start()

        fwd_core.append((to_core, to_core_f))
        fwd_other.append((to_other, to_other_f))
        fwd_member.append((members, members_f))
    for e in range(1, G):
        for k in range(nw):
            b = ((g + k) % nw) * G + (m + e) % G
            to_core = remote(X.at[b], X.at[b], sx.at[0, b], rx.at[b], (core, c))
            to_core_f = remote(Fv.at[b], Fv.at[b], sfx.at[0, b], rf.at[b], (core, c))

            @pl.when(primary)
            def _():
                block_x(b).wait()
                to_core.start()

            @pl.when(jnp.logical_and(primary, high))
            def _():
                block_f(b).wait()
                to_core_f.start()

            fwd_core.append((to_core, to_core_f))

    @pl.when(jnp.logical_not(primary))
    def _():
        for b in range(nc):
            block_x(b).wait()

        @pl.when(high)
        def _():
            for b in range(nc):
                block_f(b).wait()

    own_w.wait()
    own_s.wait()
    own_v.wait()
    for k in range(1, nw):
        src = (w + nw - k) % nw
        pltpu.make_async_copy(wqk.at[0], WQK.at[src], rw.at[src]).wait()
        pltpu.make_async_copy(small, SM.at[src], rs.at[src]).wait()

        @pl.when(w < 2)
        def _():
            pltpu.make_async_copy(wf.at[0], WF.at[src], rv.at[src]).wait()

    for s in sends_w:
        s.wait_send()
    for d, v in sends_v:

        @pl.when(d < 2)
        def _():
            v.wait_send()

    @pl.when(jnp.logical_not(is_a))
    def _():
        to_head.wait_send()
        to_head_f.wait_send()

    @pl.when(primary)
    def _():
        for a, _f in fwd_core:
            a.wait_send()
        for ms, _f in fwd_member:
            for a in ms:
                a.wait_send()

        @pl.when(high)
        def _():
            for _x, a in fwd_core:
                a.wait_send()
            for _x, ms in fwd_member:
                for a in ms:
                    a.wait_send()

    @pl.when(is_a)
    def _():
        for a, _f in fwd_other:
            a.wait_send()

        @pl.when(jnp.logical_not(high))
        def _():
            for _x, a in fwd_other:
                a.wait_send()


def gather(nw, G, x, first, wqk, wf, small):
    nc = nw * G
    rows, width = x.shape
    half = first.shape[1]
    d = width // nw
    dma = pltpu.SemaphoreType.DMA
    return pl.pallas_call(
        functools.partial(gather_kernel, nw, G),
        name="gather_tokens",
        out_shape=(
            jax.ShapeDtypeStruct((nc, rows, width), BF),
            jax.ShapeDtypeStruct((nc, rows, half), BF),
            jax.ShapeDtypeStruct((nw, d, 2 * d), BF),
            jax.ShapeDtypeStruct((nw, d, d), BF),
            jax.ShapeDtypeStruct((nw,) + small.shape, BF),
        ),
        in_specs=[ANY] * 5,
        out_specs=[ANY] * 5,
        scratch_shapes=[
            dma((nc,)),
            dma((nc,)),
            dma((nw,)),
            dma((nw,)),
            dma((nw,)),
            dma((2,)),
            dma((1 + G, nc)),
            dma((2,)),
            dma((1 + G, nc)),
            dma((nw, 3)),
            dma((3,)),
        ],
        compiler_params=pltpu.CompilerParams(collective_id=0, has_side_effects=True),
    )(x, first, wqk, wf, small)


def middle_kernel(
    T, G, crossed, p_hbm, X_hbm, cot_hbm, o_hbm, wup_hbm, wdn_hbm, wout_hbm, vec_hbm,
    mlp, mid_own, dmid_own, do_out, gup, gdn, gout, sums,
    p, x, cot, o, wup, wdn, wout, vec,
    b1, ab, b2, bs, mid, n2s, act, dus, q, b4, ab2, b5, dn, dbs,
    s1, r1, s2, r2, s3, r3, s4, r4, s5, r5, s6, r6, ld,
):
    w = lax.axis_index("wt")
    c = lax.axis_index("ctx")
    g = c // G
    m = c % G
    core = (w + 1 - 2 * (w % 2), c)
    other = ((w + 2) % 4, c)
    mine = w % 2
    theirs = 1 - mine
    rows = p.shape[0]
    half = rows // 2
    n = half // T
    R = rows // 4
    loads = [
        pltpu.make_async_copy(p_hbm, p, ld.at[0]),
        pltpu.make_async_copy(vec_hbm, vec, ld.at[1]),
    ]
    loads += [
        pltpu.make_async_copy(X_hbm.at[a * G + m], x.at[pl.ds(a * R, R)], ld.at[2 + a])
        for a in range(4)
    ]
    loads += [
        pltpu.make_async_copy(wup_hbm, wup, ld.at[6]),
        pltpu.make_async_copy(wdn_hbm, wdn, ld.at[7]),
        pltpu.make_async_copy(cot_hbm, cot, ld.at[8]),
        pltpu.make_async_copy(wout_hbm, wout, ld.at[9]),
        pltpu.make_async_copy(o_hbm, o, ld.at[10]),
    ]
    for copy in loads:
        copy.start()
    greet([core, other])

    def rs(base, t):
        return pl.ds(pl.multiple_of(base * half + t * n, n), n)

    loads[0].wait()
    first = []
    for t in range(T):
        r = remote(p.at[rs(theirs, t)], b1.at[t], s1.at[t], r1.at[t], core)
        r.start()
        first.append(r)
    second = []
    for t in range(T):
        first[t].wait_recv()
        ab[t] = (p[rs(mine, t), :].astype(F32) + b1[t].astype(F32)).astype(BF)
        r = remote(ab.at[t], b2.at[t], s2.at[t], r2.at[t], other)
        r.start()
        second.append(r)
    for copy in loads[1:]:
        copy.wait()
    out_b = vec[0:1, :]
    gain = vec[1:2, :]
    shift = vec[2:3, :]
    up_b = vec[3:4, :]
    sums[...] = jnp.zeros_like(sums)

    def two(ref, t):
        return jnp.concatenate([ref[rs(mine, t), :], ref[rs(theirs, t), :]], axis=0)

    def put(ref, t, value):
        ref[rs(mine, t), :] = value[:n]
        ref[rs(theirs, t), :] = value[n:]

    def add_sum(at, value):
        sums[at : at + 1, :] += jnp.sum(value, axis=0, keepdims=True)

    def chain(t):
        pltpu.make_async_copy(b4.at[t], b4.at[t], r4.at[t]).wait()
        ab2[t] = (q[rs(mine, t), :].astype(F32) + b4[t].astype(F32)).astype(BF)
        remote(ab2.at[t], b5.at[t], s5.at[t], r5.at[t], other).start()

    def forward(t, carry):
        pltpu.make_async_copy(b2.at[t], b2.at[t], r2.at[t]).wait()
        bs[rs(mine, t), :] = (ab[t].astype(F32) + b2[t].astype(F32)).astype(BF)
        remote(bs.at[rs(mine, t)], bs.at[rs(mine, t)], s3.at[t], r3.at[t], core).start()

        @pl.when(t > 0)
        def _():
            chain(t - 1)

        pltpu.make_async_copy(bs.at[rs(theirs, t)], bs.at[rs(theirs, t)], r3.at[t]).wait()
        value = two(x, t).astype(F32) + two(bs, t).astype(F32) + out_b
        put(mid, t, value)
        centred = value - jnp.mean(value, axis=-1, keepdims=True)
        inverse = lax.rsqrt(jnp.mean(centred * centred, axis=-1, keepdims=True) + EPS)
        n2 = (centred * inverse * gain + shift).astype(BF)
        put(n2s, t, n2)
        u = product(n2, wup[...]) + up_b
        th = jnp.tanh(SLOPE * (u + CUBIC * u * u * u))
        a = (0.5 * u * (1.0 + th)).astype(BF)
        slope = 0.5 * (1.0 + th) + 0.5 * u * (1.0 - th * th) * SLOPE * (1.0 + 3.0 * CUBIC * u * u)
        put(act, t, a)
        ct = two(cot, t)
        du = (product_right(ct, wdn[...]) * slope).astype(BF)
        put(dus, t, du)
        put(q, t, product_right(du, wup[...]).astype(BF))
        remote(q.at[rs(theirs, t)], b4.at[t], s4.at[t], r4.at[t], core).start()
        put(mlp, t, product(a, wdn[...]).astype(BF))
        add_sum(0, du.astype(F32))
        add_sum(1, ct.astype(F32))
        return carry

    lax.fori_loop(0, T, forward, 0)
    chain(T - 1)

    width = p.shape[1]
    tile = 256

    def grads(i, carry):
        at = pl.ds(pl.multiple_of(i * tile, tile), tile)
        gup[at, :] = product_left(n2s[:, at], dus[...]).astype(BF)
        gdn[at, :] = product_left(act[:, at], cot[...]).astype(BF)
        return carry

    lax.fori_loop(0, width // tile, grads, 0)
    def backward(t, carry):
        pltpu.make_async_copy(b5.at[t], b5.at[t], r5.at[t]).wait()
        dn[rs(mine, t), :] = (ab2[t].astype(F32) + b5[t].astype(F32)).astype(BF)
        remote(dn.at[rs(mine, t)], dn.at[rs(mine, t)], s6.at[t], r6.at[t], core).start()
        pltpu.make_async_copy(dn.at[rs(theirs, t)], dn.at[rs(theirs, t)], r6.at[t]).wait()
        value = two(mid, t)
        centred = value - jnp.mean(value, axis=-1, keepdims=True)
        inverse = lax.rsqrt(jnp.mean(centred * centred, axis=-1, keepdims=True) + EPS)
        normal = centred * inverse
        dn2 = two(dn, t).astype(F32)
        add_sum(3, dn2 * normal)
        add_sum(4, dn2)
        dx = dn2 * gain
        dx = dx - jnp.mean(dx, axis=-1, keepdims=True) - normal * jnp.mean(
            dx * normal, axis=-1, keepdims=True
        )
        dmid = two(cot, t).astype(F32) + inverse * dx
        db = dmid.astype(BF)
        put(dbs, t, db)
        add_sum(2, db.astype(F32))
        put(do_out, t, product_right(db, wout[...]).astype(BF))
        return carry

    lax.fori_loop(0, T, backward, 0)
    gout[...] = product_left(o[...], dbs[...]).astype(BF)
    block_at = 2 * (w % 2) + w // 2 if crossed else w
    own = pl.ds(pl.multiple_of(block_at * R, R), R)
    mid_own[...] = mid[own, :]
    dmid_own[...] = dbs[own, :]
    for t in range(T):
        first[t].wait_send()
        second[t].wait_send()
        remote(bs.at[rs(mine, t)], bs.at[rs(mine, t)], s3.at[t], r3.at[t], core).wait_send()
        remote(q.at[rs(theirs, t)], b4.at[t], s4.at[t], r4.at[t], core).wait_send()
        remote(ab2.at[t], b5.at[t], s5.at[t], r5.at[t], other).wait_send()
        remote(dn.at[rs(mine, t)], dn.at[rs(mine, t)], s6.at[t], r6.at[t], core).wait_send()


def middle(G, crossed, p, X, cot, o, wup, wdn, wout, vec):
    T = 4
    rows, width = p.shape
    n = rows // 2 // T
    R = rows // 4
    d = o.shape[1]
    dma = pltpu.SemaphoreType.DMA
    full = pltpu.VMEM((rows, width), BF)
    part = pltpu.VMEM((T, n, width), BF)
    square = pltpu.VMEM((width, width), BF)
    return pl.pallas_call(
        functools.partial(middle_kernel, T, G, crossed),
        name="middle",
        out_shape=(
            jax.ShapeDtypeStruct((rows, width), BF),
            jax.ShapeDtypeStruct((R, width), F32),
            jax.ShapeDtypeStruct((R, width), BF),
            jax.ShapeDtypeStruct((rows, d), BF),
            jax.ShapeDtypeStruct((width, width), BF),
            jax.ShapeDtypeStruct((width, width), BF),
            jax.ShapeDtypeStruct((d, width), BF),
            jax.ShapeDtypeStruct((8, width), F32),
        ),
        in_specs=[ANY] * 8,
        out_specs=[VM] * 8,
        scratch_shapes=[
            full, full, full, pltpu.VMEM((rows, d), BF), square, square,
            pltpu.VMEM((d, width), BF), pltpu.VMEM((8, width), F32),
            part, part, part, full, pltpu.VMEM((rows, width), F32), full, full, full, full,
            part, part, part, full, full,
        ]
        + [dma((T,))] * 12
        + [dma((11,))],
        compiler_params=pltpu.CompilerParams(
            collective_id=1, has_side_effects=True, vmem_limit_bytes=62 << 20
        ),
        cost_estimate=pl.CostEstimate(
            flops=14 * rows * width * width, bytes_accessed=40 << 20, transcendentals=rows * width
        ),
    )(p, X, cot, o, wup, wdn, wout, vec)


def scatter_kernel(G, D, out, b1, ab, b2, st, b3, s1, r1, s2, r2, s3, r3):
    w = lax.axis_index("wt")
    c = lax.axis_index("ctx")
    g = c // G
    m = c % G
    core = w + 1 - 2 * (w % 2)
    other = (w + 2) % 4
    par = w % 2
    hi = w // 2
    greet([(core, c), (other, c)] + [(w, g * G + (m + e) % G) for e in range(1, G)])
    order = [e for e in range(1, G)] + [0]
    firsts = {}
    for j in (1, 0):
        for e in order:
            jj = (hi + j) % 2
            mm = (m + e) % G
            b = (2 * jj + 1 - par) * G + mm
            slot = jj * G + mm
            r = remote(D.at[b], b1.at[slot], s1.at[slot], r1.at[slot], (core, c))
            r.start()
            firsts[(j, e)] = r

    def arrived1(slot):
        pltpu.make_async_copy(b1.at[slot], b1.at[slot], r1.at[slot]).wait()

    seconds = []
    for e in order:
        jj = 1 - hi
        mm = (m + e) % G
        slot = jj * G + mm
        arrived1(slot)
        ab[mm] = (D[(2 * jj + par) * G + mm].astype(F32) + b1[slot].astype(F32)).astype(BF)
        r = remote(ab.at[mm], b2.at[mm], s2.at[mm], r2.at[mm], (other, c))
        r.start()
        seconds.append(r)
    thirds = []
    for e in order:
        mm = (m + e) % G
        slot = hi * G + mm
        arrived1(slot)
        pltpu.make_async_copy(b2.at[mm], b2.at[mm], r2.at[mm]).wait()
        total = D[w * G + mm].astype(F32) + b1[slot].astype(F32) + b2[mm].astype(F32)
        if e == 0:
            for f in range(1, G):
                q = (m + f) % G
                pltpu.make_async_copy(b3.at[q], b3.at[q], r3.at[q]).wait()
                total = total + b3[q].astype(F32)
            out[...] = total.astype(out.dtype)
        else:
            st[mm] = total.astype(BF)
            r = remote(st.at[mm], b3.at[m], s3.at[mm], r3.at[m], (w, g * G + mm))
            r.start()
            thirds.append(r)
    for r in list(firsts.values()) + seconds + thirds:
        r.wait_send()


def scatter_sum(G, D):
    nc, rows, C = D.shape
    dma = pltpu.SemaphoreType.DMA
    return pl.pallas_call(
        functools.partial(scatter_kernel, G),
        name="scatter_sum",
        out_shape=jax.ShapeDtypeStruct((rows, C), F32),
        in_specs=[VM],
        out_specs=VM,
        scratch_shapes=[
            pltpu.VMEM((2 * G, rows, C), BF),
            pltpu.VMEM((G, rows, C), BF),
            pltpu.VMEM((G, rows, C), BF),
            pltpu.VMEM((G, rows, C), BF),
            pltpu.VMEM((G, rows, C), BF),
            dma((2 * G,)),
            dma((2 * G,)),
            dma((G,)),
            dma((G,)),
            dma((G,)),
            dma((G,)),
        ],
        compiler_params=pltpu.CompilerParams(
            collective_id=3, has_side_effects=True, vmem_limit_bytes=60 << 20
        ),
    )(D)


def head_mask(shape, h):
    lane = lax.broadcasted_iota(jnp.int32, shape, 1)
    return jnp.logical_and(lane >= h * HEAD_DIM, lane < (h + 1) * HEAD_DIM)


def split_heads(H, value):
    zero = jnp.zeros_like(value)
    return [jnp.where(head_mask(value.shape, h), value, zero) for h in range(H)]


def spread(H, shape, values):
    out = jnp.broadcast_to(values[H - 1], shape)
    for h in range(H - 2, -1, -1):
        out = jnp.where(head_mask(shape, h), values[h], out)
    return out


def attend_tile(H, q, k_ref, v_ref, bias_ref, at_bias, chunks=None):
    rows, width = q.shape
    N = k_ref.shape[0]
    step_keys = min(N, 1024)
    qh = split_heads(H, q * jnp.asarray(HEAD_DIM**-0.5, BF))
    top_half = lax.broadcasted_iota(jnp.int32, (rows, 1), 0) < BLK

    def step(j, carry):
        tops, sums, acc = carry
        at = pl.ds(pl.multiple_of(j * step_keys, step_keys), step_keys)
        kc = k_ref[at, :]
        vc = v_ref[at, :]
        low = bias_ref[at_bias, :, at]
        high = bias_ref[at_bias + 1, :, at]
        new_tops, new_sums, shrink, parts = [], [], [], []
        for h in range(H):
            s = product_right(qh[h], kc)
            s = jnp.concatenate([s[:BLK] + low, s[BLK:] + high], axis=0)
            top = jnp.maximum(tops[h], jnp.max(s, axis=1, keepdims=True))
            a = jnp.exp(tops[h] - top)
            p = jnp.exp(s - top)
            new_sums.append(sums[h] * a + jnp.sum(p, axis=1, keepdims=True))
            new_tops.append(top)
            shrink.append(a)
            parts.append(product(p.astype(BF), vc))
        acc = acc * spread(H, acc.shape, shrink) + spread(H, acc.shape, parts)
        return new_tops, new_sums, acc

    start = (
        [jnp.full((rows, 1), NEG, F32)] * H,
        [jnp.zeros((rows, 1), F32)] * H,
        jnp.zeros((rows, width), F32),
    )
    chunks = N // step_keys if chunks is None else chunks
    tops, sums, acc = lax.fori_loop(0, chunks, step, start)
    out = (acc / spread(H, acc.shape, sums)).astype(BF)
    lse = []
    for h in range(H):
        column = tops[h] + jnp.log(sums[h])
        lse.append(jnp.transpose(jnp.broadcast_to(column, (rows, BLK)))[0:1, :])
    lse = jnp.concatenate(lse + [jnp.zeros((8 - H, rows), F32)], axis=0)
    return out, lse


def attend_kernel(H, qpos, q_ref, k_ref, v_ref, bias_ref, o_ref, lse_ref):
    o, lse = attend_tile(H, q_ref[...], k_ref, v_ref, bias_ref, 2 * pl.program_id(0))
    o_ref[...] = o
    lse_ref[0] = lse


def attend(H, qpos, bias, q, k, v):
    n = qpos.shape[0]
    width = H * HEAD_DIM
    N = k.shape[0]
    rows = 2 * BLK
    whole = pl.BlockSpec((N, width), lambda i, *_: (0, 0))
    return pl.pallas_call(
        functools.partial(attend_kernel, H),
        name="attend",
        out_shape=(
            jax.ShapeDtypeStruct((n * rows, width), BF),
            jax.ShapeDtypeStruct((n, 8, rows), F32),
        ),
        grid_spec=pltpu.PrefetchScalarGridSpec(
            num_scalar_prefetch=1,
            grid=(n,),
            in_specs=[
                pl.BlockSpec((rows, width), lambda i, qp: (qp[i], 0)),
                whole,
                whole,
                pl.BlockSpec((2 * n, 1, N), lambda i, *_: (0, 0, 0)),
            ],
            out_specs=[
                pl.BlockSpec((rows, width), lambda i, *_: (i, 0)),
                pl.BlockSpec((1, 8, rows), lambda i, *_: (i, 0, 0)),
            ],
        ),
        compiler_params=pltpu.CompilerParams(vmem_limit_bytes=48 << 20),
    )(qpos, q, k, v, bias)


def attend_back_tile(
    H, q, do, o, lse, k_ref, v_ref, kt, dk, dv, lift_ref, tile, chunks=None, poll=None
):
    rows, width = q.shape
    N = k_ref.shape[0]
    scale = HEAD_DIM**-0.5
    qh = split_heads(H, q * jnp.asarray(scale, BF))
    doh = split_heads(H, do)
    qcat = jnp.concatenate(qh, axis=0)
    docat = jnp.concatenate(doh, axis=0)
    pick = lax.broadcasted_iota(jnp.int32, (8, width), 1)
    base = lax.broadcasted_iota(jnp.int32, (8, width), 0) * HEAD_DIM
    pick = jnp.logical_and(pick >= base, pick < base + HEAD_DIM).astype(F32)
    delta = lax.dot_general(
        pick,
        do.astype(F32) * o.astype(F32),
        (((1,), (1,)), ((), ())),
        precision=lax.Precision.HIGHEST,
        preferred_element_type=F32,
    )

    def step(j, dqt):
        at = pl.ds(pl.multiple_of(j * CHUNK, CHUNK), CHUNK)
        kc = k_ref[at, :]
        vc = v_ref[at, :]
        ps, dss, dqs = [], [], []
        for h in range(H):
            s = product_right(kc, qh[h])
            dp = product_right(vc, doh[h])
            pieces, dpieces = [], []
            for b in range(CHUNK // BLK):
                lift = lift_ref[tile, pl.ds(j * (CHUNK // BLK) + b, 1), :]
                cut = slice(b * BLK, (b + 1) * BLK)
                p = jnp.exp(s[cut] - (lse[h : h + 1, :] + lift))
                pieces.append(p.astype(BF))
                dpieces.append((p * (dp[cut] - delta[h : h + 1, :])).astype(BF))
            p = jnp.concatenate(pieces, axis=0)
            ds = jnp.concatenate(dpieces, axis=0)
            ps.append(p)
            dss.append(ds)
            dqs.append(product(kt[h * HEAD_DIM : (h + 1) * HEAD_DIM, at], ds))
        dv[at, :] += product(jnp.concatenate(ps, axis=1), docat)
        dk[at, :] += product(jnp.concatenate(dss, axis=1), qcat)
        if poll is not None:
            poll(j)
        return dqt + jnp.concatenate(dqs, axis=0)

    chunks = N // CHUNK if chunks is None else chunks
    dqt = lax.fori_loop(0, chunks, step, jnp.zeros((width, rows), F32))
    return dqt * scale


def flip_rows(src, dst):
    def flip(b, carry):
        at = pl.ds(pl.multiple_of(b * BLK, BLK), BLK)
        dst[:, at] = jnp.transpose(src[at, :])
        return carry

    lax.fori_loop(0, src.shape[0] // BLK, flip, 0)


def attend_back_kernel(
    H, qpos, q_ref, k_ref, v_ref, o_ref, do_ref, lse_ref, lift_ref, dqk_ref, dv_ref, kt, dk, dv
):
    i = pl.program_id(0)
    width = H * HEAD_DIM

    @pl.when(i == 0)
    def _():
        flip_rows(k_ref, kt)
        dk[...] = jnp.zeros_like(dk)
        dv[...] = jnp.zeros_like(dv)
        dqk_ref[...] = jnp.zeros_like(dqk_ref)

    dqt = attend_back_tile(
        H, q_ref[...], do_ref[...], o_ref[...], lse_ref[0], k_ref, v_ref, kt, dk, dv, lift_ref, i
    )
    rows = 2 * BLK
    here = pl.ds(pl.multiple_of(qpos[i] * rows, rows), rows)
    dqk_ref[here, 0:width] = jnp.transpose(dqt).astype(BF)

    @pl.when(i == pl.num_programs(0) - 1)
    def _():
        dqk_ref[:, width : 2 * width] = dk[...].astype(BF)
        dv_ref[...] = dv[...].astype(BF)


def attend_back(H, qpos, lift, q, k, v, o, do, lse):
    n = qpos.shape[0]
    width = H * HEAD_DIM
    N = k.shape[0]
    rows = 2 * BLK
    whole = pl.BlockSpec((N, width), lambda i, *_: (0, 0))
    row = pl.BlockSpec((rows, width), lambda i, *_: (i, 0))
    return pl.pallas_call(
        functools.partial(attend_back_kernel, H),
        name="attend_back",
        out_shape=(
            jax.ShapeDtypeStruct((N, 2 * width), BF),
            jax.ShapeDtypeStruct((N, width), BF),
        ),
        grid_spec=pltpu.PrefetchScalarGridSpec(
            num_scalar_prefetch=1,
            grid=(n,),
            in_specs=[
                pl.BlockSpec((rows, width), lambda i, qp: (qp[i], 0)),
                whole,
                whole,
                row,
                row,
                pl.BlockSpec((1, 8, rows), lambda i, *_: (i, 0, 0)),
                pl.BlockSpec((n, N // BLK, rows), lambda i, *_: (0, 0, 0)),
            ],
            out_specs=[
                pl.BlockSpec((N, 2 * width), lambda i, *_: (0, 0)),
                pl.BlockSpec((N, width), lambda i, *_: (0, 0)),
            ],
            scratch_shapes=[
                pltpu.VMEM((width, N), BF),
                pltpu.VMEM((N, width), F32),
                pltpu.VMEM((N, width), F32),
            ],
        ),
        compiler_params=pltpu.CompilerParams(vmem_limit_bytes=60 << 20),
    )(qpos, q, k, v, o, do, lse, lift)


def head_kernel(
    G, H,
    deal, out_b, gain_one, shift_one, gain_two, shift_two, down_b, up_b, qv_b,
    x_h, first_h, wqkv_h, cot_h, wup_h, wout_h,
    X_o, xh_o, k_o, v_o, wup_o, cot_o, q, o, lse, part, wqk, wf, vec,
    X, Fv, xh, k, v, small, vq, bias, wout, wl, wqk_h, wf_h, Y, line, small_l,
    rx, rf, rw, rv, rs, rc, ru, sh, sx, sf, sw, sc, su, loc, out, ry, sy,
):
    nw = 4
    w = lax.axis_index("wt")
    c = lax.axis_index("ctx")
    g = c // G
    m = c % G
    nc = nw * G
    R, width = x_h.shape
    d = width // nw
    par = w % 2
    core = (w + 1 - 2 * par, c)
    seq = 2 * (g % 2) + g // 2
    og = 2 * par + w // 2
    goal = og * G + m
    two = (w + 2) % nw
    goal_two = (2 * par + two // 2) * G + m
    is_a = w == seq
    primary = (w + seq) % 2 == 0
    high = w >= 2
    low = w < 2
    peers = [
        ((w + a) % nw, ((g + e) % nw) * G + m) for a in range(nw) for e in range(nw) if a or e
    ]
    peers += [(w, g * G + (m + e) % G) for e in range(1, G)]
    loads = [
        pltpu.make_async_copy(a, b, loc.at[i])
        for i, (a, b) in enumerate(((wqkv_h, wl), (wout_h, wout)))
    ]
    for copy in loads:
        copy.start()
    greet(peers)

    here = goal == c
    here_two = goal_two == c
    to_y = remote(x_h, Y, sh.at[0], ry.at[0], (two, c))
    to_one = remote(x_h, X.at[c], sh.at[1], rx.at[c], (w, goal))
    to_two = remote(Y, X.at[c], sh.at[4], rx.at[c], (w, goal_two))
    to_first = remote(first_h, Fv.at[c], sh.at[2], rf.at[c], (w, goal))
    home_cot = jnp.logical_and(here, is_a)
    own_cot = pl.ds(pl.multiple_of(g * R, R), R)
    to_cot = remote(cot_h, cot_o.at[own_cot], sh.at[3], rc.at[g], (seq, goal))
    to_y.start()

    @pl.when(here)
    def _():
        pltpu.make_async_copy(x_h, X.at[c], rx.at[c]).start()
        pltpu.make_async_copy(first_h, Fv.at[c], rf.at[c]).start()

    @pl.when(jnp.logical_not(here))
    def _():
        to_one.start()
        to_first.start()

    line[...] = jnp.zeros_like(line)
    for a, ref in enumerate((out_b, gain_one, shift_one, gain_two, shift_two, down_b)):
        at = a // 2
        line[at : at + 1, (a % 2) * d : (a % 2 + 1) * d] = ref[...].astype(F32).reshape(1, d)
    for a in range(2):
        half = up_b[a * 2 * d : (a + 1) * 2 * d].astype(F32).reshape(1, 2 * d)
        line[3 + a : 4 + a, :] = half
    line[5:6, : 6 * d // 4] = qv_b[...].astype(F32).reshape(1, 6 * d // 4)
    small_l[...] = line[...].astype(BF)
    loads[0].wait()
    for a in range(nw):
        for half in range(2):
            at = half * width + a * d
            wqk_h[a, :, half * d : (half + 1) * d] = wl[:, at : at + d]
    for a in range(2):
        at = 2 * width + a * d
        wf_h[a] = wl[:, at : at + d]

    def rows_of(a):
        return pl.ds(pl.multiple_of(a * d, 16), d)

    weights, fresh = [], []
    for e in range(1, nw):
        to = (w + e) % nw
        weights.append(remote(small_l, small.at[w], sw.at[e, 0], rs.at[w], (to, c)))
        weights.append(remote(wqk_h.at[to], wqk.at[rows_of(w)], sw.at[e, 1], rw.at[w], (to, c)))
        fresh.append(
            (to, remote(wf_h.at[to % 2], wf.at[rows_of(w)], sw.at[e, 2], rv.at[w], (to, c)))
        )
    for r in weights:
        r.start()
    for to, r in fresh:

        @pl.when(to < 2)
        def _():
            r.start()

    pltpu.make_async_copy(small_l, small.at[w], rs.at[w]).start()
    pltpu.make_async_copy(wqk_h.at[w], wqk.at[rows_of(w)], rw.at[w]).start()

    @pl.when(low)
    def _():
        pltpu.make_async_copy(wf_h.at[par], wf.at[rows_of(w)], rv.at[w]).start()

    @pl.when(high)
    def _():
        wf[...] = jnp.zeros_like(wf)

    def got(ref, sem):
        pltpu.make_async_copy(ref, ref, sem).wait()

    got(Y, ry.at[0])

    @pl.when(here_two)
    def _():
        pltpu.make_async_copy(Y, X.at[c], rx.at[c]).start()

    @pl.when(jnp.logical_not(here_two))
    def _():
        to_two.start()

    def core_x(b):
        return remote(X.at[b], X.at[b], sx.at[0, b], rx.at[b], core)

    def core_f(b):
        return remote(Fv.at[b], Fv.at[b], sf.at[0, b], rf.at[b], core)

    def member_x(b, e):
        return remote(X.at[b], X.at[b], sx.at[e, b], rx.at[b], (w, g * G + (m + e) % G))

    def member_f(b, e):
        return remote(Fv.at[b], Fv.at[b], sf.at[e, b], rf.at[b], (w, g * G + (m + e) % G))

    def cross_f(b):
        return remote(Fv.at[b], Fv.at[b], sy.at[b], rf.at[b], (two, c))

    crossing = jnp.logical_and(is_a, low)

    def take(b, onward):
        got(X.at[b], rx.at[b])

        if onward:

            @pl.when(crossing)
            def _():
                got(Fv.at[b], rf.at[b])
                cross_f(b).start()

        @pl.when(primary)
        def _():
            for e in range(1, G if onward else 1):
                member_x(b, e).start()
            core_x(b).start()

        @pl.when(high)
        def _():
            got(Fv.at[b], rf.at[b])

            @pl.when(primary)
            def _():
                for e in range(1, G if onward else 1):
                    member_f(b, e).start()
                core_f(b).start()

    half_rows = nc * R // 2

    def halves(ref, b, gap, value):
        ref[pl.ds(pl.multiple_of(b * BLK, BLK), BLK), :] = value[:BLK]
        ref[pl.ds(pl.multiple_of(b * BLK + gap, BLK), BLK), :] = value[BLK:]

    def project(b, a):
        at = pl.ds(pl.multiple_of(b * R, R), R)
        value = X[b].astype(F32)
        centred = value - jnp.mean(value, axis=-1, keepdims=True)
        inverse = lax.rsqrt(jnp.mean(centred * centred, axis=-1, keepdims=True) + EPS)
        normal = centred * inverse
        xh[at, :] = normal.astype(BF)
        n = (normal * vec[4:5, :] + vec[5:6, :]).astype(BF)
        qk = product(n, wqk[...])
        halves(k, b, half_rows, qk[:, d : 2 * d].astype(BF))
        if a is not None:
            halves(q, a, 2 * R, (qk[:, :d] + vq[1:2, 0:d]).astype(BF))

        @pl.when(low)
        def _():
            halves(v, b, half_rows, (product(n, wf[...]) + vq[2:3, 0:d]).astype(BF))

        @pl.when(high)
        def _():
            f = Fv[b]
            halves(v, b, half_rows, jnp.where(par == 0, f[:, :d], f[:, d:]))

    for t in range(nw):
        for e in range(2):
            own_pair = deal[(2 * (t % 2) + e) * G + m]
            for b in range(nc):
                seen = deal[b] <= own_pair if t < 2 else deal[b] >= own_pair
                at = b * BLK + (half_rows if t >= 2 else 0)
                bias[2 * t + e, :, at : at + BLK] = jnp.full(
                    (1, BLK), jnp.where(seen, 0.0, NEG), F32
                )
            if t >= 2:
                bias[2 * t + e, :, 0:half_rows] = jnp.zeros((1, half_rows), F32)
    take(g * G + m, True)
    loads[1].wait()
    for a in range(nw):
        got(small.at[a], rs.at[a])
        got(wqk.at[rows_of(a)], rw.at[a])

        @pl.when(low)
        def _():
            got(wf.at[rows_of(a)], rv.at[a])

    nb = 6 * d // 4
    for a in range(nw):
        piece = small[a].astype(F32)
        for row, src in ((0, 0), (1, 3), (2, 4), (4, 1), (5, 2), (6, 5)):
            at = src // 2
            value = piece[at : at + 1, (src % 2) * d : (src % 2 + 1) * d]
            vec[row : row + 1, a * d : (a + 1) * d] = value
        vq[0:1, a * nb : (a + 1) * nb] = piece[5:6, :nb]
    piece = small[w].astype(F32)
    vec[3:4, : 2 * d] = piece[3:4, :]
    vec[3:4, 2 * d :] = piece[4:5, :]
    vec[7:8, :] = jnp.zeros((1, width), F32)
    q_bias = vq[0:1, 0:d]
    for a in range(1, nw):
        q_bias = jnp.where(w == a, vq[0:1, a * d : (a + 1) * d], q_bias)
    f_bias = jnp.where(
        par == 0, vq[0:1, width : width + d], vq[0:1, width + d : width + 2 * d]
    )
    vq[1:2, 0:d] = q_bias
    vq[2:3, 0:d] = f_bias
    project(g * G + m, g)

    def own(i, carry):
        a = (g + i) % nw
        take(a * G + m, True)
        project(a * G + m, a)
        return carry

    lax.fori_loop(1, nw, own, 0)

    @pl.when(home_cot)
    def _():
        pltpu.make_async_copy(cot_h, cot_o.at[own_cot], rc.at[g]).start()

    @pl.when(jnp.logical_not(home_cot))
    def _():
        to_cot.start()

    ups = []
    for e in range(1, nw):
        to = (w + e) % nw
        src = wup_h.at[:, pl.ds(pl.multiple_of(to * width, BLK), width)]
        ups.append(remote(src, wup_o.at[rows_of(w)], su.at[e], ru.at[w], (to, c)))
    for r in ups:
        r.start()
    src = wup_h.at[:, pl.ds(pl.multiple_of(w * width, BLK), width)]
    pltpu.make_async_copy(src, wup_o.at[rows_of(w)], ru.at[w]).start()

    def others(i, carry):
        b = ((g + i % nw) % nw) * G + (m + 1 + i // nw) % G
        take(b, False)
        project(b, None)
        return carry

    lax.fori_loop(0, nw * (G - 1), others, 0)
    outs = [(X, X_o), (xh, xh_o), (k, k_o), (v, v_o)]
    outs = [pltpu.make_async_copy(a, b, out.at[i]) for i, (a, b) in enumerate(outs)]
    for copy in outs:
        copy.start()

    def cot_rows(a):
        return cot_o.at[pl.ds(pl.multiple_of(a * R, R), R)]

    og_two = 2 * par + two // 2
    spread_cot = [
        remote(cot_rows(og), cot_rows(og), sc.at[0], rc.at[og], (two, c)),
        remote(cot_rows(og), cot_rows(og), sc.at[1], rc.at[og], core),
        remote(cot_rows(og_two), cot_rows(og_two), sc.at[2], rc.at[og_two], core),
    ]
    got(cot_rows(og), rc.at[og])
    spread_cot[0].start()
    spread_cot[1].start()

    def attend_one(t, carry):
        at = pl.ds(pl.multiple_of(t * R, R), R)
        ot, lt = attend_tile(H, q[at, :], k, v, bias, 2 * t, 1 + t // 2)
        lse[t] = lt
        pt = product(ot, wout[...]).astype(BF)
        for e in range(2):
            to = (2 * (t % 2) + e) * R + (t // 2) * BLK
            to = pl.ds(pl.multiple_of(to, BLK), BLK)
            o[to, :] = ot[e * BLK : (e + 1) * BLK]
            part[to, :] = pt[e * BLK : (e + 1) * BLK]
        return carry

    lax.fori_loop(0, nw, attend_one, 0)

    got(cot_rows(og_two), rc.at[og_two])
    spread_cot[2].start()
    for copy in outs:
        copy.wait()
    for a in range(nw):
        got(wup_o.at[rows_of(a)], ru.at[a])

    for hi in range(2):
        a = 2 * (1 - par) + hi
        got(cot_rows(a), rc.at[a])

    for r in weights + ups + spread_cot + [to_y]:
        r.wait_send()
    for to, r in fresh:

        @pl.when(to < 2)
        def _():
            r.wait_send()

    @pl.when(jnp.logical_not(here))
    def _():
        to_one.wait_send()
        to_first.wait_send()

    @pl.when(jnp.logical_not(here_two))
    def _():
        to_two.wait_send()

    @pl.when(crossing)
    def _():
        for a in range(nw):
            cross_f(a * G + m).wait_send()

    @pl.when(jnp.logical_not(home_cot))
    def _():
        to_cot.wait_send()

    @pl.when(primary)
    def _():

        def sent(b, carry):
            core_x(b).wait_send()

            @pl.when(b % G == m)
            def _():
                for e in range(1, G):
                    member_x(b, e).wait_send()

            @pl.when(high)
            def _():
                core_f(b).wait_send()

                @pl.when(b % G == m)
                def _():
                    for e in range(1, G):
                        member_f(b, e).wait_send()

            return carry

        lax.fori_loop(0, nc, sent, 0)


def head(G, H, deal, vectors, x, first, wqkv, cot, wup, wout):
    nw = 4
    nc = nw * G
    R, width = x.shape
    d = width // nw
    N = nc * R
    dma = pltpu.SemaphoreType.DMA
    vm = pltpu.VMEM
    shape = jax.ShapeDtypeStruct
    operands = (deal,) + vectors + (x, first, wqkv, cot, wup, wout)
    return pl.pallas_call(
        functools.partial(head_kernel, G, H),
        name="head",
        out_shape=(
            shape((nc, R, width), BF),
            shape((N, width), BF),
            shape((N, d), BF),
            shape((N, d), BF),
            shape((width, width), BF),
            shape((nw * R, width), BF),
            shape((nw * R, d), BF),
            shape((nw * R, d), BF),
            shape((nw, 8, R), F32),
            shape((nw * R, width), BF),
            shape((width, 2 * d), BF),
            shape((width, d), BF),
            shape((8, width), F32),
        ),
        in_specs=[pl.BlockSpec(memory_space=pltpu.SMEM)] + [VM] * len(vectors) + [ANY] * 6,
        out_specs=[ANY] * 6 + [VM] * 7,
        scratch_shapes=[
            vm((nc, R, width), BF), vm((nc, R, 2 * d), BF), vm((N, width), BF), vm((N, d), BF),
            vm((N, d), BF), vm((nw, 8, 2 * d), BF), vm((8, 6 * d), F32),
            vm((2 * nw, 1, N), F32), vm(wout.shape, BF), vm(wqkv.shape, BF),
            vm((nw, d, 2 * d), BF), vm((2, d, d), BF), vm((R, width), BF),
            vm((8, 2 * d), F32), vm((8, 2 * d), BF),
            dma((nc,)), dma((nc,)), dma((nw,)), dma((nw,)), dma((nw,)), dma((nw,)), dma((nw,)),
            dma((6,)), dma((G, nc)), dma((G, nc)), dma((nw, 3)), dma((nw,)), dma((nw,)),
            dma((2,)), dma((4,)), dma((1,)), dma((nc,)),
        ],
        compiler_params=pltpu.CompilerParams(
            collective_id=0, has_side_effects=True, vmem_limit_bytes=56 << 20
        ),
        cost_estimate=pl.CostEstimate(
            flops=14 << 30, bytes_accessed=40 << 20, transcendentals=6 << 20
        ),
    )(*operands)


class Ring:
    def __init__(self, nc, pos, right, left, seg, chains, A, slots, out, ss, sr):
        self.nc, self.pos, self.right, self.left, self.seg = nc, pos, right, left, seg
        self.chains, self.A, self.slots, self.out, self.ss, self.sr = chains, A, slots, out, ss, sr
        self.steps = 2 * (nc - 1)
        self.cut = A.shape[1] // chains

    def at(self, half, j):
        j = (j + 2 * self.nc) % self.nc
        return pl.ds(pl.multiple_of((half * self.nc + j) * self.seg, 16), self.seg)

    def cols(self, i):
        if self.chains == 1:
            return pl.ds(0, self.cut)
        return pl.ds(pl.multiple_of(i * self.cut, BLK), self.cut)

    def reduce_copies(self, i, s):
        k = self.cols(i)
        return [
            remote(
                self.A.at[self.at(h, j), k],
                self.slots.at[h, s, :, k],
                self.ss.at[h, i, s],
                self.sr.at[h, i, s],
                to,
            )
            for h, j, to in ((0, self.pos - s, self.right), (1, self.pos + s, self.left))
        ]

    def gather_copies(self, i, s):
        k = self.cols(i)
        t = s - (self.nc - 1)
        return [
            remote(
                self.out.at[self.at(h, j), k],
                self.out.at[self.at(h, j), k],
                self.ss.at[h, i, s],
                self.sr.at[h, i, s],
                to,
            )
            for h, j, to in ((0, self.pos + 1 - t, self.right), (1, self.pos - 1 + t, self.left))
        ]

    def send(self, i, s, gathering=False):
        for r in (self.gather_copies if gathering else self.reduce_copies)(i, s):
            r.start()

    def begin(self):
        for i in range(self.chains):
            self.send(i, 0)

    def add(self, i, s):
        k = self.cols(i)
        for h, j in ((0, self.pos - s - 1), (1, self.pos + s + 1)):
            at = self.at(h, j)
            slot = self.slots.at[h, s, :, k]
            pltpu.make_async_copy(slot, slot, self.sr.at[h, i, s]).wait()
            value = self.A[at, k].astype(F32) + self.slots[h, s, :, k].astype(F32)
            self.A[at, k] = value.astype(BF)

    def keep(self, i):
        k = self.cols(i)
        for h, j in ((0, self.pos + 1), (1, self.pos - 1)):
            self.out[self.at(h, j), k] = self.A[self.at(h, j), k]

    def arrive(self, i, s):
        t = s - (self.nc - 1)
        for h, j in ((0, self.pos - t), (1, self.pos + t)):
            at = self.out.at[self.at(h, j), self.cols(i)]
            pltpu.make_async_copy(at, at, self.sr.at[h, i, s]).wait()

    def step(self, s):
        for i in range(self.chains):
            self.turn(i, s)

    def turn(self, i, s):
        last = self.nc - 2
        if isinstance(s, int):
            when = lambda cond: (lambda body: body() if cond else None)
            both = lambda a, b: a and b
        else:
            when, both = pl.when, jnp.logical_and

        @when(s < last)
        def _():
            self.add(i, s)
            self.send(i, s + 1)

        @when(s == last)
        def _():
            self.add(i, last)
            self.keep(i)
            self.send(i, last + 1, True)

        @when(both(s > last, s < self.steps))
        def _():
            self.arrive(i, s)

        @when(both(s > last, s < self.steps - 1))
        def _():
            self.send(i, s + 1, True)

    def drain(self):
        for gathering in (False, True):

            def one(t, carry):
                i, s = t % self.chains, t // self.chains
                for r in (self.gather_copies if gathering else self.reduce_copies)(i, s):
                    r.wait_send()
                return carry

            half = self.steps * self.chains // 2
            lax.fori_loop(half * gathering, half * (1 + gathering), one, 0)


class SplitRing(Ring):
    def __init__(self, nc, pos, right, left, seg, chains, A, slots, out, ss, sr, own, sems):
        super().__init__(nc, pos, right, left, seg, chains, A, slots, out, ss, sr)
        self.turns = nc - 1
        self.w, self.c = own
        self.s_ex, self.r_ex, self.s_hop, self.r_hop = sems
        self.group = nc // 2
        self.reach = (nc // 2, nc // 2 - 1)

    def turn(self, i, s):
        last = self.nc - 2
        if isinstance(s, int):
            when = lambda cond: (lambda body: body() if cond else None)
        else:
            when = pl.when

        @when(s <= last)
        def _():
            self.add(i, s)

        @when(s < last)
        def _():
            self.send(i, s + 1)

    def parts(self):
        for h, j in ((0, self.pos + 1), (1, self.pos - 1)):
            j = (j + self.nc) % self.nc
            to = 2 * h + j // self.group
            src = self.A.at[self.at(h, j)]
            dst = self.out.at[j % self.group, self.w]
            yield h, to, src, dst

    def exchange(self):
        for h, to, src, dst in self.parts():
            local = pltpu.make_async_copy(src, dst, self.r_ex.at[self.w])
            far = remote(src, dst, self.s_ex.at[h], self.r_ex.at[self.w], (to, self.c))

            @pl.when(to == self.w)
            def _():
                local.start()

            @pl.when(to != self.w)
            def _():
                far.start()

    def held(self, position):
        j = (position + 1 - 2 * (self.w // 2) + 2 * self.nc) % self.nc
        return j // self.group == self.w % 2, j % self.group

    def hop_copy(self, way, h, j):
        ref = self.out.at[j]
        to = (self.right, self.left)[way]
        return remote(ref, ref, self.s_hop.at[way, h], self.r_hop.at[way, h], to)

    def spread(self):
        have, j = self.held(self.pos)

        @pl.when(have)
        def _():
            for a in range(4):
                ref = self.out.at[j, a]
                pltpu.make_async_copy(ref, ref, self.r_ex.at[a]).wait()
            for way in range(2):
                self.hop_copy(way, 1, j).start()

    def hop(self, h):
        for way in range(2):
            if h > self.reach[way]:
                continue
            have, j = self.held(self.pos - h if way == 0 else self.pos + h)

            @pl.when(have)
            def _():
                ref = self.out.at[j]
                pltpu.make_async_copy(ref, ref, self.r_hop.at[way, h]).wait()
                if h < self.reach[way]:
                    self.hop_copy(way, h + 1, j).start()

    def drain(self):
        def one(t, carry):
            i, s = t % self.chains, t // self.chains
            for r in self.reduce_copies(i, s):
                r.wait_send()
            return carry

        lax.fori_loop(0, self.turns * self.chains, one, 0)
        for h, to, src, dst in self.parts():

            @pl.when(to != self.w)
            def _():
                remote(src, dst, self.s_ex.at[h], self.r_ex.at[self.w], (to, self.c)).wait_send()

        for way in range(2):
            for h in range(self.reach[way]):
                have, j = self.held(self.pos - h if way == 0 else self.pos + h)

                @pl.when(have)
                def _():
                    self.hop_copy(way, h + 1, j).wait_send()


def tail_kernel(
    G, H, seg_a, seg_u, seg_b,
    deal, q_h, k_h, v_h, o_h, do_h, lse_h, xh_h, X_h, wqk_h, wf_h, vec_h, dmid_h,
    up_h, down_h, gout_h, vsums, mlp_h, mid_h,
    layer_out, tokens_out, first_out, up_out, down_out, gout_out, qkv_out, rows_out,
    q, k, v, o, do, lse, lift, xh, X, wqk, wf, vec, dmid,
    kt, dk, dv, dqk, dvb, D, b1, ab, b2, st, b3, tot, tb, tr,
    A, slots_a, res_a, U, slots_u, res_u, gq, slots_b, res_b, gain_t, shift_t, sums_t, line, f1, fs, fr,
    mlp, mid, lb, ly, lr, sl, rl, sL, rL, s1, r1, s2, r2, s3, r3, sT, rT, ssa, sra, ssu, sru, seu, reu, shu, rhu, ssb, srb, seb, reb, shb, rhb, sf1, rf1, sf2, rf2, ld,
):
    w = lax.axis_index("wt")
    c = lax.axis_index("ctx")
    nw = 4
    nc = nw * G
    g = c // G
    m = c % G
    par = w % 2
    hi = w // 2
    core = (w + 1 - 2 * par, c)
    other = ((w + 2) % nw, c)
    R, width = dmid.shape
    d = width // nw
    N = xh.shape[0]
    odd = c % 2
    pos = (c // 2) * (1 - odd) + (nc - 1 - c // 2) * odd

    def ctx_at(p):
        p = (p + nc) % nc
        h = p // (nc // 2)
        return 2 * p * (1 - h) + (2 * (nc - 1 - p) + 1) * h

    right = (w, ctx_at(pos + 1))
    left = (w, ctx_at(pos - 1))
    loads = [
        (up_h, U),
        (down_h, A.at[pl.ds(0, width)]),
        (gout_h, A.at[pl.ds(width, d)]),
        (k_h, k), (v_h, v), (q_h, q), (o_h, o), (do_h, do), (lse_h, lse),
        (xh_h, xh), (X_h, X), (wqk_h, wqk), (wf_h, wf), (vec_h, vec), (dmid_h, dmid), (mid_h, mid), (mlp_h, mlp),
    ]
    loads = [pltpu.make_async_copy(a, b, ld.at[i]) for i, (a, b) in enumerate(loads)]
    for copy in loads:
        copy.start()
    peers = [
        ((w + a) % nw, ((g + e) % nw) * G + m) for a in range(nw) for e in range(nw) if a or e
    ]
    peers += [(w, g * G + (m + e) % G) for e in range(1, G)]
    greet(peers + [right, left])
    ring_a = Ring(nc, pos, right, left, seg_a, 2, A, slots_a, res_a, ssa, sra)
    ring_u = SplitRing(
        nc, pos, right, left, seg_u, 2, U, slots_u, res_u, ssu, sru, (w, c), (seu, reu, shu, rhu)
    )
    ring_b = SplitRing(
        nc, pos, right, left, seg_b, 1, gq, slots_b, res_b, ssb, srb, (w, c), (seb, reb, shb, rhb)
    )
    for copy in loads[:3]:
        copy.wait()
    foot = A.shape[0] - width - d
    line_a = jnp.concatenate([vsums[0:1, :], jnp.zeros((15, width), F32)], axis=0)
    A[width + d : width + d + 16, :] = line_a.astype(BF)
    A[width + d + 16 :, :] = jnp.zeros((foot - 16, width), BF)
    share = vsums[1:5, 0:d]
    for a in range(1, nw):
        share = jnp.where(w == a, vsums[1:5, a * d : (a + 1) * d], share)
    pack = jnp.concatenate([share[a : a + 1, :] for a in range(4)], axis=1)
    pack = jnp.concatenate([jnp.zeros((1, width), F32), pack, jnp.zeros((14, width), F32)], axis=0)
    A[width + d : width + d + 16, :] = (line_a + pack).astype(BF)
    ring_u.begin()
    ring_a.begin()
    for copy in loads[3:9] + loads[15:]:
        copy.wait()
    seq = 2 * (g % 2) + g // 2
    og = 2 * par + hi
    home = (seq, og * G + m)
    home_self = jnp.logical_and(og == g, w == seq)
    shares = []
    for e in range(1, nw):
        to = (w + e) % nw
        src = mlp.at[pl.ds(pl.multiple_of((2 * (to % 2) + to // 2) * R, R), R)]
        r = remote(src, lb.at[w], sl.at[e], rl.at[w], (to, c))
        r.start()
        shares.append(r)

    flip_rows(k, kt)
    dk[...] = jnp.zeros_like(dk)
    dv[...] = jnp.zeros_like(dv)
    dqk[...] = jnp.zeros_like(dqk)
    wide = H * HEAD_DIM

    def poll(n):
        for r in range(4):

            @pl.when(n % 4 == r)
            def _():
                (ring_a if r % 2 else ring_u).turn(r // 2, n // 4)

    pairs = lax.broadcasted_iota(jnp.int32, (1, 2 * BLK), 1) < BLK
    for t in range(nw):
        mine = [deal[(2 * (t % 2) + e) * G + m] for e in range(2)]
        for b in range(nc):
            unseen = [
                jnp.where(deal[b] <= a if t < 2 else deal[b] >= a, 0.0, -NEG) for a in mine
            ]
            at = b if t < 2 else nc + b
            lift[t, at : at + 1, :] = jnp.where(pairs, unseen[0], unseen[1])
        if t >= 2:
            lift[t, 0:nc, :] = jnp.zeros((nc, 2 * BLK), F32)

    def tile(t, carry):
        rows = []
        for e in range(2):
            at = (2 * (t % 2) + e) * R + (t // 2) * BLK
            rows.append(pl.ds(pl.multiple_of(at, BLK), BLK))
        pick = lambda ref: jnp.concatenate([ref[rows[0], :], ref[rows[1], :]], axis=0)
        mine = pl.ds(pl.multiple_of(t * R, R), R)

        def polls_at(j):
            n = 2 * (t + t // 3 + j)
            poll(n)
            poll(n + 1)

        dqt = attend_back_tile(
            H, q[mine, :], pick(do), pick(o), lse[t], k, v, kt, dk, dv, lift, t, 1 + t // 2,
            polls_at,
        )
        dq = jnp.transpose(dqt).astype(BF)
        for e in range(2):
            at = ((2 * (t % 2) + e) * G + m) * R + (t // 2) * BLK
            at = pl.ds(pl.multiple_of(at, BLK), BLK)
            dqk[at, 0:wide] = dq[e * BLK : (e + 1) * BLK]
        return carry

    lax.fori_loop(0, nw, tile, 0)

    def deal_back(b, carry):
        for e in range(2):
            src = pl.ds(pl.multiple_of(b * BLK + e * (N // 2), BLK), BLK)
            to = pl.ds(pl.multiple_of(b * R + e * BLK, BLK), BLK)
            dqk[to, wide : 2 * wide] = dk[src, :].astype(BF)
            dvb[to, :] = dv[src, :].astype(BF)
        return carry

    lax.fori_loop(0, nc, deal_back, 0)
    polls = 12
    for copy in loads[9:15]:
        copy.wait()

    layer = mid[...] + vec[6:7, :] + mlp[pl.ds(pl.multiple_of(og * R, R), R), :].astype(F32)
    for e in range(1, nw):
        src = (w + e) % nw
        pltpu.make_async_copy(lb.at[src], lb.at[src], rl.at[src]).wait()
        layer = layer + lb[src].astype(F32)
    ly[...] = layer.astype(BF)
    layer_back = remote(ly, lr, sL.at[0], rL.at[0], home)
    layer_stay = pltpu.make_async_copy(ly, lr, rL.at[0])

    @pl.when(home_self)
    def _():
        layer_stay.start()

    @pl.when(jnp.logical_not(home_self))
    def _():
        layer_back.start()

    upper = w >= 2
    first_copies = []
    for e in range(1, G):
        mm = (m + e) % G
        for gp in range(nw):
            src = dvb.at[pl.ds(pl.multiple_of((gp * G + mm) * R, R), R)]
            first_copies.append(
                remote(src, f1.at[m, gp], sf1.at[e, gp], rf1.at[m, gp], (w, g * G + mm))
            )

    @pl.when(upper)
    def _():
        for r in first_copies:
            r.start()

    tile_d = 128
    ones = jnp.ones((N, BLK), BF)
    row_qk = product_left(ones, dqk[...])[0:1, :]
    row_f = product_left(ones, dvb[...])[0:1, :]
    sum_qk = product_left(dqk[...], ones)
    sum_f = product_left(dvb[...], ones)
    gain_t[...] = jnp.transpose(jnp.broadcast_to(vec[4:5, :], (BLK, width)))
    shift_t[...] = jnp.transpose(jnp.broadcast_to(vec[5:6, :], (BLK, width)))
    lane = lax.broadcasted_iota(jnp.int32, (d, BLK), 1)
    edge = gq.shape[1] - BLK
    for a in range(nw):
        sums_t[a * d : (a + 1) * d, :] = jnp.where(
            lane == 66, sum_qk[:wide], jnp.where(lane == 67, sum_qk[wide:], sum_f)
        )
    lane = lax.broadcasted_iota(jnp.int32, (tile_d, BLK), 1)

    def grads(i, carry):
        at = pl.ds(pl.multiple_of(i * tile_d, tile_d), tile_d)
        x_qk = product_left(xh[:, at], dqk[...])
        x_f = product_left(xh[:, at], dvb[...])
        w_qk = wqk[at, :].astype(F32)
        w_f = wf[at, :].astype(F32)
        add = lambda a, b: jnp.sum(a, axis=1, keepdims=True) + jnp.sum(b, axis=1, keepdims=True)
        for_gain = add(w_qk * x_qk, w_f * x_f)
        for_shift = add(w_qk * row_qk, w_f * row_f)
        gain = gain_t[at, 0:1]
        shift = shift_t[at, 0:1]
        gq[at, 0 : 2 * wide] = (gain * x_qk + shift * row_qk).astype(BF)
        gq[at, 2 * wide : 3 * wide] = (gain * x_f + shift * row_f).astype(BF)
        ends = gq[at, edge:].astype(F32)
        ends = jnp.where(lane == 64, for_gain, jnp.where(lane == 65, for_shift, ends))
        ends = jnp.where(lane > 65, sums_t[at, :], ends)
        gq[at, edge:] = jnp.where(lane < 69, ends, 0.0).astype(BF)
        poll(polls + i)
        return carry

    lax.fori_loop(0, width // tile_d, grads, 0)
    polls += width // tile_d
    ring_b.begin()

    def block(i, carry):
        phase = i // (2 * G)
        jj = (hi + 1 - (i // G) % 2 + 2) % 2
        mm = (m + 1 + i % G) % G
        parity = (1 - par) * (1 - phase) + par * phase
        b = (2 * parity + jj) * G + mm
        at = pl.ds(pl.multiple_of(b * R, R), R)
        dn = product_right(dqk[at, :], wqk[...]) + product_right(dvb[at, :], wf[...])
        D[b] = dn.astype(BF)

        @pl.when(phase == 0)
        def _():
            slot = jj * G + mm
            remote(D.at[b], b1.at[slot], s1.at[slot], r1.at[slot], core).start()

        poll(polls + i)

        @pl.when(i % 4 == 3)
        def _():
            ring_b.step(i // 4)

        return carry

    lax.fori_loop(0, nc, block, 0)
    polls += nc
    done_b = nc // 4

    order = list(range(1, G)) + [0]

    def chip_sum(jj, mm):
        slot = jj * G + mm
        pltpu.make_async_copy(b1.at[slot], b1.at[slot], r1.at[slot]).wait()
        return D[(2 * par + jj) * G + mm].astype(F32) + b1[slot].astype(F32)

    seconds = []
    for e in order:
        mm = (m + e) % G
        ab[mm] = chip_sum(1 - hi, mm).astype(BF)
        r = remote(ab.at[mm], b2.at[mm], s2.at[mm], r2.at[mm], other)
        r.start()
        seconds.append(r)
    thirds = []

    def sum_chips():
        for e in order:
            mm = (m + e) % G
            total = chip_sum(hi, mm)
            pltpu.make_async_copy(b2.at[mm], b2.at[mm], r2.at[mm]).wait()
            total = total + b2[mm].astype(F32)
            if e:
                st[mm] = total.astype(BF)
                r = remote(st.at[mm], b3.at[m], s3.at[mm], r3.at[m], (w, g * G + mm))
                r.start()
                thirds.append(r)
            else:
                tot[...] = total

    def sum_first():
        @pl.when(upper)
        def _():
            for gp in range(nw):
                total = dvb[pl.ds(pl.multiple_of((gp * G + m) * R, R), R), :].astype(F32)
                for e in range(1, G):
                    mm = (m + e) % G
                    pltpu.make_async_copy(f1.at[mm, gp], f1.at[mm, gp], rf1.at[mm, gp]).wait()
                    total = total + f1[mm, gp].astype(F32)
                fs[gp] = total.astype(BF)
                own = jnp.logical_and(w == seq, g == gp)

                @pl.when(own)
                def _():
                    pltpu.make_async_copy(fs.at[gp], fr.at[par], rf2.at[par]).start()

                @pl.when(jnp.logical_not(own))
                def _():
                    remote(
                        fs.at[gp], fr.at[par], sf2.at[gp], rf2.at[par], (seq, gp * G + m)
                    ).start()

    back = remote(tb, tr, sT.at[0], rT.at[0], home)
    stay = pltpu.make_async_copy(tb, tr, rT.at[0])

    def norm_back():
        total = tot[...]
        for e in range(1, G):
            mm = (m + e) % G
            pltpu.make_async_copy(b3.at[mm], b3.at[mm], r3.at[mm]).wait()
            total = total + b3[mm].astype(F32)
        value = X[og * G + m].astype(F32)
        centred = value - jnp.mean(value, axis=-1, keepdims=True)
        inverse = lax.rsqrt(jnp.mean(centred * centred, axis=-1, keepdims=True) + EPS)
        normal = centred * inverse
        dx = total * vec[4:5, :]
        dx = dx - jnp.mean(dx, axis=-1, keepdims=True) - normal * jnp.mean(
            dx * normal, axis=-1, keepdims=True
        )
        tb[...] = (dmid[...].astype(F32) + inverse * dx).astype(BF)

        @pl.when(home_self)
        def _():
            stay.start()

        @pl.when(jnp.logical_not(home_self))
        def _():
            back.start()

    turns = []
    extras = [ring_u.exchange, ring_u.spread]
    extras += [functools.partial(ring_u.hop, h) for h in range(1, ring_u.reach[0] + 1)]
    for n in range(polls, 4 * ring_a.steps):
        r, s = n % 4, n // 4
        if r % 2:
            turns.append(functools.partial(ring_a.turn, r // 2, s))
        elif s < ring_u.turns:
            turns.append(functools.partial(ring_u.turn, r // 2, s))
        elif r == 0 or n == polls:
            turns.append(extras.pop(0) if extras else lambda: None)
    turns += extras

    def others():
        for _ in range(2):
            if turns:
                turns.pop(0)()

    for at_b in range(done_b, ring_b.turns):
        ring_b.step(at_b)
        others()
        if at_b == done_b:
            sum_first()
    ring_b.exchange()
    others()
    sum_chips()
    ring_b.spread()
    others()
    for h in range(1, ring_b.reach[0] + 1):
        ring_b.hop(h)
        others()
        if h == 3:
            norm_back()
    while turns:
        others()

    down_out[...] = res_a[0:width, :].astype(F32)
    gout_out[...] = res_a[width : width + d, :].astype(F32)
    for j in range(ring_u.group):
        rows = slice(j * seg_u, (j + 1) * seg_u)
        for a in range(nw):
            up_out[rows, a * width : (a + 1) * width] = res_u[j, a].astype(F32)
    for j in range(ring_b.group):
        rows = slice(j * seg_b, (j + 1) * seg_b)
        for a in range(nw):
            for part in range(2):
                at = part * width + a * d
                qkv_out[rows, at : at + d] = res_b[j, a, :, part * d : (part + 1) * d].astype(F32)
            if a < 2:
                at = 2 * width + a * d
                qkv_out[rows, at : at + d] = res_b[j, a, :, 2 * d : 3 * d].astype(F32)
            at = a * d + j * seg_b
            sums_t[at : at + seg_b, :] = res_b[j, a, :, edge:].astype(F32)
    ends = jnp.transpose(sums_t[...])
    nb = 6 * d // 4
    line[:, 0:width] = ends[66:67, :]
    line[:, width : width + 2 * d] = ends[68:69, : 2 * d]
    share = line[:, 0:nb]
    for a in range(1, nw):
        share = jnp.where(w == a, line[:, a * nb : (a + 1) * nb], share)
    rows_out[...] = jnp.zeros_like(rows_out)
    rows_out[0:2, :] = res_a[width + d : width + d + 16, :].astype(F32)[0:2]
    for row in range(2):
        total = ends[64 + row : 65 + row, 0:d]
        for a in range(1, nw):
            total = total + ends[64 + row : 65 + row, a * d : (a + 1) * d]
        rows_out[2:3, row * d : (row + 1) * d] = total
    rows_out[3:4, 0:nb] = share
    pltpu.make_async_copy(tr, tr, rT.at[0]).wait()
    tokens_out[...] = tr[...].astype(F32)
    for u in range(2):
        pltpu.make_async_copy(fr.at[u], fr.at[u], rf2.at[u]).wait()
        first_out[:, u * d : (u + 1) * d] = fr[u].astype(F32)

    pltpu.make_async_copy(lr, lr, rL.at[0]).wait()
    layer_out[...] = lr[...]
    ring_a.drain()
    ring_u.drain()
    ring_b.drain()
    for r in seconds + thirds + shares:
        r.wait_send()

    @pl.when(jnp.logical_not(home_self))
    def _():
        back.wait_send()
        layer_back.wait_send()

    @pl.when(upper)
    def _():
        for r in first_copies:
            r.wait_send()
        for gp in range(nw):

            @pl.when(jnp.logical_not(jnp.logical_and(w == seq, g == gp)))
            def _():
                remote(
                    fs.at[gp], fr.at[par], sf2.at[gp], rf2.at[par], (seq, gp * G + m)
                ).wait_send()

    def drain(i, carry):
        jj = (hi + 1 - (i // G) % 2 + 2) % 2
        mm = (m + 1 + i % G) % G
        slot = jj * G + mm
        b = (2 * (1 - par) + jj) * G + mm
        remote(D.at[b], b1.at[slot], s1.at[slot], r1.at[slot], core).wait_send()
        return carry

    lax.fori_loop(0, 2 * G, drain, 0)


def tail(
    G, H, deal, q, k, v, o, do, lse, xh, X, wqk, wf, vec, dmid, up, down, gout, vsums, mlp, mid
):
    nw = 4
    nc = nw * G
    R, width = dmid.shape
    d = width // nw
    N = xh.shape[0]
    wide = H * HEAD_DIM
    seg_a = -(-(width + d + 16) // (2 * nc * 16)) * 16
    seg_u = seg_b = width // (2 * nc)
    cols = 5 * BLK
    dma = pltpu.SemaphoreType.DMA
    vm = pltpu.VMEM
    steps = 2 * (nc - 1)
    operands = (
        deal, q, k, v, o, do, lse, xh, X, wqk, wf, vec, dmid, up, down, gout, vsums, mlp, mid
    )
    return pl.pallas_call(
        functools.partial(tail_kernel, G, H, seg_a, seg_u, seg_b),
        name="tail",
        out_shape=(
            jax.ShapeDtypeStruct((R, width), BF),
            jax.ShapeDtypeStruct((R, width), F32),
            jax.ShapeDtypeStruct((R, 2 * d), F32),
            jax.ShapeDtypeStruct((d, nw * width), F32),
            jax.ShapeDtypeStruct((width, width), F32),
            jax.ShapeDtypeStruct((d, width), F32),
            jax.ShapeDtypeStruct((d, 2 * width + 2 * d), F32),
            jax.ShapeDtypeStruct((8, width), F32),
        ),
        in_specs=[pl.BlockSpec(memory_space=pltpu.SMEM)] + [ANY] * (len(operands) - 4) + [VM] + [ANY] * 2,
        out_specs=[VM] * 8,
        scratch_shapes=[vm(a.shape, a.dtype) for a in operands[1:7]]
        + [vm((nw, 2 * nc, R), F32)]
        + [vm(a.shape, a.dtype) for a in operands[7:13]]
        + [
            vm((wide, N), BF), vm((N, wide), F32), vm((N, wide), F32), vm((N, 2 * wide), BF),
            vm((N, wide), BF), vm((nc, R, width), BF), vm((2 * G, R, width), BF),
            vm((G, R, width), BF), vm((G, R, width), BF), vm((G, R, width), BF),
            vm((G, R, width), BF), vm((R, width), F32), vm((R, width), BF), vm((R, width), BF),
            vm((2 * nc * seg_a, width), BF), vm((2, nc - 1, seg_a, width), BF),
            vm((2 * nc * seg_a, width), BF),
            vm((width, width), BF), vm((2, nc - 1, seg_u, width), BF),
            vm((nc // 2, nw, seg_u, width), BF),
            vm((width, cols), BF), vm((2, nc - 1, seg_b, cols), BF),
            vm((nc // 2, nw, seg_b, cols), BF),
            vm((width, BLK), F32), vm((width, BLK), F32), vm((width, BLK), F32),
            vm((1, 6 * d), F32),
            vm((G, nw, R, d), BF), vm((nw, R, d), BF), vm((2, R, d), BF),
            vm((nw * R, width), BF), vm((R, width), F32), vm((nw, R, width), BF),
            vm((R, width), BF), vm((R, width), BF), dma((nw,)), dma((nw,)), dma((1,)), dma((1,)),
            dma((2 * G,)), dma((2 * G,)), dma((G,)), dma((G,)), dma((G,)), dma((G,)),
            dma((1,)), dma((1,)), dma((2, 2, steps)), dma((2, 2, steps)),
        ]
        + [
            dma(a)
            for chains in (2, 1)
            for a in (
                (2, chains, nc - 1), (2, chains, nc - 1), (2,), (nw,), (2, nc // 2 + 1),
                (2, nc // 2 + 1),
            )
        ]
        + [
            dma((G, nw)), dma((G, nw)),
            dma((nw,)), dma((2,)), dma((len(operands),)),
        ],
        compiler_params=pltpu.CompilerParams(
            collective_id=2, has_side_effects=True, vmem_limit_bytes=63 << 20
        ),
        cost_estimate=pl.CostEstimate(
            flops=40 << 30, bytes_accessed=60 << 20, transcendentals=6 << 20
        ),
    )(*operands)


def on_device(
    nw,
    nc,
    tokens,
    first_values,
    cotangent,
    deal,
    w_qkv,
    bias_qv,
    w_out,
    bias_out,
    gain_one,
    shift_one,
    gain_two,
    shift_two,
    w_up,
    bias_up,
    w_down,
    bias_down,
):
    G = nc // nw
    w = lax.axis_index("wt")
    c = lax.axis_index("ctx")
    m = c % G
    rows, width = tokens.shape[1:]
    d = width // nw
    H = HEADS // nw
    both = ("wt", "ctx")
    seq = lambda g: 2 * (g % 2) + g // 2
    swap = [
        (a * nc + g * G + e, seq(g) * nc + a * G + e)
        for a in range(nw)
        for g in range(nw)
        for e in range(G)
    ]
    ring = [[(a, (a + k) % nw) for a in range(nw)] for k in range(nw)]

    def exchange(pieces):
        out = jnp.zeros_like(pieces)
        mine = lax.dynamic_index_in_dim(pieces, w, 0, keepdims=True)
        out = lax.dynamic_update_slice_in_dim(out, mine, w, 0)
        for k in range(1, nw):
            piece = lax.dynamic_index_in_dim(pieces, (w + k) % nw, 0, keepdims=True)
            got = lax.ppermute(piece, "wt", ring[k])
            out = lax.dynamic_update_slice_in_dim(out, got, (w + nw - k) % nw, 0)
        return out

    qk = w_qkv[:, : 2 * width].reshape(d, 2, nw, d).transpose(2, 0, 1, 3).reshape(nw, d, 2 * d)
    wf = w_qkv[:, 2 * width :].reshape(d, 2, d).transpose(1, 0, 2)
    nb = bias_qv.shape[0]
    ids = dealt_blocks(deal)
    qpos = jnp.arange(nw, dtype=jnp.int32) * G + m
    qid = jnp.take(ids.reshape(nc, 2), qpos, axis=0)
    hidden = (ids[None, None, :] > qid[:, :, None]).astype(F32) * -NEG
    bias = jnp.repeat(-hidden.reshape(2 * nw, 2 * nc), BLK, axis=1)[:, None, :]
    lift = jnp.repeat(hidden.transpose(0, 2, 1), BLK, axis=2)

    def mine(vector):
        return lax.dynamic_slice_in_dim(vector, w * d, d)

    if nc <= 8:
        vectors = (
            bias_out, gain_one, shift_one, gain_two, shift_two, bias_down, bias_up, bias_qv
        )
        X, xhat, k, v, Wup, cot, q, o, lse, part, Wqk, Wf, vec = head(
            G, H, deal, vectors, tokens[0], first_values[0], w_qkv, cotangent[0], w_up, w_out
        )
        mlp, mid_own, d_mid, d_o, g_up, g_down, g_out, vsums = middle(
            G, True, part, X, cot, o, Wup, w_down, w_out, vec
        )
        layer, grad_tokens, grad_first, s_up, s_down, s_out, s_qkv, sums = tail(
            G, H, deal, q, k, v, o, d_o, lse, xhat, X, Wqk, Wf, vec,
            d_mid, g_up, g_down, g_out, vsums, mlp, mid_own,
        )
        return (
            layer[None],
            grad_tokens[None],
            grad_first[None],
            s_qkv,
            sums[3, :nb],
            s_out,
            sums[1, d : 2 * d],
            sums[2, :d],
            sums[2, d : 2 * d],
            sums[1, 2 * d : 3 * d],
            sums[1, 3 * d :],
            s_up,
            sums[0],
            s_down,
            sums[1, :d],
        )

    small = jnp.concatenate(
        [bias_qv, bias_out, gain_one, shift_one, gain_two, shift_two, bias_down]
    )
    lanes = 16 * BLK
    small = jnp.concatenate([small, jnp.zeros((lanes - small.shape[0],), BF)]).reshape(16, BLK)
    X, Fv, WQK, WF, SM = gather(nw, G, tokens[0], first_values[0], qk, wf, small)
    X = X.reshape(nc * rows, width)
    Wqk = WQK.reshape(width, 2 * d)
    low = w < 2
    Wf = jnp.where(low, WF.reshape(width, d), jnp.zeros((width, d), BF))
    SM = SM.reshape(nw, lanes).astype(F32)
    qv_vector = SM[:, :nb].reshape(-1)
    vectors = [SM[:, nb + a * d : nb + (a + 1) * d].reshape(-1) for a in range(6)]
    out_vector, gain_a, shift_a, gain_b, shift_b, down_vector = vectors

    x32 = X.astype(F32)
    mean = jnp.mean(x32, axis=-1, keepdims=True)
    centred = x32 - mean
    inverse = lax.rsqrt(jnp.mean(centred * centred, axis=-1, keepdims=True) + EPS)
    n1 = (centred * inverse * gain_a + shift_a).astype(BF)
    pqk = product(n1, Wqk)
    q_bias = lax.dynamic_slice_in_dim(qv_vector, w * d, d)
    f_bias = lax.dynamic_slice_in_dim(qv_vector, width + (w % 2) * d, d)
    q = (pqk[:, :d] + q_bias).astype(BF)
    k = pqk[:, d:].astype(BF)
    f = (product(n1, Wf) + f_bias).astype(BF)
    Fv = Fv.reshape(nc * rows, 2 * d)
    first = jnp.where(w % 2 == 0, Fv[:, :d], Fv[:, d:])
    v = jnp.where(low, f, first)

    o, lse = attend(H, qpos, bias, q, k, v)

    part = product(o, w_out).astype(BF)
    pieces, spread = lax.optimization_barrier((w_up, cotangent[0], X))[:2]
    Wup = exchange(pieces.reshape(d, nw, width).transpose(1, 0, 2)).reshape(width, width)
    unswap = [(b, a) for a, b in swap]
    cot = lax.all_gather(lax.ppermute(spread, both, unswap), "wt", axis=0, tiled=True)
    vec = jnp.stack([out_vector, gain_b, shift_b, bias_up.astype(F32)] + [out_vector] * 4)
    mlp, mid_own, d_mid, d_o, g_up, g_down, g_out, vsums = middle(
        G, False, part, X.reshape(nc, rows, width), cot, o, Wup, w_down, w_out, vec
    )

    mlp = lax.psum_scatter(mlp, "wt", scatter_dimension=0, tiled=True)
    layer = (mid_own + mlp.astype(F32) + down_vector).astype(BF)
    layer = lax.ppermute(layer, both, swap)
    up_rows = exchange(g_up.reshape(nw, d, width)).transpose(1, 0, 2)
    s_up, s_down = lax.psum((up_rows.reshape(d, nw * width), g_down), "ctx")
    dqk, dv = attend_back(H, qpos, lift, q, k, v, o, d_o, lse)
    zero = jnp.zeros_like(dv)
    df = jnp.where(low, dv, zero)
    dn1 = product_right(dqk, Wqk) + product_right(df, Wf)
    dn1_low = dn1.astype(BF)
    blank = jnp.zeros_like(dv)
    left = jnp.where(w == 2, dv, blank)
    right = jnp.where(w == 3, dv, blank)
    total = scatter_sum(
        G, jnp.concatenate([dn1_low, left, right], axis=1).reshape(nc, rows, width + 2 * d)
    )
    grad_first = lax.ppermute(total[:, width:].astype(BF), both, swap).astype(F32)
    block = (w * G + m) * rows
    x_own = lax.dynamic_slice_in_dim(X, block, rows).astype(F32)
    _, pull_one = jax.vjp(lambda a: norm_rows(a, gain_a, shift_a), x_own)
    d_x = d_mid.astype(F32) + pull_one(total[:, :width])[0]
    grad_tokens = lax.ppermute(d_x.astype(BF), both, swap).astype(F32)

    g_qk = product_left(n1, dqk)
    g_f = product_left(n1, df)
    normal = centred * inverse
    g_gain_one = jnp.sum(dn1_low.astype(F32) * normal, axis=0)
    g_shift_one = jnp.sum(dn1_low.astype(F32), axis=0)
    cols = jnp.concatenate(
        [
            g_qk.astype(BF),
            g_f.astype(BF),
            g_gain_one[:, None].astype(BF),
            g_shift_one[:, None].astype(BF),
            jnp.zeros((width, 62), BF),
        ],
        axis=1,
    ).reshape(nw, d, 640)
    sums = jnp.concatenate(
        [jnp.sum(dqk.astype(F32), axis=0), jnp.sum(df.astype(F32), axis=0), jnp.zeros((64,), F32)]
    ).astype(BF)
    foot = jnp.concatenate([sums[None], jnp.zeros((7, 640), BF)], axis=0)
    pack = jnp.concatenate([cols, jnp.broadcast_to(foot[None], (nw, 8, 640))], axis=1)
    pack = exchange(pack)
    vecs = jnp.concatenate(
        [
            vsums[0],
            mine(vsums[1]),
            mine(vsums[2]),
            mine(vsums[3]),
            mine(vsums[4]),
        ]
    ).astype(BF)
    pack = pack.at[0, d + 1 : d + 4, :512].set(vecs.reshape(3, 512))
    pack, s_up, s_down = lax.optimization_barrier((pack, s_up, s_down))
    pack, s_out = lax.psum((pack, g_out), "ctx")
    body = pack[:, :d]
    s_qkv = jnp.concatenate(
        [body[a, :, e * d : (e + 1) * d] for e in (0, 1) for a in range(nw)]
        + [body[a, :, 2 * d : 3 * d] for a in range(2)],
        axis=1,
    ).astype(F32)
    s_gain_one = jnp.sum(body[:, :, 576].astype(F32), axis=0)
    s_shift_one = jnp.sum(body[:, :, 577].astype(F32), axis=0)
    ends = pack[:, d]
    bias_all = jnp.concatenate([ends[:, :d].reshape(-1), ends[:2, 2 * d : 3 * d].reshape(-1)])
    s_bias_qv = lax.dynamic_slice_in_dim(bias_all, w * nb, nb).astype(F32)
    vecs = pack[0, d + 1 : d + 4, :512].reshape(-1).astype(F32)
    s_bias_up = vecs[:width]
    s_bias_down, s_bias_out, s_gain_two, s_shift_two = [
        vecs[width + a * d : width + (a + 1) * d] for a in range(4)
    ]
    return (
        layer[None],
        grad_tokens[None],
        grad_first[None],
        s_qkv,
        s_bias_qv,
        s_out.astype(F32),
        s_bias_out,
        s_gain_one,
        s_shift_one,
        s_gain_two,
        s_shift_two,
        s_up.astype(F32),
        s_bias_up,
        s_down.astype(F32),
        s_bias_down,
    )


def solution(mesh):
    rows3 = P("wt", "ctx", None)
    mat = P("wt", None)
    vec = P("wt")
    in_specs = (rows3, rows3, rows3, P(), mat, vec, mat) + (vec,) * 5 + (mat, vec, mat, vec)
    out_specs = (
        (rows3, rows3, rows3, mat, vec, mat) + (vec,) * 5 + (mat, vec, mat, vec)
    )
    return jax.shard_map(
        functools.partial(on_device, mesh.shape["wt"], mesh.shape["ctx"]),
        mesh=mesh,
        in_specs=in_specs,
        out_specs=out_specs,
        check_vma=False,
    )
```

```python
import functools

import jax
import jax.numpy as jnp
from jax import lax
from jax.experimental import pallas as pl
from jax.experimental.pallas import tpu as pltpu
from jax.sharding import PartitionSpec as P

HEADS = 12
HEAD_DIM = 64
BLK = 128
CHUNK = 1024

EPS = 1e-05
SLOPE = 0.7978845608028654
CUBIC = 0.044715
NEG = -1e30

BF = jnp.bfloat16
F32 = jnp.float32
MESH = pl.DeviceIdType.MESH
ANY = pl.BlockSpec(memory_space=pl.ANY)
VM = pl.BlockSpec(memory_space=pltpu.VMEM)


def norm_rows(value, gain, shift):
    mean = jnp.mean(value, axis=-1, keepdims=True)
    centred = value - mean
    inverse = lax.rsqrt(jnp.mean(centred * centred, axis=-1, keepdims=True) + EPS)
    return centred * inverse * gain + shift


def gelu_tanh(value):
    return 0.5 * value * (1.0 + jnp.tanh(SLOPE * (value + CUBIC * value * value * value)))


def product(left, right):
    return jnp.dot(left, right, preferred_element_type=F32)


def product_left(left, right):
    return lax.dot_general(left, right, (((0,), (0,)), ((), ())), preferred_element_type=F32)


def product_right(left, right):
    return lax.dot_general(left, right, (((1,), (1,)), ((), ())), preferred_element_type=F32)


def dealt_blocks(deal):
    count = deal.shape[0] * 2
    pairs = jnp.repeat(deal, 2)
    parity = jnp.arange(count, dtype=jnp.int32) % 2
    return jnp.where(parity == 0, pairs, count - 1 - pairs)


def remote(src, dst, send, recv, device):
    return pltpu.make_async_remote_copy(
        src_ref=src,
        dst_ref=dst,
        send_sem=send,
        recv_sem=recv,
        device_id=device,
        device_id_type=MESH,
    )


def greet(peers):
    barrier = pltpu.get_barrier_semaphore()
    for peer in peers:
        pl.semaphore_signal(barrier, inc=1, device_id=peer, device_id_type=MESH)
    pl.semaphore_wait(barrier, len(peers))


def gather_kernel(
    nw, G, x, first, wqk, wf, small, X, Fv, WQK, WF, SM, rx, rf, rw, rv, rs, sa, sx, sfa, sfx, sw, loc
):
    w = lax.axis_index("wt")
    c = lax.axis_index("ctx")
    g = c // G
    m = c % G
    nc = nw * G
    core = w + 1 - 2 * (w % 2)
    other = (w + 2) % nw
    rel = lambda k: (w + k) % nw
    peers = [(rel(k), c) for k in range(1, nw)]
    peers += [(w, ((g + k) % nw) * G + m) for k in range(1, nw)]
    peers += [(w, g * G + (m + k) % G) for k in range(1, G)]
    greet(peers)
    seq = 2 * (g % 2) + g // 2
    goal = (2 * (w % 2) + w // 2) * G + m
    is_a = w == seq
    primary = (w + seq) % 2 == 0
    high = w >= 2
    copies = []

    to_head = remote(x, X.at[c], sa.at[0], rx.at[c], (w, goal))
    to_head_f = remote(first, Fv.at[c], sa.at[1], rf.at[c], (w, goal))
    own_x = pltpu.make_async_copy(x, X.at[c], rx.at[c])
    own_f = pltpu.make_async_copy(first, Fv.at[c], rf.at[c])

    @pl.when(is_a)
    def _():
        own_x.start()
        own_f.start()

    @pl.when(jnp.logical_not(is_a))
    def _():
        to_head.start()
        to_head_f.start()

    own_w = pltpu.make_async_copy(wqk.at[w], WQK.at[w], loc.at[0])
    own_s = pltpu.make_async_copy(small, SM.at[w], loc.at[1])
    own_w.start()
    own_s.start()
    own_v = pltpu.make_async_copy(wf.at[w % 2], WF.at[w], loc.at[2])
    own_v.start()
    sends_w, sends_v, sends_s = [], [], []
    for k in range(1, nw):
        d = rel(k)
        s = remote(small, SM.at[w], sw.at[k, 0], rs.at[w], (d, c))
        s.start()
        q = remote(wqk.at[d], WQK.at[w], sw.at[k, 1], rw.at[w], (d, c))
        q.start()
        v = remote(wf.at[d % 2], WF.at[w], sw.at[k, 2], rv.at[w], (d, c))
        sends_w += [s, q]
        sends_v.append((d, v))

        @pl.when(d < 2)
        def _():
            v.start()

    def block_x(b):
        return pltpu.make_async_copy(X.at[b], X.at[b], rx.at[b])

    def block_f(b):
        return pltpu.make_async_copy(Fv.at[b], Fv.at[b], rf.at[b])

    fwd_core, fwd_other, fwd_member = [], [], []
    for k in range(nw):
        gp = (g + k) % nw
        b = gp * G + m
        to_core = remote(X.at[b], X.at[b], sx.at[0, b], rx.at[b], (core, c))
        to_other = remote(X.at[b], X.at[b], sx.at[1, b], rx.at[b], (other, c))
        to_core_f = remote(Fv.at[b], Fv.at[b], sfx.at[0, b], rf.at[b], (core, c))
        to_other_f = remote(Fv.at[b], Fv.at[b], sfx.at[1, b], rf.at[b], (other, c))
        members = [
            remote(X.at[b], X.at[b], sx.at[1 + e, b], rx.at[b], (w, g * G + (m + e) % G))
            for e in range(1, G)
        ]
        members_f = [
            remote(Fv.at[b], Fv.at[b], sfx.at[1 + e, b], rf.at[b], (w, g * G + (m + e) % G))
            for e in range(1, G)
        ]

        @pl.when(primary)
        def _():
            block_x(b).wait()

            @pl.when(is_a)
            def _():
                to_other.start()

            for r in members:
                r.start()
            to_core.start()

        @pl.when(jnp.logical_and(is_a, jnp.logical_not(high)))
        def _():
            block_f(b).wait()
            to_other_f.start()

        @pl.when(jnp.logical_and(primary, high))
        def _():
            block_f(b).wait()
            for r in members_f:
                r.start()
            to_core_f.start()

        fwd_core.append((to_core, to_core_f))
        fwd_other.append((to_other, to_other_f))
        fwd_member.append((members, members_f))
    for e in range(1, G):
        for k in range(nw):
            b = ((g + k) % nw) * G + (m + e) % G
            to_core = remote(X.at[b], X.at[b], sx.at[0, b], rx.at[b], (core, c))
            to_core_f = remote(Fv.at[b], Fv.at[b], sfx.at[0, b], rf.at[b], (core, c))

            @pl.when(primary)
            def _():
                block_x(b).wait()
                to_core.start()

            @pl.when(jnp.logical_and(primary, high))
            def _():
                block_f(b).wait()
                to_core_f.start()

            fwd_core.append((to_core, to_core_f))

    @pl.when(jnp.logical_not(primary))
    def _():
        for b in range(nc):
            block_x(b).wait()

        @pl.when(high)
        def _():
            for b in range(nc):
                block_f(b).wait()

    own_w.wait()
    own_s.wait()
    own_v.wait()
    for k in range(1, nw):
        src = (w + nw - k) % nw
        pltpu.make_async_copy(wqk.at[0], WQK.at[src], rw.at[src]).wait()
        pltpu.make_async_copy(small, SM.at[src], rs.at[src]).wait()

        @pl.when(w < 2)
        def _():
            pltpu.make_async_copy(wf.at[0], WF.at[src], rv.at[src]).wait()

    for s in sends_w:
        s.wait_send()
    for d, v in sends_v:

        @pl.when(d < 2)
        def _():
            v.wait_send()

    @pl.when(jnp.logical_not(is_a))
    def _():
        to_head.wait_send()
        to_head_f.wait_send()

    @pl.when(primary)
    def _():
        for a, _f in fwd_core:
            a.wait_send()
        for ms, _f in fwd_member:
            for a in ms:
                a.wait_send()

        @pl.when(high)
        def _():
            for _x, a in fwd_core:
                a.wait_send()
            for _x, ms in fwd_member:
                for a in ms:
                    a.wait_send()

    @pl.when(is_a)
    def _():
        for a, _f in fwd_other:
            a.wait_send()

        @pl.when(jnp.logical_not(high))
        def _():
            for _x, a in fwd_other:
                a.wait_send()


def gather(nw, G, x, first, wqk, wf, small):
    nc = nw * G
    rows, width = x.shape
    half = first.shape[1]
    d = width // nw
    dma = pltpu.SemaphoreType.DMA
    return pl.pallas_call(
        functools.partial(gather_kernel, nw, G),
        name="gather_tokens",
        out_shape=(
            jax.ShapeDtypeStruct((nc, rows, width), BF),
            jax.ShapeDtypeStruct((nc, rows, half), BF),
            jax.ShapeDtypeStruct((nw, d, 2 * d), BF),
            jax.ShapeDtypeStruct((nw, d, d), BF),
            jax.ShapeDtypeStruct((nw,) + small.shape, BF),
        ),
        in_specs=[ANY] * 5,
        out_specs=[ANY] * 5,
        scratch_shapes=[
            dma((nc,)),
            dma((nc,)),
            dma((nw,)),
            dma((nw,)),
            dma((nw,)),
            dma((2,)),
            dma((1 + G, nc)),
            dma((2,)),
            dma((1 + G, nc)),
            dma((nw, 3)),
            dma((3,)),
        ],
        compiler_params=pltpu.CompilerParams(collective_id=0, has_side_effects=True),
    )(x, first, wqk, wf, small)


def middle_kernel(
    T, G, crossed, p_hbm, X_hbm, cot_hbm, o_hbm, wup_hbm, wdn_hbm, wout_hbm, vec_hbm,
    mlp, mid_own, dmid_own, do_out, gup, gdn, gout, sums,
    p, x, cot, o, wup, wdn, wout, vec,
    b1, ab, b2, bs, mid, n2s, act, dus, q, b4, ab2, b5, dn, dbs,
    s1, r1, s2, r2, s3, r3, s4, r4, s5, r5, s6, r6, ld, *rings,
):
    w = lax.axis_index("wt")
    c = lax.axis_index("ctx")
    g = c // G
    m = c % G
    core = (w + 1 - 2 * (w % 2), c)
    other = ((w + 2) % 4, c)
    mine = w % 2
    theirs = 1 - mine
    rows = p.shape[0]
    half = rows // 2
    n = half // T
    R = rows // 4
    loads = [
        pltpu.make_async_copy(p_hbm, p, ld.at[0]),
        pltpu.make_async_copy(vec_hbm, vec, ld.at[1]),
    ]
    loads += [
        pltpu.make_async_copy(X_hbm.at[a * G + m], x.at[pl.ds(a * R, R)], ld.at[2 + a])
        for a in range(4)
    ]
    loads += [
        pltpu.make_async_copy(wup_hbm, wup, ld.at[6]),
        pltpu.make_async_copy(wdn_hbm, wdn, ld.at[7]),
        pltpu.make_async_copy(cot_hbm, cot, ld.at[8]),
        pltpu.make_async_copy(wout_hbm, wout, ld.at[9]),
        pltpu.make_async_copy(o_hbm, o, ld.at[10]),
    ]
    for copy in loads:
        copy.start()
    peers = [core, other]
    if crossed:
        slots_u, slots_d, ssu, sru, ssd, srd = rings
        nc = 4 * G
        pos, right, left = ring_place(nc)
        seg = p.shape[1] // (2 * nc)
        ring_u = Ring(nc, pos, right, left, seg, 2, gup, slots_u, None, ssu, sru)
        ring_d = Ring(nc, pos, right, left, seg, 2, gdn, slots_d, None, ssd, srd)
        peers += [right, left]
    greet(peers)

    def rs(base, t):
        return pl.ds(pl.multiple_of(base * half + t * n, n), n)

    loads[0].wait()
    first = []
    for t in range(T):
        r = remote(p.at[rs(theirs, t)], b1.at[t], s1.at[t], r1.at[t], core)
        r.start()
        first.append(r)
    second = []
    for t in range(T):
        first[t].wait_recv()
        ab[t] = (p[rs(mine, t), :].astype(F32) + b1[t].astype(F32)).astype(BF)
        r = remote(ab.at[t], b2.at[t], s2.at[t], r2.at[t], other)
        r.start()
        second.append(r)
    for copy in loads[1:]:
        copy.wait()
    out_b = vec[0:1, :]
    gain = vec[1:2, :]
    shift = vec[2:3, :]
    up_b = vec[3:4, :]
    sums[...] = jnp.zeros_like(sums)

    def two(ref, t):
        return jnp.concatenate([ref[rs(mine, t), :], ref[rs(theirs, t), :]], axis=0)

    def put(ref, t, value):
        ref[rs(mine, t), :] = value[:n]
        ref[rs(theirs, t), :] = value[n:]

    def add_sum(at, value):
        sums[at : at + 1, :] += jnp.sum(value, axis=0, keepdims=True)

    def chain(t):
        pltpu.make_async_copy(b4.at[t], b4.at[t], r4.at[t]).wait()
        ab2[t] = (q[rs(mine, t), :].astype(F32) + b4[t].astype(F32)).astype(BF)
        remote(ab2.at[t], b5.at[t], s5.at[t], r5.at[t], other).start()

    def forward(t, carry):
        pltpu.make_async_copy(b2.at[t], b2.at[t], r2.at[t]).wait()
        bs[rs(mine, t), :] = (ab[t].astype(F32) + b2[t].astype(F32)).astype(BF)
        remote(bs.at[rs(mine, t)], bs.at[rs(mine, t)], s3.at[t], r3.at[t], core).start()

        @pl.when(t > 0)
        def _():
            chain(t - 1)

        pltpu.make_async_copy(bs.at[rs(theirs, t)], bs.at[rs(theirs, t)], r3.at[t]).wait()
        value = two(x, t).astype(F32) + two(bs, t).astype(F32) + out_b
        put(mid, t, value)
        centred = value - jnp.mean(value, axis=-1, keepdims=True)
        inverse = lax.rsqrt(jnp.mean(centred * centred, axis=-1, keepdims=True) + EPS)
        n2 = (centred * inverse * gain + shift).astype(BF)
        put(n2s, t, n2)
        u = product(n2, wup[...]) + up_b
        th = jnp.tanh(SLOPE * (u + CUBIC * u * u * u))
        a = (0.5 * u * (1.0 + th)).astype(BF)
        slope = 0.5 * (1.0 + th) + 0.5 * u * (1.0 - th * th) * SLOPE * (1.0 + 3.0 * CUBIC * u * u)
        put(act, t, a)
        ct = two(cot, t)
        du = (product_right(ct, wdn[...]) * slope).astype(BF)
        put(dus, t, du)
        put(q, t, product_right(du, wup[...]).astype(BF))
        remote(q.at[rs(theirs, t)], b4.at[t], s4.at[t], r4.at[t], core).start()
        put(mlp, t, product(a, wdn[...]).astype(BF))
        add_sum(0, du.astype(F32))
        add_sum(1, ct.astype(F32))
        return carry

    lax.fori_loop(0, T, forward, 0)
    chain(T - 1)

    width = p.shape[1]
    tile = 256

    def grads(i, carry):
        at = pl.ds(pl.multiple_of(i * tile, tile), tile)
        gup[at, :] = product_left(n2s[:, at], dus[...]).astype(BF)
        gdn[at, :] = product_left(act[:, at], cot[...]).astype(BF)
        return carry

    lax.fori_loop(0, width // tile, grads, 0)
    if crossed:
        ring_u.begin()
        ring_d.begin()

    def backward(t, carry):
        pltpu.make_async_copy(b5.at[t], b5.at[t], r5.at[t]).wait()
        dn[rs(mine, t), :] = (ab2[t].astype(F32) + b5[t].astype(F32)).astype(BF)
        remote(dn.at[rs(mine, t)], dn.at[rs(mine, t)], s6.at[t], r6.at[t], core).start()
        pltpu.make_async_copy(dn.at[rs(theirs, t)], dn.at[rs(theirs, t)], r6.at[t]).wait()
        value = two(mid, t)
        centred = value - jnp.mean(value, axis=-1, keepdims=True)
        inverse = lax.rsqrt(jnp.mean(centred * centred, axis=-1, keepdims=True) + EPS)
        normal = centred * inverse
        dn2 = two(dn, t).astype(F32)
        add_sum(3, dn2 * normal)
        add_sum(4, dn2)
        dx = dn2 * gain
        dx = dx - jnp.mean(dx, axis=-1, keepdims=True) - normal * jnp.mean(
            dx * normal, axis=-1, keepdims=True
        )
        dmid = two(cot, t).astype(F32) + inverse * dx
        db = dmid.astype(BF)
        put(dbs, t, db)
        add_sum(2, db.astype(F32))
        put(do_out, t, product_right(db, wout[...]).astype(BF))
        if crossed:

            @pl.when(t >= T - EARLY)
            def _():
                ring_u.early(t - (T - EARLY), EARLY)
                ring_d.early(t - (T - EARLY), EARLY)

        return carry

    lax.fori_loop(0, T, backward, 0)
    gout[...] = product_left(o[...], dbs[...]).astype(BF)
    if crossed:
        ring_u.early_drain(EARLY)
        ring_d.early_drain(EARLY)
    block_at = 2 * (w % 2) + w // 2 if crossed else w
    own = pl.ds(pl.multiple_of(block_at * R, R), R)
    mid_own[...] = mid[own, :]
    dmid_own[...] = dbs[own, :]
    for t in range(T):
        first[t].wait_send()
        second[t].wait_send()
        remote(bs.at[rs(mine, t)], bs.at[rs(mine, t)], s3.at[t], r3.at[t], core).wait_send()
        remote(q.at[rs(theirs, t)], b4.at[t], s4.at[t], r4.at[t], core).wait_send()
        remote(ab2.at[t], b5.at[t], s5.at[t], r5.at[t], other).wait_send()
        remote(dn.at[rs(mine, t)], dn.at[rs(mine, t)], s6.at[t], r6.at[t], core).wait_send()


def middle(G, crossed, p, X, cot, o, wup, wdn, wout, vec):
    T = 4
    rows, width = p.shape
    n = rows // 2 // T
    R = rows // 4
    d = o.shape[1]
    dma = pltpu.SemaphoreType.DMA
    full = pltpu.VMEM((rows, width), BF)
    part = pltpu.VMEM((T, n, width), BF)
    square = pltpu.VMEM((width, width), BF)
    return pl.pallas_call(
        functools.partial(middle_kernel, T, G, crossed),
        name="middle",
        out_shape=(
            jax.ShapeDtypeStruct((rows, width), BF),
            jax.ShapeDtypeStruct((R, width), F32),
            jax.ShapeDtypeStruct((R, width), BF),
            jax.ShapeDtypeStruct((rows, d), BF),
            jax.ShapeDtypeStruct((width, width), BF),
            jax.ShapeDtypeStruct((width, width), BF),
            jax.ShapeDtypeStruct((d, width), BF),
            jax.ShapeDtypeStruct((8, width), F32),
        ),
        in_specs=[ANY] * 8,
        out_specs=[VM] * 8,
        scratch_shapes=[
            full, full, full, pltpu.VMEM((rows, d), BF), square, square,
            pltpu.VMEM((d, width), BF), pltpu.VMEM((8, width), F32),
            part, part, part, full, pltpu.VMEM((rows, width), F32), full, full, full, full,
            part, part, part, full, full,
        ]
        + [dma((T,))] * 12
        + [dma((11,))]
        + (
            [pltpu.VMEM((2, EARLY, width // (8 * G), width), BF)] * 2 + [dma((2, 2, EARLY))] * 4
            if crossed
            else []
        ),
        compiler_params=pltpu.CompilerParams(
            collective_id=1, has_side_effects=True, vmem_limit_bytes=62 << 20
        ),
        cost_estimate=pl.CostEstimate(
            flops=14 * rows * width * width, bytes_accessed=40 << 20, transcendentals=rows * width
        ),
    )(p, X, cot, o, wup, wdn, wout, vec)


def scatter_kernel(G, D, out, b1, ab, b2, st, b3, s1, r1, s2, r2, s3, r3):
    w = lax.axis_index("wt")
    c = lax.axis_index("ctx")
    g = c // G
    m = c % G
    core = w + 1 - 2 * (w % 2)
    other = (w + 2) % 4
    par = w % 2
    hi = w // 2
    greet([(core, c), (other, c)] + [(w, g * G + (m + e) % G) for e in range(1, G)])
    order = [e for e in range(1, G)] + [0]
    firsts = {}
    for j in (1, 0):
        for e in order:
            jj = (hi + j) % 2
            mm = (m + e) % G
            b = (2 * jj + 1 - par) * G + mm
            slot = jj * G + mm
            r = remote(D.at[b], b1.at[slot], s1.at[slot], r1.at[slot], (core, c))
            r.start()
            firsts[(j, e)] = r

    def arrived1(slot):
        pltpu.make_async_copy(b1.at[slot], b1.at[slot], r1.at[slot]).wait()

    seconds = []
    for e in order:
        jj = 1 - hi
        mm = (m + e) % G
        slot = jj * G + mm
        arrived1(slot)
        ab[mm] = (D[(2 * jj + par) * G + mm].astype(F32) + b1[slot].astype(F32)).astype(BF)
        r = remote(ab.at[mm], b2.at[mm], s2.at[mm], r2.at[mm], (other, c))
        r.start()
        seconds.append(r)
    thirds = []
    for e in order:
        mm = (m + e) % G
        slot = hi * G + mm
        arrived1(slot)
        pltpu.make_async_copy(b2.at[mm], b2.at[mm], r2.at[mm]).wait()
        total = D[w * G + mm].astype(F32) + b1[slot].astype(F32) + b2[mm].astype(F32)
        if e == 0:
            for f in range(1, G):
                q = (m + f) % G
                pltpu.make_async_copy(b3.at[q], b3.at[q], r3.at[q]).wait()
                total = total + b3[q].astype(F32)
            out[...] = total.astype(out.dtype)
        else:
            st[mm] = total.astype(BF)
            r = remote(st.at[mm], b3.at[m], s3.at[mm], r3.at[m], (w, g * G + mm))
            r.start()
            thirds.append(r)
    for r in list(firsts.values()) + seconds + thirds:
        r.wait_send()


def scatter_sum(G, D):
    nc, rows, C = D.shape
    dma = pltpu.SemaphoreType.DMA
    return pl.pallas_call(
        functools.partial(scatter_kernel, G),
        name="scatter_sum",
        out_shape=jax.ShapeDtypeStruct((rows, C), F32),
        in_specs=[VM],
        out_specs=VM,
        scratch_shapes=[
            pltpu.VMEM((2 * G, rows, C), BF),
            pltpu.VMEM((G, rows, C), BF),
            pltpu.VMEM((G, rows, C), BF),
            pltpu.VMEM((G, rows, C), BF),
            pltpu.VMEM((G, rows, C), BF),
            dma((2 * G,)),
            dma((2 * G,)),
            dma((G,)),
            dma((G,)),
            dma((G,)),
            dma((G,)),
        ],
        compiler_params=pltpu.CompilerParams(
            collective_id=3, has_side_effects=True, vmem_limit_bytes=60 << 20
        ),
    )(D)


def head_mask(shape, h):
    lane = lax.broadcasted_iota(jnp.int32, shape, 1)
    return jnp.logical_and(lane >= h * HEAD_DIM, lane < (h + 1) * HEAD_DIM)


def split_heads(H, value):
    zero = jnp.zeros_like(value)
    return [jnp.where(head_mask(value.shape, h), value, zero) for h in range(H)]


def spread(H, shape, values):
    out = jnp.broadcast_to(values[H - 1], shape)
    for h in range(H - 2, -1, -1):
        out = jnp.where(head_mask(shape, h), values[h], out)
    return out


def attend_tile(H, q, k_ref, v_ref, bias_ref, at_bias, chunks=None):
    rows, width = q.shape
    N = k_ref.shape[0]
    step_keys = min(N, 1024)
    qh = split_heads(H, q * jnp.asarray(HEAD_DIM**-0.5, BF))
    top_half = lax.broadcasted_iota(jnp.int32, (rows, 1), 0) < BLK

    def step(j, carry):
        tops, sums, acc = carry
        at = pl.ds(pl.multiple_of(j * step_keys, step_keys), step_keys)
        kc = k_ref[at, :]
        vc = v_ref[at, :]
        low = bias_ref[at_bias, :, at]
        high = bias_ref[at_bias + 1, :, at]
        new_tops, new_sums, shrink, parts = [], [], [], []
        for h in range(H):
            s = product_right(qh[h], kc)
            s = jnp.concatenate([s[:BLK] + low, s[BLK:] + high], axis=0)
            top = jnp.maximum(tops[h], jnp.max(s, axis=1, keepdims=True))
            a = jnp.exp(tops[h] - top)
            p = jnp.exp(s - top)
            new_sums.append(sums[h] * a + jnp.sum(p, axis=1, keepdims=True))
            new_tops.append(top)
            shrink.append(a)
            parts.append(product(p.astype(BF), vc))
        acc = acc * spread(H, acc.shape, shrink) + spread(H, acc.shape, parts)
        return new_tops, new_sums, acc

    start = (
        [jnp.full((rows, 1), NEG, F32)] * H,
        [jnp.zeros((rows, 1), F32)] * H,
        jnp.zeros((rows, width), F32),
    )
    chunks = N // step_keys if chunks is None else chunks
    tops, sums, acc = lax.fori_loop(0, chunks, step, start)
    out = (acc / spread(H, acc.shape, sums)).astype(BF)
    lse = []
    for h in range(H):
        column = tops[h] + jnp.log(sums[h])
        lse.append(jnp.transpose(jnp.broadcast_to(column, (rows, BLK)))[0:1, :])
    lse = jnp.concatenate(lse + [jnp.zeros((8 - H, rows), F32)], axis=0)
    return out, lse


def attend_kernel(H, qpos, q_ref, k_ref, v_ref, bias_ref, o_ref, lse_ref):
    o, lse = attend_tile(H, q_ref[...], k_ref, v_ref, bias_ref, 2 * pl.program_id(0))
    o_ref[...] = o
    lse_ref[0] = lse


def attend(H, qpos, bias, q, k, v):
    n = qpos.shape[0]
    width = H * HEAD_DIM
    N = k.shape[0]
    rows = 2 * BLK
    whole = pl.BlockSpec((N, width), lambda i, *_: (0, 0))
    return pl.pallas_call(
        functools.partial(attend_kernel, H),
        name="attend",
        out_shape=(
            jax.ShapeDtypeStruct((n * rows, width), BF),
            jax.ShapeDtypeStruct((n, 8, rows), F32),
        ),
        grid_spec=pltpu.PrefetchScalarGridSpec(
            num_scalar_prefetch=1,
            grid=(n,),
            in_specs=[
                pl.BlockSpec((rows, width), lambda i, qp: (qp[i], 0)),
                whole,
                whole,
                pl.BlockSpec((2 * n, 1, N), lambda i, *_: (0, 0, 0)),
            ],
            out_specs=[
                pl.BlockSpec((rows, width), lambda i, *_: (i, 0)),
                pl.BlockSpec((1, 8, rows), lambda i, *_: (i, 0, 0)),
            ],
        ),
        compiler_params=pltpu.CompilerParams(vmem_limit_bytes=48 << 20),
    )(qpos, q, k, v, bias)


def attend_back_tile(
    H, q, do, o, lse, k_ref, v_ref, kt, dk, dv, lift_ref, tile, chunks=None, poll=None
):
    rows, width = q.shape
    N = k_ref.shape[0]
    scale = HEAD_DIM**-0.5
    qh = split_heads(H, q * jnp.asarray(scale, BF))
    doh = split_heads(H, do)
    qcat = jnp.concatenate(qh, axis=0)
    docat = jnp.concatenate(doh, axis=0)
    pick = lax.broadcasted_iota(jnp.int32, (8, width), 1)
    base = lax.broadcasted_iota(jnp.int32, (8, width), 0) * HEAD_DIM
    pick = jnp.logical_and(pick >= base, pick < base + HEAD_DIM).astype(F32)
    delta = lax.dot_general(
        pick,
        do.astype(F32) * o.astype(F32),
        (((1,), (1,)), ((), ())),
        precision=lax.Precision.HIGHEST,
        preferred_element_type=F32,
    )

    def step(j, dqt):
        at = pl.ds(pl.multiple_of(j * CHUNK, CHUNK), CHUNK)
        kc = k_ref[at, :]
        vc = v_ref[at, :]
        ps, dss, dqs = [], [], []
        for h in range(H):
            s = product_right(kc, qh[h])
            dp = product_right(vc, doh[h])
            pieces, dpieces = [], []
            for b in range(CHUNK // BLK):
                lift = lift_ref[tile, pl.ds(j * (CHUNK // BLK) + b, 1), :]
                cut = slice(b * BLK, (b + 1) * BLK)
                p = jnp.exp(s[cut] - (lse[h : h + 1, :] + lift))
                pieces.append(p.astype(BF))
                dpieces.append((p * (dp[cut] - delta[h : h + 1, :])).astype(BF))
            p = jnp.concatenate(pieces, axis=0)
            ds = jnp.concatenate(dpieces, axis=0)
            ps.append(p)
            dss.append(ds)
            dqs.append(product(kt[h * HEAD_DIM : (h + 1) * HEAD_DIM, at], ds))
        dv[at, :] += product(jnp.concatenate(ps, axis=1), docat)
        dk[at, :] += product(jnp.concatenate(dss, axis=1), qcat)
        if poll is not None:
            poll(j)
        return dqt + jnp.concatenate(dqs, axis=0)

    chunks = N // CHUNK if chunks is None else chunks
    dqt = lax.fori_loop(0, chunks, step, jnp.zeros((width, rows), F32))
    return dqt * scale


def flip_rows(src, dst):
    def flip(b, carry):
        at = pl.ds(pl.multiple_of(b * BLK, BLK), BLK)
        dst[:, at] = jnp.transpose(src[at, :])
        return carry

    lax.fori_loop(0, src.shape[0] // BLK, flip, 0)


def attend_back_kernel(
    H, qpos, q_ref, k_ref, v_ref, o_ref, do_ref, lse_ref, lift_ref, dqk_ref, dv_ref, kt, dk, dv
):
    i = pl.program_id(0)
    width = H * HEAD_DIM

    @pl.when(i == 0)
    def _():
        flip_rows(k_ref, kt)
        dk[...] = jnp.zeros_like(dk)
        dv[...] = jnp.zeros_like(dv)
        dqk_ref[...] = jnp.zeros_like(dqk_ref)

    dqt = attend_back_tile(
        H, q_ref[...], do_ref[...], o_ref[...], lse_ref[0], k_ref, v_ref, kt, dk, dv, lift_ref, i
    )
    rows = 2 * BLK
    here = pl.ds(pl.multiple_of(qpos[i] * rows, rows), rows)
    dqk_ref[here, 0:width] = jnp.transpose(dqt).astype(BF)

    @pl.when(i == pl.num_programs(0) - 1)
    def _():
        dqk_ref[:, width : 2 * width] = dk[...].astype(BF)
        dv_ref[...] = dv[...].astype(BF)


def attend_back(H, qpos, lift, q, k, v, o, do, lse):
    n = qpos.shape[0]
    width = H * HEAD_DIM
    N = k.shape[0]
    rows = 2 * BLK
    whole = pl.BlockSpec((N, width), lambda i, *_: (0, 0))
    row = pl.BlockSpec((rows, width), lambda i, *_: (i, 0))
    return pl.pallas_call(
        functools.partial(attend_back_kernel, H),
        name="attend_back",
        out_shape=(
            jax.ShapeDtypeStruct((N, 2 * width), BF),
            jax.ShapeDtypeStruct((N, width), BF),
        ),
        grid_spec=pltpu.PrefetchScalarGridSpec(
            num_scalar_prefetch=1,
            grid=(n,),
            in_specs=[
                pl.BlockSpec((rows, width), lambda i, qp: (qp[i], 0)),
                whole,
                whole,
                row,
                row,
                pl.BlockSpec((1, 8, rows), lambda i, *_: (i, 0, 0)),
                pl.BlockSpec((n, N // BLK, rows), lambda i, *_: (0, 0, 0)),
            ],
            out_specs=[
                pl.BlockSpec((N, 2 * width), lambda i, *_: (0, 0)),
                pl.BlockSpec((N, width), lambda i, *_: (0, 0)),
            ],
            scratch_shapes=[
                pltpu.VMEM((width, N), BF),
                pltpu.VMEM((N, width), F32),
                pltpu.VMEM((N, width), F32),
            ],
        ),
        compiler_params=pltpu.CompilerParams(vmem_limit_bytes=60 << 20),
    )(qpos, q, k, v, o, do, lse, lift)


def head_kernel(
    G, H,
    deal, out_b, gain_one, shift_one, gain_two, shift_two, down_b, up_b, qv_b,
    x_h, first_h, wqkv_h, cot_h, wup_h, wout_h,
    X_o, xh_o, k_o, v_o, wup_o, cot_o, q, o, lse, part, wqk, wf, vec,
    X, Fv, xh, k, v, small, vq, bias, wout, wl, wqk_h, wf_h, Y, line, small_l,
    rx, rf, rw, rv, rs, rc, ru, sh, sx, sf, sw, sc, su, loc, out, ry, sy,
):
    nw = 4
    w = lax.axis_index("wt")
    c = lax.axis_index("ctx")
    g = c // G
    m = c % G
    nc = nw * G
    R, width = x_h.shape
    d = width // nw
    par = w % 2
    core = (w + 1 - 2 * par, c)
    seq = 2 * (g % 2) + g // 2
    og = 2 * par + w // 2
    goal = og * G + m
    two = (w + 2) % nw
    goal_two = (2 * par + two // 2) * G + m
    is_a = w == seq
    primary = (w + seq) % 2 == 0
    high = w >= 2
    low = w < 2
    peers = [
        ((w + a) % nw, ((g + e) % nw) * G + m) for a in range(nw) for e in range(nw) if a or e
    ]
    peers += [(w, g * G + (m + e) % G) for e in range(1, G)]
    loads = [
        pltpu.make_async_copy(a, b, loc.at[i])
        for i, (a, b) in enumerate(((wqkv_h, wl), (wout_h, wout)))
    ]
    for copy in loads:
        copy.start()
    greet(peers)

    here = goal == c
    here_two = goal_two == c
    to_y = remote(x_h, Y, sh.at[0], ry.at[0], (two, c))
    to_one = remote(x_h, X.at[c], sh.at[1], rx.at[c], (w, goal))
    to_two = remote(Y, X.at[c], sh.at[4], rx.at[c], (w, goal_two))
    to_first = remote(first_h, Fv.at[c], sh.at[2], rf.at[c], (w, goal))
    home_cot = jnp.logical_and(here, is_a)
    own_cot = pl.ds(pl.multiple_of(g * R, R), R)
    to_cot = remote(cot_h, cot_o.at[own_cot], sh.at[3], rc.at[g], (seq, goal))
    to_y.start()

    @pl.when(here)
    def _():
        pltpu.make_async_copy(x_h, X.at[c], rx.at[c]).start()
        pltpu.make_async_copy(first_h, Fv.at[c], rf.at[c]).start()

    @pl.when(jnp.logical_not(here))
    def _():
        to_one.start()
        to_first.start()

    line[...] = jnp.zeros_like(line)
    for a, ref in enumerate((out_b, gain_one, shift_one, gain_two, shift_two, down_b)):
        at = a // 2
        line[at : at + 1, (a % 2) * d : (a % 2 + 1) * d] = ref[...].astype(F32).reshape(1, d)
    for a in range(2):
        half = up_b[a * 2 * d : (a + 1) * 2 * d].astype(F32).reshape(1, 2 * d)
        line[3 + a : 4 + a, :] = half
    line[5:6, : 6 * d // 4] = qv_b[...].astype(F32).reshape(1, 6 * d // 4)
    small_l[...] = line[...].astype(BF)
    loads[0].wait()
    for a in range(nw):
        for half in range(2):
            at = half * width + a * d
            wqk_h[a, :, half * d : (half + 1) * d] = wl[:, at : at + d]
    for a in range(2):
        at = 2 * width + a * d
        wf_h[a] = wl[:, at : at + d]

    def rows_of(a):
        return pl.ds(pl.multiple_of(a * d, 16), d)

    weights, fresh = [], []
    for e in range(1, nw):
        to = (w + e) % nw
        weights.append(remote(small_l, small.at[w], sw.at[e, 0], rs.at[w], (to, c)))
        weights.append(remote(wqk_h.at[to], wqk.at[rows_of(w)], sw.at[e, 1], rw.at[w], (to, c)))
        fresh.append(
            (to, remote(wf_h.at[to % 2], wf.at[rows_of(w)], sw.at[e, 2], rv.at[w], (to, c)))
        )
    for r in weights:
        r.start()
    for to, r in fresh:

        @pl.when(to < 2)
        def _():
            r.start()

    pltpu.make_async_copy(small_l, small.at[w], rs.at[w]).start()
    pltpu.make_async_copy(wqk_h.at[w], wqk.at[rows_of(w)], rw.at[w]).start()

    @pl.when(low)
    def _():
        pltpu.make_async_copy(wf_h.at[par], wf.at[rows_of(w)], rv.at[w]).start()

    @pl.when(high)
    def _():
        wf[...] = jnp.zeros_like(wf)

    def got(ref, sem):
        pltpu.make_async_copy(ref, ref, sem).wait()

    got(Y, ry.at[0])

    @pl.when(here_two)
    def _():
        pltpu.make_async_copy(Y, X.at[c], rx.at[c]).start()

    @pl.when(jnp.logical_not(here_two))
    def _():
        to_two.start()

    def core_x(b):
        return remote(X.at[b], X.at[b], sx.at[0, b], rx.at[b], core)

    def core_f(b):
        return remote(Fv.at[b], Fv.at[b], sf.at[0, b], rf.at[b], core)

    def member_x(b, e):
        return remote(X.at[b], X.at[b], sx.at[e, b], rx.at[b], (w, g * G + (m + e) % G))

    def member_f(b, e):
        return remote(Fv.at[b], Fv.at[b], sf.at[e, b], rf.at[b], (w, g * G + (m + e) % G))

    def cross_f(b):
        return remote(Fv.at[b], Fv.at[b], sy.at[b], rf.at[b], (two, c))

    crossing = jnp.logical_and(is_a, low)

    def take(b, onward):
        got(X.at[b], rx.at[b])

        if onward:

            @pl.when(crossing)
            def _():
                got(Fv.at[b], rf.at[b])
                cross_f(b).start()

        @pl.when(primary)
        def _():
            for e in range(1, G if onward else 1):
                member_x(b, e).start()
            core_x(b).start()

        @pl.when(high)
        def _():
            got(Fv.at[b], rf.at[b])

            @pl.when(primary)
            def _():
                for e in range(1, G if onward else 1):
                    member_f(b, e).start()
                core_f(b).start()

    half_rows = nc * R // 2

    def halves(ref, b, gap, value):
        ref[pl.ds(pl.multiple_of(b * BLK, BLK), BLK), :] = value[:BLK]
        ref[pl.ds(pl.multiple_of(b * BLK + gap, BLK), BLK), :] = value[BLK:]

    def project(b, a):
        at = pl.ds(pl.multiple_of(b * R, R), R)
        value = X[b].astype(F32)
        centred = value - jnp.mean(value, axis=-1, keepdims=True)
        inverse = lax.rsqrt(jnp.mean(centred * centred, axis=-1, keepdims=True) + EPS)
        normal = centred * inverse
        xh[at, :] = normal.astype(BF)
        n = (normal * vec[4:5, :] + vec[5:6, :]).astype(BF)
        qk = product(n, wqk[...])
        halves(k, b, half_rows, qk[:, d : 2 * d].astype(BF))
        if a is not None:
            halves(q, a, 2 * R, (qk[:, :d] + vq[1:2, 0:d]).astype(BF))

        @pl.when(low)
        def _():
            halves(v, b, half_rows, (product(n, wf[...]) + vq[2:3, 0:d]).astype(BF))

        @pl.when(high)
        def _():
            f = Fv[b]
            halves(v, b, half_rows, jnp.where(par == 0, f[:, :d], f[:, d:]))

    for t in range(nw):
        for e in range(2):
            own_pair = deal[(2 * (t % 2) + e) * G + m]
            for b in range(nc):
                seen = deal[b] <= own_pair if t < 2 else deal[b] >= own_pair
                at = b * BLK + (half_rows if t >= 2 else 0)
                bias[2 * t + e, :, at : at + BLK] = jnp.full(
                    (1, BLK), jnp.where(seen, 0.0, NEG), F32
                )
            if t >= 2:
                bias[2 * t + e, :, 0:half_rows] = jnp.zeros((1, half_rows), F32)
    take(g * G + m, True)
    loads[1].wait()
    for a in range(nw):
        got(small.at[a], rs.at[a])
        got(wqk.at[rows_of(a)], rw.at[a])

        @pl.when(low)
        def _():
            got(wf.at[rows_of(a)], rv.at[a])

    nb = 6 * d // 4
    for a in range(nw):
        piece = small[a].astype(F32)
        for row, src in ((0, 0), (1, 3), (2, 4), (4, 1), (5, 2), (6, 5)):
            at = src // 2
            value = piece[at : at + 1, (src % 2) * d : (src % 2 + 1) * d]
            vec[row : row + 1, a * d : (a + 1) * d] = value
        vq[0:1, a * nb : (a + 1) * nb] = piece[5:6, :nb]
    piece = small[w].astype(F32)
    vec[3:4, : 2 * d] = piece[3:4, :]
    vec[3:4, 2 * d :] = piece[4:5, :]
    vec[7:8, :] = jnp.zeros((1, width), F32)
    q_bias = vq[0:1, 0:d]
    for a in range(1, nw):
        q_bias = jnp.where(w == a, vq[0:1, a * d : (a + 1) * d], q_bias)
    f_bias = jnp.where(
        par == 0, vq[0:1, width : width + d], vq[0:1, width + d : width + 2 * d]
    )
    vq[1:2, 0:d] = q_bias
    vq[2:3, 0:d] = f_bias
    project(g * G + m, g)

    def own(i, carry):
        a = (g + i) % nw
        take(a * G + m, True)
        project(a * G + m, a)
        return carry

    lax.fori_loop(1, nw, own, 0)

    @pl.when(home_cot)
    def _():
        pltpu.make_async_copy(cot_h, cot_o.at[own_cot], rc.at[g]).start()

    @pl.when(jnp.logical_not(home_cot))
    def _():
        to_cot.start()

    ups = []
    for e in range(1, nw):
        to = (w + e) % nw
        src = wup_h.at[:, pl.ds(pl.multiple_of(to * width, BLK), width)]
        ups.append(remote(src, wup_o.at[rows_of(w)], su.at[e], ru.at[w], (to, c)))
    for r in ups:
        r.start()
    src = wup_h.at[:, pl.ds(pl.multiple_of(w * width, BLK), width)]
    pltpu.make_async_copy(src, wup_o.at[rows_of(w)], ru.at[w]).start()

    def others(i, carry):
        b = ((g + i % nw) % nw) * G + (m + 1 + i // nw) % G
        take(b, False)
        project(b, None)
        return carry

    lax.fori_loop(0, nw * (G - 1), others, 0)
    outs = [(X, X_o), (xh, xh_o), (k, k_o), (v, v_o)]
    outs = [pltpu.make_async_copy(a, b, out.at[i]) for i, (a, b) in enumerate(outs)]
    for copy in outs:
        copy.start()

    def cot_rows(a):
        return cot_o.at[pl.ds(pl.multiple_of(a * R, R), R)]

    og_two = 2 * par + two // 2
    spread_cot = [
        remote(cot_rows(og), cot_rows(og), sc.at[0], rc.at[og], (two, c)),
        remote(cot_rows(og), cot_rows(og), sc.at[1], rc.at[og], core),
        remote(cot_rows(og_two), cot_rows(og_two), sc.at[2], rc.at[og_two], core),
    ]
    got(cot_rows(og), rc.at[og])
    spread_cot[0].start()
    spread_cot[1].start()

    def attend_one(t, carry):
        at = pl.ds(pl.multiple_of(t * R, R), R)
        ot, lt = attend_tile(H, q[at, :], k, v, bias, 2 * t, 1 + t // 2)
        lse[t] = lt
        pt = product(ot, wout[...]).astype(BF)
        for e in range(2):
            to = (2 * (t % 2) + e) * R + (t // 2) * BLK
            to = pl.ds(pl.multiple_of(to, BLK), BLK)
            o[to, :] = ot[e * BLK : (e + 1) * BLK]
            part[to, :] = pt[e * BLK : (e + 1) * BLK]
        return carry

    lax.fori_loop(0, nw, attend_one, 0)

    got(cot_rows(og_two), rc.at[og_two])
    spread_cot[2].start()
    for copy in outs:
        copy.wait()
    for a in range(nw):
        got(wup_o.at[rows_of(a)], ru.at[a])

    for hi in range(2):
        a = 2 * (1 - par) + hi
        got(cot_rows(a), rc.at[a])

    for r in weights + ups + spread_cot + [to_y]:
        r.wait_send()
    for to, r in fresh:

        @pl.when(to < 2)
        def _():
            r.wait_send()

    @pl.when(jnp.logical_not(here))
    def _():
        to_one.wait_send()
        to_first.wait_send()

    @pl.when(jnp.logical_not(here_two))
    def _():
        to_two.wait_send()

    @pl.when(crossing)
    def _():
        for a in range(nw):
            cross_f(a * G + m).wait_send()

    @pl.when(jnp.logical_not(home_cot))
    def _():
        to_cot.wait_send()

    @pl.when(primary)
    def _():

        def sent(b, carry):
            core_x(b).wait_send()

            @pl.when(b % G == m)
            def _():
                for e in range(1, G):
                    member_x(b, e).wait_send()

            @pl.when(high)
            def _():
                core_f(b).wait_send()

                @pl.when(b % G == m)
                def _():
                    for e in range(1, G):
                        member_f(b, e).wait_send()

            return carry

        lax.fori_loop(0, nc, sent, 0)


def head(G, H, deal, vectors, x, first, wqkv, cot, wup, wout):
    nw = 4
    nc = nw * G
    R, width = x.shape
    d = width // nw
    N = nc * R
    dma = pltpu.SemaphoreType.DMA
    vm = pltpu.VMEM
    shape = jax.ShapeDtypeStruct
    operands = (deal,) + vectors + (x, first, wqkv, cot, wup, wout)
    return pl.pallas_call(
        functools.partial(head_kernel, G, H),
        name="head",
        out_shape=(
            shape((nc, R, width), BF),
            shape((N, width), BF),
            shape((N, d), BF),
            shape((N, d), BF),
            shape((width, width), BF),
            shape((nw * R, width), BF),
            shape((nw * R, d), BF),
            shape((nw * R, d), BF),
            shape((nw, 8, R), F32),
            shape((nw * R, width), BF),
            shape((width, 2 * d), BF),
            shape((width, d), BF),
            shape((8, width), F32),
        ),
        in_specs=[pl.BlockSpec(memory_space=pltpu.SMEM)] + [VM] * len(vectors) + [ANY] * 6,
        out_specs=[ANY] * 6 + [VM] * 7,
        scratch_shapes=[
            vm((nc, R, width), BF), vm((nc, R, 2 * d), BF), vm((N, width), BF), vm((N, d), BF),
            vm((N, d), BF), vm((nw, 8, 2 * d), BF), vm((8, 6 * d), F32),
            vm((2 * nw, 1, N), F32), vm(wout.shape, BF), vm(wqkv.shape, BF),
            vm((nw, d, 2 * d), BF), vm((2, d, d), BF), vm((R, width), BF),
            vm((8, 2 * d), F32), vm((8, 2 * d), BF),
            dma((nc,)), dma((nc,)), dma((nw,)), dma((nw,)), dma((nw,)), dma((nw,)), dma((nw,)),
            dma((6,)), dma((G, nc)), dma((G, nc)), dma((nw, 3)), dma((nw,)), dma((nw,)),
            dma((2,)), dma((4,)), dma((1,)), dma((nc,)),
        ],
        compiler_params=pltpu.CompilerParams(
            collective_id=0, has_side_effects=True, vmem_limit_bytes=56 << 20
        ),
        cost_estimate=pl.CostEstimate(
            flops=14 << 30, bytes_accessed=40 << 20, transcendentals=6 << 20
        ),
    )(*operands)


EARLY = 3


def ring_place(nc):
    w, c = lax.axis_index("wt"), lax.axis_index("ctx")
    odd = c % 2
    pos = (c // 2) * (1 - odd) + (nc - 1 - c // 2) * odd

    def ctx_at(p):
        p = (p + nc) % nc
        h = p // (nc // 2)
        return 2 * p * (1 - h) + (2 * (nc - 1 - p) + 1) * h

    return pos, (w, ctx_at(pos + 1)), (w, ctx_at(pos - 1))


class Ring:
    def __init__(self, nc, pos, right, left, seg, chains, A, slots, out, ss, sr):
        self.nc, self.pos, self.right, self.left, self.seg = nc, pos, right, left, seg
        self.chains, self.A, self.slots, self.out, self.ss, self.sr = chains, A, slots, out, ss, sr
        self.steps = 2 * (nc - 1)
        self.cut = A.shape[1] // chains

    def at(self, half, j):
        j = (j + 2 * self.nc) % self.nc
        return pl.ds(pl.multiple_of((half * self.nc + j) * self.seg, 16), self.seg)

    def cols(self, i):
        if self.chains == 1:
            return pl.ds(0, self.cut)
        return pl.ds(pl.multiple_of(i * self.cut, BLK), self.cut)

    def reduce_copies(self, i, s):
        k = self.cols(i)
        return [
            remote(
                self.A.at[self.at(h, j), k],
                self.slots.at[h, s, :, k],
                self.ss.at[h, i, s],
                self.sr.at[h, i, s],
                to,
            )
            for h, j, to in ((0, self.pos - s, self.right), (1, self.pos + s, self.left))
        ]

    def gather_copies(self, i, s):
        k = self.cols(i)
        t = s - (self.nc - 1)
        return [
            remote(
                self.out.at[self.at(h, j), k],
                self.out.at[self.at(h, j), k],
                self.ss.at[h, i, s],
                self.sr.at[h, i, s],
                to,
            )
            for h, j, to in ((0, self.pos + 1 - t, self.right), (1, self.pos - 1 + t, self.left))
        ]

    def send(self, i, s, gathering=False):
        for r in (self.gather_copies if gathering else self.reduce_copies)(i, s):
            r.start()

    start = 0

    def begin(self, start=0):
        self.start = start
        for i in range(self.chains):
            self.send(i, start)

    def add(self, i, s):
        k = self.cols(i)
        for h, j in ((0, self.pos - s - 1), (1, self.pos + s + 1)):
            at = self.at(h, j)
            slot = self.slots.at[h, s, :, k]
            pltpu.make_async_copy(slot, slot, self.sr.at[h, i, s]).wait()
            value = self.A[at, k].astype(F32) + self.slots[h, s, :, k].astype(F32)
            self.A[at, k] = value.astype(BF)

    def early(self, s, steps):
        for i in range(self.chains):
            self.add(i, s)

        @pl.when(s < steps - 1)
        def _():
            for i in range(self.chains):
                self.send(i, s + 1)

    def early_drain(self, steps):
        for s in range(steps):
            for i in range(self.chains):
                for r in self.reduce_copies(i, s):
                    r.wait_send()

    def keep(self, i):
        k = self.cols(i)
        for h, j in ((0, self.pos + 1), (1, self.pos - 1)):
            self.out[self.at(h, j), k] = self.A[self.at(h, j), k]

    def arrive(self, i, s):
        t = s - (self.nc - 1)
        for h, j in ((0, self.pos - t), (1, self.pos + t)):
            at = self.out.at[self.at(h, j), self.cols(i)]
            pltpu.make_async_copy(at, at, self.sr.at[h, i, s]).wait()

    def step(self, s):
        for i in range(self.chains):
            self.turn(i, s)

    def turn(self, i, s):
        last = self.nc - 2
        if isinstance(s, int):
            when = lambda cond: (lambda body: body() if cond else None)
            both = lambda a, b: a and b
        else:
            when, both = pl.when, jnp.logical_and

        @when(s < last)
        def _():
            self.add(i, s)
            self.send(i, s + 1)

        @when(s == last)
        def _():
            self.add(i, last)
            self.keep(i)
            self.send(i, last + 1, True)

        @when(both(s > last, s < self.steps))
        def _():
            self.arrive(i, s)

        @when(both(s > last, s < self.steps - 1))
        def _():
            self.send(i, s + 1, True)

    def drain(self):
        for gathering in (False, True):

            def one(t, carry):
                i, s = t % self.chains, t // self.chains
                for r in (self.gather_copies if gathering else self.reduce_copies)(i, s):
                    r.wait_send()
                return carry

            half = self.steps * self.chains // 2
            low = half if gathering else self.start * self.chains
            lax.fori_loop(low, half * (1 + gathering), one, 0)


class SplitRing(Ring):
    def __init__(self, nc, pos, right, left, seg, chains, A, slots, out, ss, sr, own, sems):
        super().__init__(nc, pos, right, left, seg, chains, A, slots, out, ss, sr)
        self.turns = nc - 1
        self.w, self.c = own
        self.s_ex, self.r_ex, self.s_hop, self.r_hop = sems
        self.group = nc // 2
        self.reach = (nc // 2, nc // 2 - 1)

    def turn(self, i, s):
        last = self.nc - 2
        if isinstance(s, int):
            when = lambda cond: (lambda body: body() if cond else None)
        else:
            when = pl.when

        @when(s <= last)
        def _():
            self.add(i, s)

        @when(s < last)
        def _():
            self.send(i, s + 1)

    def parts(self):
        for h, j in ((0, self.pos + 1), (1, self.pos - 1)):
            j = (j + self.nc) % self.nc
            to = 2 * h + j // self.group
            src = self.A.at[self.at(h, j)]
            dst = self.out.at[j % self.group, self.w]
            yield h, to, src, dst

    def exchange(self):
        for h, to, src, dst in self.parts():
            local = pltpu.make_async_copy(src, dst, self.r_ex.at[self.w])
            far = remote(src, dst, self.s_ex.at[h], self.r_ex.at[self.w], (to, self.c))

            @pl.when(to == self.w)
            def _():
                local.start()

            @pl.when(to != self.w)
            def _():
                far.start()

    def held(self, position):
        j = (position + 1 - 2 * (self.w // 2) + 2 * self.nc) % self.nc
        return j // self.group == self.w % 2, j % self.group

    def hop_copy(self, way, h, j):
        ref = self.out.at[j]
        to = (self.right, self.left)[way]
        return remote(ref, ref, self.s_hop.at[way, h], self.r_hop.at[way, h], to)

    def spread(self):
        have, j = self.held(self.pos)

        @pl.when(have)
        def _():
            for a in range(4):
                ref = self.out.at[j, a]
                pltpu.make_async_copy(ref, ref, self.r_ex.at[a]).wait()
            for way in range(2):
                self.hop_copy(way, 1, j).start()

    def hop(self, h):
        for way in range(2):
            if h > self.reach[way]:
                continue
            have, j = self.held(self.pos - h if way == 0 else self.pos + h)

            @pl.when(have)
            def _():
                ref = self.out.at[j]
                pltpu.make_async_copy(ref, ref, self.r_hop.at[way, h]).wait()
                if h < self.reach[way]:
                    self.hop_copy(way, h + 1, j).start()

    def drain(self):
        def one(t, carry):
            i, s = t % self.chains, t // self.chains
            for r in self.reduce_copies(i, s):
                r.wait_send()
            return carry

        lax.fori_loop(self.start * self.chains, self.turns * self.chains, one, 0)
        for h, to, src, dst in self.parts():

            @pl.when(to != self.w)
            def _():
                remote(src, dst, self.s_ex.at[h], self.r_ex.at[self.w], (to, self.c)).wait_send()

        for way in range(2):
            for h in range(self.reach[way]):
                have, j = self.held(self.pos - h if way == 0 else self.pos + h)

                @pl.when(have)
                def _():
                    self.hop_copy(way, h + 1, j).wait_send()


def tail_kernel(
    G, H, seg_o, seg_u, seg_b,
    deal, q_h, k_h, v_h, o_h, do_h, lse_h, xh_h, X_h, wqk_h, wf_h, vec_h, dmid_h,
    up_h, down_h, gout_h, vsums, mlp_h, mid_h,
    layer_out, tokens_out, first_out, up_out, down_out, gout_out, qkv_out, rows_out,
    q, k, v, o, do, lse, lift, xh, X, wqk, wf, vec, dmid,
    kt, dk, dv, dqk, dvb, D, b1, ab, b2, st, b3, tot, tb, tr,
    O, slots_o, res_o, A, slots_a, res_a, U, slots_u, res_u, gq, slots_b, res_b, gain_t, shift_t, sums_t, line, f1, fs, fr,
    mlp, mid, lb, ly, lr, sl, rl, sL, rL, s1, r1, s2, r2, s3, r3, sT, rT, sso, sro, ssa, sra, ssu, sru, seu, reu, shu, rhu, ssb, srb, seb, reb, shb, rhb, sf1, rf1, sf2, rf2, ld,
):
    w = lax.axis_index("wt")
    c = lax.axis_index("ctx")
    nw = 4
    nc = nw * G
    g = c // G
    m = c % G
    par = w % 2
    hi = w // 2
    core = (w + 1 - 2 * par, c)
    other = ((w + 2) % nw, c)
    R, width = dmid.shape
    d = width // nw
    N = xh.shape[0]
    pos, right, left = ring_place(nc)
    loads = [
        (up_h, U),
        (down_h, A),
        (gout_h, O.at[pl.ds(0, d)]),
        (k_h, k), (v_h, v), (q_h, q), (o_h, o), (do_h, do), (lse_h, lse),
        (xh_h, xh), (X_h, X), (wqk_h, wqk), (wf_h, wf), (vec_h, vec), (dmid_h, dmid), (mid_h, mid), (mlp_h, mlp),
    ]
    loads = [pltpu.make_async_copy(a, b, ld.at[i]) for i, (a, b) in enumerate(loads)]
    for copy in loads:
        copy.start()
    peers = [
        ((w + a) % nw, ((g + e) % nw) * G + m) for a in range(nw) for e in range(nw) if a or e
    ]
    peers += [(w, g * G + (m + e) % G) for e in range(1, G)]
    greet(peers + [right, left])
    ring_o = Ring(nc, pos, right, left, seg_o, 1, O, slots_o, res_o, sso, sro)
    ring_a = Ring(nc, pos, right, left, seg_u, 2, A, slots_a, res_a, ssa, sra)
    ring_u = SplitRing(
        nc, pos, right, left, seg_u, 2, U, slots_u, res_u, ssu, sru, (w, c), (seu, reu, shu, rhu)
    )
    ring_b = SplitRing(
        nc, pos, right, left, seg_b, 1, gq, slots_b, res_b, ssb, srb, (w, c), (seb, reb, shb, rhb)
    )
    for copy in loads[:3]:
        copy.wait()
    foot = O.shape[0] - d
    line_a = jnp.concatenate([vsums[0:1, :], jnp.zeros((15, width), F32)], axis=0)
    O[d + 16 :, :] = jnp.zeros((foot - 16, width), BF)
    share = vsums[1:5, 0:d]
    for a in range(1, nw):
        share = jnp.where(w == a, vsums[1:5, a * d : (a + 1) * d], share)
    pack = jnp.concatenate([share[a : a + 1, :] for a in range(4)], axis=1)
    pack = jnp.concatenate([jnp.zeros((1, width), F32), pack, jnp.zeros((14, width), F32)], axis=0)
    O[d : d + 16, :] = (line_a + pack).astype(BF)
    ring_u.begin(EARLY)
    ring_a.begin(EARLY)
    ring_o.begin()
    for copy in loads[3:9] + loads[15:]:
        copy.wait()
    seq = 2 * (g % 2) + g // 2
    og = 2 * par + hi
    home = (seq, og * G + m)
    home_self = jnp.logical_and(og == g, w == seq)
    shares = []
    for e in range(1, nw):
        to = (w + e) % nw
        src = mlp.at[pl.ds(pl.multiple_of((2 * (to % 2) + to // 2) * R, R), R)]
        r = remote(src, lb.at[w], sl.at[e], rl.at[w], (to, c))
        r.start()
        shares.append(r)

    flip_rows(k, kt)
    dk[...] = jnp.zeros_like(dk)
    dv[...] = jnp.zeros_like(dv)
    dqk[...] = jnp.zeros_like(dqk)
    wide = H * HEAD_DIM

    def poll(n):
        for r in range(4):

            @pl.when(n % 4 == r)
            def _():
                (ring_a if r % 2 else ring_u).turn(r // 2, EARLY + n // 4)
                if r == 3:
                    ring_o.turn(0, n // 4)

    pairs = lax.broadcasted_iota(jnp.int32, (1, 2 * BLK), 1) < BLK
    for t in range(nw):
        mine = [deal[(2 * (t % 2) + e) * G + m] for e in range(2)]
        for b in range(nc):
            unseen = [
                jnp.where(deal[b] <= a if t < 2 else deal[b] >= a, 0.0, -NEG) for a in mine
            ]
            at = b if t < 2 else nc + b
            lift[t, at : at + 1, :] = jnp.where(pairs, unseen[0], unseen[1])
        if t >= 2:
            lift[t, 0:nc, :] = jnp.zeros((nc, 2 * BLK), F32)

    def tile(t, carry):
        rows = []
        for e in range(2):
            at = (2 * (t % 2) + e) * R + (t // 2) * BLK
            rows.append(pl.ds(pl.multiple_of(at, BLK), BLK))
        pick = lambda ref: jnp.concatenate([ref[rows[0], :], ref[rows[1], :]], axis=0)
        mine = pl.ds(pl.multiple_of(t * R, R), R)

        def polls_at(j):
            n = 2 * (t + t // 3 + j)
            poll(n)
            poll(n + 1)

        dqt = attend_back_tile(
            H, q[mine, :], pick(do), pick(o), lse[t], k, v, kt, dk, dv, lift, t, 1 + t // 2,
            polls_at,
        )
        dq = jnp.transpose(dqt).astype(BF)
        for e in range(2):
            at = ((2 * (t % 2) + e) * G + m) * R + (t // 2) * BLK
            at = pl.ds(pl.multiple_of(at, BLK), BLK)
            dqk[at, 0:wide] = dq[e * BLK : (e + 1) * BLK]
        return carry

    lax.fori_loop(0, nw, tile, 0)

    def deal_back(b, carry):
        for e in range(2):
            src = pl.ds(pl.multiple_of(b * BLK + e * (N // 2), BLK), BLK)
            to = pl.ds(pl.multiple_of(b * R + e * BLK, BLK), BLK)
            dqk[to, wide : 2 * wide] = dk[src, :].astype(BF)
            dvb[to, :] = dv[src, :].astype(BF)
        return carry

    lax.fori_loop(0, nc, deal_back, 0)
    polls = 12
    for copy in loads[9:15]:
        copy.wait()

    layer = mid[...] + vec[6:7, :] + mlp[pl.ds(pl.multiple_of(og * R, R), R), :].astype(F32)
    for e in range(1, nw):
        src = (w + e) % nw
        pltpu.make_async_copy(lb.at[src], lb.at[src], rl.at[src]).wait()
        layer = layer + lb[src].astype(F32)
    ly[...] = layer.astype(BF)
    layer_back = remote(ly, lr, sL.at[0], rL.at[0], home)
    layer_stay = pltpu.make_async_copy(ly, lr, rL.at[0])

    @pl.when(home_self)
    def _():
        layer_stay.start()

    @pl.when(jnp.logical_not(home_self))
    def _():
        layer_back.start()

    upper = w >= 2
    first_copies = []
    for e in range(1, G):
        mm = (m + e) % G
        for gp in range(nw):
            src = dvb.at[pl.ds(pl.multiple_of((gp * G + mm) * R, R), R)]
            first_copies.append(
                remote(src, f1.at[m, gp], sf1.at[e, gp], rf1.at[m, gp], (w, g * G + mm))
            )

    @pl.when(upper)
    def _():
        for r in first_copies:
            r.start()

    tile_d = 128
    ones = jnp.ones((N, BLK), BF)
    row_qk = product_left(ones, dqk[...])[0:1, :]
    row_f = product_left(ones, dvb[...])[0:1, :]
    sum_qk = product_left(dqk[...], ones)
    sum_f = product_left(dvb[...], ones)
    gain_t[...] = jnp.transpose(jnp.broadcast_to(vec[4:5, :], (BLK, width)))
    shift_t[...] = jnp.transpose(jnp.broadcast_to(vec[5:6, :], (BLK, width)))
    lane = lax.broadcasted_iota(jnp.int32, (d, BLK), 1)
    edge = gq.shape[1] - BLK
    for a in range(nw):
        sums_t[a * d : (a + 1) * d, :] = jnp.where(
            lane == 66, sum_qk[:wide], jnp.where(lane == 67, sum_qk[wide:], sum_f)
        )
    lane = lax.broadcasted_iota(jnp.int32, (tile_d, BLK), 1)

    def grads(i, carry):
        at = pl.ds(pl.multiple_of(i * tile_d, tile_d), tile_d)
        x_qk = product_left(xh[:, at], dqk[...])
        x_f = product_left(xh[:, at], dvb[...])
        w_qk = wqk[at, :].astype(F32)
        w_f = wf[at, :].astype(F32)
        add = lambda a, b: jnp.sum(a, axis=1, keepdims=True) + jnp.sum(b, axis=1, keepdims=True)
        for_gain = add(w_qk * x_qk, w_f * x_f)
        for_shift = add(w_qk * row_qk, w_f * row_f)
        gain = gain_t[at, 0:1]
        shift = shift_t[at, 0:1]
        gq[at, 0 : 2 * wide] = (gain * x_qk + shift * row_qk).astype(BF)
        gq[at, 2 * wide : 3 * wide] = (gain * x_f + shift * row_f).astype(BF)
        ends = gq[at, edge:].astype(F32)
        ends = jnp.where(lane == 64, for_gain, jnp.where(lane == 65, for_shift, ends))
        ends = jnp.where(lane > 65, sums_t[at, :], ends)
        gq[at, edge:] = jnp.where(lane < 69, ends, 0.0).astype(BF)
        poll(polls + i)
        return carry

    lax.fori_loop(0, width // tile_d, grads, 0)
    polls += width // tile_d
    ring_u.exchange()
    ring_b.begin()

    def block(i, carry):
        phase = i // (2 * G)
        jj = (hi + 1 - (i // G) % 2 + 2) % 2
        mm = (m + 1 + i % G) % G
        parity = (1 - par) * (1 - phase) + par * phase
        b = (2 * parity + jj) * G + mm
        at = pl.ds(pl.multiple_of(b * R, R), R)
        dn = product_right(dqk[at, :], wqk[...]) + product_right(dvb[at, :], wf[...])
        D[b] = dn.astype(BF)

        @pl.when(phase == 0)
        def _():
            slot = jj * G + mm
            remote(D.at[b], b1.at[slot], s1.at[slot], r1.at[slot], core).start()

        poll(polls + i)

        @pl.when(i % 4 == 3)
        def _():
            ring_b.step(i // 4)

        return carry

    lax.fori_loop(0, nc, block, 0)
    polls += nc
    done_b = nc // 4

    order = list(range(1, G)) + [0]

    def chip_sum(jj, mm):
        slot = jj * G + mm
        pltpu.make_async_copy(b1.at[slot], b1.at[slot], r1.at[slot]).wait()
        return D[(2 * par + jj) * G + mm].astype(F32) + b1[slot].astype(F32)

    seconds = []
    for e in order:
        mm = (m + e) % G
        ab[mm] = chip_sum(1 - hi, mm).astype(BF)
        r = remote(ab.at[mm], b2.at[mm], s2.at[mm], r2.at[mm], other)
        r.start()
        seconds.append(r)
    thirds = []

    def sum_chips():
        for e in order:
            mm = (m + e) % G
            total = chip_sum(hi, mm)
            pltpu.make_async_copy(b2.at[mm], b2.at[mm], r2.at[mm]).wait()
            total = total + b2[mm].astype(F32)
            if e:
                st[mm] = total.astype(BF)
                r = remote(st.at[mm], b3.at[m], s3.at[mm], r3.at[m], (w, g * G + mm))
                r.start()
                thirds.append(r)
            else:
                tot[...] = total

    def sum_first():
        @pl.when(upper)
        def _():
            for gp in range(nw):
                total = dvb[pl.ds(pl.multiple_of((gp * G + m) * R, R), R), :].astype(F32)
                for e in range(1, G):
                    mm = (m + e) % G
                    pltpu.make_async_copy(f1.at[mm, gp], f1.at[mm, gp], rf1.at[mm, gp]).wait()
                    total = total + f1[mm, gp].astype(F32)
                fs[gp] = total.astype(BF)
                own = jnp.logical_and(w == seq, g == gp)

                @pl.when(own)
                def _():
                    pltpu.make_async_copy(fs.at[gp], fr.at[par], rf2.at[par]).start()

                @pl.when(jnp.logical_not(own))
                def _():
                    remote(
                        fs.at[gp], fr.at[par], sf2.at[gp], rf2.at[par], (seq, gp * G + m)
                    ).start()

    back = remote(tb, tr, sT.at[0], rT.at[0], home)
    stay = pltpu.make_async_copy(tb, tr, rT.at[0])

    def norm_back():
        total = tot[...]
        for e in range(1, G):
            mm = (m + e) % G
            pltpu.make_async_copy(b3.at[mm], b3.at[mm], r3.at[mm]).wait()
            total = total + b3[mm].astype(F32)
        value = X[og * G + m].astype(F32)
        centred = value - jnp.mean(value, axis=-1, keepdims=True)
        inverse = lax.rsqrt(jnp.mean(centred * centred, axis=-1, keepdims=True) + EPS)
        normal = centred * inverse
        dx = total * vec[4:5, :]
        dx = dx - jnp.mean(dx, axis=-1, keepdims=True) - normal * jnp.mean(
            dx * normal, axis=-1, keepdims=True
        )
        tb[...] = (dmid[...].astype(F32) + inverse * dx).astype(BF)

        @pl.when(home_self)
        def _():
            stay.start()

        @pl.when(jnp.logical_not(home_self))
        def _():
            back.start()

    turns = []
    extras = [ring_u.spread]
    extras += [functools.partial(ring_u.hop, h) for h in range(1, ring_u.reach[0] + 1)]
    small = [functools.partial(ring_o.turn, 0, a) for a in range((polls + 0) // 4, ring_o.steps)]
    for n in range(polls, 4 * (ring_a.steps - EARLY)):
        r, s = n % 4, EARLY + n // 4
        if r % 2 and s < ring_a.steps:
            turns.append(functools.partial(ring_a.turn, r // 2, s))
        if (r == 0 or n == polls) and extras:
            turns.append(extras.pop(0))
    turns += extras

    def others():
        if small:
            small.pop(0)()
        for _ in range(2):
            if turns:
                turns.pop(0)()

    for at_b in range(done_b, ring_b.turns):
        ring_b.step(at_b)
        others()
        if at_b == done_b:
            sum_first()
        if at_b == 5:
            sum_chips()
    ring_b.exchange()
    others()
    ring_b.spread()
    others()
    for h in range(1, ring_b.reach[0] + 1):
        ring_b.hop(h)
        others()
        if h == 2:
            norm_back()
    while turns or small:
        others()

    down_out[...] = res_a[0:width, :]
    gout_out[...] = res_o[0:d, :]
    for j in range(ring_u.group):
        rows = slice(j * seg_u, (j + 1) * seg_u)
        for a in range(nw):
            up_out[rows, a * width : (a + 1) * width] = res_u[j, a]
    for j in range(ring_b.group):
        rows = slice(j * seg_b, (j + 1) * seg_b)
        for a in range(nw):
            for part in range(2):
                at = part * width + a * d
                qkv_out[rows, at : at + d] = res_b[j, a, :, part * d : (part + 1) * d]
            if a < 2:
                at = 2 * width + a * d
                qkv_out[rows, at : at + d] = res_b[j, a, :, 2 * d : 3 * d]
            at = a * d + j * seg_b
            sums_t[at : at + seg_b, :] = res_b[j, a, :, edge:].astype(F32)
    ends = jnp.transpose(sums_t[...])
    nb = 6 * d // 4
    line[:, 0:width] = ends[66:67, :]
    line[:, width : width + 2 * d] = ends[68:69, : 2 * d]
    share = line[:, 0:nb]
    for a in range(1, nw):
        share = jnp.where(w == a, line[:, a * nb : (a + 1) * nb], share)
    rows_out[...] = jnp.zeros_like(rows_out)
    rows_out[0:2, :] = res_o[d : d + 16, :].astype(F32)[0:2]
    for row in range(2):
        total = ends[64 + row : 65 + row, 0:d]
        for a in range(1, nw):
            total = total + ends[64 + row : 65 + row, a * d : (a + 1) * d]
        rows_out[2:3, row * d : (row + 1) * d] = total
    rows_out[3:4, 0:nb] = share
    pltpu.make_async_copy(tr, tr, rT.at[0]).wait()
    tokens_out[...] = tr[...]
    for u in range(2):
        pltpu.make_async_copy(fr.at[u], fr.at[u], rf2.at[u]).wait()
        first_out[:, u * d : (u + 1) * d] = fr[u]

    pltpu.make_async_copy(lr, lr, rL.at[0]).wait()
    layer_out[...] = lr[...]
    ring_o.drain()
    ring_a.drain()
    ring_u.drain()
    ring_b.drain()
    for r in seconds + thirds + shares:
        r.wait_send()

    @pl.when(jnp.logical_not(home_self))
    def _():
        back.wait_send()
        layer_back.wait_send()

    @pl.when(upper)
    def _():
        for r in first_copies:
            r.wait_send()
        for gp in range(nw):

            @pl.when(jnp.logical_not(jnp.logical_and(w == seq, g == gp)))
            def _():
                remote(
                    fs.at[gp], fr.at[par], sf2.at[gp], rf2.at[par], (seq, gp * G + m)
                ).wait_send()

    def drain(i, carry):
        jj = (hi + 1 - (i // G) % 2 + 2) % 2
        mm = (m + 1 + i % G) % G
        slot = jj * G + mm
        b = (2 * (1 - par) + jj) * G + mm
        remote(D.at[b], b1.at[slot], s1.at[slot], r1.at[slot], core).wait_send()
        return carry

    lax.fori_loop(0, 2 * G, drain, 0)


def tail(
    G, H, deal, q, k, v, o, do, lse, xh, X, wqk, wf, vec, dmid, up, down, gout, vsums, mlp, mid
):
    nw = 4
    nc = nw * G
    R, width = dmid.shape
    d = width // nw
    N = xh.shape[0]
    wide = H * HEAD_DIM
    seg_o = -(-(d + 16) // (2 * nc * 16)) * 16
    seg_u = seg_b = width // (2 * nc)
    cols = 5 * BLK
    dma = pltpu.SemaphoreType.DMA
    vm = pltpu.VMEM
    steps = 2 * (nc - 1)
    operands = (
        deal, q, k, v, o, do, lse, xh, X, wqk, wf, vec, dmid, up, down, gout, vsums, mlp, mid
    )
    return pl.pallas_call(
        functools.partial(tail_kernel, G, H, seg_o, seg_u, seg_b),
        name="tail",
        out_shape=(
            jax.ShapeDtypeStruct((R, width), BF),
            jax.ShapeDtypeStruct((R, width), BF),
            jax.ShapeDtypeStruct((R, 2 * d), BF),
            jax.ShapeDtypeStruct((d, nw * width), BF),
            jax.ShapeDtypeStruct((width, width), BF),
            jax.ShapeDtypeStruct((d, width), BF),
            jax.ShapeDtypeStruct((d, 2 * width + 2 * d), BF),
            jax.ShapeDtypeStruct((8, width), F32),
        ),
        in_specs=[pl.BlockSpec(memory_space=pltpu.SMEM)] + [ANY] * (len(operands) - 4) + [VM] + [ANY] * 2,
        out_specs=[VM] * 8,
        scratch_shapes=[vm(a.shape, a.dtype) for a in operands[1:7]]
        + [vm((nw, 2 * nc, R), F32)]
        + [vm(a.shape, a.dtype) for a in operands[7:13]]
        + [
            vm((wide, N), BF), vm((N, wide), F32), vm((N, wide), F32), vm((N, 2 * wide), BF),
            vm((N, wide), BF), vm((nc, R, width), BF), vm((2 * G, R, width), BF),
            vm((G, R, width), BF), vm((G, R, width), BF), vm((G, R, width), BF),
            vm((G, R, width), BF), vm((R, width), F32), vm((R, width), BF), vm((R, width), BF),
            vm((2 * nc * seg_o, width), BF), vm((2, nc - 1, seg_o, width), BF),
            vm((2 * nc * seg_o, width), BF),
            vm((width, width), BF), vm((2, nc - 1, seg_u, width), BF), vm((width, width), BF),
            vm((width, width), BF), vm((2, nc - 1, seg_u, width), BF),
            vm((nc // 2, nw, seg_u, width), BF),
            vm((width, cols), BF), vm((2, nc - 1, seg_b, cols), BF),
            vm((nc // 2, nw, seg_b, cols), BF),
            vm((width, BLK), F32), vm((width, BLK), F32), vm((width, BLK), F32),
            vm((1, 6 * d), F32),
            vm((G, nw, R, d), BF), vm((nw, R, d), BF), vm((2, R, d), BF),
            vm((nw * R, width), BF), vm((R, width), F32), vm((nw, R, width), BF),
            vm((R, width), BF), vm((R, width), BF), dma((nw,)), dma((nw,)), dma((1,)), dma((1,)),
            dma((2 * G,)), dma((2 * G,)), dma((G,)), dma((G,)), dma((G,)), dma((G,)),
            dma((1,)), dma((1,)), dma((2, 1, steps)), dma((2, 1, steps)),
            dma((2, 2, steps)), dma((2, 2, steps)),
        ]
        + [
            dma(a)
            for chains in (2, 1)
            for a in (
                (2, chains, nc - 1), (2, chains, nc - 1), (2,), (nw,), (2, nc // 2 + 1),
                (2, nc // 2 + 1),
            )
        ]
        + [
            dma((G, nw)), dma((G, nw)),
            dma((nw,)), dma((2,)), dma((len(operands),)),
        ],
        compiler_params=pltpu.CompilerParams(
            collective_id=2, has_side_effects=True, vmem_limit_bytes=63 << 20
        ),
        cost_estimate=pl.CostEstimate(
            flops=40 << 30, bytes_accessed=60 << 20, transcendentals=6 << 20
        ),
    )(*operands)


def on_device(
    nw,
    nc,
    tokens,
    first_values,
    cotangent,
    deal,
    w_qkv,
    bias_qv,
    w_out,
    bias_out,
    gain_one,
    shift_one,
    gain_two,
    shift_two,
    w_up,
    bias_up,
    w_down,
    bias_down,
):
    G = nc // nw
    w = lax.axis_index("wt")
    c = lax.axis_index("ctx")
    m = c % G
    rows, width = tokens.shape[1:]
    d = width // nw
    H = HEADS // nw
    both = ("wt", "ctx")
    seq = lambda g: 2 * (g % 2) + g // 2
    swap = [
        (a * nc + g * G + e, seq(g) * nc + a * G + e)
        for a in range(nw)
        for g in range(nw)
        for e in range(G)
    ]
    ring = [[(a, (a + k) % nw) for a in range(nw)] for k in range(nw)]

    def exchange(pieces):
        out = jnp.zeros_like(pieces)
        mine = lax.dynamic_index_in_dim(pieces, w, 0, keepdims=True)
        out = lax.dynamic_update_slice_in_dim(out, mine, w, 0)
        for k in range(1, nw):
            piece = lax.dynamic_index_in_dim(pieces, (w + k) % nw, 0, keepdims=True)
            got = lax.ppermute(piece, "wt", ring[k])
            out = lax.dynamic_update_slice_in_dim(out, got, (w + nw - k) % nw, 0)
        return out

    qk = w_qkv[:, : 2 * width].reshape(d, 2, nw, d).transpose(2, 0, 1, 3).reshape(nw, d, 2 * d)
    wf = w_qkv[:, 2 * width :].reshape(d, 2, d).transpose(1, 0, 2)
    nb = bias_qv.shape[0]
    ids = dealt_blocks(deal)
    qpos = jnp.arange(nw, dtype=jnp.int32) * G + m
    qid = jnp.take(ids.reshape(nc, 2), qpos, axis=0)
    hidden = (ids[None, None, :] > qid[:, :, None]).astype(F32) * -NEG
    bias = jnp.repeat(-hidden.reshape(2 * nw, 2 * nc), BLK, axis=1)[:, None, :]
    lift = jnp.repeat(hidden.transpose(0, 2, 1), BLK, axis=2)

    def mine(vector):
        return lax.dynamic_slice_in_dim(vector, w * d, d)

    if nc <= 8:
        vectors = (
            bias_out, gain_one, shift_one, gain_two, shift_two, bias_down, bias_up, bias_qv
        )
        X, xhat, k, v, Wup, cot, q, o, lse, part, Wqk, Wf, vec = head(
            G, H, deal, vectors, tokens[0], first_values[0], w_qkv, cotangent[0], w_up, w_out
        )
        mlp, mid_own, d_mid, d_o, g_up, g_down, g_out, vsums = middle(
            G, True, part, X, cot, o, Wup, w_down, w_out, vec
        )
        layer, grad_tokens, grad_first, s_up, s_down, s_out, s_qkv, sums = tail(
            G, H, deal, q, k, v, o, d_o, lse, xhat, X, Wqk, Wf, vec,
            d_mid, g_up, g_down, g_out, vsums, mlp, mid_own,
        )
        return (
            layer[None],
            grad_tokens.astype(F32)[None],
            grad_first.astype(F32)[None],
            s_qkv.astype(F32),
            sums[3, :nb],
            s_out.astype(F32),
            sums[1, d : 2 * d],
            sums[2, :d],
            sums[2, d : 2 * d],
            sums[1, 2 * d : 3 * d],
            sums[1, 3 * d :],
            s_up.astype(F32),
            sums[0],
            s_down.astype(F32),
            sums[1, :d],
        )

    small = jnp.concatenate(
        [bias_qv, bias_out, gain_one, shift_one, gain_two, shift_two, bias_down]
    )
    lanes = 16 * BLK
    small = jnp.concatenate([small, jnp.zeros((lanes - small.shape[0],), BF)]).reshape(16, BLK)
    X, Fv, WQK, WF, SM = gather(nw, G, tokens[0], first_values[0], qk, wf, small)
    X = X.reshape(nc * rows, width)
    Wqk = WQK.reshape(width, 2 * d)
    low = w < 2
    Wf = jnp.where(low, WF.reshape(width, d), jnp.zeros((width, d), BF))
    SM = SM.reshape(nw, lanes).astype(F32)
    qv_vector = SM[:, :nb].reshape(-1)
    vectors = [SM[:, nb + a * d : nb + (a + 1) * d].reshape(-1) for a in range(6)]
    out_vector, gain_a, shift_a, gain_b, shift_b, down_vector = vectors

    x32 = X.astype(F32)
    mean = jnp.mean(x32, axis=-1, keepdims=True)
    centred = x32 - mean
    inverse = lax.rsqrt(jnp.mean(centred * centred, axis=-1, keepdims=True) + EPS)
    n1 = (centred * inverse * gain_a + shift_a).astype(BF)
    pqk = product(n1, Wqk)
    q_bias = lax.dynamic_slice_in_dim(qv_vector, w * d, d)
    f_bias = lax.dynamic_slice_in_dim(qv_vector, width + (w % 2) * d, d)
    q = (pqk[:, :d] + q_bias).astype(BF)
    k = pqk[:, d:].astype(BF)
    f = (product(n1, Wf) + f_bias).astype(BF)
    Fv = Fv.reshape(nc * rows, 2 * d)
    first = jnp.where(w % 2 == 0, Fv[:, :d], Fv[:, d:])
    v = jnp.where(low, f, first)

    o, lse = attend(H, qpos, bias, q, k, v)

    part = product(o, w_out).astype(BF)
    pieces, spread = lax.optimization_barrier((w_up, cotangent[0], X))[:2]
    Wup = exchange(pieces.reshape(d, nw, width).transpose(1, 0, 2)).reshape(width, width)
    unswap = [(b, a) for a, b in swap]
    cot = lax.all_gather(lax.ppermute(spread, both, unswap), "wt", axis=0, tiled=True)
    vec = jnp.stack([out_vector, gain_b, shift_b, bias_up.astype(F32)] + [out_vector] * 4)
    mlp, mid_own, d_mid, d_o, g_up, g_down, g_out, vsums = middle(
        G, False, part, X.reshape(nc, rows, width), cot, o, Wup, w_down, w_out, vec
    )

    mlp = lax.psum_scatter(mlp, "wt", scatter_dimension=0, tiled=True)
    layer = (mid_own + mlp.astype(F32) + down_vector).astype(BF)
    layer = lax.ppermute(layer, both, swap)
    up_rows = exchange(g_up.reshape(nw, d, width)).transpose(1, 0, 2)
    s_up, s_down = lax.psum((up_rows.reshape(d, nw * width), g_down), "ctx")
    dqk, dv = attend_back(H, qpos, lift, q, k, v, o, d_o, lse)
    zero = jnp.zeros_like(dv)
    df = jnp.where(low, dv, zero)
    dn1 = product_right(dqk, Wqk) + product_right(df, Wf)
    dn1_low = dn1.astype(BF)
    blank = jnp.zeros_like(dv)
    left = jnp.where(w == 2, dv, blank)
    right = jnp.where(w == 3, dv, blank)
    total = scatter_sum(
        G, jnp.concatenate([dn1_low, left, right], axis=1).reshape(nc, rows, width + 2 * d)
    )
    grad_first = lax.ppermute(total[:, width:].astype(BF), both, swap).astype(F32)
    block = (w * G + m) * rows
    x_own = lax.dynamic_slice_in_dim(X, block, rows).astype(F32)
    _, pull_one = jax.vjp(lambda a: norm_rows(a, gain_a, shift_a), x_own)
    d_x = d_mid.astype(F32) + pull_one(total[:, :width])[0]
    grad_tokens = lax.ppermute(d_x.astype(BF), both, swap).astype(F32)

    g_qk = product_left(n1, dqk)
    g_f = product_left(n1, df)
    normal = centred * inverse
    g_gain_one = jnp.sum(dn1_low.astype(F32) * normal, axis=0)
    g_shift_one = jnp.sum(dn1_low.astype(F32), axis=0)
    cols = jnp.concatenate(
        [
            g_qk.astype(BF),
            g_f.astype(BF),
            g_gain_one[:, None].astype(BF),
            g_shift_one[:, None].astype(BF),
            jnp.zeros((width, 62), BF),
        ],
        axis=1,
    ).reshape(nw, d, 640)
    sums = jnp.concatenate(
        [jnp.sum(dqk.astype(F32), axis=0), jnp.sum(df.astype(F32), axis=0), jnp.zeros((64,), F32)]
    ).astype(BF)
    foot = jnp.concatenate([sums[None], jnp.zeros((7, 640), BF)], axis=0)
    pack = jnp.concatenate([cols, jnp.broadcast_to(foot[None], (nw, 8, 640))], axis=1)
    pack = exchange(pack)
    vecs = jnp.concatenate(
        [
            vsums[0],
            mine(vsums[1]),
            mine(vsums[2]),
            mine(vsums[3]),
            mine(vsums[4]),
        ]
    ).astype(BF)
    pack = pack.at[0, d + 1 : d + 4, :512].set(vecs.reshape(3, 512))
    pack, s_up, s_down = lax.optimization_barrier((pack, s_up, s_down))
    pack, s_out = lax.psum((pack, g_out), "ctx")
    body = pack[:, :d]
    s_qkv = jnp.concatenate(
        [body[a, :, e * d : (e + 1) * d] for e in (0, 1) for a in range(nw)]
        + [body[a, :, 2 * d : 3 * d] for a in range(2)],
        axis=1,
    ).astype(F32)
    s_gain_one = jnp.sum(body[:, :, 576].astype(F32), axis=0)
    s_shift_one = jnp.sum(body[:, :, 577].astype(F32), axis=0)
    ends = pack[:, d]
    bias_all = jnp.concatenate([ends[:, :d].reshape(-1), ends[:2, 2 * d : 3 * d].reshape(-1)])
    s_bias_qv = lax.dynamic_slice_in_dim(bias_all, w * nb, nb).astype(F32)
    vecs = pack[0, d + 1 : d + 4, :512].reshape(-1).astype(F32)
    s_bias_up = vecs[:width]
    s_bias_down, s_bias_out, s_gain_two, s_shift_two = [
        vecs[width + a * d : width + (a + 1) * d] for a in range(4)
    ]
    return (
        layer[None],
        grad_tokens[None],
        grad_first[None],
        s_qkv,
        s_bias_qv,
        s_out.astype(F32),
        s_bias_out,
        s_gain_one,
        s_shift_one,
        s_gain_two,
        s_shift_two,
        s_up.astype(F32),
        s_bias_up,
        s_down.astype(F32),
        s_bias_down,
    )


def solution(mesh):
    rows3 = P("wt", "ctx", None)
    mat = P("wt", None)
    vec = P("wt")
    in_specs = (rows3, rows3, rows3, P(), mat, vec, mat) + (vec,) * 5 + (mat, vec, mat, vec)
    out_specs = (
        (rows3, rows3, rows3, mat, vec, mat) + (vec,) * 5 + (mat, vec, mat, vec)
    )
    return jax.shard_map(
        functools.partial(on_device, mesh.shape["wt"], mesh.shape["ctx"]),
        mesh=mesh,
        in_specs=in_specs,
        out_specs=out_specs,
        check_vma=False,
    )
```

```python
import functools

import jax
import jax.numpy as jnp
from jax import lax
from jax.experimental import pallas as pl
from jax.experimental.pallas import tpu as pltpu
from jax.sharding import PartitionSpec as P

HEADS = 12
HEAD_DIM = 64
BLK = 128
CHUNK = 1024

EPS = 1e-05
SLOPE = 0.7978845608028654
CUBIC = 0.044715
NEG = -1e30

BF = jnp.bfloat16
F32 = jnp.float32
MESH = pl.DeviceIdType.MESH
ANY = pl.BlockSpec(memory_space=pl.ANY)
VM = pl.BlockSpec(memory_space=pltpu.VMEM)


def norm_rows(value, gain, shift):
    mean = jnp.mean(value, axis=-1, keepdims=True)
    centred = value - mean
    inverse = lax.rsqrt(jnp.mean(centred * centred, axis=-1, keepdims=True) + EPS)
    return centred * inverse * gain + shift


def gelu_tanh(value):
    return 0.5 * value * (1.0 + jnp.tanh(SLOPE * (value + CUBIC * value * value * value)))


def product(left, right):
    return jnp.dot(left, right, preferred_element_type=F32)


def product_left(left, right):
    return lax.dot_general(left, right, (((0,), (0,)), ((), ())), preferred_element_type=F32)


def product_right(left, right):
    return lax.dot_general(left, right, (((1,), (1,)), ((), ())), preferred_element_type=F32)


def dealt_blocks(deal):
    count = deal.shape[0] * 2
    pairs = jnp.repeat(deal, 2)
    parity = jnp.arange(count, dtype=jnp.int32) % 2
    return jnp.where(parity == 0, pairs, count - 1 - pairs)


def remote(src, dst, send, recv, device):
    return pltpu.make_async_remote_copy(
        src_ref=src,
        dst_ref=dst,
        send_sem=send,
        recv_sem=recv,
        device_id=device,
        device_id_type=MESH,
    )


def greet(peers):
    barrier = pltpu.get_barrier_semaphore()
    for peer in peers:
        pl.semaphore_signal(barrier, inc=1, device_id=peer, device_id_type=MESH)
    pl.semaphore_wait(barrier, len(peers))


def gather_kernel(
    nw, G, x, first, wqk, wf, small, X, Fv, WQK, WF, SM, rx, rf, rw, rv, rs, sa, sx, sfa, sfx, sw, loc
):
    w = lax.axis_index("wt")
    c = lax.axis_index("ctx")
    g = c // G
    m = c % G
    nc = nw * G
    core = w + 1 - 2 * (w % 2)
    other = (w + 2) % nw
    rel = lambda k: (w + k) % nw
    peers = [(rel(k), c) for k in range(1, nw)]
    peers += [(w, ((g + k) % nw) * G + m) for k in range(1, nw)]
    peers += [(w, g * G + (m + k) % G) for k in range(1, G)]
    greet(peers)
    seq = 2 * (g % 2) + g // 2
    goal = (2 * (w % 2) + w // 2) * G + m
    is_a = w == seq
    primary = (w + seq) % 2 == 0
    high = w >= 2
    copies = []

    to_head = remote(x, X.at[c], sa.at[0], rx.at[c], (w, goal))
    to_head_f = remote(first, Fv.at[c], sa.at[1], rf.at[c], (w, goal))
    own_x = pltpu.make_async_copy(x, X.at[c], rx.at[c])
    own_f = pltpu.make_async_copy(first, Fv.at[c], rf.at[c])

    @pl.when(is_a)
    def _():
        own_x.start()
        own_f.start()

    @pl.when(jnp.logical_not(is_a))
    def _():
        to_head.start()
        to_head_f.start()

    own_w = pltpu.make_async_copy(wqk.at[w], WQK.at[w], loc.at[0])
    own_s = pltpu.make_async_copy(small, SM.at[w], loc.at[1])
    own_w.start()
    own_s.start()
    own_v = pltpu.make_async_copy(wf.at[w % 2], WF.at[w], loc.at[2])
    own_v.start()
    sends_w, sends_v, sends_s = [], [], []
    for k in range(1, nw):
        d = rel(k)
        s = remote(small, SM.at[w], sw.at[k, 0], rs.at[w], (d, c))
        s.start()
        q = remote(wqk.at[d], WQK.at[w], sw.at[k, 1], rw.at[w], (d, c))
        q.start()
        v = remote(wf.at[d % 2], WF.at[w], sw.at[k, 2], rv.at[w], (d, c))
        sends_w += [s, q]
        sends_v.append((d, v))

        @pl.when(d < 2)
        def _():
            v.start()

    def block_x(b):
        return pltpu.make_async_copy(X.at[b], X.at[b], rx.at[b])

    def block_f(b):
        return pltpu.make_async_copy(Fv.at[b], Fv.at[b], rf.at[b])

    fwd_core, fwd_other, fwd_member = [], [], []
    for k in range(nw):
        gp = (g + k) % nw
        b = gp * G + m
        to_core = remote(X.at[b], X.at[b], sx.at[0, b], rx.at[b], (core, c))
        to_other = remote(X.at[b], X.at[b], sx.at[1, b], rx.at[b], (other, c))
        to_core_f = remote(Fv.at[b], Fv.at[b], sfx.at[0, b], rf.at[b], (core, c))
        to_other_f = remote(Fv.at[b], Fv.at[b], sfx.at[1, b], rf.at[b], (other, c))
        members = [
            remote(X.at[b], X.at[b], sx.at[1 + e, b], rx.at[b], (w, g * G + (m + e) % G))
            for e in range(1, G)
        ]
        members_f = [
            remote(Fv.at[b], Fv.at[b], sfx.at[1 + e, b], rf.at[b], (w, g * G + (m + e) % G))
            for e in range(1, G)
        ]

        @pl.when(primary)
        def _():
            block_x(b).wait()

            @pl.when(is_a)
            def _():
                to_other.start()

            for r in members:
                r.start()
            to_core.start()

        @pl.when(jnp.logical_and(is_a, jnp.logical_not(high)))
        def _():
            block_f(b).wait()
            to_other_f.start()

        @pl.when(jnp.logical_and(primary, high))
        def _():
            block_f(b).wait()
            for r in members_f:
                r.start()
            to_core_f.start()

        fwd_core.append((to_core, to_core_f))
        fwd_other.append((to_other, to_other_f))
        fwd_member.append((members, members_f))
    for e in range(1, G):
        for k in range(nw):
            b = ((g + k) % nw) * G + (m + e) % G
            to_core = remote(X.at[b], X.at[b], sx.at[0, b], rx.at[b], (core, c))
            to_core_f = remote(Fv.at[b], Fv.at[b], sfx.at[0, b], rf.at[b], (core, c))

            @pl.when(primary)
            def _():
                block_x(b).wait()
                to_core.start()

            @pl.when(jnp.logical_and(primary, high))
            def _():
                block_f(b).wait()
                to_core_f.start()

            fwd_core.append((to_core, to_core_f))

    @pl.when(jnp.logical_not(primary))
    def _():
        for b in range(nc):
            block_x(b).wait()

        @pl.when(high)
        def _():
            for b in range(nc):
                block_f(b).wait()

    own_w.wait()
    own_s.wait()
    own_v.wait()
    for k in range(1, nw):
        src = (w + nw - k) % nw
        pltpu.make_async_copy(wqk.at[0], WQK.at[src], rw.at[src]).wait()
        pltpu.make_async_copy(small, SM.at[src], rs.at[src]).wait()

        @pl.when(w < 2)
        def _():
            pltpu.make_async_copy(wf.at[0], WF.at[src], rv.at[src]).wait()

    for s in sends_w:
        s.wait_send()
    for d, v in sends_v:

        @pl.when(d < 2)
        def _():
            v.wait_send()

    @pl.when(jnp.logical_not(is_a))
    def _():
        to_head.wait_send()
        to_head_f.wait_send()

    @pl.when(primary)
    def _():
        for a, _f in fwd_core:
            a.wait_send()
        for ms, _f in fwd_member:
            for a in ms:
                a.wait_send()

        @pl.when(high)
        def _():
            for _x, a in fwd_core:
                a.wait_send()
            for _x, ms in fwd_member:
                for a in ms:
                    a.wait_send()

    @pl.when(is_a)
    def _():
        for a, _f in fwd_other:
            a.wait_send()

        @pl.when(jnp.logical_not(high))
        def _():
            for _x, a in fwd_other:
                a.wait_send()


def gather(nw, G, x, first, wqk, wf, small):
    nc = nw * G
    rows, width = x.shape
    half = first.shape[1]
    d = width // nw
    dma = pltpu.SemaphoreType.DMA
    return pl.pallas_call(
        functools.partial(gather_kernel, nw, G),
        name="gather_tokens",
        out_shape=(
            jax.ShapeDtypeStruct((nc, rows, width), BF),
            jax.ShapeDtypeStruct((nc, rows, half), BF),
            jax.ShapeDtypeStruct((nw, d, 2 * d), BF),
            jax.ShapeDtypeStruct((nw, d, d), BF),
            jax.ShapeDtypeStruct((nw,) + small.shape, BF),
        ),
        in_specs=[ANY] * 5,
        out_specs=[ANY] * 5,
        scratch_shapes=[
            dma((nc,)),
            dma((nc,)),
            dma((nw,)),
            dma((nw,)),
            dma((nw,)),
            dma((2,)),
            dma((1 + G, nc)),
            dma((2,)),
            dma((1 + G, nc)),
            dma((nw, 3)),
            dma((3,)),
        ],
        compiler_params=pltpu.CompilerParams(collective_id=0, has_side_effects=True),
    )(x, first, wqk, wf, small)


def middle_kernel(
    T, G, crossed, p_hbm, X_hbm, cot_hbm, o_hbm, wup_hbm, wdn_hbm, wout_hbm, vec_hbm,
    mlp, mid_own, dmid_own, do_out, gup, gdn, gout, sums,
    p, x, cot, o, wup, wdn, wout, vec,
    b1, ab, b2, bs, mid, n2s, act, dus, q, b4, ab2, b5, dn, dbs,
    s1, r1, s2, r2, s3, r3, s4, r4, s5, r5, s6, r6, ld, *rings,
):
    w = lax.axis_index("wt")
    c = lax.axis_index("ctx")
    g = c // G
    m = c % G
    core = (w + 1 - 2 * (w % 2), c)
    other = ((w + 2) % 4, c)
    mine = w % 2
    theirs = 1 - mine
    rows = p.shape[0]
    half = rows // 2
    n = half // T
    R = rows // 4
    loads = [
        pltpu.make_async_copy(p_hbm, p, ld.at[0]),
        pltpu.make_async_copy(vec_hbm, vec, ld.at[1]),
    ]
    loads += [
        pltpu.make_async_copy(X_hbm.at[a * G + m], x.at[pl.ds(a * R, R)], ld.at[2 + a])
        for a in range(4)
    ]
    loads += [
        pltpu.make_async_copy(wup_hbm, wup, ld.at[6]),
        pltpu.make_async_copy(wdn_hbm, wdn, ld.at[7]),
        pltpu.make_async_copy(cot_hbm, cot, ld.at[8]),
        pltpu.make_async_copy(wout_hbm, wout, ld.at[9]),
        pltpu.make_async_copy(o_hbm, o, ld.at[10]),
    ]
    for copy in loads:
        copy.start()
    peers = [core, other]
    if crossed:
        slots_u, slots_d, ssu, sru, ssd, srd = rings
        nc = 4 * G
        pos, right, left = ring_place(nc)
        seg = p.shape[1] // (2 * nc)
        ring_u = Ring(nc, pos, right, left, seg, 2, gup, slots_u, None, ssu, sru)
        ring_d = Ring(nc, pos, right, left, seg, 2, gdn, slots_d, None, ssd, srd)
        peers += [right, left]
    greet(peers)

    def rs(base, t):
        return pl.ds(pl.multiple_of(base * half + t * n, n), n)

    loads[0].wait()
    first = []
    for t in range(T):
        r = remote(p.at[rs(theirs, t)], b1.at[t], s1.at[t], r1.at[t], core)
        r.start()
        first.append(r)
    second = []
    for t in range(T):
        first[t].wait_recv()
        ab[t] = (p[rs(mine, t), :].astype(F32) + b1[t].astype(F32)).astype(BF)
        r = remote(ab.at[t], b2.at[t], s2.at[t], r2.at[t], other)
        r.start()
        second.append(r)
    for copy in loads[1:]:
        copy.wait()
    out_b = vec[0:1, :]
    gain = vec[1:2, :]
    shift = vec[2:3, :]
    up_b = vec[3:4, :]
    sums[...] = jnp.zeros_like(sums)

    def two(ref, t):
        return jnp.concatenate([ref[rs(mine, t), :], ref[rs(theirs, t), :]], axis=0)

    def put(ref, t, value):
        ref[rs(mine, t), :] = value[:n]
        ref[rs(theirs, t), :] = value[n:]

    def add_sum(at, value):
        sums[at : at + 1, :] += jnp.sum(value, axis=0, keepdims=True)

    def chain(t):
        pltpu.make_async_copy(b4.at[t], b4.at[t], r4.at[t]).wait()
        ab2[t] = (q[rs(mine, t), :].astype(F32) + b4[t].astype(F32)).astype(BF)
        remote(ab2.at[t], b5.at[t], s5.at[t], r5.at[t], other).start()

    def forward(t, carry):
        pltpu.make_async_copy(b2.at[t], b2.at[t], r2.at[t]).wait()
        bs[rs(mine, t), :] = (ab[t].astype(F32) + b2[t].astype(F32)).astype(BF)
        remote(bs.at[rs(mine, t)], bs.at[rs(mine, t)], s3.at[t], r3.at[t], core).start()

        @pl.when(t > 0)
        def _():
            chain(t - 1)

        pltpu.make_async_copy(bs.at[rs(theirs, t)], bs.at[rs(theirs, t)], r3.at[t]).wait()
        value = two(x, t).astype(F32) + two(bs, t).astype(F32) + out_b
        put(mid, t, value)
        centred = value - jnp.mean(value, axis=-1, keepdims=True)
        inverse = lax.rsqrt(jnp.mean(centred * centred, axis=-1, keepdims=True) + EPS)
        n2 = (centred * inverse * gain + shift).astype(BF)
        put(n2s, t, n2)
        u = product(n2, wup[...]) + up_b
        th = jnp.tanh(SLOPE * (u + CUBIC * u * u * u))
        a = (0.5 * u * (1.0 + th)).astype(BF)
        slope = 0.5 * (1.0 + th) + 0.5 * u * (1.0 - th * th) * SLOPE * (1.0 + 3.0 * CUBIC * u * u)
        put(act, t, a)
        ct = two(cot, t)
        du = (product_right(ct, wdn[...]) * slope).astype(BF)
        put(dus, t, du)
        put(q, t, product_right(du, wup[...]).astype(BF))
        remote(q.at[rs(theirs, t)], b4.at[t], s4.at[t], r4.at[t], core).start()
        put(mlp, t, product(a, wdn[...]).astype(BF))
        add_sum(0, du.astype(F32))
        add_sum(1, ct.astype(F32))
        return carry

    lax.fori_loop(0, T, forward, 0)
    chain(T - 1)

    width = p.shape[1]
    tile = 256

    def grads(i, carry):
        at = pl.ds(pl.multiple_of(i * tile, tile), tile)
        gup[at, :] = product_left(n2s[:, at], dus[...]).astype(BF)
        gdn[at, :] = product_left(act[:, at], cot[...]).astype(BF)
        return carry

    lax.fori_loop(0, width // tile, grads, 0)
    if crossed:
        ring_u.begin()
        ring_d.begin()

    def backward(t, carry):
        pltpu.make_async_copy(b5.at[t], b5.at[t], r5.at[t]).wait()
        dn[rs(mine, t), :] = (ab2[t].astype(F32) + b5[t].astype(F32)).astype(BF)
        remote(dn.at[rs(mine, t)], dn.at[rs(mine, t)], s6.at[t], r6.at[t], core).start()
        pltpu.make_async_copy(dn.at[rs(theirs, t)], dn.at[rs(theirs, t)], r6.at[t]).wait()
        value = two(mid, t)
        centred = value - jnp.mean(value, axis=-1, keepdims=True)
        inverse = lax.rsqrt(jnp.mean(centred * centred, axis=-1, keepdims=True) + EPS)
        normal = centred * inverse
        dn2 = two(dn, t).astype(F32)
        add_sum(3, dn2 * normal)
        add_sum(4, dn2)
        dx = dn2 * gain
        dx = dx - jnp.mean(dx, axis=-1, keepdims=True) - normal * jnp.mean(
            dx * normal, axis=-1, keepdims=True
        )
        dmid = two(cot, t).astype(F32) + inverse * dx
        db = dmid.astype(BF)
        put(dbs, t, db)
        add_sum(2, db.astype(F32))
        put(do_out, t, product_right(db, wout[...]).astype(BF))
        if crossed:

            @pl.when(t >= T - EARLY)
            def _():
                ring_u.early(t - (T - EARLY), EARLY)
                ring_d.early(t - (T - EARLY), EARLY)

        return carry

    lax.fori_loop(0, T, backward, 0)
    gout[...] = product_left(o[...], dbs[...]).astype(BF)
    if crossed:
        ring_u.early_drain(EARLY)
        ring_d.early_drain(EARLY)
    block_at = 2 * (w % 2) + w // 2 if crossed else w
    own = pl.ds(pl.multiple_of(block_at * R, R), R)
    mid_own[...] = mid[own, :]
    dmid_own[...] = dbs[own, :]
    for t in range(T):
        first[t].wait_send()
        second[t].wait_send()
        remote(bs.at[rs(mine, t)], bs.at[rs(mine, t)], s3.at[t], r3.at[t], core).wait_send()
        remote(q.at[rs(theirs, t)], b4.at[t], s4.at[t], r4.at[t], core).wait_send()
        remote(ab2.at[t], b5.at[t], s5.at[t], r5.at[t], other).wait_send()
        remote(dn.at[rs(mine, t)], dn.at[rs(mine, t)], s6.at[t], r6.at[t], core).wait_send()


def middle(G, crossed, p, X, cot, o, wup, wdn, wout, vec):
    T = 4
    rows, width = p.shape
    n = rows // 2 // T
    R = rows // 4
    d = o.shape[1]
    dma = pltpu.SemaphoreType.DMA
    full = pltpu.VMEM((rows, width), BF)
    part = pltpu.VMEM((T, n, width), BF)
    square = pltpu.VMEM((width, width), BF)
    return pl.pallas_call(
        functools.partial(middle_kernel, T, G, crossed),
        name="middle",
        out_shape=(
            jax.ShapeDtypeStruct((rows, width), BF),
            jax.ShapeDtypeStruct((R, width), F32),
            jax.ShapeDtypeStruct((R, width), BF),
            jax.ShapeDtypeStruct((rows, d), BF),
            jax.ShapeDtypeStruct((width, width), BF),
            jax.ShapeDtypeStruct((width, width), BF),
            jax.ShapeDtypeStruct((d, width), BF),
            jax.ShapeDtypeStruct((8, width), F32),
        ),
        in_specs=[ANY] * 8,
        out_specs=[VM] * 8,
        scratch_shapes=[
            full, full, full, pltpu.VMEM((rows, d), BF), square, square,
            pltpu.VMEM((d, width), BF), pltpu.VMEM((8, width), F32),
            part, part, part, full, pltpu.VMEM((rows, width), F32), full, full, full, full,
            part, part, part, full, full,
        ]
        + [dma((T,))] * 12
        + [dma((11,))]
        + (
            [pltpu.VMEM((2, EARLY, width // (8 * G), width), BF)] * 2 + [dma((2, 2, EARLY))] * 4
            if crossed
            else []
        ),
        compiler_params=pltpu.CompilerParams(
            collective_id=1, has_side_effects=True, vmem_limit_bytes=62 << 20
        ),
        cost_estimate=pl.CostEstimate(
            flops=14 * rows * width * width, bytes_accessed=40 << 20, transcendentals=rows * width
        ),
    )(p, X, cot, o, wup, wdn, wout, vec)


def scatter_kernel(G, D, out, b1, ab, b2, st, b3, s1, r1, s2, r2, s3, r3):
    w = lax.axis_index("wt")
    c = lax.axis_index("ctx")
    g = c // G
    m = c % G
    core = w + 1 - 2 * (w % 2)
    other = (w + 2) % 4
    par = w % 2
    hi = w // 2
    greet([(core, c), (other, c)] + [(w, g * G + (m + e) % G) for e in range(1, G)])
    order = [e for e in range(1, G)] + [0]
    firsts = {}
    for j in (1, 0):
        for e in order:
            jj = (hi + j) % 2
            mm = (m + e) % G
            b = (2 * jj + 1 - par) * G + mm
            slot = jj * G + mm
            r = remote(D.at[b], b1.at[slot], s1.at[slot], r1.at[slot], (core, c))
            r.start()
            firsts[(j, e)] = r

    def arrived1(slot):
        pltpu.make_async_copy(b1.at[slot], b1.at[slot], r1.at[slot]).wait()

    seconds = []
    for e in order:
        jj = 1 - hi
        mm = (m + e) % G
        slot = jj * G + mm
        arrived1(slot)
        ab[mm] = (D[(2 * jj + par) * G + mm].astype(F32) + b1[slot].astype(F32)).astype(BF)
        r = remote(ab.at[mm], b2.at[mm], s2.at[mm], r2.at[mm], (other, c))
        r.start()
        seconds.append(r)
    thirds = []
    for e in order:
        mm = (m + e) % G
        slot = hi * G + mm
        arrived1(slot)
        pltpu.make_async_copy(b2.at[mm], b2.at[mm], r2.at[mm]).wait()
        total = D[w * G + mm].astype(F32) + b1[slot].astype(F32) + b2[mm].astype(F32)
        if e == 0:
            for f in range(1, G):
                q = (m + f) % G
                pltpu.make_async_copy(b3.at[q], b3.at[q], r3.at[q]).wait()
                total = total + b3[q].astype(F32)
            out[...] = total.astype(out.dtype)
        else:
            st[mm] = total.astype(BF)
            r = remote(st.at[mm], b3.at[m], s3.at[mm], r3.at[m], (w, g * G + mm))
            r.start()
            thirds.append(r)
    for r in list(firsts.values()) + seconds + thirds:
        r.wait_send()


def scatter_sum(G, D):
    nc, rows, C = D.shape
    dma = pltpu.SemaphoreType.DMA
    return pl.pallas_call(
        functools.partial(scatter_kernel, G),
        name="scatter_sum",
        out_shape=jax.ShapeDtypeStruct((rows, C), F32),
        in_specs=[VM],
        out_specs=VM,
        scratch_shapes=[
            pltpu.VMEM((2 * G, rows, C), BF),
            pltpu.VMEM((G, rows, C), BF),
            pltpu.VMEM((G, rows, C), BF),
            pltpu.VMEM((G, rows, C), BF),
            pltpu.VMEM((G, rows, C), BF),
            dma((2 * G,)),
            dma((2 * G,)),
            dma((G,)),
            dma((G,)),
            dma((G,)),
            dma((G,)),
        ],
        compiler_params=pltpu.CompilerParams(
            collective_id=3, has_side_effects=True, vmem_limit_bytes=60 << 20
        ),
    )(D)


def head_mask(shape, h):
    lane = lax.broadcasted_iota(jnp.int32, shape, 1)
    return jnp.logical_and(lane >= h * HEAD_DIM, lane < (h + 1) * HEAD_DIM)


def split_heads(H, value):
    zero = jnp.zeros_like(value)
    return [jnp.where(head_mask(value.shape, h), value, zero) for h in range(H)]


def spread(H, shape, values):
    out = jnp.broadcast_to(values[H - 1], shape)
    for h in range(H - 2, -1, -1):
        out = jnp.where(head_mask(shape, h), values[h], out)
    return out


def attend_tile(H, q, k_ref, v_ref, bias_ref, at_bias, chunks=None):
    rows, width = q.shape
    N = k_ref.shape[0]
    step_keys = min(N, 1024)
    qh = split_heads(H, q * jnp.asarray(HEAD_DIM**-0.5, BF))
    top_half = lax.broadcasted_iota(jnp.int32, (rows, 1), 0) < BLK

    def step(j, carry):
        tops, sums, acc = carry
        at = pl.ds(pl.multiple_of(j * step_keys, step_keys), step_keys)
        kc = k_ref[at, :]
        vc = v_ref[at, :]
        low = bias_ref[at_bias, :, at]
        high = bias_ref[at_bias + 1, :, at]
        new_tops, new_sums, shrink, parts = [], [], [], []
        for h in range(H):
            s = product_right(qh[h], kc)
            s = jnp.concatenate([s[:BLK] + low, s[BLK:] + high], axis=0)
            top = jnp.maximum(tops[h], jnp.max(s, axis=1, keepdims=True))
            a = jnp.exp(tops[h] - top)
            p = jnp.exp(s - top)
            new_sums.append(sums[h] * a + jnp.sum(p, axis=1, keepdims=True))
            new_tops.append(top)
            shrink.append(a)
            parts.append(product(p.astype(BF), vc))
        acc = acc * spread(H, acc.shape, shrink) + spread(H, acc.shape, parts)
        return new_tops, new_sums, acc

    start = (
        [jnp.full((rows, 1), NEG, F32)] * H,
        [jnp.zeros((rows, 1), F32)] * H,
        jnp.zeros((rows, width), F32),
    )
    chunks = N // step_keys if chunks is None else chunks
    tops, sums, acc = lax.fori_loop(0, chunks, step, start)
    out = (acc / spread(H, acc.shape, sums)).astype(BF)
    lse = []
    for h in range(H):
        column = tops[h] + jnp.log(sums[h])
        lse.append(jnp.transpose(jnp.broadcast_to(column, (rows, BLK)))[0:1, :])
    lse = jnp.concatenate(lse + [jnp.zeros((8 - H, rows), F32)], axis=0)
    return out, lse


def attend_kernel(H, qpos, q_ref, k_ref, v_ref, bias_ref, o_ref, lse_ref):
    o, lse = attend_tile(H, q_ref[...], k_ref, v_ref, bias_ref, 2 * pl.program_id(0))
    o_ref[...] = o
    lse_ref[0] = lse


def attend(H, qpos, bias, q, k, v):
    n = qpos.shape[0]
    width = H * HEAD_DIM
    N = k.shape[0]
    rows = 2 * BLK
    whole = pl.BlockSpec((N, width), lambda i, *_: (0, 0))
    return pl.pallas_call(
        functools.partial(attend_kernel, H),
        name="attend",
        out_shape=(
            jax.ShapeDtypeStruct((n * rows, width), BF),
            jax.ShapeDtypeStruct((n, 8, rows), F32),
        ),
        grid_spec=pltpu.PrefetchScalarGridSpec(
            num_scalar_prefetch=1,
            grid=(n,),
            in_specs=[
                pl.BlockSpec((rows, width), lambda i, qp: (qp[i], 0)),
                whole,
                whole,
                pl.BlockSpec((2 * n, 1, N), lambda i, *_: (0, 0, 0)),
            ],
            out_specs=[
                pl.BlockSpec((rows, width), lambda i, *_: (i, 0)),
                pl.BlockSpec((1, 8, rows), lambda i, *_: (i, 0, 0)),
            ],
        ),
        compiler_params=pltpu.CompilerParams(vmem_limit_bytes=48 << 20),
    )(qpos, q, k, v, bias)


def attend_back_tile(
    H, q, do, o, lse, k_ref, v_ref, kt, dk, dv, lift_ref, tile, chunks=None, poll=None
):
    rows, width = q.shape
    N = k_ref.shape[0]
    scale = HEAD_DIM**-0.5
    qh = split_heads(H, q * jnp.asarray(scale, BF))
    doh = split_heads(H, do)
    qcat = jnp.concatenate(qh, axis=0)
    docat = jnp.concatenate(doh, axis=0)
    pick = lax.broadcasted_iota(jnp.int32, (8, width), 1)
    base = lax.broadcasted_iota(jnp.int32, (8, width), 0) * HEAD_DIM
    pick = jnp.logical_and(pick >= base, pick < base + HEAD_DIM).astype(F32)
    delta = lax.dot_general(
        pick,
        do.astype(F32) * o.astype(F32),
        (((1,), (1,)), ((), ())),
        precision=lax.Precision.HIGHEST,
        preferred_element_type=F32,
    )

    def step(j, dqt):
        at = pl.ds(pl.multiple_of(j * CHUNK, CHUNK), CHUNK)
        kc = k_ref[at, :]
        vc = v_ref[at, :]
        ps, dss, dqs = [], [], []
        for h in range(H):
            s = product_right(kc, qh[h])
            dp = product_right(vc, doh[h])
            pieces, dpieces = [], []
            for b in range(CHUNK // BLK):
                lift = lift_ref[tile, pl.ds(j * (CHUNK // BLK) + b, 1), :]
                cut = slice(b * BLK, (b + 1) * BLK)
                p = jnp.exp(s[cut] - (lse[h : h + 1, :] + lift))
                pieces.append(p.astype(BF))
                dpieces.append((p * (dp[cut] - delta[h : h + 1, :])).astype(BF))
            p = jnp.concatenate(pieces, axis=0)
            ds = jnp.concatenate(dpieces, axis=0)
            ps.append(p)
            dss.append(ds)
            dqs.append(product(kt[h * HEAD_DIM : (h + 1) * HEAD_DIM, at], ds))
        dv[at, :] += product(jnp.concatenate(ps, axis=1), docat)
        dk[at, :] += product(jnp.concatenate(dss, axis=1), qcat)
        if poll is not None:
            poll(j)
        return dqt + jnp.concatenate(dqs, axis=0)

    chunks = N // CHUNK if chunks is None else chunks
    dqt = lax.fori_loop(0, chunks, step, jnp.zeros((width, rows), F32))
    return dqt * scale


def flip_rows(src, dst):
    def flip(b, carry):
        at = pl.ds(pl.multiple_of(b * BLK, BLK), BLK)
        dst[:, at] = jnp.transpose(src[at, :])
        return carry

    lax.fori_loop(0, src.shape[0] // BLK, flip, 0)


def attend_back_kernel(
    H, qpos, q_ref, k_ref, v_ref, o_ref, do_ref, lse_ref, lift_ref, dqk_ref, dv_ref, kt, dk, dv
):
    i = pl.program_id(0)
    width = H * HEAD_DIM

    @pl.when(i == 0)
    def _():
        flip_rows(k_ref, kt)
        dk[...] = jnp.zeros_like(dk)
        dv[...] = jnp.zeros_like(dv)
        dqk_ref[...] = jnp.zeros_like(dqk_ref)

    dqt = attend_back_tile(
        H, q_ref[...], do_ref[...], o_ref[...], lse_ref[0], k_ref, v_ref, kt, dk, dv, lift_ref, i
    )
    rows = 2 * BLK
    here = pl.ds(pl.multiple_of(qpos[i] * rows, rows), rows)
    dqk_ref[here, 0:width] = jnp.transpose(dqt).astype(BF)

    @pl.when(i == pl.num_programs(0) - 1)
    def _():
        dqk_ref[:, width : 2 * width] = dk[...].astype(BF)
        dv_ref[...] = dv[...].astype(BF)


def attend_back(H, qpos, lift, q, k, v, o, do, lse):
    n = qpos.shape[0]
    width = H * HEAD_DIM
    N = k.shape[0]
    rows = 2 * BLK
    whole = pl.BlockSpec((N, width), lambda i, *_: (0, 0))
    row = pl.BlockSpec((rows, width), lambda i, *_: (i, 0))
    return pl.pallas_call(
        functools.partial(attend_back_kernel, H),
        name="attend_back",
        out_shape=(
            jax.ShapeDtypeStruct((N, 2 * width), BF),
            jax.ShapeDtypeStruct((N, width), BF),
        ),
        grid_spec=pltpu.PrefetchScalarGridSpec(
            num_scalar_prefetch=1,
            grid=(n,),
            in_specs=[
                pl.BlockSpec((rows, width), lambda i, qp: (qp[i], 0)),
                whole,
                whole,
                row,
                row,
                pl.BlockSpec((1, 8, rows), lambda i, *_: (i, 0, 0)),
                pl.BlockSpec((n, N // BLK, rows), lambda i, *_: (0, 0, 0)),
            ],
            out_specs=[
                pl.BlockSpec((N, 2 * width), lambda i, *_: (0, 0)),
                pl.BlockSpec((N, width), lambda i, *_: (0, 0)),
            ],
            scratch_shapes=[
                pltpu.VMEM((width, N), BF),
                pltpu.VMEM((N, width), F32),
                pltpu.VMEM((N, width), F32),
            ],
        ),
        compiler_params=pltpu.CompilerParams(vmem_limit_bytes=60 << 20),
    )(qpos, q, k, v, o, do, lse, lift)


def head_kernel(
    G, H,
    deal, out_b, gain_one, shift_one, gain_two, shift_two, down_b, up_b, qv_b,
    x_h, first_h, wqkv_h, cot_h, wup_h, wout_h,
    X_o, xh_o, k_o, v_o, wup_o, cot_o, q, o, lse, part, wqk, wf, vec,
    X, Fv, xh, k, v, small, vq, bias, wout, wl, wqk_h, wf_h, Y, line, small_l,
    rx, rf, rw, rv, rs, rc, ru, sh, sx, sf, sw, sc, su, loc, out, ry, sy,
):
    nw = 4
    w = lax.axis_index("wt")
    c = lax.axis_index("ctx")
    g = c // G
    m = c % G
    nc = nw * G
    R, width = x_h.shape
    d = width // nw
    par = w % 2
    core = (w + 1 - 2 * par, c)
    seq = 2 * (g % 2) + g // 2
    og = 2 * par + w // 2
    goal = og * G + m
    two = (w + 2) % nw
    goal_two = (2 * par + two // 2) * G + m
    is_a = w == seq
    primary = (w + seq) % 2 == 0
    high = w >= 2
    low = w < 2
    peers = [
        ((w + a) % nw, ((g + e) % nw) * G + m) for a in range(nw) for e in range(nw) if a or e
    ]
    peers += [(w, g * G + (m + e) % G) for e in range(1, G)]
    loads = [
        pltpu.make_async_copy(a, b, loc.at[i])
        for i, (a, b) in enumerate(((wqkv_h, wl), (wout_h, wout)))
    ]
    for copy in loads:
        copy.start()
    greet(peers)

    here = goal == c
    here_two = goal_two == c
    to_y = remote(x_h, Y, sh.at[0], ry.at[0], (two, c))
    to_one = remote(x_h, X.at[c], sh.at[1], rx.at[c], (w, goal))
    to_two = remote(Y, X.at[c], sh.at[4], rx.at[c], (w, goal_two))
    to_first = remote(first_h, Fv.at[c], sh.at[2], rf.at[c], (w, goal))
    home_cot = jnp.logical_and(here, is_a)
    own_cot = pl.ds(pl.multiple_of(g * R, R), R)
    to_cot = remote(cot_h, cot_o.at[own_cot], sh.at[3], rc.at[g], (seq, goal))
    to_y.start()

    @pl.when(here)
    def _():
        pltpu.make_async_copy(x_h, X.at[c], rx.at[c]).start()
        pltpu.make_async_copy(first_h, Fv.at[c], rf.at[c]).start()

    @pl.when(jnp.logical_not(here))
    def _():
        to_one.start()
        to_first.start()

    line[...] = jnp.zeros_like(line)
    for a, ref in enumerate((out_b, gain_one, shift_one, gain_two, shift_two, down_b)):
        at = a // 2
        line[at : at + 1, (a % 2) * d : (a % 2 + 1) * d] = ref[...].astype(F32).reshape(1, d)
    for a in range(2):
        half = up_b[a * 2 * d : (a + 1) * 2 * d].astype(F32).reshape(1, 2 * d)
        line[3 + a : 4 + a, :] = half
    line[5:6, : 6 * d // 4] = qv_b[...].astype(F32).reshape(1, 6 * d // 4)
    small_l[...] = line[...].astype(BF)
    loads[0].wait()
    for a in range(nw):
        for half in range(2):
            at = half * width + a * d
            wqk_h[a, :, half * d : (half + 1) * d] = wl[:, at : at + d]
    for a in range(2):
        at = 2 * width + a * d
        wf_h[a] = wl[:, at : at + d]

    def rows_of(a):
        return pl.ds(pl.multiple_of(a * d, 16), d)

    weights, fresh = [], []
    for e in range(1, nw):
        to = (w + e) % nw
        weights.append(remote(small_l, small.at[w], sw.at[e, 0], rs.at[w], (to, c)))
        weights.append(remote(wqk_h.at[to], wqk.at[rows_of(w)], sw.at[e, 1], rw.at[w], (to, c)))
        fresh.append(
            (to, remote(wf_h.at[to % 2], wf.at[rows_of(w)], sw.at[e, 2], rv.at[w], (to, c)))
        )
    for r in weights:
        r.start()
    for to, r in fresh:

        @pl.when(to < 2)
        def _():
            r.start()

    pltpu.make_async_copy(small_l, small.at[w], rs.at[w]).start()
    pltpu.make_async_copy(wqk_h.at[w], wqk.at[rows_of(w)], rw.at[w]).start()

    @pl.when(low)
    def _():
        pltpu.make_async_copy(wf_h.at[par], wf.at[rows_of(w)], rv.at[w]).start()

    @pl.when(high)
    def _():
        wf[...] = jnp.zeros_like(wf)

    def got(ref, sem):
        pltpu.make_async_copy(ref, ref, sem).wait()

    got(Y, ry.at[0])

    @pl.when(here_two)
    def _():
        pltpu.make_async_copy(Y, X.at[c], rx.at[c]).start()

    @pl.when(jnp.logical_not(here_two))
    def _():
        to_two.start()

    def core_x(b):
        return remote(X.at[b], X.at[b], sx.at[0, b], rx.at[b], core)

    def core_f(b):
        return remote(Fv.at[b], Fv.at[b], sf.at[0, b], rf.at[b], core)

    def member_x(b, e):
        return remote(X.at[b], X.at[b], sx.at[e, b], rx.at[b], (w, g * G + (m + e) % G))

    def member_f(b, e):
        return remote(Fv.at[b], Fv.at[b], sf.at[e, b], rf.at[b], (w, g * G + (m + e) % G))

    def cross_f(b):
        return remote(Fv.at[b], Fv.at[b], sy.at[b], rf.at[b], (two, c))

    crossing = jnp.logical_and(is_a, low)

    def take(b, onward):
        got(X.at[b], rx.at[b])

        if onward:

            @pl.when(crossing)
            def _():
                got(Fv.at[b], rf.at[b])
                cross_f(b).start()

        @pl.when(primary)
        def _():
            for e in range(1, G if onward else 1):
                member_x(b, e).start()
            core_x(b).start()

        @pl.when(high)
        def _():
            got(Fv.at[b], rf.at[b])

            @pl.when(primary)
            def _():
                for e in range(1, G if onward else 1):
                    member_f(b, e).start()
                core_f(b).start()

    half_rows = nc * R // 2

    def halves(ref, b, gap, value):
        ref[pl.ds(pl.multiple_of(b * BLK, BLK), BLK), :] = value[:BLK]
        ref[pl.ds(pl.multiple_of(b * BLK + gap, BLK), BLK), :] = value[BLK:]

    def project(b, a):
        at = pl.ds(pl.multiple_of(b * R, R), R)
        value = X[b].astype(F32)
        centred = value - jnp.mean(value, axis=-1, keepdims=True)
        inverse = lax.rsqrt(jnp.mean(centred * centred, axis=-1, keepdims=True) + EPS)
        normal = centred * inverse
        xh[at, :] = normal.astype(BF)
        n = (normal * vec[4:5, :] + vec[5:6, :]).astype(BF)
        qk = product(n, wqk[...])
        halves(k, b, half_rows, qk[:, d : 2 * d].astype(BF))
        if a is not None:
            halves(q, a, 2 * R, (qk[:, :d] + vq[1:2, 0:d]).astype(BF))

        @pl.when(low)
        def _():
            halves(v, b, half_rows, (product(n, wf[...]) + vq[2:3, 0:d]).astype(BF))

        @pl.when(high)
        def _():
            f = Fv[b]
            halves(v, b, half_rows, jnp.where(par == 0, f[:, :d], f[:, d:]))

    for t in range(nw):
        for e in range(2):
            own_pair = deal[(2 * (t % 2) + e) * G + m]
            for b in range(nc):
                seen = deal[b] <= own_pair if t < 2 else deal[b] >= own_pair
                at = b * BLK + (half_rows if t >= 2 else 0)
                bias[2 * t + e, :, at : at + BLK] = jnp.full(
                    (1, BLK), jnp.where(seen, 0.0, NEG), F32
                )
            if t >= 2:
                bias[2 * t + e, :, 0:half_rows] = jnp.zeros((1, half_rows), F32)
    take(g * G + m, True)
    loads[1].wait()
    for a in range(nw):
        got(small.at[a], rs.at[a])
        got(wqk.at[rows_of(a)], rw.at[a])

        @pl.when(low)
        def _():
            got(wf.at[rows_of(a)], rv.at[a])

    nb = 6 * d // 4
    for a in range(nw):
        piece = small[a].astype(F32)
        for row, src in ((0, 0), (1, 3), (2, 4), (4, 1), (5, 2), (6, 5)):
            at = src // 2
            value = piece[at : at + 1, (src % 2) * d : (src % 2 + 1) * d]
            vec[row : row + 1, a * d : (a + 1) * d] = value
        vq[0:1, a * nb : (a + 1) * nb] = piece[5:6, :nb]
    piece = small[w].astype(F32)
    vec[3:4, : 2 * d] = piece[3:4, :]
    vec[3:4, 2 * d :] = piece[4:5, :]
    vec[7:8, :] = jnp.zeros((1, width), F32)
    q_bias = vq[0:1, 0:d]
    for a in range(1, nw):
        q_bias = jnp.where(w == a, vq[0:1, a * d : (a + 1) * d], q_bias)
    f_bias = jnp.where(
        par == 0, vq[0:1, width : width + d], vq[0:1, width + d : width + 2 * d]
    )
    vq[1:2, 0:d] = q_bias
    vq[2:3, 0:d] = f_bias
    project(g * G + m, g)

    def own(i, carry):
        a = (g + i) % nw
        take(a * G + m, True)
        project(a * G + m, a)
        return carry

    lax.fori_loop(1, nw, own, 0)

    @pl.when(home_cot)
    def _():
        pltpu.make_async_copy(cot_h, cot_o.at[own_cot], rc.at[g]).start()

    @pl.when(jnp.logical_not(home_cot))
    def _():
        to_cot.start()

    ups = []
    for e in range(1, nw):
        to = (w + e) % nw
        src = wup_h.at[:, pl.ds(pl.multiple_of(to * width, BLK), width)]
        ups.append(remote(src, wup_o.at[rows_of(w)], su.at[e], ru.at[w], (to, c)))
    for r in ups:
        r.start()
    src = wup_h.at[:, pl.ds(pl.multiple_of(w * width, BLK), width)]
    pltpu.make_async_copy(src, wup_o.at[rows_of(w)], ru.at[w]).start()

    def others(i, carry):
        b = ((g + i % nw) % nw) * G + (m + 1 + i // nw) % G
        take(b, False)
        project(b, None)
        return carry

    lax.fori_loop(0, nw * (G - 1), others, 0)
    outs = [(X, X_o), (xh, xh_o), (k, k_o), (v, v_o)]
    outs = [pltpu.make_async_copy(a, b, out.at[i]) for i, (a, b) in enumerate(outs)]
    for copy in outs:
        copy.start()

    def cot_rows(a):
        return cot_o.at[pl.ds(pl.multiple_of(a * R, R), R)]

    og_two = 2 * par + two // 2
    spread_cot = [
        remote(cot_rows(og), cot_rows(og), sc.at[0], rc.at[og], (two, c)),
        remote(cot_rows(og), cot_rows(og), sc.at[1], rc.at[og], core),
        remote(cot_rows(og_two), cot_rows(og_two), sc.at[2], rc.at[og_two], core),
    ]
    got(cot_rows(og), rc.at[og])
    spread_cot[0].start()
    spread_cot[1].start()

    def attend_one(t, carry):
        at = pl.ds(pl.multiple_of(t * R, R), R)
        ot, lt = attend_tile(H, q[at, :], k, v, bias, 2 * t, 1 + t // 2)
        lse[t] = lt
        pt = product(ot, wout[...]).astype(BF)
        for e in range(2):
            to = (2 * (t % 2) + e) * R + (t // 2) * BLK
            to = pl.ds(pl.multiple_of(to, BLK), BLK)
            o[to, :] = ot[e * BLK : (e + 1) * BLK]
            part[to, :] = pt[e * BLK : (e + 1) * BLK]
        return carry

    lax.fori_loop(0, nw, attend_one, 0)

    got(cot_rows(og_two), rc.at[og_two])
    spread_cot[2].start()
    for copy in outs:
        copy.wait()
    for a in range(nw):
        got(wup_o.at[rows_of(a)], ru.at[a])

    for hi in range(2):
        a = 2 * (1 - par) + hi
        got(cot_rows(a), rc.at[a])

    for r in weights + ups + spread_cot + [to_y]:
        r.wait_send()
    for to, r in fresh:

        @pl.when(to < 2)
        def _():
            r.wait_send()

    @pl.when(jnp.logical_not(here))
    def _():
        to_one.wait_send()
        to_first.wait_send()

    @pl.when(jnp.logical_not(here_two))
    def _():
        to_two.wait_send()

    @pl.when(crossing)
    def _():
        for a in range(nw):
            cross_f(a * G + m).wait_send()

    @pl.when(jnp.logical_not(home_cot))
    def _():
        to_cot.wait_send()

    @pl.when(primary)
    def _():

        def sent(b, carry):
            core_x(b).wait_send()

            @pl.when(b % G == m)
            def _():
                for e in range(1, G):
                    member_x(b, e).wait_send()

            @pl.when(high)
            def _():
                core_f(b).wait_send()

                @pl.when(b % G == m)
                def _():
                    for e in range(1, G):
                        member_f(b, e).wait_send()

            return carry

        lax.fori_loop(0, nc, sent, 0)


def head(G, H, deal, vectors, x, first, wqkv, cot, wup, wout):
    nw = 4
    nc = nw * G
    R, width = x.shape
    d = width // nw
    N = nc * R
    dma = pltpu.SemaphoreType.DMA
    vm = pltpu.VMEM
    shape = jax.ShapeDtypeStruct
    operands = (deal,) + vectors + (x, first, wqkv, cot, wup, wout)
    return pl.pallas_call(
        functools.partial(head_kernel, G, H),
        name="head",
        out_shape=(
            shape((nc, R, width), BF),
            shape((N, width), BF),
            shape((N, d), BF),
            shape((N, d), BF),
            shape((width, width), BF),
            shape((nw * R, width), BF),
            shape((nw * R, d), BF),
            shape((nw * R, d), BF),
            shape((nw, 8, R), F32),
            shape((nw * R, width), BF),
            shape((width, 2 * d), BF),
            shape((width, d), BF),
            shape((8, width), F32),
        ),
        in_specs=[pl.BlockSpec(memory_space=pltpu.SMEM)] + [VM] * len(vectors) + [ANY] * 6,
        out_specs=[ANY] * 6 + [VM] * 7,
        scratch_shapes=[
            vm((nc, R, width), BF), vm((nc, R, 2 * d), BF), vm((N, width), BF), vm((N, d), BF),
            vm((N, d), BF), vm((nw, 8, 2 * d), BF), vm((8, 6 * d), F32),
            vm((2 * nw, 1, N), F32), vm(wout.shape, BF), vm(wqkv.shape, BF),
            vm((nw, d, 2 * d), BF), vm((2, d, d), BF), vm((R, width), BF),
            vm((8, 2 * d), F32), vm((8, 2 * d), BF),
            dma((nc,)), dma((nc,)), dma((nw,)), dma((nw,)), dma((nw,)), dma((nw,)), dma((nw,)),
            dma((6,)), dma((G, nc)), dma((G, nc)), dma((nw, 3)), dma((nw,)), dma((nw,)),
            dma((2,)), dma((4,)), dma((1,)), dma((nc,)),
        ],
        compiler_params=pltpu.CompilerParams(
            collective_id=0, has_side_effects=True, vmem_limit_bytes=56 << 20
        ),
        cost_estimate=pl.CostEstimate(
            flops=14 << 30, bytes_accessed=40 << 20, transcendentals=6 << 20
        ),
    )(*operands)


EARLY = 3


def ring_place(nc):
    w, c = lax.axis_index("wt"), lax.axis_index("ctx")
    odd = c % 2
    pos = (c // 2) * (1 - odd) + (nc - 1 - c // 2) * odd

    def ctx_at(p):
        p = (p + nc) % nc
        h = p // (nc // 2)
        return 2 * p * (1 - h) + (2 * (nc - 1 - p) + 1) * h

    return pos, (w, ctx_at(pos + 1)), (w, ctx_at(pos - 1))


class Ring:
    def __init__(self, nc, pos, right, left, seg, chains, A, slots, out, ss, sr):
        self.nc, self.pos, self.right, self.left, self.seg = nc, pos, right, left, seg
        self.chains, self.A, self.slots, self.out, self.ss, self.sr = chains, A, slots, out, ss, sr
        self.steps = 2 * (nc - 1)
        self.cut = A.shape[1] // chains

    def at(self, half, j):
        j = (j + 2 * self.nc) % self.nc
        return pl.ds(pl.multiple_of((half * self.nc + j) * self.seg, 16), self.seg)

    def cols(self, i):
        if self.chains == 1:
            return pl.ds(0, self.cut)
        return pl.ds(pl.multiple_of(i * self.cut, BLK), self.cut)

    def reduce_copies(self, i, s):
        k = self.cols(i)
        return [
            remote(
                self.A.at[self.at(h, j), k],
                self.slots.at[h, s, :, k],
                self.ss.at[h, i, s],
                self.sr.at[h, i, s],
                to,
            )
            for h, j, to in ((0, self.pos - s, self.right), (1, self.pos + s, self.left))
        ]

    def gather_copies(self, i, s):
        k = self.cols(i)
        t = s - (self.nc - 1)
        return [
            remote(
                self.out.at[self.at(h, j), k],
                self.out.at[self.at(h, j), k],
                self.ss.at[h, i, s],
                self.sr.at[h, i, s],
                to,
            )
            for h, j, to in ((0, self.pos + 1 - t, self.right), (1, self.pos - 1 + t, self.left))
        ]

    def send(self, i, s, gathering=False):
        for r in (self.gather_copies if gathering else self.reduce_copies)(i, s):
            r.start()

    start = 0

    def begin(self, start=0):
        self.start = start
        for i in range(self.chains):
            self.send(i, start)

    def add(self, i, s):
        k = self.cols(i)
        for h, j in ((0, self.pos - s - 1), (1, self.pos + s + 1)):
            at = self.at(h, j)
            slot = self.slots.at[h, s, :, k]
            pltpu.make_async_copy(slot, slot, self.sr.at[h, i, s]).wait()
            value = self.A[at, k].astype(F32) + self.slots[h, s, :, k].astype(F32)
            self.A[at, k] = value.astype(BF)

    def early(self, s, steps):
        for i in range(self.chains):
            self.add(i, s)

        @pl.when(s < steps - 1)
        def _():
            for i in range(self.chains):
                self.send(i, s + 1)

    def early_drain(self, steps):
        for s in range(steps):
            for i in range(self.chains):
                for r in self.reduce_copies(i, s):
                    r.wait_send()

    def keep(self, i):
        k = self.cols(i)
        for h, j in ((0, self.pos + 1), (1, self.pos - 1)):
            self.out[self.at(h, j), k] = self.A[self.at(h, j), k]

    def arrive(self, i, s):
        t = s - (self.nc - 1)
        for h, j in ((0, self.pos - t), (1, self.pos + t)):
            at = self.out.at[self.at(h, j), self.cols(i)]
            pltpu.make_async_copy(at, at, self.sr.at[h, i, s]).wait()

    def step(self, s):
        for i in range(self.chains):
            self.turn(i, s)

    def turn(self, i, s):
        last = self.nc - 2
        if isinstance(s, int):
            when = lambda cond: (lambda body: body() if cond else None)
            both = lambda a, b: a and b
        else:
            when, both = pl.when, jnp.logical_and

        @when(s < last)
        def _():
            self.add(i, s)
            self.send(i, s + 1)

        @when(s == last)
        def _():
            self.add(i, last)
            self.keep(i)
            self.send(i, last + 1, True)

        @when(both(s > last, s < self.steps))
        def _():
            self.arrive(i, s)

        @when(both(s > last, s < self.steps - 1))
        def _():
            self.send(i, s + 1, True)

    def drain(self):
        for gathering in (False, True):

            def one(t, carry):
                i, s = t % self.chains, t // self.chains
                for r in (self.gather_copies if gathering else self.reduce_copies)(i, s):
                    r.wait_send()
                return carry

            half = self.steps * self.chains // 2
            low = half if gathering else self.start * self.chains
            lax.fori_loop(low, half * (1 + gathering), one, 0)


class SplitRing(Ring):
    def __init__(self, nc, pos, right, left, seg, chains, A, slots, out, ss, sr, own, sems):
        super().__init__(nc, pos, right, left, seg, chains, A, slots, out, ss, sr)
        self.turns = nc - 1
        self.w, self.c = own
        self.s_ex, self.r_ex, self.s_hop, self.r_hop = sems
        self.group = nc // 2
        self.reach = (nc // 2, nc // 2 - 1)

    def turn(self, i, s):
        last = self.nc - 2
        if isinstance(s, int):
            when = lambda cond: (lambda body: body() if cond else None)
        else:
            when = pl.when

        @when(s <= last)
        def _():
            self.add(i, s)

        @when(s < last)
        def _():
            self.send(i, s + 1)

    def parts(self):
        for h, j in ((0, self.pos + 1), (1, self.pos - 1)):
            j = (j + self.nc) % self.nc
            to = 2 * h + j // self.group
            src = self.A.at[self.at(h, j)]
            dst = self.out.at[j % self.group, self.w]
            yield h, to, src, dst

    def exchange(self):
        for h, to, src, dst in self.parts():
            local = pltpu.make_async_copy(src, dst, self.r_ex.at[self.w])
            far = remote(src, dst, self.s_ex.at[h], self.r_ex.at[self.w], (to, self.c))

            @pl.when(to == self.w)
            def _():
                local.start()

            @pl.when(to != self.w)
            def _():
                far.start()

    def held(self, position):
        j = (position + 1 - 2 * (self.w // 2) + 2 * self.nc) % self.nc
        return j // self.group == self.w % 2, j % self.group

    def hop_copy(self, way, h, j):
        ref = self.out.at[j]
        to = (self.right, self.left)[way]
        return remote(ref, ref, self.s_hop.at[way, h], self.r_hop.at[way, h], to)

    def spread(self):
        have, j = self.held(self.pos)

        @pl.when(have)
        def _():
            for a in range(4):
                ref = self.out.at[j, a]
                pltpu.make_async_copy(ref, ref, self.r_ex.at[a]).wait()
            for way in range(2):
                self.hop_copy(way, 1, j).start()

    def hop(self, h):
        for way in range(2):
            if h > self.reach[way]:
                continue
            have, j = self.held(self.pos - h if way == 0 else self.pos + h)

            @pl.when(have)
            def _():
                ref = self.out.at[j]
                pltpu.make_async_copy(ref, ref, self.r_hop.at[way, h]).wait()
                if h < self.reach[way]:
                    self.hop_copy(way, h + 1, j).start()

    def drain(self):
        def one(t, carry):
            i, s = t % self.chains, t // self.chains
            for r in self.reduce_copies(i, s):
                r.wait_send()
            return carry

        lax.fori_loop(self.start * self.chains, self.turns * self.chains, one, 0)
        for h, to, src, dst in self.parts():

            @pl.when(to != self.w)
            def _():
                remote(src, dst, self.s_ex.at[h], self.r_ex.at[self.w], (to, self.c)).wait_send()

        for way in range(2):
            for h in range(self.reach[way]):
                have, j = self.held(self.pos - h if way == 0 else self.pos + h)

                @pl.when(have)
                def _():
                    self.hop_copy(way, h + 1, j).wait_send()


def tail_kernel(
    G, H, seg_o, seg_u, seg_b,
    deal, q_h, k_h, v_h, o_h, do_h, lse_h, xh_h, X_h, wqk_h, wf_h, vec_h, dmid_h,
    up_h, down_h, gout_h, vsums, mlp_h, mid_h,
    layer_out, tokens_out, first_out, up_out, down_out, gout_out, qkv_out, rows_out,
    q, k, v, o, do, lse, lift, xh, X, wqk, wf, vec, dmid,
    kt, dk, dv, dqk, dvb, D, b1, ab, b2, st, b3, tot, tb, tr,
    O, slots_o, res_o, A, slots_a, res_a, U, slots_u, res_u, gq, slots_b, res_b, gain_t, shift_t, sums_t, line, f1, fs, fr,
    mlp, mid, lb, ly, lr, sl, rl, sL, rL, s1, r1, s2, r2, s3, r3, sT, rT, sso, sro, ssa, sra, ssu, sru, seu, reu, shu, rhu, ssb, srb, seb, reb, shb, rhb, sf1, rf1, sf2, rf2, ld,
):
    w = lax.axis_index("wt")
    c = lax.axis_index("ctx")
    nw = 4
    nc = nw * G
    g = c // G
    m = c % G
    par = w % 2
    hi = w // 2
    core = (w + 1 - 2 * par, c)
    other = ((w + 2) % nw, c)
    R, width = dmid.shape
    d = width // nw
    N = xh.shape[0]
    pos, right, left = ring_place(nc)
    loads = [
        (up_h, U),
        (down_h, A),
        (gout_h, O.at[pl.ds(0, d)]),
        (k_h, k), (v_h, v), (q_h, q), (o_h, o), (do_h, do), (lse_h, lse),
        (xh_h, xh), (X_h, X), (wqk_h, wqk), (wf_h, wf), (vec_h, vec), (dmid_h, dmid), (mid_h, mid), (mlp_h, mlp),
    ]
    loads = [pltpu.make_async_copy(a, b, ld.at[i]) for i, (a, b) in enumerate(loads)]
    for copy in loads:
        copy.start()
    peers = [
        ((w + a) % nw, ((g + e) % nw) * G + m) for a in range(nw) for e in range(nw) if a or e
    ]
    peers += [(w, g * G + (m + e) % G) for e in range(1, G)]
    greet(peers + [right, left])
    ring_o = Ring(nc, pos, right, left, seg_o, 1, O, slots_o, res_o, sso, sro)
    ring_a = Ring(nc, pos, right, left, seg_u, 2, A, slots_a, res_a, ssa, sra)
    ring_u = SplitRing(
        nc, pos, right, left, seg_u, 2, U, slots_u, res_u, ssu, sru, (w, c), (seu, reu, shu, rhu)
    )
    ring_b = SplitRing(
        nc, pos, right, left, seg_b, 1, gq, slots_b, res_b, ssb, srb, (w, c), (seb, reb, shb, rhb)
    )
    for copy in loads[:3]:
        copy.wait()
    foot = O.shape[0] - d
    line_a = jnp.concatenate([vsums[0:1, :], jnp.zeros((15, width), F32)], axis=0)
    O[d + 16 :, :] = jnp.zeros((foot - 16, width), BF)
    share = vsums[1:5, 0:d]
    for a in range(1, nw):
        share = jnp.where(w == a, vsums[1:5, a * d : (a + 1) * d], share)
    pack = jnp.concatenate([share[a : a + 1, :] for a in range(4)], axis=1)
    pack = jnp.concatenate([jnp.zeros((1, width), F32), pack, jnp.zeros((14, width), F32)], axis=0)
    O[d : d + 16, :] = (line_a + pack).astype(BF)
    ring_u.begin(EARLY)
    ring_a.begin(EARLY)
    ring_o.begin()
    for copy in loads[3:9] + loads[15:]:
        copy.wait()
    seq = 2 * (g % 2) + g // 2
    og = 2 * par + hi
    home = (seq, og * G + m)
    home_self = jnp.logical_and(og == g, w == seq)
    shares = []
    for e in range(1, nw):
        to = (w + e) % nw
        src = mlp.at[pl.ds(pl.multiple_of((2 * (to % 2) + to // 2) * R, R), R)]
        r = remote(src, lb.at[w], sl.at[e], rl.at[w], (to, c))
        r.start()
        shares.append(r)

    flip_rows(k, kt)
    dk[...] = jnp.zeros_like(dk)
    dv[...] = jnp.zeros_like(dv)
    dqk[...] = jnp.zeros_like(dqk)
    wide = H * HEAD_DIM

    def poll(n):
        for r in range(4):

            @pl.when(n % 4 == r)
            def _():
                (ring_a if r % 2 else ring_u).turn(r // 2, EARLY + n // 4)
                if r == 3:
                    ring_o.turn(0, n // 4)

    pairs = lax.broadcasted_iota(jnp.int32, (1, 2 * BLK), 1) < BLK
    for t in range(nw):
        mine = [deal[(2 * (t % 2) + e) * G + m] for e in range(2)]
        for b in range(nc):
            unseen = [
                jnp.where(deal[b] <= a if t < 2 else deal[b] >= a, 0.0, -NEG) for a in mine
            ]
            at = b if t < 2 else nc + b
            lift[t, at : at + 1, :] = jnp.where(pairs, unseen[0], unseen[1])
        if t >= 2:
            lift[t, 0:nc, :] = jnp.zeros((nc, 2 * BLK), F32)

    def tile(t, carry):
        rows = []
        for e in range(2):
            at = (2 * (t % 2) + e) * R + (t // 2) * BLK
            rows.append(pl.ds(pl.multiple_of(at, BLK), BLK))
        pick = lambda ref: jnp.concatenate([ref[rows[0], :], ref[rows[1], :]], axis=0)
        mine = pl.ds(pl.multiple_of(t * R, R), R)

        def polls_at(j):
            n = 2 * (t + t // 3 + j)
            poll(n)
            poll(n + 1)

        dqt = attend_back_tile(
            H, q[mine, :], pick(do), pick(o), lse[t], k, v, kt, dk, dv, lift, t, 1 + t // 2,
            polls_at,
        )
        dq = jnp.transpose(dqt).astype(BF)
        for e in range(2):
            at = ((2 * (t % 2) + e) * G + m) * R + (t // 2) * BLK
            at = pl.ds(pl.multiple_of(at, BLK), BLK)
            dqk[at, 0:wide] = dq[e * BLK : (e + 1) * BLK]
        return carry

    lax.fori_loop(0, nw, tile, 0)

    def deal_back(b, carry):
        for e in range(2):
            src = pl.ds(pl.multiple_of(b * BLK + e * (N // 2), BLK), BLK)
            to = pl.ds(pl.multiple_of(b * R + e * BLK, BLK), BLK)
            dqk[to, wide : 2 * wide] = dk[src, :].astype(BF)
            dvb[to, :] = dv[src, :].astype(BF)
        return carry

    lax.fori_loop(0, nc, deal_back, 0)
    polls = 12
    for copy in loads[9:15]:
        copy.wait()

    layer = mid[...] + vec[6:7, :] + mlp[pl.ds(pl.multiple_of(og * R, R), R), :].astype(F32)
    for e in range(1, nw):
        src = (w + e) % nw
        pltpu.make_async_copy(lb.at[src], lb.at[src], rl.at[src]).wait()
        layer = layer + lb[src].astype(F32)
    ly[...] = layer.astype(BF)
    layer_back = remote(ly, lr, sL.at[0], rL.at[0], home)
    layer_stay = pltpu.make_async_copy(ly, lr, rL.at[0])

    @pl.when(home_self)
    def _():
        layer_stay.start()

    @pl.when(jnp.logical_not(home_self))
    def _():
        layer_back.start()

    upper = w >= 2
    first_copies = []
    for e in range(1, G):
        mm = (m + e) % G
        for gp in range(nw):
            src = dvb.at[pl.ds(pl.multiple_of((gp * G + mm) * R, R), R)]
            first_copies.append(
                remote(src, f1.at[m, gp], sf1.at[e, gp], rf1.at[m, gp], (w, g * G + mm))
            )

    @pl.when(upper)
    def _():
        for r in first_copies:
            r.start()

    tile_d = 128
    ones = jnp.ones((N, BLK), BF)
    row_qk = product_left(ones, dqk[...])[0:1, :]
    row_f = product_left(ones, dvb[...])[0:1, :]
    sum_qk = product_left(dqk[...], ones)
    sum_f = product_left(dvb[...], ones)
    gain_t[...] = jnp.transpose(jnp.broadcast_to(vec[4:5, :], (BLK, width)))
    shift_t[...] = jnp.transpose(jnp.broadcast_to(vec[5:6, :], (BLK, width)))
    lane = lax.broadcasted_iota(jnp.int32, (d, BLK), 1)
    edge = gq.shape[1] - BLK
    for a in range(nw):
        sums_t[a * d : (a + 1) * d, :] = jnp.where(
            lane == 66, sum_qk[:wide], jnp.where(lane == 67, sum_qk[wide:], sum_f)
        )
    lane = lax.broadcasted_iota(jnp.int32, (tile_d, BLK), 1)

    def grads(i, carry):
        at = pl.ds(pl.multiple_of(i * tile_d, tile_d), tile_d)
        x_qk = product_left(xh[:, at], dqk[...])
        x_f = product_left(xh[:, at], dvb[...])
        w_qk = wqk[at, :].astype(F32)
        w_f = wf[at, :].astype(F32)
        add = lambda a, b: jnp.sum(a, axis=1, keepdims=True) + jnp.sum(b, axis=1, keepdims=True)
        for_gain = add(w_qk * x_qk, w_f * x_f)
        for_shift = add(w_qk * row_qk, w_f * row_f)
        gain = gain_t[at, 0:1]
        shift = shift_t[at, 0:1]
        gq[at, 0 : 2 * wide] = (gain * x_qk + shift * row_qk).astype(BF)
        gq[at, 2 * wide : 3 * wide] = (gain * x_f + shift * row_f).astype(BF)
        ends = gq[at, edge:].astype(F32)
        ends = jnp.where(lane == 64, for_gain, jnp.where(lane == 65, for_shift, ends))
        ends = jnp.where(lane > 65, sums_t[at, :], ends)
        gq[at, edge:] = jnp.where(lane < 69, ends, 0.0).astype(BF)
        poll(polls + i)
        return carry

    lax.fori_loop(0, width // tile_d, grads, 0)
    polls += width // tile_d
    ring_u.exchange()
    ring_b.begin()

    def block(i, carry):
        phase = i // (2 * G)
        jj = (hi + 1 - (i // G) % 2 + 2) % 2
        mm = (m + 1 + i % G) % G
        parity = (1 - par) * (1 - phase) + par * phase
        b = (2 * parity + jj) * G + mm
        at = pl.ds(pl.multiple_of(b * R, R), R)
        dn = product_right(dqk[at, :], wqk[...]) + product_right(dvb[at, :], wf[...])
        D[b] = dn.astype(BF)

        @pl.when(phase == 0)
        def _():
            slot = jj * G + mm
            remote(D.at[b], b1.at[slot], s1.at[slot], r1.at[slot], core).start()

        poll(polls + i)

        @pl.when(i % 4 == 3)
        def _():
            ring_b.step(i // 4)

        return carry

    lax.fori_loop(0, nc, block, 0)
    polls += nc
    done_b = nc // 4

    order = list(range(1, G)) + [0]

    def chip_sum(jj, mm):
        slot = jj * G + mm
        pltpu.make_async_copy(b1.at[slot], b1.at[slot], r1.at[slot]).wait()
        return D[(2 * par + jj) * G + mm].astype(F32) + b1[slot].astype(F32)

    seconds = []
    for e in order:
        mm = (m + e) % G
        ab[mm] = chip_sum(1 - hi, mm).astype(BF)
        r = remote(ab.at[mm], b2.at[mm], s2.at[mm], r2.at[mm], other)
        r.start()
        seconds.append(r)
    thirds = []

    def sum_chips():
        for e in order:
            mm = (m + e) % G
            total = chip_sum(hi, mm)
            pltpu.make_async_copy(b2.at[mm], b2.at[mm], r2.at[mm]).wait()
            total = total + b2[mm].astype(F32)
            if e:
                st[mm] = total.astype(BF)
                r = remote(st.at[mm], b3.at[m], s3.at[mm], r3.at[m], (w, g * G + mm))
                r.start()
                thirds.append(r)
            else:
                tot[...] = total

    def sum_first():
        @pl.when(upper)
        def _():
            for gp in range(nw):
                total = dvb[pl.ds(pl.multiple_of((gp * G + m) * R, R), R), :].astype(F32)
                for e in range(1, G):
                    mm = (m + e) % G
                    pltpu.make_async_copy(f1.at[mm, gp], f1.at[mm, gp], rf1.at[mm, gp]).wait()
                    total = total + f1[mm, gp].astype(F32)
                fs[gp] = total.astype(BF)
                own = jnp.logical_and(w == seq, g == gp)

                @pl.when(own)
                def _():
                    pltpu.make_async_copy(fs.at[gp], fr.at[par], rf2.at[par]).start()

                @pl.when(jnp.logical_not(own))
                def _():
                    remote(
                        fs.at[gp], fr.at[par], sf2.at[gp], rf2.at[par], (seq, gp * G + m)
                    ).start()

    back = remote(tb, tr, sT.at[0], rT.at[0], home)
    stay = pltpu.make_async_copy(tb, tr, rT.at[0])

    def norm_back():
        total = tot[...]
        for e in range(1, G):
            mm = (m + e) % G
            pltpu.make_async_copy(b3.at[mm], b3.at[mm], r3.at[mm]).wait()
            total = total + b3[mm].astype(F32)
        value = X[og * G + m].astype(F32)
        centred = value - jnp.mean(value, axis=-1, keepdims=True)
        inverse = lax.rsqrt(jnp.mean(centred * centred, axis=-1, keepdims=True) + EPS)
        normal = centred * inverse
        dx = total * vec[4:5, :]
        dx = dx - jnp.mean(dx, axis=-1, keepdims=True) - normal * jnp.mean(
            dx * normal, axis=-1, keepdims=True
        )
        tb[...] = (dmid[...].astype(F32) + inverse * dx).astype(BF)

        @pl.when(home_self)
        def _():
            stay.start()

        @pl.when(jnp.logical_not(home_self))
        def _():
            back.start()

    turns = []
    extras = [ring_u.spread]
    extras += [functools.partial(ring_u.hop, h) for h in range(1, ring_u.reach[0] + 1)]
    small = [functools.partial(ring_o.turn, 0, a) for a in range((polls + 0) // 4, ring_o.steps)]
    for n in range(polls, 4 * (ring_a.steps - EARLY)):
        r, s = n % 4, EARLY + n // 4
        if r % 2 and s < ring_a.steps:
            turns.append(functools.partial(ring_a.turn, r // 2, s))
        if (r == 0 or n == polls) and extras:
            turns.append(extras.pop(0))
    turns += extras

    def others():
        if small:
            small.pop(0)()
        for _ in range(2):
            if turns:
                turns.pop(0)()

    for at_b in range(done_b, ring_b.turns):
        ring_b.step(at_b)
        others()
        if at_b == done_b + 2:
            sum_first()
        if at_b == 5:
            sum_chips()
    ring_b.exchange()
    others()
    ring_b.spread()
    others()
    for h in range(1, ring_b.reach[0] + 1):
        ring_b.hop(h)
        others()
        if h == 2:
            norm_back()
    while turns or small:
        others()

    down_out[...] = res_a[0:width, :]
    gout_out[...] = res_o[0:d, :]
    for j in range(ring_u.group):
        rows = slice(j * seg_u, (j + 1) * seg_u)
        for a in range(nw):
            up_out[rows, a * width : (a + 1) * width] = res_u[j, a]
    for j in range(ring_b.group):
        rows = slice(j * seg_b, (j + 1) * seg_b)
        for a in range(nw):
            for part in range(2):
                at = part * width + a * d
                qkv_out[rows, at : at + d] = res_b[j, a, :, part * d : (part + 1) * d]
            if a < 2:
                at = 2 * width + a * d
                qkv_out[rows, at : at + d] = res_b[j, a, :, 2 * d : 3 * d]
            at = a * d + j * seg_b
            sums_t[at : at + seg_b, :] = res_b[j, a, :, edge:].astype(F32)
    ends = jnp.transpose(sums_t[...])
    nb = 6 * d // 4
    line[:, 0:width] = ends[66:67, :]
    line[:, width : width + 2 * d] = ends[68:69, : 2 * d]
    share = line[:, 0:nb]
    for a in range(1, nw):
        share = jnp.where(w == a, line[:, a * nb : (a + 1) * nb], share)
    rows_out[...] = jnp.zeros_like(rows_out)
    rows_out[0:2, :] = res_o[d : d + 16, :].astype(F32)[0:2]
    for row in range(2):
        total = ends[64 + row : 65 + row, 0:d]
        for a in range(1, nw):
            total = total + ends[64 + row : 65 + row, a * d : (a + 1) * d]
        rows_out[2:3, row * d : (row + 1) * d] = total
    rows_out[3:4, 0:nb] = share
    pltpu.make_async_copy(tr, tr, rT.at[0]).wait()
    tokens_out[...] = tr[...]
    for u in range(2):
        pltpu.make_async_copy(fr.at[u], fr.at[u], rf2.at[u]).wait()
        first_out[:, u * d : (u + 1) * d] = fr[u]

    pltpu.make_async_copy(lr, lr, rL.at[0]).wait()
    layer_out[...] = lr[...]
    ring_o.drain()
    ring_a.drain()
    ring_u.drain()
    ring_b.drain()
    for r in seconds + thirds + shares:
        r.wait_send()

    @pl.when(jnp.logical_not(home_self))
    def _():
        back.wait_send()
        layer_back.wait_send()

    @pl.when(upper)
    def _():
        for r in first_copies:
            r.wait_send()
        for gp in range(nw):

            @pl.when(jnp.logical_not(jnp.logical_and(w == seq, g == gp)))
            def _():
                remote(
                    fs.at[gp], fr.at[par], sf2.at[gp], rf2.at[par], (seq, gp * G + m)
                ).wait_send()

    def drain(i, carry):
        jj = (hi + 1 - (i // G) % 2 + 2) % 2
        mm = (m + 1 + i % G) % G
        slot = jj * G + mm
        b = (2 * (1 - par) + jj) * G + mm
        remote(D.at[b], b1.at[slot], s1.at[slot], r1.at[slot], core).wait_send()
        return carry

    lax.fori_loop(0, 2 * G, drain, 0)


def tail(
    G, H, deal, q, k, v, o, do, lse, xh, X, wqk, wf, vec, dmid, up, down, gout, vsums, mlp, mid
):
    nw = 4
    nc = nw * G
    R, width = dmid.shape
    d = width // nw
    N = xh.shape[0]
    wide = H * HEAD_DIM
    seg_o = -(-(d + 16) // (2 * nc * 16)) * 16
    seg_u = seg_b = width // (2 * nc)
    cols = 5 * BLK
    dma = pltpu.SemaphoreType.DMA
    vm = pltpu.VMEM
    steps = 2 * (nc - 1)
    operands = (
        deal, q, k, v, o, do, lse, xh, X, wqk, wf, vec, dmid, up, down, gout, vsums, mlp, mid
    )
    return pl.pallas_call(
        functools.partial(tail_kernel, G, H, seg_o, seg_u, seg_b),
        name="tail",
        out_shape=(
            jax.ShapeDtypeStruct((R, width), BF),
            jax.ShapeDtypeStruct((R, width), BF),
            jax.ShapeDtypeStruct((R, 2 * d), BF),
            jax.ShapeDtypeStruct((d, nw * width), BF),
            jax.ShapeDtypeStruct((width, width), BF),
            jax.ShapeDtypeStruct((d, width), BF),
            jax.ShapeDtypeStruct((d, 2 * width + 2 * d), BF),
            jax.ShapeDtypeStruct((8, width), F32),
        ),
        in_specs=[pl.BlockSpec(memory_space=pltpu.SMEM)] + [ANY] * (len(operands) - 4) + [VM] + [ANY] * 2,
        out_specs=[VM] * 8,
        scratch_shapes=[vm(a.shape, a.dtype) for a in operands[1:7]]
        + [vm((nw, 2 * nc, R), F32)]
        + [vm(a.shape, a.dtype) for a in operands[7:13]]
        + [
            vm((wide, N), BF), vm((N, wide), F32), vm((N, wide), F32), vm((N, 2 * wide), BF),
            vm((N, wide), BF), vm((nc, R, width), BF), vm((2 * G, R, width), BF),
            vm((G, R, width), BF), vm((G, R, width), BF), vm((G, R, width), BF),
            vm((G, R, width), BF), vm((R, width), F32), vm((R, width), BF), vm((R, width), BF),
            vm((2 * nc * seg_o, width), BF), vm((2, nc - 1, seg_o, width), BF),
            vm((2 * nc * seg_o, width), BF),
            vm((width, width), BF), vm((2, nc - 1, seg_u, width), BF), vm((width, width), BF),
            vm((width, width), BF), vm((2, nc - 1, seg_u, width), BF),
            vm((nc // 2, nw, seg_u, width), BF),
            vm((width, cols), BF), vm((2, nc - 1, seg_b, cols), BF),
            vm((nc // 2, nw, seg_b, cols), BF),
            vm((width, BLK), F32), vm((width, BLK), F32), vm((width, BLK), F32),
            vm((1, 6 * d), F32),
            vm((G, nw, R, d), BF), vm((nw, R, d), BF), vm((2, R, d), BF),
            vm((nw * R, width), BF), vm((R, width), F32), vm((nw, R, width), BF),
            vm((R, width), BF), vm((R, width), BF), dma((nw,)), dma((nw,)), dma((1,)), dma((1,)),
            dma((2 * G,)), dma((2 * G,)), dma((G,)), dma((G,)), dma((G,)), dma((G,)),
            dma((1,)), dma((1,)), dma((2, 1, steps)), dma((2, 1, steps)),
            dma((2, 2, steps)), dma((2, 2, steps)),
        ]
        + [
            dma(a)
            for chains in (2, 1)
            for a in (
                (2, chains, nc - 1), (2, chains, nc - 1), (2,), (nw,), (2, nc // 2 + 1),
                (2, nc // 2 + 1),
            )
        ]
        + [
            dma((G, nw)), dma((G, nw)),
            dma((nw,)), dma((2,)), dma((len(operands),)),
        ],
        compiler_params=pltpu.CompilerParams(
            collective_id=2, has_side_effects=True, vmem_limit_bytes=63 << 20
        ),
        cost_estimate=pl.CostEstimate(
            flops=40 << 30, bytes_accessed=60 << 20, transcendentals=6 << 20
        ),
    )(*operands)


def on_device(
    nw,
    nc,
    tokens,
    first_values,
    cotangent,
    deal,
    w_qkv,
    bias_qv,
    w_out,
    bias_out,
    gain_one,
    shift_one,
    gain_two,
    shift_two,
    w_up,
    bias_up,
    w_down,
    bias_down,
):
    G = nc // nw
    w = lax.axis_index("wt")
    c = lax.axis_index("ctx")
    m = c % G
    rows, width = tokens.shape[1:]
    d = width // nw
    H = HEADS // nw
    both = ("wt", "ctx")
    seq = lambda g: 2 * (g % 2) + g // 2
    swap = [
        (a * nc + g * G + e, seq(g) * nc + a * G + e)
        for a in range(nw)
        for g in range(nw)
        for e in range(G)
    ]
    ring = [[(a, (a + k) % nw) for a in range(nw)] for k in range(nw)]

    def exchange(pieces):
        out = jnp.zeros_like(pieces)
        mine = lax.dynamic_index_in_dim(pieces, w, 0, keepdims=True)
        out = lax.dynamic_update_slice_in_dim(out, mine, w, 0)
        for k in range(1, nw):
            piece = lax.dynamic_index_in_dim(pieces, (w + k) % nw, 0, keepdims=True)
            got = lax.ppermute(piece, "wt", ring[k])
            out = lax.dynamic_update_slice_in_dim(out, got, (w + nw - k) % nw, 0)
        return out

    qk = w_qkv[:, : 2 * width].reshape(d, 2, nw, d).transpose(2, 0, 1, 3).reshape(nw, d, 2 * d)
    wf = w_qkv[:, 2 * width :].reshape(d, 2, d).transpose(1, 0, 2)
    nb = bias_qv.shape[0]
    ids = dealt_blocks(deal)
    qpos = jnp.arange(nw, dtype=jnp.int32) * G + m
    qid = jnp.take(ids.reshape(nc, 2), qpos, axis=0)
    hidden = (ids[None, None, :] > qid[:, :, None]).astype(F32) * -NEG
    bias = jnp.repeat(-hidden.reshape(2 * nw, 2 * nc), BLK, axis=1)[:, None, :]
    lift = jnp.repeat(hidden.transpose(0, 2, 1), BLK, axis=2)

    def mine(vector):
        return lax.dynamic_slice_in_dim(vector, w * d, d)

    if nc <= 8:
        vectors = (
            bias_out, gain_one, shift_one, gain_two, shift_two, bias_down, bias_up, bias_qv
        )
        X, xhat, k, v, Wup, cot, q, o, lse, part, Wqk, Wf, vec = head(
            G, H, deal, vectors, tokens[0], first_values[0], w_qkv, cotangent[0], w_up, w_out
        )
        mlp, mid_own, d_mid, d_o, g_up, g_down, g_out, vsums = middle(
            G, True, part, X, cot, o, Wup, w_down, w_out, vec
        )
        layer, grad_tokens, grad_first, s_up, s_down, s_out, s_qkv, sums = tail(
            G, H, deal, q, k, v, o, d_o, lse, xhat, X, Wqk, Wf, vec,
            d_mid, g_up, g_down, g_out, vsums, mlp, mid_own,
        )
        return (
            layer[None],
            grad_tokens.astype(F32)[None],
            grad_first.astype(F32)[None],
            s_qkv.astype(F32),
            sums[3, :nb],
            s_out.astype(F32),
            sums[1, d : 2 * d],
            sums[2, :d],
            sums[2, d : 2 * d],
            sums[1, 2 * d : 3 * d],
            sums[1, 3 * d :],
            s_up.astype(F32),
            sums[0],
            s_down.astype(F32),
            sums[1, :d],
        )

    small = jnp.concatenate(
        [bias_qv, bias_out, gain_one, shift_one, gain_two, shift_two, bias_down]
    )
    lanes = 16 * BLK
    small = jnp.concatenate([small, jnp.zeros((lanes - small.shape[0],), BF)]).reshape(16, BLK)
    X, Fv, WQK, WF, SM = gather(nw, G, tokens[0], first_values[0], qk, wf, small)
    X = X.reshape(nc * rows, width)
    Wqk = WQK.reshape(width, 2 * d)
    low = w < 2
    Wf = jnp.where(low, WF.reshape(width, d), jnp.zeros((width, d), BF))
    SM = SM.reshape(nw, lanes).astype(F32)
    qv_vector = SM[:, :nb].reshape(-1)
    vectors = [SM[:, nb + a * d : nb + (a + 1) * d].reshape(-1) for a in range(6)]
    out_vector, gain_a, shift_a, gain_b, shift_b, down_vector = vectors

    x32 = X.astype(F32)
    mean = jnp.mean(x32, axis=-1, keepdims=True)
    centred = x32 - mean
    inverse = lax.rsqrt(jnp.mean(centred * centred, axis=-1, keepdims=True) + EPS)
    n1 = (centred * inverse * gain_a + shift_a).astype(BF)
    pqk = product(n1, Wqk)
    q_bias = lax.dynamic_slice_in_dim(qv_vector, w * d, d)
    f_bias = lax.dynamic_slice_in_dim(qv_vector, width + (w % 2) * d, d)
    q = (pqk[:, :d] + q_bias).astype(BF)
    k = pqk[:, d:].astype(BF)
    f = (product(n1, Wf) + f_bias).astype(BF)
    Fv = Fv.reshape(nc * rows, 2 * d)
    first = jnp.where(w % 2 == 0, Fv[:, :d], Fv[:, d:])
    v = jnp.where(low, f, first)

    o, lse = attend(H, qpos, bias, q, k, v)

    part = product(o, w_out).astype(BF)
    pieces, spread = lax.optimization_barrier((w_up, cotangent[0], X))[:2]
    Wup = exchange(pieces.reshape(d, nw, width).transpose(1, 0, 2)).reshape(width, width)
    unswap = [(b, a) for a, b in swap]
    cot = lax.all_gather(lax.ppermute(spread, both, unswap), "wt", axis=0, tiled=True)
    vec = jnp.stack([out_vector, gain_b, shift_b, bias_up.astype(F32)] + [out_vector] * 4)
    mlp, mid_own, d_mid, d_o, g_up, g_down, g_out, vsums = middle(
        G, False, part, X.reshape(nc, rows, width), cot, o, Wup, w_down, w_out, vec
    )

    mlp = lax.psum_scatter(mlp, "wt", scatter_dimension=0, tiled=True)
    layer = (mid_own + mlp.astype(F32) + down_vector).astype(BF)
    layer = lax.ppermute(layer, both, swap)
    up_rows = exchange(g_up.reshape(nw, d, width)).transpose(1, 0, 2)
    s_up, s_down = lax.psum((up_rows.reshape(d, nw * width), g_down), "ctx")
    dqk, dv = attend_back(H, qpos, lift, q, k, v, o, d_o, lse)
    zero = jnp.zeros_like(dv)
    df = jnp.where(low, dv, zero)
    dn1 = product_right(dqk, Wqk) + product_right(df, Wf)
    dn1_low = dn1.astype(BF)
    blank = jnp.zeros_like(dv)
    left = jnp.where(w == 2, dv, blank)
    right = jnp.where(w == 3, dv, blank)
    total = scatter_sum(
        G, jnp.concatenate([dn1_low, left, right], axis=1).reshape(nc, rows, width + 2 * d)
    )
    grad_first = lax.ppermute(total[:, width:].astype(BF), both, swap).astype(F32)
    block = (w * G + m) * rows
    x_own = lax.dynamic_slice_in_dim(X, block, rows).astype(F32)
    _, pull_one = jax.vjp(lambda a: norm_rows(a, gain_a, shift_a), x_own)
    d_x = d_mid.astype(F32) + pull_one(total[:, :width])[0]
    grad_tokens = lax.ppermute(d_x.astype(BF), both, swap).astype(F32)

    g_qk = product_left(n1, dqk)
    g_f = product_left(n1, df)
    normal = centred * inverse
    g_gain_one = jnp.sum(dn1_low.astype(F32) * normal, axis=0)
    g_shift_one = jnp.sum(dn1_low.astype(F32), axis=0)
    cols = jnp.concatenate(
        [
            g_qk.astype(BF),
            g_f.astype(BF),
            g_gain_one[:, None].astype(BF),
            g_shift_one[:, None].astype(BF),
            jnp.zeros((width, 62), BF),
        ],
        axis=1,
    ).reshape(nw, d, 640)
    sums = jnp.concatenate(
        [jnp.sum(dqk.astype(F32), axis=0), jnp.sum(df.astype(F32), axis=0), jnp.zeros((64,), F32)]
    ).astype(BF)
    foot = jnp.concatenate([sums[None], jnp.zeros((7, 640), BF)], axis=0)
    pack = jnp.concatenate([cols, jnp.broadcast_to(foot[None], (nw, 8, 640))], axis=1)
    pack = exchange(pack)
    vecs = jnp.concatenate(
        [
            vsums[0],
            mine(vsums[1]),
            mine(vsums[2]),
            mine(vsums[3]),
            mine(vsums[4]),
        ]
    ).astype(BF)
    pack = pack.at[0, d + 1 : d + 4, :512].set(vecs.reshape(3, 512))
    pack, s_up, s_down = lax.optimization_barrier((pack, s_up, s_down))
    pack, s_out = lax.psum((pack, g_out), "ctx")
    body = pack[:, :d]
    s_qkv = jnp.concatenate(
        [body[a, :, e * d : (e + 1) * d] for e in (0, 1) for a in range(nw)]
        + [body[a, :, 2 * d : 3 * d] for a in range(2)],
        axis=1,
    ).astype(F32)
    s_gain_one = jnp.sum(body[:, :, 576].astype(F32), axis=0)
    s_shift_one = jnp.sum(body[:, :, 577].astype(F32), axis=0)
    ends = pack[:, d]
    bias_all = jnp.concatenate([ends[:, :d].reshape(-1), ends[:2, 2 * d : 3 * d].reshape(-1)])
    s_bias_qv = lax.dynamic_slice_in_dim(bias_all, w * nb, nb).astype(F32)
    vecs = pack[0, d + 1 : d + 4, :512].reshape(-1).astype(F32)
    s_bias_up = vecs[:width]
    s_bias_down, s_bias_out, s_gain_two, s_shift_two = [
        vecs[width + a * d : width + (a + 1) * d] for a in range(4)
    ]
    return (
        layer[None],
        grad_tokens[None],
        grad_first[None],
        s_qkv,
        s_bias_qv,
        s_out.astype(F32),
        s_bias_out,
        s_gain_one,
        s_shift_one,
        s_gain_two,
        s_shift_two,
        s_up.astype(F32),
        s_bias_up,
        s_down.astype(F32),
        s_bias_down,
    )


def solution(mesh):
    rows3 = P("wt", "ctx", None)
    mat = P("wt", None)
    vec = P("wt")
    in_specs = (rows3, rows3, rows3, P(), mat, vec, mat) + (vec,) * 5 + (mat, vec, mat, vec)
    out_specs = (
        (rows3, rows3, rows3, mat, vec, mat) + (vec,) * 5 + (mat, vec, mat, vec)
    )
    return jax.shard_map(
        functools.partial(on_device, mesh.shape["wt"], mesh.shape["ctx"]),
        mesh=mesh,
        in_specs=in_specs,
        out_specs=out_specs,
        check_vma=False,
    )
```

```python
import functools

import jax
import jax.numpy as jnp
from jax import lax
from jax.experimental import pallas as pl
from jax.experimental.pallas import tpu as pltpu
from jax.sharding import PartitionSpec as P

HEADS = 12
HEAD_DIM = 64
BLK = 128
CHUNK = 1024

EPS = 1e-05
SLOPE = 0.7978845608028654
CUBIC = 0.044715
NEG = -1e30

BF = jnp.bfloat16
F32 = jnp.float32
MESH = pl.DeviceIdType.MESH
ANY = pl.BlockSpec(memory_space=pl.ANY)
VM = pl.BlockSpec(memory_space=pltpu.VMEM)


def norm_rows(value, gain, shift):
    mean = jnp.mean(value, axis=-1, keepdims=True)
    centred = value - mean
    inverse = lax.rsqrt(jnp.mean(centred * centred, axis=-1, keepdims=True) + EPS)
    return centred * inverse * gain + shift


def gelu_tanh(value):
    return 0.5 * value * (1.0 + jnp.tanh(SLOPE * (value + CUBIC * value * value * value)))


def product(left, right):
    return jnp.dot(left, right, preferred_element_type=F32)


def product_left(left, right):
    return lax.dot_general(left, right, (((0,), (0,)), ((), ())), preferred_element_type=F32)


def product_right(left, right):
    return lax.dot_general(left, right, (((1,), (1,)), ((), ())), preferred_element_type=F32)


def dealt_blocks(deal):
    count = deal.shape[0] * 2
    pairs = jnp.repeat(deal, 2)
    parity = jnp.arange(count, dtype=jnp.int32) % 2
    return jnp.where(parity == 0, pairs, count - 1 - pairs)


def remote(src, dst, send, recv, device):
    return pltpu.make_async_remote_copy(
        src_ref=src,
        dst_ref=dst,
        send_sem=send,
        recv_sem=recv,
        device_id=device,
        device_id_type=MESH,
    )


def greet(peers):
    barrier = pltpu.get_barrier_semaphore()
    for peer in peers:
        pl.semaphore_signal(barrier, inc=1, device_id=peer, device_id_type=MESH)
    pl.semaphore_wait(barrier, len(peers))


def gather_kernel(
    nw, G, x, first, wqk, wf, small, X, Fv, WQK, WF, SM, rx, rf, rw, rv, rs, sa, sx, sfa, sfx, sw, loc
):
    w = lax.axis_index("wt")
    c = lax.axis_index("ctx")
    g = c // G
    m = c % G
    nc = nw * G
    core = w + 1 - 2 * (w % 2)
    other = (w + 2) % nw
    rel = lambda k: (w + k) % nw
    peers = [(rel(k), c) for k in range(1, nw)]
    peers += [(w, ((g + k) % nw) * G + m) for k in range(1, nw)]
    peers += [(w, g * G + (m + k) % G) for k in range(1, G)]
    greet(peers)
    seq = 2 * (g % 2) + g // 2
    goal = (2 * (w % 2) + w // 2) * G + m
    is_a = w == seq
    primary = (w + seq) % 2 == 0
    high = w >= 2
    copies = []

    to_head = remote(x, X.at[c], sa.at[0], rx.at[c], (w, goal))
    to_head_f = remote(first, Fv.at[c], sa.at[1], rf.at[c], (w, goal))
    own_x = pltpu.make_async_copy(x, X.at[c], rx.at[c])
    own_f = pltpu.make_async_copy(first, Fv.at[c], rf.at[c])

    @pl.when(is_a)
    def _():
        own_x.start()
        own_f.start()

    @pl.when(jnp.logical_not(is_a))
    def _():
        to_head.start()
        to_head_f.start()

    own_w = pltpu.make_async_copy(wqk.at[w], WQK.at[w], loc.at[0])
    own_s = pltpu.make_async_copy(small, SM.at[w], loc.at[1])
    own_w.start()
    own_s.start()
    own_v = pltpu.make_async_copy(wf.at[w % 2], WF.at[w], loc.at[2])
    own_v.start()
    sends_w, sends_v, sends_s = [], [], []
    for k in range(1, nw):
        d = rel(k)
        s = remote(small, SM.at[w], sw.at[k, 0], rs.at[w], (d, c))
        s.start()
        q = remote(wqk.at[d], WQK.at[w], sw.at[k, 1], rw.at[w], (d, c))
        q.start()
        v = remote(wf.at[d % 2], WF.at[w], sw.at[k, 2], rv.at[w], (d, c))
        sends_w += [s, q]
        sends_v.append((d, v))

        @pl.when(d < 2)
        def _():
            v.start()

    def block_x(b):
        return pltpu.make_async_copy(X.at[b], X.at[b], rx.at[b])

    def block_f(b):
        return pltpu.make_async_copy(Fv.at[b], Fv.at[b], rf.at[b])

    fwd_core, fwd_other, fwd_member = [], [], []
    for k in range(nw):
        gp = (g + k) % nw
        b = gp * G + m
        to_core = remote(X.at[b], X.at[b], sx.at[0, b], rx.at[b], (core, c))
        to_other = remote(X.at[b], X.at[b], sx.at[1, b], rx.at[b], (other, c))
        to_core_f = remote(Fv.at[b], Fv.at[b], sfx.at[0, b], rf.at[b], (core, c))
        to_other_f = remote(Fv.at[b], Fv.at[b], sfx.at[1, b], rf.at[b], (other, c))
        members = [
            remote(X.at[b], X.at[b], sx.at[1 + e, b], rx.at[b], (w, g * G + (m + e) % G))
            for e in range(1, G)
        ]
        members_f = [
            remote(Fv.at[b], Fv.at[b], sfx.at[1 + e, b], rf.at[b], (w, g * G + (m + e) % G))
            for e in range(1, G)
        ]

        @pl.when(primary)
        def _():
            block_x(b).wait()

            @pl.when(is_a)
            def _():
                to_other.start()

            for r in members:
                r.start()
            to_core.start()

        @pl.when(jnp.logical_and(is_a, jnp.logical_not(high)))
        def _():
            block_f(b).wait()
            to_other_f.start()

        @pl.when(jnp.logical_and(primary, high))
        def _():
            block_f(b).wait()
            for r in members_f:
                r.start()
            to_core_f.start()

        fwd_core.append((to_core, to_core_f))
        fwd_other.append((to_other, to_other_f))
        fwd_member.append((members, members_f))
    for e in range(1, G):
        for k in range(nw):
            b = ((g + k) % nw) * G + (m + e) % G
            to_core = remote(X.at[b], X.at[b], sx.at[0, b], rx.at[b], (core, c))
            to_core_f = remote(Fv.at[b], Fv.at[b], sfx.at[0, b], rf.at[b], (core, c))

            @pl.when(primary)
            def _():
                block_x(b).wait()
                to_core.start()

            @pl.when(jnp.logical_and(primary, high))
            def _():
                block_f(b).wait()
                to_core_f.start()

            fwd_core.append((to_core, to_core_f))

    @pl.when(jnp.logical_not(primary))
    def _():
        for b in range(nc):
            block_x(b).wait()

        @pl.when(high)
        def _():
            for b in range(nc):
                block_f(b).wait()

    own_w.wait()
    own_s.wait()
    own_v.wait()
    for k in range(1, nw):
        src = (w + nw - k) % nw
        pltpu.make_async_copy(wqk.at[0], WQK.at[src], rw.at[src]).wait()
        pltpu.make_async_copy(small, SM.at[src], rs.at[src]).wait()

        @pl.when(w < 2)
        def _():
            pltpu.make_async_copy(wf.at[0], WF.at[src], rv.at[src]).wait()

    for s in sends_w:
        s.wait_send()
    for d, v in sends_v:

        @pl.when(d < 2)
        def _():
            v.wait_send()

    @pl.when(jnp.logical_not(is_a))
    def _():
        to_head.wait_send()
        to_head_f.wait_send()

    @pl.when(primary)
    def _():
        for a, _f in fwd_core:
            a.wait_send()
        for ms, _f in fwd_member:
            for a in ms:
                a.wait_send()

        @pl.when(high)
        def _():
            for _x, a in fwd_core:
                a.wait_send()
            for _x, ms in fwd_member:
                for a in ms:
                    a.wait_send()

    @pl.when(is_a)
    def _():
        for a, _f in fwd_other:
            a.wait_send()

        @pl.when(jnp.logical_not(high))
        def _():
            for _x, a in fwd_other:
                a.wait_send()


def gather(nw, G, x, first, wqk, wf, small):
    nc = nw * G
    rows, width = x.shape
    half = first.shape[1]
    d = width // nw
    dma = pltpu.SemaphoreType.DMA
    return pl.pallas_call(
        functools.partial(gather_kernel, nw, G),
        name="gather_tokens",
        out_shape=(
            jax.ShapeDtypeStruct((nc, rows, width), BF),
            jax.ShapeDtypeStruct((nc, rows, half), BF),
            jax.ShapeDtypeStruct((nw, d, 2 * d), BF),
            jax.ShapeDtypeStruct((nw, d, d), BF),
            jax.ShapeDtypeStruct((nw,) + small.shape, BF),
        ),
        in_specs=[ANY] * 5,
        out_specs=[ANY] * 5,
        scratch_shapes=[
            dma((nc,)),
            dma((nc,)),
            dma((nw,)),
            dma((nw,)),
            dma((nw,)),
            dma((2,)),
            dma((1 + G, nc)),
            dma((2,)),
            dma((1 + G, nc)),
            dma((nw, 3)),
            dma((3,)),
        ],
        compiler_params=pltpu.CompilerParams(collective_id=0, has_side_effects=True),
    )(x, first, wqk, wf, small)


def middle_kernel(
    T, G, crossed, p_hbm, X_hbm, cot_hbm, o_hbm, wup_hbm, wdn_hbm, wout_hbm, vec_hbm,
    mlp, mid_own, dmid_own, do_out, gup, gdn, gout, sums,
    p, x, cot, o, wup, wdn, wout, vec,
    b1, ab, b2, bs, mid, n2s, act, dus, q, b4, ab2, b5, dn, dbs,
    s1, r1, s2, r2, s3, r3, s4, r4, s5, r5, s6, r6, ld, *rings,
):
    w = lax.axis_index("wt")
    c = lax.axis_index("ctx")
    g = c // G
    m = c % G
    core = (w + 1 - 2 * (w % 2), c)
    other = ((w + 2) % 4, c)
    mine = w % 2
    theirs = 1 - mine
    rows = p.shape[0]
    half = rows // 2
    n = half // T
    R = rows // 4
    loads = [
        pltpu.make_async_copy(p_hbm, p, ld.at[0]),
        pltpu.make_async_copy(vec_hbm, vec, ld.at[1]),
    ]
    loads += [
        pltpu.make_async_copy(X_hbm.at[a * G + m], x.at[pl.ds(a * R, R)], ld.at[2 + a])
        for a in range(4)
    ]
    loads += [
        pltpu.make_async_copy(wup_hbm, wup, ld.at[6]),
        pltpu.make_async_copy(wdn_hbm, wdn, ld.at[7]),
        pltpu.make_async_copy(cot_hbm, cot, ld.at[8]),
        pltpu.make_async_copy(wout_hbm, wout, ld.at[9]),
        pltpu.make_async_copy(o_hbm, o, ld.at[10]),
    ]
    for copy in loads:
        copy.start()
    peers = [core, other]
    if crossed:
        slots_u, slots_d, ssu, sru, ssd, srd = rings
        nc = 4 * G
        pos, right, left = ring_place(nc)
        seg = p.shape[1] // (2 * nc)
        ring_u = Ring(nc, pos, right, left, seg, 2, gup, slots_u, None, ssu, sru)
        ring_d = Ring(nc, pos, right, left, seg, 2, gdn, slots_d, None, ssd, srd)
        peers += [right, left]
    greet(peers)

    def rs(base, t):
        return pl.ds(pl.multiple_of(base * half + t * n, n), n)

    loads[0].wait()
    first = []
    for t in range(T):
        r = remote(p.at[rs(theirs, t)], b1.at[t], s1.at[t], r1.at[t], core)
        r.start()
        first.append(r)
    second = []
    for t in range(T):
        first[t].wait_recv()
        ab[t] = (p[rs(mine, t), :].astype(F32) + b1[t].astype(F32)).astype(BF)
        r = remote(ab.at[t], b2.at[t], s2.at[t], r2.at[t], other)
        r.start()
        second.append(r)
    for copy in loads[1:]:
        copy.wait()
    out_b = vec[0:1, :]
    gain = vec[1:2, :]
    shift = vec[2:3, :]
    up_b = vec[3:4, :]
    sums[...] = jnp.zeros_like(sums)

    def two(ref, t):
        return jnp.concatenate([ref[rs(mine, t), :], ref[rs(theirs, t), :]], axis=0)

    def put(ref, t, value):
        ref[rs(mine, t), :] = value[:n]
        ref[rs(theirs, t), :] = value[n:]

    def add_sum(at, value):
        sums[at : at + 1, :] += jnp.sum(value, axis=0, keepdims=True)

    def chain(t):
        pltpu.make_async_copy(b4.at[t], b4.at[t], r4.at[t]).wait()
        ab2[t] = (q[rs(mine, t), :].astype(F32) + b4[t].astype(F32)).astype(BF)
        remote(ab2.at[t], b5.at[t], s5.at[t], r5.at[t], other).start()

    def forward(t, carry):
        pltpu.make_async_copy(b2.at[t], b2.at[t], r2.at[t]).wait()
        bs[rs(mine, t), :] = (ab[t].astype(F32) + b2[t].astype(F32)).astype(BF)
        remote(bs.at[rs(mine, t)], bs.at[rs(mine, t)], s3.at[t], r3.at[t], core).start()

        @pl.when(t > 0)
        def _():
            chain(t - 1)

        pltpu.make_async_copy(bs.at[rs(theirs, t)], bs.at[rs(theirs, t)], r3.at[t]).wait()
        value = two(x, t).astype(F32) + two(bs, t).astype(F32) + out_b
        put(mid, t, value)
        centred = value - jnp.mean(value, axis=-1, keepdims=True)
        inverse = lax.rsqrt(jnp.mean(centred * centred, axis=-1, keepdims=True) + EPS)
        n2 = (centred * inverse * gain + shift).astype(BF)
        put(n2s, t, n2)
        u = product(n2, wup[...]) + up_b
        th = jnp.tanh(SLOPE * (u + CUBIC * u * u * u))
        a = (0.5 * u * (1.0 + th)).astype(BF)
        slope = 0.5 * (1.0 + th) + 0.5 * u * (1.0 - th * th) * SLOPE * (1.0 + 3.0 * CUBIC * u * u)
        put(act, t, a)
        ct = two(cot, t)
        du = (product_right(ct, wdn[...]) * slope).astype(BF)
        put(dus, t, du)
        put(q, t, product_right(du, wup[...]).astype(BF))
        remote(q.at[rs(theirs, t)], b4.at[t], s4.at[t], r4.at[t], core).start()
        put(mlp, t, product(a, wdn[...]).astype(BF))
        add_sum(0, du.astype(F32))
        add_sum(1, ct.astype(F32))
        return carry

    lax.fori_loop(0, T, forward, 0)
    chain(T - 1)

    width = p.shape[1]
    tile = 256

    def grads(i, carry):
        at = pl.ds(pl.multiple_of(i * tile, tile), tile)
        gup[at, :] = product_left(n2s[:, at], dus[...]).astype(BF)
        gdn[at, :] = product_left(act[:, at], cot[...]).astype(BF)
        return carry

    lax.fori_loop(0, width // tile, grads, 0)
    if crossed:
        ring_u.begin()
        ring_d.begin()

    def backward(t, carry):
        pltpu.make_async_copy(b5.at[t], b5.at[t], r5.at[t]).wait()
        dn[rs(mine, t), :] = (ab2[t].astype(F32) + b5[t].astype(F32)).astype(BF)
        remote(dn.at[rs(mine, t)], dn.at[rs(mine, t)], s6.at[t], r6.at[t], core).start()
        pltpu.make_async_copy(dn.at[rs(theirs, t)], dn.at[rs(theirs, t)], r6.at[t]).wait()
        value = two(mid, t)
        centred = value - jnp.mean(value, axis=-1, keepdims=True)
        inverse = lax.rsqrt(jnp.mean(centred * centred, axis=-1, keepdims=True) + EPS)
        normal = centred * inverse
        dn2 = two(dn, t).astype(F32)
        add_sum(3, dn2 * normal)
        add_sum(4, dn2)
        dx = dn2 * gain
        dx = dx - jnp.mean(dx, axis=-1, keepdims=True) - normal * jnp.mean(
            dx * normal, axis=-1, keepdims=True
        )
        dmid = two(cot, t).astype(F32) + inverse * dx
        db = dmid.astype(BF)
        put(dbs, t, db)
        add_sum(2, db.astype(F32))
        put(do_out, t, product_right(db, wout[...]).astype(BF))
        if crossed:

            @pl.when(t >= T - EARLY)
            def _():
                ring_u.early(t - (T - EARLY), EARLY)
                ring_d.early(t - (T - EARLY), EARLY)

        return carry

    lax.fori_loop(0, T, backward, 0)
    gout[...] = product_left(o[...], dbs[...]).astype(BF)
    if crossed:
        ring_u.early_drain(EARLY)
        ring_d.early_drain(EARLY)
    block_at = 2 * (w % 2) + w // 2 if crossed else w
    own = pl.ds(pl.multiple_of(block_at * R, R), R)
    mid_own[...] = mid[own, :]
    dmid_own[...] = dbs[own, :]
    for t in range(T):
        first[t].wait_send()
        second[t].wait_send()
        remote(bs.at[rs(mine, t)], bs.at[rs(mine, t)], s3.at[t], r3.at[t], core).wait_send()
        remote(q.at[rs(theirs, t)], b4.at[t], s4.at[t], r4.at[t], core).wait_send()
        remote(ab2.at[t], b5.at[t], s5.at[t], r5.at[t], other).wait_send()
        remote(dn.at[rs(mine, t)], dn.at[rs(mine, t)], s6.at[t], r6.at[t], core).wait_send()


def middle(G, crossed, p, X, cot, o, wup, wdn, wout, vec):
    T = 4
    rows, width = p.shape
    n = rows // 2 // T
    R = rows // 4
    d = o.shape[1]
    dma = pltpu.SemaphoreType.DMA
    full = pltpu.VMEM((rows, width), BF)
    part = pltpu.VMEM((T, n, width), BF)
    square = pltpu.VMEM((width, width), BF)
    return pl.pallas_call(
        functools.partial(middle_kernel, T, G, crossed),
        name="middle",
        out_shape=(
            jax.ShapeDtypeStruct((rows, width), BF),
            jax.ShapeDtypeStruct((R, width), F32),
            jax.ShapeDtypeStruct((R, width), BF),
            jax.ShapeDtypeStruct((rows, d), BF),
            jax.ShapeDtypeStruct((width, width), BF),
            jax.ShapeDtypeStruct((width, width), BF),
            jax.ShapeDtypeStruct((d, width), BF),
            jax.ShapeDtypeStruct((8, width), F32),
        ),
        in_specs=[ANY] * 8,
        out_specs=[VM] * 8,
        scratch_shapes=[
            full, full, full, pltpu.VMEM((rows, d), BF), square, square,
            pltpu.VMEM((d, width), BF), pltpu.VMEM((8, width), F32),
            part, part, part, full, pltpu.VMEM((rows, width), F32), full, full, full, full,
            part, part, part, full, full,
        ]
        + [dma((T,))] * 12
        + [dma((11,))]
        + (
            [pltpu.VMEM((2, EARLY, width // (8 * G), width), BF)] * 2 + [dma((2, 2, EARLY))] * 4
            if crossed
            else []
        ),
        compiler_params=pltpu.CompilerParams(
            collective_id=1, has_side_effects=True, vmem_limit_bytes=62 << 20
        ),
        cost_estimate=pl.CostEstimate(
            flops=14 * rows * width * width, bytes_accessed=40 << 20, transcendentals=rows * width
        ),
    )(p, X, cot, o, wup, wdn, wout, vec)


def scatter_kernel(G, D, out, b1, ab, b2, st, b3, s1, r1, s2, r2, s3, r3):
    w = lax.axis_index("wt")
    c = lax.axis_index("ctx")
    g = c // G
    m = c % G
    core = w + 1 - 2 * (w % 2)
    other = (w + 2) % 4
    par = w % 2
    hi = w // 2
    greet([(core, c), (other, c)] + [(w, g * G + (m + e) % G) for e in range(1, G)])
    order = [e for e in range(1, G)] + [0]
    firsts = {}
    for j in (1, 0):
        for e in order:
            jj = (hi + j) % 2
            mm = (m + e) % G
            b = (2 * jj + 1 - par) * G + mm
            slot = jj * G + mm
            r = remote(D.at[b], b1.at[slot], s1.at[slot], r1.at[slot], (core, c))
            r.start()
            firsts[(j, e)] = r

    def arrived1(slot):
        pltpu.make_async_copy(b1.at[slot], b1.at[slot], r1.at[slot]).wait()

    seconds = []
    for e in order:
        jj = 1 - hi
        mm = (m + e) % G
        slot = jj * G + mm
        arrived1(slot)
        ab[mm] = (D[(2 * jj + par) * G + mm].astype(F32) + b1[slot].astype(F32)).astype(BF)
        r = remote(ab.at[mm], b2.at[mm], s2.at[mm], r2.at[mm], (other, c))
        r.start()
        seconds.append(r)
    thirds = []
    for e in order:
        mm = (m + e) % G
        slot = hi * G + mm
        arrived1(slot)
        pltpu.make_async_copy(b2.at[mm], b2.at[mm], r2.at[mm]).wait()
        total = D[w * G + mm].astype(F32) + b1[slot].astype(F32) + b2[mm].astype(F32)
        if e == 0:
            for f in range(1, G):
                q = (m + f) % G
                pltpu.make_async_copy(b3.at[q], b3.at[q], r3.at[q]).wait()
                total = total + b3[q].astype(F32)
            out[...] = total.astype(out.dtype)
        else:
            st[mm] = total.astype(BF)
            r = remote(st.at[mm], b3.at[m], s3.at[mm], r3.at[m], (w, g * G + mm))
            r.start()
            thirds.append(r)
    for r in list(firsts.values()) + seconds + thirds:
        r.wait_send()


def scatter_sum(G, D):
    nc, rows, C = D.shape
    dma = pltpu.SemaphoreType.DMA
    return pl.pallas_call(
        functools.partial(scatter_kernel, G),
        name="scatter_sum",
        out_shape=jax.ShapeDtypeStruct((rows, C), F32),
        in_specs=[VM],
        out_specs=VM,
        scratch_shapes=[
            pltpu.VMEM((2 * G, rows, C), BF),
            pltpu.VMEM((G, rows, C), BF),
            pltpu.VMEM((G, rows, C), BF),
            pltpu.VMEM((G, rows, C), BF),
            pltpu.VMEM((G, rows, C), BF),
            dma((2 * G,)),
            dma((2 * G,)),
            dma((G,)),
            dma((G,)),
            dma((G,)),
            dma((G,)),
        ],
        compiler_params=pltpu.CompilerParams(
            collective_id=3, has_side_effects=True, vmem_limit_bytes=60 << 20
        ),
    )(D)


def head_mask(shape, h):
    lane = lax.broadcasted_iota(jnp.int32, shape, 1)
    return jnp.logical_and(lane >= h * HEAD_DIM, lane < (h + 1) * HEAD_DIM)


def split_heads(H, value):
    zero = jnp.zeros_like(value)
    return [jnp.where(head_mask(value.shape, h), value, zero) for h in range(H)]


def spread(H, shape, values):
    out = jnp.broadcast_to(values[H - 1], shape)
    for h in range(H - 2, -1, -1):
        out = jnp.where(head_mask(shape, h), values[h], out)
    return out


def attend_tile(H, q, k_ref, v_ref, bias_ref, at_bias, chunks=None):
    rows, width = q.shape
    N = k_ref.shape[0]
    step_keys = min(N, 1024)
    qh = split_heads(H, q * jnp.asarray(HEAD_DIM**-0.5, BF))
    top_half = lax.broadcasted_iota(jnp.int32, (rows, 1), 0) < BLK

    def step(j, carry):
        tops, sums, acc = carry
        at = pl.ds(pl.multiple_of(j * step_keys, step_keys), step_keys)
        kc = k_ref[at, :]
        vc = v_ref[at, :]
        low = bias_ref[at_bias, :, at]
        high = bias_ref[at_bias + 1, :, at]
        new_tops, new_sums, shrink, parts = [], [], [], []
        for h in range(H):
            s = product_right(qh[h], kc)
            s = jnp.concatenate([s[:BLK] + low, s[BLK:] + high], axis=0)
            top = jnp.maximum(tops[h], jnp.max(s, axis=1, keepdims=True))
            a = jnp.exp(tops[h] - top)
            p = jnp.exp(s - top)
            new_sums.append(sums[h] * a + jnp.sum(p, axis=1, keepdims=True))
            new_tops.append(top)
            shrink.append(a)
            parts.append(product(p.astype(BF), vc))
        acc = acc * spread(H, acc.shape, shrink) + spread(H, acc.shape, parts)
        return new_tops, new_sums, acc

    start = (
        [jnp.full((rows, 1), NEG, F32)] * H,
        [jnp.zeros((rows, 1), F32)] * H,
        jnp.zeros((rows, width), F32),
    )
    chunks = N // step_keys if chunks is None else chunks
    tops, sums, acc = lax.fori_loop(0, chunks, step, start)
    out = (acc / spread(H, acc.shape, sums)).astype(BF)
    lse = []
    for h in range(H):
        column = tops[h] + jnp.log(sums[h])
        lse.append(jnp.transpose(jnp.broadcast_to(column, (rows, BLK)))[0:1, :])
    lse = jnp.concatenate(lse + [jnp.zeros((8 - H, rows), F32)], axis=0)
    return out, lse


def attend_kernel(H, qpos, q_ref, k_ref, v_ref, bias_ref, o_ref, lse_ref):
    o, lse = attend_tile(H, q_ref[...], k_ref, v_ref, bias_ref, 2 * pl.program_id(0))
    o_ref[...] = o
    lse_ref[0] = lse


def attend(H, qpos, bias, q, k, v):
    n = qpos.shape[0]
    width = H * HEAD_DIM
    N = k.shape[0]
    rows = 2 * BLK
    whole = pl.BlockSpec((N, width), lambda i, *_: (0, 0))
    return pl.pallas_call(
        functools.partial(attend_kernel, H),
        name="attend",
        out_shape=(
            jax.ShapeDtypeStruct((n * rows, width), BF),
            jax.ShapeDtypeStruct((n, 8, rows), F32),
        ),
        grid_spec=pltpu.PrefetchScalarGridSpec(
            num_scalar_prefetch=1,
            grid=(n,),
            in_specs=[
                pl.BlockSpec((rows, width), lambda i, qp: (qp[i], 0)),
                whole,
                whole,
                pl.BlockSpec((2 * n, 1, N), lambda i, *_: (0, 0, 0)),
            ],
            out_specs=[
                pl.BlockSpec((rows, width), lambda i, *_: (i, 0)),
                pl.BlockSpec((1, 8, rows), lambda i, *_: (i, 0, 0)),
            ],
        ),
        compiler_params=pltpu.CompilerParams(vmem_limit_bytes=48 << 20),
    )(qpos, q, k, v, bias)


def attend_back_tile(
    H, q, do, o, lse, k_ref, v_ref, kt, dk, dv, lift_ref, tile, chunks=None, poll=None
):
    rows, width = q.shape
    N = k_ref.shape[0]
    scale = HEAD_DIM**-0.5
    qh = split_heads(H, q * jnp.asarray(scale, BF))
    doh = split_heads(H, do)
    qcat = jnp.concatenate(qh, axis=0)
    docat = jnp.concatenate(doh, axis=0)
    pick = lax.broadcasted_iota(jnp.int32, (8, width), 1)
    base = lax.broadcasted_iota(jnp.int32, (8, width), 0) * HEAD_DIM
    pick = jnp.logical_and(pick >= base, pick < base + HEAD_DIM).astype(F32)
    delta = lax.dot_general(
        pick,
        do.astype(F32) * o.astype(F32),
        (((1,), (1,)), ((), ())),
        precision=lax.Precision.HIGHEST,
        preferred_element_type=F32,
    )

    def step(j, dqt):
        at = pl.ds(pl.multiple_of(j * CHUNK, CHUNK), CHUNK)
        kc = k_ref[at, :]
        vc = v_ref[at, :]
        ps, dss, dqs = [], [], []
        for h in range(H):
            s = product_right(kc, qh[h])
            dp = product_right(vc, doh[h])
            pieces, dpieces = [], []
            for b in range(CHUNK // BLK):
                lift = lift_ref[tile, pl.ds(j * (CHUNK // BLK) + b, 1), :]
                cut = slice(b * BLK, (b + 1) * BLK)
                p = jnp.exp(s[cut] - (lse[h : h + 1, :] + lift))
                pieces.append(p.astype(BF))
                dpieces.append((p * (dp[cut] - delta[h : h + 1, :])).astype(BF))
            p = jnp.concatenate(pieces, axis=0)
            ds = jnp.concatenate(dpieces, axis=0)
            ps.append(p)
            dss.append(ds)
            dqs.append(product(kt[h * HEAD_DIM : (h + 1) * HEAD_DIM, at], ds))
        dv[at, :] += product(jnp.concatenate(ps, axis=1), docat)
        dk[at, :] += product(jnp.concatenate(dss, axis=1), qcat)
        if poll is not None:
            poll(j)
        return dqt + jnp.concatenate(dqs, axis=0)

    chunks = N // CHUNK if chunks is None else chunks
    dqt = lax.fori_loop(0, chunks, step, jnp.zeros((width, rows), F32))
    return dqt * scale


def flip_rows(src, dst):
    def flip(b, carry):
        at = pl.ds(pl.multiple_of(b * BLK, BLK), BLK)
        dst[:, at] = jnp.transpose(src[at, :])
        return carry

    lax.fori_loop(0, src.shape[0] // BLK, flip, 0)


def attend_back_kernel(
    H, qpos, q_ref, k_ref, v_ref, o_ref, do_ref, lse_ref, lift_ref, dqk_ref, dv_ref, kt, dk, dv
):
    i = pl.program_id(0)
    width = H * HEAD_DIM

    @pl.when(i == 0)
    def _():
        flip_rows(k_ref, kt)
        dk[...] = jnp.zeros_like(dk)
        dv[...] = jnp.zeros_like(dv)
        dqk_ref[...] = jnp.zeros_like(dqk_ref)

    dqt = attend_back_tile(
        H, q_ref[...], do_ref[...], o_ref[...], lse_ref[0], k_ref, v_ref, kt, dk, dv, lift_ref, i
    )
    rows = 2 * BLK
    here = pl.ds(pl.multiple_of(qpos[i] * rows, rows), rows)
    dqk_ref[here, 0:width] = jnp.transpose(dqt).astype(BF)

    @pl.when(i == pl.num_programs(0) - 1)
    def _():
        dqk_ref[:, width : 2 * width] = dk[...].astype(BF)
        dv_ref[...] = dv[...].astype(BF)


def attend_back(H, qpos, lift, q, k, v, o, do, lse):
    n = qpos.shape[0]
    width = H * HEAD_DIM
    N = k.shape[0]
    rows = 2 * BLK
    whole = pl.BlockSpec((N, width), lambda i, *_: (0, 0))
    row = pl.BlockSpec((rows, width), lambda i, *_: (i, 0))
    return pl.pallas_call(
        functools.partial(attend_back_kernel, H),
        name="attend_back",
        out_shape=(
            jax.ShapeDtypeStruct((N, 2 * width), BF),
            jax.ShapeDtypeStruct((N, width), BF),
        ),
        grid_spec=pltpu.PrefetchScalarGridSpec(
            num_scalar_prefetch=1,
            grid=(n,),
            in_specs=[
                pl.BlockSpec((rows, width), lambda i, qp: (qp[i], 0)),
                whole,
                whole,
                row,
                row,
                pl.BlockSpec((1, 8, rows), lambda i, *_: (i, 0, 0)),
                pl.BlockSpec((n, N // BLK, rows), lambda i, *_: (0, 0, 0)),
            ],
            out_specs=[
                pl.BlockSpec((N, 2 * width), lambda i, *_: (0, 0)),
                pl.BlockSpec((N, width), lambda i, *_: (0, 0)),
            ],
            scratch_shapes=[
                pltpu.VMEM((width, N), BF),
                pltpu.VMEM((N, width), F32),
                pltpu.VMEM((N, width), F32),
            ],
        ),
        compiler_params=pltpu.CompilerParams(vmem_limit_bytes=60 << 20),
    )(qpos, q, k, v, o, do, lse, lift)


def head_kernel(
    G, H,
    deal, out_b, gain_one, shift_one, gain_two, shift_two, down_b, up_b, qv_b,
    x_h, first_h, wqkv_h, cot_h, wup_h, wout_h,
    X_o, xh_o, k_o, v_o, wup_o, cot_o, q, o, lse, part, wqk, wf, vec,
    X, Fv, xh, k, v, small, vq, bias, wout, wl, wqk_h, wf_h, Y, line, small_l,
    rx, rf, rw, rv, rs, rc, ru, sh, sx, sf, sw, sc, su, loc, out, ry, sy,
):
    nw = 4
    w = lax.axis_index("wt")
    c = lax.axis_index("ctx")
    g = c // G
    m = c % G
    nc = nw * G
    R, width = x_h.shape
    d = width // nw
    par = w % 2
    core = (w + 1 - 2 * par, c)
    seq = 2 * (g % 2) + g // 2
    og = 2 * par + w // 2
    goal = og * G + m
    two = (w + 2) % nw
    goal_two = (2 * par + two // 2) * G + m
    is_a = w == seq
    primary = (w + seq) % 2 == 0
    high = w >= 2
    low = w < 2
    peers = [
        ((w + a) % nw, ((g + e) % nw) * G + m) for a in range(nw) for e in range(nw) if a or e
    ]
    peers += [(w, g * G + (m + e) % G) for e in range(1, G)]
    loads = [
        pltpu.make_async_copy(a, b, loc.at[i])
        for i, (a, b) in enumerate(((wqkv_h, wl), (wout_h, wout)))
    ]
    for copy in loads:
        copy.start()
    greet(peers)

    here = goal == c
    here_two = goal_two == c
    to_y = remote(x_h, Y, sh.at[0], ry.at[0], (two, c))
    to_one = remote(x_h, X.at[c], sh.at[1], rx.at[c], (w, goal))
    to_two = remote(Y, X.at[c], sh.at[4], rx.at[c], (w, goal_two))
    to_first = remote(first_h, Fv.at[c], sh.at[2], rf.at[c], (w, goal))
    home_cot = jnp.logical_and(here, is_a)
    own_cot = pl.ds(pl.multiple_of(g * R, R), R)
    to_cot = remote(cot_h, cot_o.at[own_cot], sh.at[3], rc.at[g], (seq, goal))
    to_y.start()

    @pl.when(here)
    def _():
        pltpu.make_async_copy(x_h, X.at[c], rx.at[c]).start()
        pltpu.make_async_copy(first_h, Fv.at[c], rf.at[c]).start()

    @pl.when(jnp.logical_not(here))
    def _():
        to_one.start()
        to_first.start()

    line[...] = jnp.zeros_like(line)
    for a, ref in enumerate((out_b, gain_one, shift_one, gain_two, shift_two, down_b)):
        at = a // 2
        line[at : at + 1, (a % 2) * d : (a % 2 + 1) * d] = ref[...].astype(F32).reshape(1, d)
    for a in range(2):
        half = up_b[a * 2 * d : (a + 1) * 2 * d].astype(F32).reshape(1, 2 * d)
        line[3 + a : 4 + a, :] = half
    line[5:6, : 6 * d // 4] = qv_b[...].astype(F32).reshape(1, 6 * d // 4)
    small_l[...] = line[...].astype(BF)
    loads[0].wait()
    for a in range(nw):
        for half in range(2):
            at = half * width + a * d
            wqk_h[a, :, half * d : (half + 1) * d] = wl[:, at : at + d]
    for a in range(2):
        at = 2 * width + a * d
        wf_h[a] = wl[:, at : at + d]

    def rows_of(a):
        return pl.ds(pl.multiple_of(a * d, 16), d)

    weights, fresh = [], []
    for e in range(1, nw):
        to = (w + e) % nw
        weights.append(remote(small_l, small.at[w], sw.at[e, 0], rs.at[w], (to, c)))
        weights.append(remote(wqk_h.at[to], wqk.at[rows_of(w)], sw.at[e, 1], rw.at[w], (to, c)))
        fresh.append(
            (to, remote(wf_h.at[to % 2], wf.at[rows_of(w)], sw.at[e, 2], rv.at[w], (to, c)))
        )
    for r in weights:
        r.start()
    for to, r in fresh:

        @pl.when(to < 2)
        def _():
            r.start()

    pltpu.make_async_copy(small_l, small.at[w], rs.at[w]).start()
    pltpu.make_async_copy(wqk_h.at[w], wqk.at[rows_of(w)], rw.at[w]).start()

    @pl.when(low)
    def _():
        pltpu.make_async_copy(wf_h.at[par], wf.at[rows_of(w)], rv.at[w]).start()

    @pl.when(high)
    def _():
        wf[...] = jnp.zeros_like(wf)

    def got(ref, sem):
        pltpu.make_async_copy(ref, ref, sem).wait()

    got(Y, ry.at[0])

    @pl.when(here_two)
    def _():
        pltpu.make_async_copy(Y, X.at[c], rx.at[c]).start()

    @pl.when(jnp.logical_not(here_two))
    def _():
        to_two.start()

    def core_x(b):
        return remote(X.at[b], X.at[b], sx.at[0, b], rx.at[b], core)

    def core_f(b):
        return remote(Fv.at[b], Fv.at[b], sf.at[0, b], rf.at[b], core)

    def member_x(b, e):
        return remote(X.at[b], X.at[b], sx.at[e, b], rx.at[b], (w, g * G + (m + e) % G))

    def member_f(b, e):
        return remote(Fv.at[b], Fv.at[b], sf.at[e, b], rf.at[b], (w, g * G + (m + e) % G))

    def cross_f(b):
        return remote(Fv.at[b], Fv.at[b], sy.at[b], rf.at[b], (two, c))

    crossing = jnp.logical_and(is_a, low)

    def take(b, onward):
        got(X.at[b], rx.at[b])

        if onward:

            @pl.when(crossing)
            def _():
                got(Fv.at[b], rf.at[b])
                cross_f(b).start()

        @pl.when(primary)
        def _():
            for e in range(1, G if onward else 1):
                member_x(b, e).start()
            core_x(b).start()

        @pl.when(high)
        def _():
            got(Fv.at[b], rf.at[b])

            @pl.when(primary)
            def _():
                for e in range(1, G if onward else 1):
                    member_f(b, e).start()
                core_f(b).start()

    half_rows = nc * R // 2

    def halves(ref, b, gap, value):
        ref[pl.ds(pl.multiple_of(b * BLK, BLK), BLK), :] = value[:BLK]
        ref[pl.ds(pl.multiple_of(b * BLK + gap, BLK), BLK), :] = value[BLK:]

    def project(b, a):
        at = pl.ds(pl.multiple_of(b * R, R), R)
        value = X[b].astype(F32)
        centred = value - jnp.mean(value, axis=-1, keepdims=True)
        inverse = lax.rsqrt(jnp.mean(centred * centred, axis=-1, keepdims=True) + EPS)
        normal = centred * inverse
        xh[at, :] = normal.astype(BF)
        n = (normal * vec[4:5, :] + vec[5:6, :]).astype(BF)
        qk = product(n, wqk[...])
        halves(k, b, half_rows, qk[:, d : 2 * d].astype(BF))
        if a is not None:
            halves(q, a, 2 * R, (qk[:, :d] + vq[1:2, 0:d]).astype(BF))

        @pl.when(low)
        def _():
            halves(v, b, half_rows, (product(n, wf[...]) + vq[2:3, 0:d]).astype(BF))

        @pl.when(high)
        def _():
            f = Fv[b]
            halves(v, b, half_rows, jnp.where(par == 0, f[:, :d], f[:, d:]))

    for t in range(nw):
        for e in range(2):
            own_pair = deal[(2 * (t % 2) + e) * G + m]
            for b in range(nc):
                seen = deal[b] <= own_pair if t < 2 else deal[b] >= own_pair
                at = b * BLK + (half_rows if t >= 2 else 0)
                bias[2 * t + e, :, at : at + BLK] = jnp.full(
                    (1, BLK), jnp.where(seen, 0.0, NEG), F32
                )
            if t >= 2:
                bias[2 * t + e, :, 0:half_rows] = jnp.zeros((1, half_rows), F32)
    take(g * G + m, True)
    loads[1].wait()
    for a in range(nw):
        got(small.at[a], rs.at[a])
        got(wqk.at[rows_of(a)], rw.at[a])

        @pl.when(low)
        def _():
            got(wf.at[rows_of(a)], rv.at[a])

    nb = 6 * d // 4
    for a in range(nw):
        piece = small[a].astype(F32)
        for row, src in ((0, 0), (1, 3), (2, 4), (4, 1), (5, 2), (6, 5)):
            at = src // 2
            value = piece[at : at + 1, (src % 2) * d : (src % 2 + 1) * d]
            vec[row : row + 1, a * d : (a + 1) * d] = value
        vq[0:1, a * nb : (a + 1) * nb] = piece[5:6, :nb]
    piece = small[w].astype(F32)
    vec[3:4, : 2 * d] = piece[3:4, :]
    vec[3:4, 2 * d :] = piece[4:5, :]
    vec[7:8, :] = jnp.zeros((1, width), F32)
    q_bias = vq[0:1, 0:d]
    for a in range(1, nw):
        q_bias = jnp.where(w == a, vq[0:1, a * d : (a + 1) * d], q_bias)
    f_bias = jnp.where(
        par == 0, vq[0:1, width : width + d], vq[0:1, width + d : width + 2 * d]
    )
    vq[1:2, 0:d] = q_bias
    vq[2:3, 0:d] = f_bias
    project(g * G + m, g)

    def own(i, carry):
        a = (g + i) % nw
        take(a * G + m, True)
        project(a * G + m, a)
        return carry

    lax.fori_loop(1, nw, own, 0)

    @pl.when(home_cot)
    def _():
        pltpu.make_async_copy(cot_h, cot_o.at[own_cot], rc.at[g]).start()

    @pl.when(jnp.logical_not(home_cot))
    def _():
        to_cot.start()

    ups = []
    for e in range(1, nw):
        to = (w + e) % nw
        src = wup_h.at[:, pl.ds(pl.multiple_of(to * width, BLK), width)]
        ups.append(remote(src, wup_o.at[rows_of(w)], su.at[e], ru.at[w], (to, c)))
    for r in ups:
        r.start()
    src = wup_h.at[:, pl.ds(pl.multiple_of(w * width, BLK), width)]
    pltpu.make_async_copy(src, wup_o.at[rows_of(w)], ru.at[w]).start()

    def others(i, carry):
        b = ((g + i % nw) % nw) * G + (m + 1 + i // nw) % G
        take(b, False)
        project(b, None)
        return carry

    lax.fori_loop(0, nw * (G - 1), others, 0)
    outs = [(X, X_o), (xh, xh_o), (k, k_o), (v, v_o)]
    outs = [pltpu.make_async_copy(a, b, out.at[i]) for i, (a, b) in enumerate(outs)]
    for copy in outs:
        copy.start()

    def cot_rows(a):
        return cot_o.at[pl.ds(pl.multiple_of(a * R, R), R)]

    og_two = 2 * par + two // 2
    spread_cot = [
        remote(cot_rows(og), cot_rows(og), sc.at[0], rc.at[og], (two, c)),
        remote(cot_rows(og), cot_rows(og), sc.at[1], rc.at[og], core),
        remote(cot_rows(og_two), cot_rows(og_two), sc.at[2], rc.at[og_two], core),
    ]
    got(cot_rows(og), rc.at[og])
    spread_cot[0].start()
    spread_cot[1].start()

    def attend_one(t, carry):
        at = pl.ds(pl.multiple_of(t * R, R), R)
        ot, lt = attend_tile(H, q[at, :], k, v, bias, 2 * t, 1 + t // 2)
        lse[t] = lt
        pt = product(ot, wout[...]).astype(BF)
        for e in range(2):
            to = (2 * (t % 2) + e) * R + (t // 2) * BLK
            to = pl.ds(pl.multiple_of(to, BLK), BLK)
            o[to, :] = ot[e * BLK : (e + 1) * BLK]
            part[to, :] = pt[e * BLK : (e + 1) * BLK]
        return carry

    lax.fori_loop(0, nw, attend_one, 0)

    got(cot_rows(og_two), rc.at[og_two])
    spread_cot[2].start()
    for copy in outs:
        copy.wait()
    for a in range(nw):
        got(wup_o.at[rows_of(a)], ru.at[a])

    for hi in range(2):
        a = 2 * (1 - par) + hi
        got(cot_rows(a), rc.at[a])

    for r in weights + ups + spread_cot + [to_y]:
        r.wait_send()
    for to, r in fresh:

        @pl.when(to < 2)
        def _():
            r.wait_send()

    @pl.when(jnp.logical_not(here))
    def _():
        to_one.wait_send()
        to_first.wait_send()

    @pl.when(jnp.logical_not(here_two))
    def _():
        to_two.wait_send()

    @pl.when(crossing)
    def _():
        for a in range(nw):
            cross_f(a * G + m).wait_send()

    @pl.when(jnp.logical_not(home_cot))
    def _():
        to_cot.wait_send()

    @pl.when(primary)
    def _():

        def sent(b, carry):
            core_x(b).wait_send()

            @pl.when(b % G == m)
            def _():
                for e in range(1, G):
                    member_x(b, e).wait_send()

            @pl.when(high)
            def _():
                core_f(b).wait_send()

                @pl.when(b % G == m)
                def _():
                    for e in range(1, G):
                        member_f(b, e).wait_send()

            return carry

        lax.fori_loop(0, nc, sent, 0)


def head(G, H, deal, vectors, x, first, wqkv, cot, wup, wout):
    nw = 4
    nc = nw * G
    R, width = x.shape
    d = width // nw
    N = nc * R
    dma = pltpu.SemaphoreType.DMA
    vm = pltpu.VMEM
    shape = jax.ShapeDtypeStruct
    operands = (deal,) + vectors + (x, first, wqkv, cot, wup, wout)
    return pl.pallas_call(
        functools.partial(head_kernel, G, H),
        name="head",
        out_shape=(
            shape((nc, R, width), BF),
            shape((N, width), BF),
            shape((N, d), BF),
            shape((N, d), BF),
            shape((width, width), BF),
            shape((nw * R, width), BF),
            shape((nw * R, d), BF),
            shape((nw * R, d), BF),
            shape((nw, 8, R), F32),
            shape((nw * R, width), BF),
            shape((width, 2 * d), BF),
            shape((width, d), BF),
            shape((8, width), F32),
        ),
        in_specs=[pl.BlockSpec(memory_space=pltpu.SMEM)] + [VM] * len(vectors) + [ANY] * 6,
        out_specs=[ANY] * 6 + [VM] * 7,
        scratch_shapes=[
            vm((nc, R, width), BF), vm((nc, R, 2 * d), BF), vm((N, width), BF), vm((N, d), BF),
            vm((N, d), BF), vm((nw, 8, 2 * d), BF), vm((8, 6 * d), F32),
            vm((2 * nw, 1, N), F32), vm(wout.shape, BF), vm(wqkv.shape, BF),
            vm((nw, d, 2 * d), BF), vm((2, d, d), BF), vm((R, width), BF),
            vm((8, 2 * d), F32), vm((8, 2 * d), BF),
            dma((nc,)), dma((nc,)), dma((nw,)), dma((nw,)), dma((nw,)), dma((nw,)), dma((nw,)),
            dma((6,)), dma((G, nc)), dma((G, nc)), dma((nw, 3)), dma((nw,)), dma((nw,)),
            dma((2,)), dma((4,)), dma((1,)), dma((nc,)),
        ],
        compiler_params=pltpu.CompilerParams(
            collective_id=0, has_side_effects=True, vmem_limit_bytes=56 << 20
        ),
        cost_estimate=pl.CostEstimate(
            flops=14 << 30, bytes_accessed=40 << 20, transcendentals=6 << 20
        ),
    )(*operands)


EARLY = 3


def ring_place(nc):
    w, c = lax.axis_index("wt"), lax.axis_index("ctx")
    odd = c % 2
    pos = (c // 2) * (1 - odd) + (nc - 1 - c // 2) * odd

    def ctx_at(p):
        p = (p + nc) % nc
        h = p // (nc // 2)
        return 2 * p * (1 - h) + (2 * (nc - 1 - p) + 1) * h

    return pos, (w, ctx_at(pos + 1)), (w, ctx_at(pos - 1))


class Ring:
    def __init__(self, nc, pos, right, left, seg, chains, A, slots, out, ss, sr):
        self.nc, self.pos, self.right, self.left, self.seg = nc, pos, right, left, seg
        self.chains, self.A, self.slots, self.out, self.ss, self.sr = chains, A, slots, out, ss, sr
        self.steps = 2 * (nc - 1)
        self.cut = A.shape[1] // chains

    def at(self, half, j):
        j = (j + 2 * self.nc) % self.nc
        return pl.ds(pl.multiple_of((half * self.nc + j) * self.seg, 16), self.seg)

    def cols(self, i):
        if self.chains == 1:
            return pl.ds(0, self.cut)
        return pl.ds(pl.multiple_of(i * self.cut, BLK), self.cut)

    def reduce_copies(self, i, s):
        k = self.cols(i)
        return [
            remote(
                self.A.at[self.at(h, j), k],
                self.slots.at[h, s, :, k],
                self.ss.at[h, i, s],
                self.sr.at[h, i, s],
                to,
            )
            for h, j, to in ((0, self.pos - s, self.right), (1, self.pos + s, self.left))
        ]

    def gather_copies(self, i, s):
        k = self.cols(i)
        t = s - (self.nc - 1)
        return [
            remote(
                self.out.at[self.at(h, j), k],
                self.out.at[self.at(h, j), k],
                self.ss.at[h, i, s],
                self.sr.at[h, i, s],
                to,
            )
            for h, j, to in ((0, self.pos + 1 - t, self.right), (1, self.pos - 1 + t, self.left))
        ]

    def send(self, i, s, gathering=False):
        for r in (self.gather_copies if gathering else self.reduce_copies)(i, s):
            r.start()

    start = 0

    def begin(self, start=0):
        self.start = start
        for i in range(self.chains):
            self.send(i, start)

    def add(self, i, s):
        k = self.cols(i)
        for h, j in ((0, self.pos - s - 1), (1, self.pos + s + 1)):
            at = self.at(h, j)
            slot = self.slots.at[h, s, :, k]
            pltpu.make_async_copy(slot, slot, self.sr.at[h, i, s]).wait()
            value = self.A[at, k].astype(F32) + self.slots[h, s, :, k].astype(F32)
            self.A[at, k] = value.astype(BF)

    def early(self, s, steps):
        for i in range(self.chains):
            self.add(i, s)

        @pl.when(s < steps - 1)
        def _():
            for i in range(self.chains):
                self.send(i, s + 1)

    def early_drain(self, steps):
        for s in range(steps):
            for i in range(self.chains):
                for r in self.reduce_copies(i, s):
                    r.wait_send()

    def keep(self, i):
        k = self.cols(i)
        for h, j in ((0, self.pos + 1), (1, self.pos - 1)):
            self.out[self.at(h, j), k] = self.A[self.at(h, j), k]

    def arrive(self, i, s):
        t = s - (self.nc - 1)
        for h, j in ((0, self.pos - t), (1, self.pos + t)):
            at = self.out.at[self.at(h, j), self.cols(i)]
            pltpu.make_async_copy(at, at, self.sr.at[h, i, s]).wait()

    def step(self, s):
        for i in range(self.chains):
            self.turn(i, s)

    def turn(self, i, s):
        last = self.nc - 2
        if isinstance(s, int):
            when = lambda cond: (lambda body: body() if cond else None)
            both = lambda a, b: a and b
        else:
            when, both = pl.when, jnp.logical_and

        @when(s < last)
        def _():
            self.add(i, s)
            self.send(i, s + 1)

        @when(s == last)
        def _():
            self.add(i, last)
            self.keep(i)
            self.send(i, last + 1, True)

        @when(both(s > last, s < self.steps))
        def _():
            self.arrive(i, s)

        @when(both(s > last, s < self.steps - 1))
        def _():
            self.send(i, s + 1, True)

    def drain(self):
        for gathering in (False, True):

            def one(t, carry):
                i, s = t % self.chains, t // self.chains
                for r in (self.gather_copies if gathering else self.reduce_copies)(i, s):
                    r.wait_send()
                return carry

            half = self.steps * self.chains // 2
            low = half if gathering else self.start * self.chains
            lax.fori_loop(low, half * (1 + gathering), one, 0)


class SplitRing(Ring):
    def __init__(self, nc, pos, right, left, seg, chains, A, slots, out, ss, sr, own, sems):
        super().__init__(nc, pos, right, left, seg, chains, A, slots, out, ss, sr)
        self.turns = nc - 1
        self.w, self.c = own
        self.s_ex, self.r_ex, self.s_hop, self.r_hop = sems
        self.group = nc // 2
        self.reach = (nc // 2, nc // 2 - 1)

    def turn(self, i, s):
        last = self.nc - 2
        if isinstance(s, int):
            when = lambda cond: (lambda body: body() if cond else None)
        else:
            when = pl.when

        @when(s <= last)
        def _():
            self.add(i, s)

        @when(s < last)
        def _():
            self.send(i, s + 1)

    def parts(self):
        for h, j in ((0, self.pos + 1), (1, self.pos - 1)):
            j = (j + self.nc) % self.nc
            to = 2 * h + j // self.group
            src = self.A.at[self.at(h, j)]
            dst = self.out.at[j % self.group, self.w]
            yield h, to, src, dst

    def exchange(self):
        for h, to, src, dst in self.parts():
            local = pltpu.make_async_copy(src, dst, self.r_ex.at[self.w])
            far = remote(src, dst, self.s_ex.at[h], self.r_ex.at[self.w], (to, self.c))

            @pl.when(to == self.w)
            def _():
                local.start()

            @pl.when(to != self.w)
            def _():
                far.start()

    def held(self, position):
        j = (position + 1 - 2 * (self.w // 2) + 2 * self.nc) % self.nc
        return j // self.group == self.w % 2, j % self.group

    def hop_copy(self, way, h, j):
        ref = self.out.at[j]
        to = (self.right, self.left)[way]
        return remote(ref, ref, self.s_hop.at[way, h], self.r_hop.at[way, h], to)

    def spread(self):
        have, j = self.held(self.pos)

        @pl.when(have)
        def _():
            for a in range(4):
                ref = self.out.at[j, a]
                pltpu.make_async_copy(ref, ref, self.r_ex.at[a]).wait()
            for way in range(2):
                self.hop_copy(way, 1, j).start()

    def hop(self, h):
        for way in range(2):
            if h > self.reach[way]:
                continue
            have, j = self.held(self.pos - h if way == 0 else self.pos + h)

            @pl.when(have)
            def _():
                ref = self.out.at[j]
                pltpu.make_async_copy(ref, ref, self.r_hop.at[way, h]).wait()
                if h < self.reach[way]:
                    self.hop_copy(way, h + 1, j).start()

    def drain(self):
        def one(t, carry):
            i, s = t % self.chains, t // self.chains
            for r in self.reduce_copies(i, s):
                r.wait_send()
            return carry

        lax.fori_loop(self.start * self.chains, self.turns * self.chains, one, 0)
        for h, to, src, dst in self.parts():

            @pl.when(to != self.w)
            def _():
                remote(src, dst, self.s_ex.at[h], self.r_ex.at[self.w], (to, self.c)).wait_send()

        for way in range(2):
            for h in range(self.reach[way]):
                have, j = self.held(self.pos - h if way == 0 else self.pos + h)

                @pl.when(have)
                def _():
                    self.hop_copy(way, h + 1, j).wait_send()


def tail_kernel(
    G, H, seg_o, seg_u, seg_b,
    deal, q_h, k_h, v_h, o_h, do_h, lse_h, xh_h, X_h, wqk_h, wf_h, vec_h, dmid_h,
    up_h, down_h, gout_h, vsums, mlp_h, mid_h,
    layer_out, tokens_out, first_out, up_out, down_out, gout_out, qkv_out, rows_out,
    q, k, v, o, do, lse, lift, xh, X, wqk, wf, vec, dmid,
    kt, dk, dv, dqk, dvb, D, b1, ab, b2, st, b3, tot, tb, tr,
    O, slots_o, res_o, A, slots_a, res_a, U, slots_u, res_u, gq, slots_b, res_b, gain_t, shift_t, sums_t, line, f1, fs, fr,
    mlp, mid, lb, ly, lr, sl, rl, sL, rL, s1, r1, s2, r2, s3, r3, sT, rT, sso, sro, ssa, sra, ssu, sru, seu, reu, shu, rhu, ssb, srb, seb, reb, shb, rhb, sf1, rf1, sf2, rf2, ld,
):
    w = lax.axis_index("wt")
    c = lax.axis_index("ctx")
    nw = 4
    nc = nw * G
    g = c // G
    m = c % G
    par = w % 2
    hi = w // 2
    core = (w + 1 - 2 * par, c)
    other = ((w + 2) % nw, c)
    R, width = dmid.shape
    d = width // nw
    N = xh.shape[0]
    pos, right, left = ring_place(nc)
    loads = [
        (up_h, U),
        (down_h, A),
        (gout_h, O.at[pl.ds(0, d)]),
        (k_h, k), (v_h, v), (q_h, q), (o_h, o), (do_h, do), (lse_h, lse),
        (xh_h, xh), (X_h, X), (wqk_h, wqk), (wf_h, wf), (vec_h, vec), (dmid_h, dmid), (mid_h, mid), (mlp_h, mlp),
    ]
    loads = [pltpu.make_async_copy(a, b, ld.at[i]) for i, (a, b) in enumerate(loads)]
    for copy in loads:
        copy.start()
    peers = [
        ((w + a) % nw, ((g + e) % nw) * G + m) for a in range(nw) for e in range(nw) if a or e
    ]
    peers += [(w, g * G + (m + e) % G) for e in range(1, G)]
    greet(peers + [right, left])
    ring_o = Ring(nc, pos, right, left, seg_o, 1, O, slots_o, res_o, sso, sro)
    ring_a = Ring(nc, pos, right, left, seg_u, 2, A, slots_a, res_a, ssa, sra)
    ring_u = SplitRing(
        nc, pos, right, left, seg_u, 2, U, slots_u, res_u, ssu, sru, (w, c), (seu, reu, shu, rhu)
    )
    ring_b = SplitRing(
        nc, pos, right, left, seg_b, 1, gq, slots_b, res_b, ssb, srb, (w, c), (seb, reb, shb, rhb)
    )
    for copy in loads[:3]:
        copy.wait()
    foot = O.shape[0] - d
    line_a = jnp.concatenate([vsums[0:1, :], jnp.zeros((15, width), F32)], axis=0)
    O[d + 16 :, :] = jnp.zeros((foot - 16, width), BF)
    share = vsums[1:5, 0:d]
    for a in range(1, nw):
        share = jnp.where(w == a, vsums[1:5, a * d : (a + 1) * d], share)
    pack = jnp.concatenate([share[a : a + 1, :] for a in range(4)], axis=1)
    pack = jnp.concatenate([jnp.zeros((1, width), F32), pack, jnp.zeros((14, width), F32)], axis=0)
    O[d : d + 16, :] = (line_a + pack).astype(BF)
    ring_u.begin(EARLY)
    ring_a.begin(EARLY)
    ring_o.begin()
    for copy in loads[3:9] + loads[15:]:
        copy.wait()
    seq = 2 * (g % 2) + g // 2
    og = 2 * par + hi
    home = (seq, og * G + m)
    home_self = jnp.logical_and(og == g, w == seq)
    shares = []
    for e in range(1, nw):
        to = (w + e) % nw
        src = mlp.at[pl.ds(pl.multiple_of((2 * (to % 2) + to // 2) * R, R), R)]
        r = remote(src, lb.at[w], sl.at[e], rl.at[w], (to, c))
        r.start()
        shares.append(r)

    flip_rows(k, kt)
    dk[...] = jnp.zeros_like(dk)
    dv[...] = jnp.zeros_like(dv)
    dqk[...] = jnp.zeros_like(dqk)
    wide = H * HEAD_DIM

    def poll(n):
        for r in range(4):

            @pl.when(n % 4 == r)
            def _():
                (ring_a if r % 2 else ring_u).turn(r // 2, EARLY + n // 4)
                if r == 3:
                    ring_o.turn(0, n // 4)

    pairs = lax.broadcasted_iota(jnp.int32, (1, 2 * BLK), 1) < BLK
    for t in range(nw):
        mine = [deal[(2 * (t % 2) + e) * G + m] for e in range(2)]
        for b in range(nc):
            unseen = [
                jnp.where(deal[b] <= a if t < 2 else deal[b] >= a, 0.0, -NEG) for a in mine
            ]
            at = b if t < 2 else nc + b
            lift[t, at : at + 1, :] = jnp.where(pairs, unseen[0], unseen[1])
        if t >= 2:
            lift[t, 0:nc, :] = jnp.zeros((nc, 2 * BLK), F32)

    def tile(t, carry):
        rows = []
        for e in range(2):
            at = (2 * (t % 2) + e) * R + (t // 2) * BLK
            rows.append(pl.ds(pl.multiple_of(at, BLK), BLK))
        pick = lambda ref: jnp.concatenate([ref[rows[0], :], ref[rows[1], :]], axis=0)
        mine = pl.ds(pl.multiple_of(t * R, R), R)

        def polls_at(j):
            n = 2 * (t + t // 3 + j)
            poll(n)
            poll(n + 1)

        dqt = attend_back_tile(
            H, q[mine, :], pick(do), pick(o), lse[t], k, v, kt, dk, dv, lift, t, 1 + t // 2,
            polls_at,
        )
        dq = jnp.transpose(dqt).astype(BF)
        for e in range(2):
            at = ((2 * (t % 2) + e) * G + m) * R + (t // 2) * BLK
            at = pl.ds(pl.multiple_of(at, BLK), BLK)
            dqk[at, 0:wide] = dq[e * BLK : (e + 1) * BLK]
        return carry

    lax.fori_loop(0, nw, tile, 0)

    def deal_back(b, carry):
        for e in range(2):
            src = pl.ds(pl.multiple_of(b * BLK + e * (N // 2), BLK), BLK)
            to = pl.ds(pl.multiple_of(b * R + e * BLK, BLK), BLK)
            dqk[to, wide : 2 * wide] = dk[src, :].astype(BF)
            dvb[to, :] = dv[src, :].astype(BF)
        return carry

    lax.fori_loop(0, nc, deal_back, 0)
    polls = 12
    for copy in loads[9:15]:
        copy.wait()

    layer = mid[...] + vec[6:7, :] + mlp[pl.ds(pl.multiple_of(og * R, R), R), :].astype(F32)
    for e in range(1, nw):
        src = (w + e) % nw
        pltpu.make_async_copy(lb.at[src], lb.at[src], rl.at[src]).wait()
        layer = layer + lb[src].astype(F32)
    ly[...] = layer.astype(BF)
    layer_back = remote(ly, lr, sL.at[0], rL.at[0], home)
    layer_stay = pltpu.make_async_copy(ly, lr, rL.at[0])

    @pl.when(home_self)
    def _():
        layer_stay.start()

    @pl.when(jnp.logical_not(home_self))
    def _():
        layer_back.start()

    upper = w >= 2
    first_copies = []
    for e in range(1, G):
        mm = (m + e) % G
        for gp in range(nw):
            src = dvb.at[pl.ds(pl.multiple_of((gp * G + mm) * R, R), R)]
            first_copies.append(
                remote(src, f1.at[m, gp], sf1.at[e, gp], rf1.at[m, gp], (w, g * G + mm))
            )

    @pl.when(upper)
    def _():
        for r in first_copies:
            r.start()

    tile_d = 128
    ones = jnp.ones((N, BLK), BF)
    row_qk = product_left(ones, dqk[...])[0:1, :]
    row_f = product_left(ones, dvb[...])[0:1, :]
    sum_qk = product_left(dqk[...], ones)
    sum_f = product_left(dvb[...], ones)
    gain_t[...] = jnp.transpose(jnp.broadcast_to(vec[4:5, :], (BLK, width)))
    shift_t[...] = jnp.transpose(jnp.broadcast_to(vec[5:6, :], (BLK, width)))
    lane = lax.broadcasted_iota(jnp.int32, (d, BLK), 1)
    edge = gq.shape[1] - BLK
    for a in range(nw):
        sums_t[a * d : (a + 1) * d, :] = jnp.where(
            lane == 66, sum_qk[:wide], jnp.where(lane == 67, sum_qk[wide:], sum_f)
        )
    lane = lax.broadcasted_iota(jnp.int32, (tile_d, BLK), 1)

    def grads(i, carry):
        at = pl.ds(pl.multiple_of(i * tile_d, tile_d), tile_d)
        x_qk = product_left(xh[:, at], dqk[...])
        x_f = product_left(xh[:, at], dvb[...])
        w_qk = wqk[at, :].astype(F32)
        w_f = wf[at, :].astype(F32)
        add = lambda a, b: jnp.sum(a, axis=1, keepdims=True) + jnp.sum(b, axis=1, keepdims=True)
        for_gain = add(w_qk * x_qk, w_f * x_f)
        for_shift = add(w_qk * row_qk, w_f * row_f)
        gain = gain_t[at, 0:1]
        shift = shift_t[at, 0:1]
        gq[at, 0 : 2 * wide] = (gain * x_qk + shift * row_qk).astype(BF)
        gq[at, 2 * wide : 3 * wide] = (gain * x_f + shift * row_f).astype(BF)
        ends = gq[at, edge:].astype(F32)
        ends = jnp.where(lane == 64, for_gain, jnp.where(lane == 65, for_shift, ends))
        ends = jnp.where(lane > 65, sums_t[at, :], ends)
        gq[at, edge:] = jnp.where(lane < 69, ends, 0.0).astype(BF)
        poll(polls + i)
        return carry

    lax.fori_loop(0, width // tile_d, grads, 0)
    polls += width // tile_d
    ring_u.exchange()
    ring_b.begin()

    def block(i, carry):
        phase = i // (2 * G)
        jj = (hi + 1 - (i // G) % 2 + 2) % 2
        mm = (m + 1 + i % G) % G
        parity = (1 - par) * (1 - phase) + par * phase
        b = (2 * parity + jj) * G + mm
        at = pl.ds(pl.multiple_of(b * R, R), R)
        dn = product_right(dqk[at, :], wqk[...]) + product_right(dvb[at, :], wf[...])
        D[b] = dn.astype(BF)

        @pl.when(phase == 0)
        def _():
            slot = jj * G + mm
            remote(D.at[b], b1.at[slot], s1.at[slot], r1.at[slot], core).start()

        poll(polls + i)

        @pl.when(i % 4 == 3)
        def _():
            ring_b.step(i // 4)

        return carry

    lax.fori_loop(0, nc, block, 0)
    polls += nc
    done_b = nc // 4

    order = list(range(1, G)) + [0]

    def chip_sum(jj, mm):
        slot = jj * G + mm
        pltpu.make_async_copy(b1.at[slot], b1.at[slot], r1.at[slot]).wait()
        return D[(2 * par + jj) * G + mm].astype(F32) + b1[slot].astype(F32)

    seconds = []
    for e in order:
        mm = (m + e) % G
        ab[mm] = chip_sum(1 - hi, mm).astype(BF)
        r = remote(ab.at[mm], b2.at[mm], s2.at[mm], r2.at[mm], other)
        r.start()
        seconds.append(r)
    thirds = []

    def sum_chips(which):
        for e in which:
            mm = (m + e) % G
            total = chip_sum(hi, mm)
            pltpu.make_async_copy(b2.at[mm], b2.at[mm], r2.at[mm]).wait()
            total = total + b2[mm].astype(F32)
            if e:
                st[mm] = total.astype(BF)
                r = remote(st.at[mm], b3.at[m], s3.at[mm], r3.at[m], (w, g * G + mm))
                r.start()
                thirds.append(r)
            else:
                tot[...] = total

    def sum_first():
        @pl.when(upper)
        def _():
            for gp in range(nw):
                total = dvb[pl.ds(pl.multiple_of((gp * G + m) * R, R), R), :].astype(F32)
                for e in range(1, G):
                    mm = (m + e) % G
                    pltpu.make_async_copy(f1.at[mm, gp], f1.at[mm, gp], rf1.at[mm, gp]).wait()
                    total = total + f1[mm, gp].astype(F32)
                fs[gp] = total.astype(BF)
                own = jnp.logical_and(w == seq, g == gp)

                @pl.when(own)
                def _():
                    pltpu.make_async_copy(fs.at[gp], fr.at[par], rf2.at[par]).start()

                @pl.when(jnp.logical_not(own))
                def _():
                    remote(
                        fs.at[gp], fr.at[par], sf2.at[gp], rf2.at[par], (seq, gp * G + m)
                    ).start()

    back = remote(tb, tr, sT.at[0], rT.at[0], home)
    stay = pltpu.make_async_copy(tb, tr, rT.at[0])

    def norm_back():
        total = tot[...]
        for e in range(1, G):
            mm = (m + e) % G
            pltpu.make_async_copy(b3.at[mm], b3.at[mm], r3.at[mm]).wait()
            total = total + b3[mm].astype(F32)
        value = X[og * G + m].astype(F32)
        centred = value - jnp.mean(value, axis=-1, keepdims=True)
        inverse = lax.rsqrt(jnp.mean(centred * centred, axis=-1, keepdims=True) + EPS)
        normal = centred * inverse
        dx = total * vec[4:5, :]
        dx = dx - jnp.mean(dx, axis=-1, keepdims=True) - normal * jnp.mean(
            dx * normal, axis=-1, keepdims=True
        )
        tb[...] = (dmid[...].astype(F32) + inverse * dx).astype(BF)

        @pl.when(home_self)
        def _():
            stay.start()

        @pl.when(jnp.logical_not(home_self))
        def _():
            back.start()

    turns = []
    extras = [ring_u.spread]
    extras += [functools.partial(ring_u.hop, h) for h in range(1, ring_u.reach[0] + 1)]
    small = [functools.partial(ring_o.turn, 0, a) for a in range((polls + 0) // 4, ring_o.steps)]
    for n in range(polls, 4 * (ring_a.steps - EARLY)):
        r, s = n % 4, EARLY + n // 4
        if r % 2 and s < ring_a.steps:
            turns.append(functools.partial(ring_a.turn, r // 2, s))
        if (r == 0 or n == polls) and extras:
            turns.append(extras.pop(0))
    turns += extras

    def others():
        if small:
            small.pop(0)()
        for _ in range(2):
            if turns:
                turns.pop(0)()

    def finish():
        while turns or small:
            others()
        down_out[...] = res_a[0:width, :]
        gout_out[...] = res_o[0:d, :]
        for j in range(ring_u.group):
            rows = slice(j * seg_u, (j + 1) * seg_u)
            for a in range(nw):
                up_out[rows, a * width : (a + 1) * width] = res_u[j, a]

    for at_b in range(done_b, ring_b.turns):
        ring_b.step(at_b)
        others()
        if at_b == done_b + 2:
            sum_first()
        if at_b == 4:
            sum_chips(order[:-1])
        if at_b == 5:
            sum_chips(order[-1:])
    ring_b.exchange()
    others()
    ring_b.spread()
    others()
    for h in range(1, ring_b.reach[0] + 1):
        ring_b.hop(h)
        others()
        if h == 2:
            norm_back()
            finish()
    while turns or small:
        others()

    for j in range(ring_b.group):
        rows = slice(j * seg_b, (j + 1) * seg_b)
        for a in range(nw):
            for part in range(2):
                at = part * width + a * d
                qkv_out[rows, at : at + d] = res_b[j, a, :, part * d : (part + 1) * d]
            if a < 2:
                at = 2 * width + a * d
                qkv_out[rows, at : at + d] = res_b[j, a, :, 2 * d : 3 * d]
            at = a * d + j * seg_b
            sums_t[at : at + seg_b, :] = res_b[j, a, :, edge:].astype(F32)
    ends = jnp.transpose(sums_t[...])
    nb = 6 * d // 4
    line[:, 0:width] = ends[66:67, :]
    line[:, width : width + 2 * d] = ends[68:69, : 2 * d]
    share = line[:, 0:nb]
    for a in range(1, nw):
        share = jnp.where(w == a, line[:, a * nb : (a + 1) * nb], share)
    rows_out[...] = jnp.zeros_like(rows_out)
    rows_out[0:2, :] = res_o[d : d + 16, :].astype(F32)[0:2]
    for row in range(2):
        total = ends[64 + row : 65 + row, 0:d]
        for a in range(1, nw):
            total = total + ends[64 + row : 65 + row, a * d : (a + 1) * d]
        rows_out[2:3, row * d : (row + 1) * d] = total
    rows_out[3:4, 0:nb] = share
    pltpu.make_async_copy(tr, tr, rT.at[0]).wait()
    tokens_out[...] = tr[...]
    for u in range(2):
        pltpu.make_async_copy(fr.at[u], fr.at[u], rf2.at[u]).wait()
        first_out[:, u * d : (u + 1) * d] = fr[u]

    pltpu.make_async_copy(lr, lr, rL.at[0]).wait()
    layer_out[...] = lr[...]
    ring_o.drain()
    ring_a.drain()
    ring_u.drain()
    ring_b.drain()
    for r in seconds + thirds + shares:
        r.wait_send()

    @pl.when(jnp.logical_not(home_self))
    def _():
        back.wait_send()
        layer_back.wait_send()

    @pl.when(upper)
    def _():
        for r in first_copies:
            r.wait_send()
        for gp in range(nw):

            @pl.when(jnp.logical_not(jnp.logical_and(w == seq, g == gp)))
            def _():
                remote(
                    fs.at[gp], fr.at[par], sf2.at[gp], rf2.at[par], (seq, gp * G + m)
                ).wait_send()

    def drain(i, carry):
        jj = (hi + 1 - (i // G) % 2 + 2) % 2
        mm = (m + 1 + i % G) % G
        slot = jj * G + mm
        b = (2 * (1 - par) + jj) * G + mm
        remote(D.at[b], b1.at[slot], s1.at[slot], r1.at[slot], core).wait_send()
        return carry

    lax.fori_loop(0, 2 * G, drain, 0)


def tail(
    G, H, deal, q, k, v, o, do, lse, xh, X, wqk, wf, vec, dmid, up, down, gout, vsums, mlp, mid
):
    nw = 4
    nc = nw * G
    R, width = dmid.shape
    d = width // nw
    N = xh.shape[0]
    wide = H * HEAD_DIM
    seg_o = -(-(d + 16) // (2 * nc * 16)) * 16
    seg_u = seg_b = width // (2 * nc)
    cols = 5 * BLK
    dma = pltpu.SemaphoreType.DMA
    vm = pltpu.VMEM
    steps = 2 * (nc - 1)
    operands = (
        deal, q, k, v, o, do, lse, xh, X, wqk, wf, vec, dmid, up, down, gout, vsums, mlp, mid
    )
    return pl.pallas_call(
        functools.partial(tail_kernel, G, H, seg_o, seg_u, seg_b),
        name="tail",
        out_shape=(
            jax.ShapeDtypeStruct((R, width), BF),
            jax.ShapeDtypeStruct((R, width), BF),
            jax.ShapeDtypeStruct((R, 2 * d), BF),
            jax.ShapeDtypeStruct((d, nw * width), BF),
            jax.ShapeDtypeStruct((width, width), BF),
            jax.ShapeDtypeStruct((d, width), BF),
            jax.ShapeDtypeStruct((d, 2 * width + 2 * d), BF),
            jax.ShapeDtypeStruct((8, width), F32),
        ),
        in_specs=[pl.BlockSpec(memory_space=pltpu.SMEM)] + [ANY] * (len(operands) - 4) + [VM] + [ANY] * 2,
        out_specs=[VM] * 8,
        scratch_shapes=[vm(a.shape, a.dtype) for a in operands[1:7]]
        + [vm((nw, 2 * nc, R), F32)]
        + [vm(a.shape, a.dtype) for a in operands[7:13]]
        + [
            vm((wide, N), BF), vm((N, wide), F32), vm((N, wide), F32), vm((N, 2 * wide), BF),
            vm((N, wide), BF), vm((nc, R, width), BF), vm((2 * G, R, width), BF),
            vm((G, R, width), BF), vm((G, R, width), BF), vm((G, R, width), BF),
            vm((G, R, width), BF), vm((R, width), F32), vm((R, width), BF), vm((R, width), BF),
            vm((2 * nc * seg_o, width), BF), vm((2, nc - 1, seg_o, width), BF),
            vm((2 * nc * seg_o, width), BF),
            vm((width, width), BF), vm((2, nc - 1, seg_u, width), BF), vm((width, width), BF),
            vm((width, width), BF), vm((2, nc - 1, seg_u, width), BF),
            vm((nc // 2, nw, seg_u, width), BF),
            vm((width, cols), BF), vm((2, nc - 1, seg_b, cols), BF),
            vm((nc // 2, nw, seg_b, cols), BF),
            vm((width, BLK), F32), vm((width, BLK), F32), vm((width, BLK), F32),
            vm((1, 6 * d), F32),
            vm((G, nw, R, d), BF), vm((nw, R, d), BF), vm((2, R, d), BF),
            vm((nw * R, width), BF), vm((R, width), F32), vm((nw, R, width), BF),
            vm((R, width), BF), vm((R, width), BF), dma((nw,)), dma((nw,)), dma((1,)), dma((1,)),
            dma((2 * G,)), dma((2 * G,)), dma((G,)), dma((G,)), dma((G,)), dma((G,)),
            dma((1,)), dma((1,)), dma((2, 1, steps)), dma((2, 1, steps)),
            dma((2, 2, steps)), dma((2, 2, steps)),
        ]
        + [
            dma(a)
            for chains in (2, 1)
            for a in (
                (2, chains, nc - 1), (2, chains, nc - 1), (2,), (nw,), (2, nc // 2 + 1),
                (2, nc // 2 + 1),
            )
        ]
        + [
            dma((G, nw)), dma((G, nw)),
            dma((nw,)), dma((2,)), dma((len(operands),)),
        ],
        compiler_params=pltpu.CompilerParams(
            collective_id=2, has_side_effects=True, vmem_limit_bytes=63 << 20
        ),
        cost_estimate=pl.CostEstimate(
            flops=40 << 30, bytes_accessed=60 << 20, transcendentals=6 << 20
        ),
    )(*operands)


def on_device(
    nw,
    nc,
    tokens,
    first_values,
    cotangent,
    deal,
    w_qkv,
    bias_qv,
    w_out,
    bias_out,
    gain_one,
    shift_one,
    gain_two,
    shift_two,
    w_up,
    bias_up,
    w_down,
    bias_down,
):
    G = nc // nw
    w = lax.axis_index("wt")
    c = lax.axis_index("ctx")
    m = c % G
    rows, width = tokens.shape[1:]
    d = width // nw
    H = HEADS // nw
    both = ("wt", "ctx")
    seq = lambda g: 2 * (g % 2) + g // 2
    swap = [
        (a * nc + g * G + e, seq(g) * nc + a * G + e)
        for a in range(nw)
        for g in range(nw)
        for e in range(G)
    ]
    ring = [[(a, (a + k) % nw) for a in range(nw)] for k in range(nw)]

    def exchange(pieces):
        out = jnp.zeros_like(pieces)
        mine = lax.dynamic_index_in_dim(pieces, w, 0, keepdims=True)
        out = lax.dynamic_update_slice_in_dim(out, mine, w, 0)
        for k in range(1, nw):
            piece = lax.dynamic_index_in_dim(pieces, (w + k) % nw, 0, keepdims=True)
            got = lax.ppermute(piece, "wt", ring[k])
            out = lax.dynamic_update_slice_in_dim(out, got, (w + nw - k) % nw, 0)
        return out

    qk = w_qkv[:, : 2 * width].reshape(d, 2, nw, d).transpose(2, 0, 1, 3).reshape(nw, d, 2 * d)
    wf = w_qkv[:, 2 * width :].reshape(d, 2, d).transpose(1, 0, 2)
    nb = bias_qv.shape[0]
    ids = dealt_blocks(deal)
    qpos = jnp.arange(nw, dtype=jnp.int32) * G + m
    qid = jnp.take(ids.reshape(nc, 2), qpos, axis=0)
    hidden = (ids[None, None, :] > qid[:, :, None]).astype(F32) * -NEG
    bias = jnp.repeat(-hidden.reshape(2 * nw, 2 * nc), BLK, axis=1)[:, None, :]
    lift = jnp.repeat(hidden.transpose(0, 2, 1), BLK, axis=2)

    def mine(vector):
        return lax.dynamic_slice_in_dim(vector, w * d, d)

    if nc <= 8:
        vectors = (
            bias_out, gain_one, shift_one, gain_two, shift_two, bias_down, bias_up, bias_qv
        )
        X, xhat, k, v, Wup, cot, q, o, lse, part, Wqk, Wf, vec = head(
            G, H, deal, vectors, tokens[0], first_values[0], w_qkv, cotangent[0], w_up, w_out
        )
        mlp, mid_own, d_mid, d_o, g_up, g_down, g_out, vsums = middle(
            G, True, part, X, cot, o, Wup, w_down, w_out, vec
        )
        layer, grad_tokens, grad_first, s_up, s_down, s_out, s_qkv, sums = tail(
            G, H, deal, q, k, v, o, d_o, lse, xhat, X, Wqk, Wf, vec,
            d_mid, g_up, g_down, g_out, vsums, mlp, mid_own,
        )
        return (
            layer[None],
            grad_tokens.astype(F32)[None],
            grad_first.astype(F32)[None],
            s_qkv.astype(F32),
            sums[3, :nb],
            s_out.astype(F32),
            sums[1, d : 2 * d],
            sums[2, :d],
            sums[2, d : 2 * d],
            sums[1, 2 * d : 3 * d],
            sums[1, 3 * d :],
            s_up.astype(F32),
            sums[0],
            s_down.astype(F32),
            sums[1, :d],
        )

    small = jnp.concatenate(
        [bias_qv, bias_out, gain_one, shift_one, gain_two, shift_two, bias_down]
    )
    lanes = 16 * BLK
    small = jnp.concatenate([small, jnp.zeros((lanes - small.shape[0],), BF)]).reshape(16, BLK)
    X, Fv, WQK, WF, SM = gather(nw, G, tokens[0], first_values[0], qk, wf, small)
    X = X.reshape(nc * rows, width)
    Wqk = WQK.reshape(width, 2 * d)
    low = w < 2
    Wf = jnp.where(low, WF.reshape(width, d), jnp.zeros((width, d), BF))
    SM = SM.reshape(nw, lanes).astype(F32)
    qv_vector = SM[:, :nb].reshape(-1)
    vectors = [SM[:, nb + a * d : nb + (a + 1) * d].reshape(-1) for a in range(6)]
    out_vector, gain_a, shift_a, gain_b, shift_b, down_vector = vectors

    x32 = X.astype(F32)
    mean = jnp.mean(x32, axis=-1, keepdims=True)
    centred = x32 - mean
    inverse = lax.rsqrt(jnp.mean(centred * centred, axis=-1, keepdims=True) + EPS)
    n1 = (centred * inverse * gain_a + shift_a).astype(BF)
    pqk = product(n1, Wqk)
    q_bias = lax.dynamic_slice_in_dim(qv_vector, w * d, d)
    f_bias = lax.dynamic_slice_in_dim(qv_vector, width + (w % 2) * d, d)
    q = (pqk[:, :d] + q_bias).astype(BF)
    k = pqk[:, d:].astype(BF)
    f = (product(n1, Wf) + f_bias).astype(BF)
    Fv = Fv.reshape(nc * rows, 2 * d)
    first = jnp.where(w % 2 == 0, Fv[:, :d], Fv[:, d:])
    v = jnp.where(low, f, first)

    o, lse = attend(H, qpos, bias, q, k, v)

    part = product(o, w_out).astype(BF)
    pieces, spread = lax.optimization_barrier((w_up, cotangent[0], X))[:2]
    Wup = exchange(pieces.reshape(d, nw, width).transpose(1, 0, 2)).reshape(width, width)
    unswap = [(b, a) for a, b in swap]
    cot = lax.all_gather(lax.ppermute(spread, both, unswap), "wt", axis=0, tiled=True)
    vec = jnp.stack([out_vector, gain_b, shift_b, bias_up.astype(F32)] + [out_vector] * 4)
    mlp, mid_own, d_mid, d_o, g_up, g_down, g_out, vsums = middle(
        G, False, part, X.reshape(nc, rows, width), cot, o, Wup, w_down, w_out, vec
    )

    mlp = lax.psum_scatter(mlp, "wt", scatter_dimension=0, tiled=True)
    layer = (mid_own + mlp.astype(F32) + down_vector).astype(BF)
    layer = lax.ppermute(layer, both, swap)
    up_rows = exchange(g_up.reshape(nw, d, width)).transpose(1, 0, 2)
    s_up, s_down = lax.psum((up_rows.reshape(d, nw * width), g_down), "ctx")
    dqk, dv = attend_back(H, qpos, lift, q, k, v, o, d_o, lse)
    zero = jnp.zeros_like(dv)
    df = jnp.where(low, dv, zero)
    dn1 = product_right(dqk, Wqk) + product_right(df, Wf)
    dn1_low = dn1.astype(BF)
    blank = jnp.zeros_like(dv)
    left = jnp.where(w == 2, dv, blank)
    right = jnp.where(w == 3, dv, blank)
    total = scatter_sum(
        G, jnp.concatenate([dn1_low, left, right], axis=1).reshape(nc, rows, width + 2 * d)
    )
    grad_first = lax.ppermute(total[:, width:].astype(BF), both, swap).astype(F32)
    block = (w * G + m) * rows
    x_own = lax.dynamic_slice_in_dim(X, block, rows).astype(F32)
    _, pull_one = jax.vjp(lambda a: norm_rows(a, gain_a, shift_a), x_own)
    d_x = d_mid.astype(F32) + pull_one(total[:, :width])[0]
    grad_tokens = lax.ppermute(d_x.astype(BF), both, swap).astype(F32)

    g_qk = product_left(n1, dqk)
    g_f = product_left(n1, df)
    normal = centred * inverse
    g_gain_one = jnp.sum(dn1_low.astype(F32) * normal, axis=0)
    g_shift_one = jnp.sum(dn1_low.astype(F32), axis=0)
    cols = jnp.concatenate(
        [
            g_qk.astype(BF),
            g_f.astype(BF),
            g_gain_one[:, None].astype(BF),
            g_shift_one[:, None].astype(BF),
            jnp.zeros((width, 62), BF),
        ],
        axis=1,
    ).reshape(nw, d, 640)
    sums = jnp.concatenate(
        [jnp.sum(dqk.astype(F32), axis=0), jnp.sum(df.astype(F32), axis=0), jnp.zeros((64,), F32)]
    ).astype(BF)
    foot = jnp.concatenate([sums[None], jnp.zeros((7, 640), BF)], axis=0)
    pack = jnp.concatenate([cols, jnp.broadcast_to(foot[None], (nw, 8, 640))], axis=1)
    pack = exchange(pack)
    vecs = jnp.concatenate(
        [
            vsums[0],
            mine(vsums[1]),
            mine(vsums[2]),
            mine(vsums[3]),
            mine(vsums[4]),
        ]
    ).astype(BF)
    pack = pack.at[0, d + 1 : d + 4, :512].set(vecs.reshape(3, 512))
    pack, s_up, s_down = lax.optimization_barrier((pack, s_up, s_down))
    pack, s_out = lax.psum((pack, g_out), "ctx")
    body = pack[:, :d]
    s_qkv = jnp.concatenate(
        [body[a, :, e * d : (e + 1) * d] for e in (0, 1) for a in range(nw)]
        + [body[a, :, 2 * d : 3 * d] for a in range(2)],
        axis=1,
    ).astype(F32)
    s_gain_one = jnp.sum(body[:, :, 576].astype(F32), axis=0)
    s_shift_one = jnp.sum(body[:, :, 577].astype(F32), axis=0)
    ends = pack[:, d]
    bias_all = jnp.concatenate([ends[:, :d].reshape(-1), ends[:2, 2 * d : 3 * d].reshape(-1)])
    s_bias_qv = lax.dynamic_slice_in_dim(bias_all, w * nb, nb).astype(F32)
    vecs = pack[0, d + 1 : d + 4, :512].reshape(-1).astype(F32)
    s_bias_up = vecs[:width]
    s_bias_down, s_bias_out, s_gain_two, s_shift_two = [
        vecs[width + a * d : width + (a + 1) * d] for a in range(4)
    ]
    return (
        layer[None],
        grad_tokens[None],
        grad_first[None],
        s_qkv,
        s_bias_qv,
        s_out.astype(F32),
        s_bias_out,
        s_gain_one,
        s_shift_one,
        s_gain_two,
        s_shift_two,
        s_up.astype(F32),
        s_bias_up,
        s_down.astype(F32),
        s_bias_down,
    )


def solution(mesh):
    rows3 = P("wt", "ctx", None)
    mat = P("wt", None)
    vec = P("wt")
    in_specs = (rows3, rows3, rows3, P(), mat, vec, mat) + (vec,) * 5 + (mat, vec, mat, vec)
    out_specs = (
        (rows3, rows3, rows3, mat, vec, mat) + (vec,) * 5 + (mat, vec, mat, vec)
    )
    return jax.shard_map(
        functools.partial(on_device, mesh.shape["wt"], mesh.shape["ctx"]),
        mesh=mesh,
        in_specs=in_specs,
        out_specs=out_specs,
        check_vma=False,
    )
```
